32 devices in a mesh: tok: 8 (over z, y), grp: 4 (over x, core).
Axes of the slice: x: 2, y: 2, z: 4, core: 2. Of those that a mesh axis runs over, the one named last changes fastest.
Arguments:
- tokens: bfloat16 [4, 8192, 768], P('grp', 'tok'), may hold values from -6 to 6
- cotangent: bfloat16 [4, 8192, 768], P('grp', 'tok'), may hold values from -6 to 6
- lengths: int32 [4, 3], P('grp'), may hold values from 2048 to 4096, as said below
- clusters: int32 [4, 24, 8192], P('grp', None, 'tok'), may hold values from 0 to 31, as said below
- owners: int32 [12], replicated, may hold values from 0 to 3, as said below
- master: float32 [768, 12, 768], P('tok', 'grp')
- bases: float32 [2, 12, 768, 768], P(None, 'grp')
- moment_one: float32 [768, 12, 768], P('tok', 'grp')
- moment_two: float32 [768, 12, 768], P('tok', 'grp')
- vectors: float32 [12, 768], replicated
- vector_one: float32 [12, 768], replicated
- vector_two: float32 [12, 768], replicated
Outputs:
- output: bfloat16 [4, 8192, 768], P('grp', 'tok')
- grad_tokens: float32 [4, 8192, 768], P('grp', 'tok')
- new_moment_one: float32 [768, 12, 768], P('tok', 'grp')
- new_moment_two: float32 [768, 12, 768], P('tok', 'grp')
- new_master: float32 [768, 12, 768], P('tok', 'grp')
- new_vector_one: float32 [12, 768], replicated
- new_vector_two: float32 [12, 768], replicated
- new_vectors: float32 [12, 768], replicated
The draws below stay inside these ranges and needn't reach their ends.
Inputs may be any that keep to these rules, and one draw needn't show every extreme that they name: `lengths`: in each group the items lie end to end and fill its 8192 tokens; 1 items have 4096 tokens and begin at multiples of 4096, all others have 2048. `clusters`: for every group, pair and item, each number below the item's length / 128 is given to exactly 128 of the item's tokens, and to the same number of tokens, 128 / (item length / 1024), from each run of 1024 consecutive tokens of the item. `owners`: every grp index owns exactly 12 / the size of grp blocks.
All inputs are finite; a program needn't handle non-finite values.
Results may differ from the reference program's by a relative error of at most 0.012.
The reference program's roundings to bfloat16 on the way count: a program that leaves them out, or rounds other values in their place, can miss the bound.
Values may be sent and summed in bfloat16 or wider, within the bound.
No kernel may reach another device: no remote copies, remote signals or barrier semaphores. Data moves between devices by JAX's collectives and lax.ppermute only.
A program may use at most 192 MiB of HBM per device.

```python
import jax
import jax.numpy as jnp
from jax import lax

D = 768
H = 12
FF = 3072
HEAD = 64
ROUNDS = 2
PAIRS = 24
CLUSTER = 128
TOK_DEV = 1024
GROUPS = 4
GROUP_TOK = 8192
SHORT_LEN = 2048
LONG_LEN = 4096
UNITS = 2
LONG_SEQS = 1
SEQS = 3
BLOCKS = 12
VECS = 12


def owner_table(key):
    shuffled = jax.random.permutation(jax.random.fold_in(key, 11), BLOCKS)
    return (shuffled // (BLOCKS // GROUPS)).astype(jnp.int32)


def slot_blocks(key):
    return jnp.argsort(owner_table(key), stable=True)


def weight_scales():
    index = jnp.arange(BLOCKS)
    table = jnp.full((BLOCKS,), D ** (-0.5), jnp.float32)
    table = jnp.where(index == 3, 0.5 * CLUSTER ** 0.5 * D ** (-0.5), table)
    return jnp.where(index >= 4 + FF // D, 1.5 * FF ** (-0.5), table).astype(jnp.float32)


def gradient_scales():
    index = jnp.arange(BLOCKS)
    table = jnp.where(index < 2, 0.3, jnp.where(index == 2, 0.4, jnp.where(index == 3, 0.1, jnp.where(index < 4 + FF // D, 0.75, 0.6))))
    return table.astype(jnp.float32) * float((GROUPS * GROUP_TOK) ** 0.5)


def vector_scales():
    index = jnp.arange(VECS)
    table = jnp.where(index < 2, 1.3, jnp.where(index < 4, 1.0, jnp.where(index == 4, 0.3, jnp.where(index == 5, 0.4, jnp.where(index < 8, 1.0, 0.75)))))
    return table.astype(jnp.float32) * float((GROUPS * GROUP_TOK) ** 0.5)


def one_group_lengths(key):
    picked = jax.random.permutation(key, UNITS)
    is_long = picked < LONG_SEQS
    per_unit = LONG_LEN // SHORT_LEN
    column = jnp.arange(per_unit)
    table = jnp.where(is_long[:, None], jnp.where(column[None, :] == 0, LONG_LEN, 0), SHORT_LEN)
    flat = table.reshape(-1).astype(jnp.int32)
    keep = jnp.argsort((flat == 0).astype(jnp.int32), stable=True)[:SEQS]
    return flat[keep].astype(jnp.int32)


def length_table(key):
    keys = jax.random.split(jax.random.fold_in(key, 5), GROUPS)
    return jax.vmap(one_group_lengths)(keys)


def one_group_clusters(key, item_lengths):
    item_ends = jnp.cumsum(item_lengths)
    item_starts = item_ends - item_lengths
    position = jnp.arange(GROUP_TOK, dtype=jnp.int32)
    inside = (item_starts[None, :] <= position[:, None]) & (position[:, None] < item_ends[None, :])
    start = jnp.sum(jnp.where(inside, item_starts[None, :], 0), axis=1)
    length = jnp.sum(jnp.where(inside, item_lengths[None, :], 0), axis=1)
    spans = jnp.maximum(1, length // TOK_DEV)
    run_len = length // spans
    run_start = start + (position - start) // run_len * run_len
    share = CLUSTER // spans

    def one_pair(pair_key):
        shuffled = jax.random.permutation(pair_key, GROUP_TOK)
        first_order = jnp.argsort(shuffled, stable=True)
        second_order = first_order[jnp.argsort(run_start[first_order], stable=True)]
        ranked = jnp.argsort(second_order, stable=True)
        return ((ranked - run_start) // share).astype(jnp.int32)
    return jax.vmap(one_pair)(jax.random.split(key, PAIRS))


def draw_lengths(key, part):
    return length_table(key)


def draw_clusters(key, part):
    table = length_table(key)
    keys = jax.random.split(jax.random.fold_in(key, 7), GROUPS)
    return jax.vmap(one_group_clusters)(keys, table)


def draw_owners(key, part):
    return owner_table(key)


def draw_master(key, part):
    order = slot_blocks(key)
    noise = jax.random.truncated_normal(jax.random.fold_in(key, 21), -6.0, 6.0, (D, BLOCKS, D), jnp.float32)
    return noise * weight_scales()[order][None, :, None]


def one_basis(key):
    first_key, second_key, third_key = jax.random.split(key, 3)
    shuffled = jax.random.permutation(first_key, D)
    row_sign = 2.0 * jax.random.randint(second_key, (D,), 0, 2).astype(jnp.float32) - 1.0
    col_sign = 2.0 * jax.random.randint(third_key, (D,), 0, 2).astype(jnp.float32) - 1.0
    freq = shuffled[:, None]
    column = jnp.arange(D)[None, :]
    phase = (2 * column + 1) * freq % (4 * D)
    wave = jnp.cos(jnp.pi * phase.astype(jnp.float32) / (2.0 * D))
    weight = jnp.where(freq == 0, (1.0 / D) ** 0.5, (2.0 / D) ** 0.5)
    return row_sign[:, None] * col_sign[None, :] * weight * wave


def draw_bases(key, part):
    keys = jax.random.split(jax.random.fold_in(key, 31), 2 * BLOCKS)
    return jax.vmap(one_basis)(keys).reshape(2, BLOCKS, D, D)


def draw_moment_one(key, part):
    order = slot_blocks(key)
    size = gradient_scales()[order][None, :, None]
    sign = 2.0 * jax.random.randint(jax.random.fold_in(key, 41), (D, BLOCKS, D), 0, 2).astype(jnp.float32) - 1.0
    magnitude = jax.random.uniform(jax.random.fold_in(key, 42), (D, BLOCKS, D), jnp.float32, 0.5, 1.5)
    return size * sign * magnitude


def draw_moment_two(key, part):
    order = slot_blocks(key)
    size = gradient_scales()[order][None, :, None]
    factor = jax.random.uniform(jax.random.fold_in(key, 51), (D, BLOCKS, D), jnp.float32, 1.0, 4.0)
    return size * size * factor


def draw_vectors(key, part):
    index = jnp.arange(VECS)[:, None]
    noise = jax.random.truncated_normal(jax.random.fold_in(key, 61), -3.0, 3.0, (VECS, D), jnp.float32)
    is_gain = (index == 0) | (index == 2)
    return jnp.where(is_gain, 1.0 + 0.2 * noise, 0.3 * noise)


def draw_vector_one(key, part):
    size = vector_scales()[:, None]
    sign = 2.0 * jax.random.randint(jax.random.fold_in(key, 71), (VECS, D), 0, 2).astype(jnp.float32) - 1.0
    magnitude = jax.random.uniform(jax.random.fold_in(key, 72), (VECS, D), jnp.float32, 0.5, 1.5)
    return size * sign * magnitude


def draw_vector_two(key, part):
    size = vector_scales()[:, None]
    factor = jax.random.uniform(jax.random.fold_in(key, 81), (VECS, D), jnp.float32, 1.0, 4.0)
    return size * size * factor


def steps_of(stream_key, dims, cuts, smallest, largest):
    loudness, own = 1.0, jax.random.fold_in(stream_key, 6)
    for dim, shards_of in cuts:
        draws = jnp.exp(jax.random.uniform(jax.random.fold_in(own, dim), (shards_of,), jnp.float32, smallest / len(cuts), largest / len(cuts)))
        loudness = loudness * jnp.repeat(draws, dims[dim] // shards_of).reshape([-1 if axis == dim else 1 for axis in range(len(dims))])
    return loudness


def gaussian(key, shape, width, reach, cuts=(), kind=jnp.bfloat16):
    loudness = steps_of(key, shape, cuts, -0.22, 0.18) if cuts else 1.0
    array = jax.random.normal(key, shape, jnp.float32) * width * loudness
    return jnp.minimum(jnp.maximum(array, -reach), reach).astype(kind)


def setup_inputs(seed: int = 0) -> dict:
    streams_of = jax.random.split(jax.random.key(seed), 13)
    tokens = gaussian(streams_of[0], (GROUPS, GROUP_TOK, D), 1.0, 6.0, ((0, 4), (1, 8)))
    cotangent = gaussian(streams_of[1], (GROUPS, GROUP_TOK, D), 1.0, 6.0, ((0, 4), (1, 8)))
    lengths = draw_lengths(jax.random.fold_in(streams_of[12], 71), 0)
    clusters = draw_clusters(jax.random.fold_in(streams_of[12], 71), 0)
    owners = draw_owners(jax.random.fold_in(streams_of[12], 71), 0)
    master = draw_master(jax.random.fold_in(streams_of[12], 71), 0)
    bases = draw_bases(jax.random.fold_in(streams_of[12], 71), 0)
    moment_one = draw_moment_one(jax.random.fold_in(streams_of[12], 71), 0)
    moment_two = draw_moment_two(jax.random.fold_in(streams_of[12], 71), 0)
    vectors = draw_vectors(jax.random.fold_in(streams_of[12], 71), 0)
    vector_one = draw_vector_one(jax.random.fold_in(streams_of[12], 71), 0)
    vector_two = draw_vector_two(jax.random.fold_in(streams_of[12], 71), 0)
    return dict(tokens=tokens, cotangent=cotangent, lengths=lengths, clusters=clusters, owners=owners, master=master, bases=bases, moment_one=moment_one, moment_two=moment_two, vectors=vectors, vector_one=vector_one, vector_two=vector_two)


@jax.custom_vjp
def low(v):
    return lax.optimization_barrier(v.astype(jnp.bfloat16)).astype(jnp.float32)

@jax.custom_vjp
def low_back(v):
    return v

def low_keep(v):
    return (low(v), None)

def low_pass(kept, grad):
    return (grad,)

def back_keep(v):
    return (v, None)

def back_low(kept, grad):
    return (low(grad),)
low.defvjp(low_keep, low_pass)
low_back.defvjp(back_keep, back_low)
EPS_NORM = 1e-05
ADAM_EPS = 1e-08
BETA_ONE = 0.5
BETA_TWO = 0.5
RATE_MATRIX = 0.025
RATE_VECTOR = 0.15

def product(left, right):
    return jnp.dot(left, right, precision=lax.Precision.HIGHEST, preferred_element_type=jnp.float32)

def layer_norm(values_in, gain, shift):
    centre = lax.optimization_barrier(jnp.mean(values_in, axis=-1, keepdims=True))
    offset = values_in - centre
    spread = lax.optimization_barrier(jnp.mean(offset * offset, axis=-1, keepdims=True))
    return offset * lax.rsqrt(spread + EPS_NORM) * gain + shift

def attend(grouped):
    query_rows = grouped[..., :HEAD]
    key_rows = grouped[..., HEAD:2 * HEAD]
    value_rows = grouped[..., 2 * HEAD:]
    scores = jnp.einsum('pucd,pued->puce', query_rows, key_rows, precision=lax.Precision.HIGHEST) * HEAD ** (-0.5)
    scores = low_back(scores)
    row_max = lax.optimization_barrier(jnp.max(scores, axis=-1, keepdims=True))
    expo = jnp.exp(scores - row_max)
    probs = expo / lax.optimization_barrier(jnp.sum(expo, axis=-1, keepdims=True))
    result = jnp.einsum('puce,pued->pucd', low(probs), value_rows, precision=lax.Precision.HIGHEST)
    return low_back(low(result))

def group_forward(inputs, item_lengths, cluster_local, blocks, vectors):
    w_qkv = blocks[:, 0:3, :].reshape(D, 3 * D)
    w_out = blocks[:, 3, :]
    w_up = blocks[:, 4:4 + FF // D, :].reshape(D, FF)
    w_down = jnp.transpose(blocks[:, 4 + FF // D:, :], (1, 0, 2)).reshape(FF, D)
    bias_qkv = jnp.concatenate([vectors[4], jnp.zeros((D,), jnp.float32), vectors[5]])
    qkv = low_back(low(product(inputs, w_qkv) + bias_qkv))
    heads = jnp.transpose(qkv.reshape(GROUP_TOK, 3, H, HEAD), (2, 0, 1, 3)).reshape(H, GROUP_TOK, 3 * HEAD)
    per_round = low_back(jnp.broadcast_to(heads[None], (ROUNDS, H, GROUP_TOK, 3 * HEAD)))
    per_round = per_round.reshape(PAIRS, GROUP_TOK, 3 * HEAD)
    position = jnp.arange(GROUP_TOK, dtype=jnp.int32)
    item_ends = jnp.cumsum(item_lengths).astype(jnp.int32)
    item_starts = (item_ends - item_lengths).astype(jnp.int32)
    start = lax.optimization_barrier(jnp.max(jnp.where(item_starts[None, :] <= position[:, None], item_starts[None, :], 0), axis=1)).astype(jnp.int32)
    global_cluster = (start[None, :] // CLUSTER + cluster_local).astype(jnp.int32)
    sort_order = jnp.argsort(global_cluster, axis=1, stable=True).astype(jnp.int32)
    inverse = jnp.argsort(sort_order, axis=1, stable=True).astype(jnp.int32)
    grouped = jnp.take_along_axis(per_round, sort_order[:, :, None], axis=1)
    grouped = grouped.reshape(PAIRS, GROUP_TOK // CLUSTER, CLUSTER, 3 * HEAD)
    outputs = jax.checkpoint(attend)(grouped).reshape(PAIRS, GROUP_TOK, HEAD)
    outputs = jnp.take_along_axis(outputs, inverse[:, :, None], axis=1)
    mixed = lax.optimization_barrier(jnp.mean(outputs.reshape(ROUNDS, H, GROUP_TOK, HEAD), axis=0))
    mixed = low(jnp.transpose(mixed, (1, 0, 2)).reshape(GROUP_TOK, D))
    attention = low_back(product(mixed, w_out) + vectors[6])
    hidden = layer_norm(inputs + attention, vectors[0], vectors[1])
    up_proj = low_back(product(low(hidden), w_up) + vectors[8:].reshape(FF))
    act = low(jax.nn.gelu(up_proj, approximate=False))
    down_proj = low_back(product(act, w_down) + vectors[7])
    return layer_norm(hidden + down_proj, vectors[2], vectors[3])

def reference(tokens, cotangent, lengths, clusters, owners, master, bases, moment_one, moment_two, vectors, vector_one, vector_two):
    slot_block = jnp.argsort(owners, stable=True).astype(jnp.int32)
    block_slot = jnp.argsort(slot_block, stable=True).astype(jnp.int32)
    blocks = jnp.take(master.astype(jnp.bfloat16).astype(jnp.float32), block_slot, axis=1)
    inputs = tokens.astype(jnp.float32)

    def forward(inputs, blocks, vectors):

        def one_group(items):
            return group_forward(items[0], items[1], items[2], blocks, vectors)
        return lax.map(jax.checkpoint(one_group), (inputs, lengths, clusters))
    result, pullback = jax.vjp(forward, inputs, blocks, vectors)
    grad_inputs, grad_blocks, grad_vectors = pullback(cotangent.astype(jnp.float32))
    grads = jnp.take(grad_blocks, slot_block, axis=1)
    left = bases[0]
    right = bases[1]
    inner = jnp.einsum('rse,sef->rsf', grads, right, precision=lax.Precision.HIGHEST)
    rotated = jnp.einsum('sri,rsf->isf', left, inner, precision=lax.Precision.HIGHEST)
    new_one = BETA_ONE * moment_one + (1.0 - BETA_ONE) * rotated
    new_two = BETA_TWO * moment_two + (1.0 - BETA_TWO) * rotated * rotated
    direction = new_one / (jnp.sqrt(new_two) + ADAM_EPS)
    turned = jnp.einsum('rse,sfe->rsf', direction, right, precision=lax.Precision.HIGHEST)
    change = jnp.einsum('sir,rsf->isf', left, turned, precision=lax.Precision.HIGHEST)
    new_master = master - RATE_MATRIX * change
    new_vec_one = BETA_ONE * vector_one + (1.0 - BETA_ONE) * grad_vectors
    new_vec_two = BETA_TWO * vector_two + (1.0 - BETA_TWO) * grad_vectors * grad_vectors
    new_vectors = vectors - RATE_VECTOR * new_vec_one / (jnp.sqrt(new_vec_two) + ADAM_EPS)
    return (result.astype(jnp.bfloat16), grad_inputs, new_one, new_two, new_master, new_vec_one, new_vec_two, new_vectors)
```

```python
import functools

import jax
import jax.numpy as jnp
from jax import lax
from jax.experimental import pallas as pl
from jax.experimental.pallas import tpu as pltpu
from jax.sharding import PartitionSpec as P

D = 768
H = 12
FF = 3072
HEAD = 64
ROUNDS = 2
PAIRS = 24
CLUSTER = 128
FFB = FF // D

EPS_NORM = 1e-05
ADAM_EPS = 1e-08
BETA_ONE = 0.5
BETA_TWO = 0.5
RATE_MATRIX = 0.025
RATE_VECTOR = 0.15
SQRT_HALF = 0.7071067811865476
INV_ROOT_TWO_PI = 0.3989422804014327

BF16 = jnp.bfloat16
F32 = jnp.float32

UNIT = 4
HEADS_OWN = H // UNIT
LOCAL_PAIRS = ROUNDS * HEADS_OWN
TILE = 128
WIDE = 2 * TILE


def inner_rows(left, right):
    return lax.dot_general(left, right, (((0,), (0,)), ((), ())), preferred_element_type=F32)


def outer_cols(left, right):
    return lax.dot_general(left, right, (((1,), (1,)), ((), ())), preferred_element_type=F32)


def normalize(values_in):
    centre = jnp.mean(values_in, axis=-1, keepdims=True)
    offset = values_in - centre
    spread = jnp.mean(offset * offset, axis=-1, keepdims=True)
    rstd = lax.rsqrt(spread + EPS_NORM)
    return (offset * rstd, rstd)


def norm_back(grad_normed, normed, rstd):
    first_mean = jnp.mean(grad_normed, axis=-1, keepdims=True)
    second_mean = jnp.mean(grad_normed * normed, axis=-1, keepdims=True)
    return rstd * (grad_normed - first_mean - normed * second_mean)


def gelu_slope(values_in):
    return (
        0.5 * (1.0 + lax.erf(values_in * SQRT_HALF))
        + values_in * jnp.exp(-0.5 * values_in * values_in) * INV_ROOT_TWO_PI
    )


def sort_body(order_ref, rows_ref, out_ref, column_ref):
    count = rows_ref.shape[0]

    @pl.when(pl.program_id(0) == 0)
    def _():
        column_ref[...] = jnp.transpose(order_ref[...])

    head = pl.program_id(0)
    chunk = 256
    lane = lax.broadcasted_iota(jnp.int32, (chunk, count), 1)
    for step in range(HEADS_OWN):

        @pl.when(head == step)
        def _():
            for turn in range(ROUNDS):
                pair = step * ROUNDS + turn
                for part in range(count // chunk):
                    where = pl.ds(part * chunk, chunk)
                    picked = (column_ref[where, pair : pair + 1] == lane).astype(F32).astype(BF16)
                    out_ref[turn, where, :] = jnp.dot(
                        picked, rows_ref[...], preferred_element_type=F32
                    ).astype(BF16)


def sort_rows(order, rows, width):
    count = rows.shape[0]
    return pl.pallas_call(
        sort_body,
        grid=(HEADS_OWN,),
        in_specs=[
            pl.BlockSpec((8, count), lambda h: (0, 0)),
            pl.BlockSpec((count, width), lambda h: (0, h)),
        ],
        out_specs=pl.BlockSpec((ROUNDS, count, width), lambda h: (h, 0, 0)),
        out_shape=jax.ShapeDtypeStruct((LOCAL_PAIRS, count, width), BF16),
        scratch_shapes=[pltpu.VMEM((count, 8), jnp.int32)],
        compiler_params=pltpu.CompilerParams(vmem_limit_bytes=48 << 20),
        name="sort_rows",
    )(order, rows)


def sort_grads_body(order_ref, rows_ref, out_ref, column_ref):
    count = rows_ref.shape[0]

    @pl.when(pl.program_id(0) == 0)
    def _():
        column_ref[...] = jnp.transpose(order_ref[...])

    head = pl.program_id(0)
    chunk = 256
    lane = lax.broadcasted_iota(jnp.int32, (chunk, count), 1)
    low = lax.broadcasted_iota(jnp.int32, (count, TILE), 1) < HEAD
    for step in range(HEADS_OWN):

        @pl.when(head == step)
        def _():
            tile = rows_ref[:, (step // 2) * TILE : (step // 2 + 1) * TILE]
            mask = low if step % 2 == 0 else jnp.logical_not(low)
            tile = jnp.where(mask, tile.astype(F32), 0.0).astype(BF16)
            for turn in range(ROUNDS):
                pair = step * ROUNDS + turn
                for part in range(count // chunk):
                    where = pl.ds(part * chunk, chunk)
                    picked = (column_ref[where, pair : pair + 1] == lane).astype(F32).astype(BF16)
                    out_ref[turn, where, :] = jnp.dot(
                        picked, tile, preferred_element_type=F32
                    ).astype(BF16)


def sort_grads(order, rows):
    count = rows.shape[0]
    return pl.pallas_call(
        sort_grads_body,
        grid=(HEADS_OWN,),
        in_specs=[
            pl.BlockSpec((8, count), lambda h: (0, 0)),
            pl.BlockSpec((count, WIDE), lambda h: (0, 0)),
        ],
        out_specs=pl.BlockSpec((ROUNDS, count, TILE), lambda h: (h, 0, 0)),
        out_shape=jax.ShapeDtypeStruct((LOCAL_PAIRS, count, TILE), BF16),
        scratch_shapes=[pltpu.VMEM((count, 8), jnp.int32)],
        compiler_params=pltpu.CompilerParams(vmem_limit_bytes=48 << 20),
        name="sort_grads",
    )(order, rows)


def clusters_of(count):
    share_long = CLUSTER // UNIT
    share_short = 2 * share_long
    return (
        [(tuple(range(UNIT)), share_long, count // share_long)],
        [
            (tuple(range(half * UNIT // 2, (half + 1) * UNIT // 2)), share_short, count // share_short)
            for half in range(2)
        ],
    )


def for_each_cluster(is_long, count, unroll, work):
    long_plan, short_plan = clusters_of(count)
    for wanted, plan in ((1, long_plan), (0, short_plan)):

        @pl.when(is_long == wanted)
        def _(plan=plan):
            for runs, share, clusters in plan:

                def step(group, carry, runs=runs, share=share):
                    for inner in range(unroll):
                        first = pl.multiple_of((group * unroll + inner) * share, share)
                        work(runs, pl.ds(first, share), share)
                    return carry

                lax.fori_loop(0, clusters // unroll, step, 0)


def softmax(rows):
    first, second = rows[:, :TILE], rows[:, TILE:]
    scores = outer_cols(first, second) * (HEAD**-0.5)
    peak = jnp.max(scores, axis=-1, keepdims=True)
    expo = jnp.exp(scores - peak)
    return first, second, expo / jnp.sum(expo, axis=-1, keepdims=True)


def attend_body(long_ref, *refs):
    grouped, results = refs[:UNIT], refs[UNIT:]
    count = grouped[0].shape[1]

    def work(runs, where, share):
        rows = jnp.concatenate([grouped[r][0, where, :] for r in runs], axis=0)
        first, _, probs = softmax(rows)
        mixed = jnp.dot(probs.astype(BF16), first, preferred_element_type=F32).astype(BF16)
        for i, r in enumerate(runs):
            results[r][0, where, :] = mixed[i * share : (i + 1) * share]

    for_each_cluster(long_ref[0], count, 4, work)


def attend(is_long, grouped):
    count = grouped[0].shape[1]
    return pl.pallas_call(
        attend_body,
        grid_spec=pltpu.PrefetchScalarGridSpec(
            num_scalar_prefetch=1,
            grid=(LOCAL_PAIRS,),
            in_specs=[pl.BlockSpec((1, count, WIDE), lambda p, _: (p, 0, 0))] * UNIT,
            out_specs=[pl.BlockSpec((1, count, TILE), lambda p, _: (p, 0, 0))] * UNIT,
        ),
        out_shape=[jax.ShapeDtypeStruct((LOCAL_PAIRS, count, TILE), BF16)] * UNIT,
        compiler_params=pltpu.CompilerParams(vmem_limit_bytes=48 << 20),
        name="attend",
    )(is_long, *grouped)


def attend_back_body(long_ref, *refs):
    grouped, grads, results = refs[:UNIT], refs[UNIT : 2 * UNIT], refs[2 * UNIT :]
    count = grouped[0].shape[1]
    odd = (pl.program_id(0) // ROUNDS) % 2
    lane = lax.broadcasted_iota(jnp.int32, (CLUSTER, TILE), 1)
    value_lane = (lane < HEAD) == (odd == 0)
    scale = HEAD**-0.5

    def work(runs, where, share):
        rows = jnp.concatenate([grouped[r][0, where, :] for r in runs], axis=0)
        grad = jnp.concatenate([grads[r][0, where, :] for r in runs], axis=0)
        first, second, probs = softmax(rows)
        probs_low = probs.astype(BF16)
        grad_probs = outer_cols(grad, first)
        centre = jnp.sum(probs * grad_probs, axis=-1, keepdims=True)
        grad_scores = (probs * (grad_probs - centre)).astype(BF16)
        grad_values = inner_rows(probs_low, grad)
        grad_query = jnp.dot(grad_scores, second, preferred_element_type=F32) * scale
        grad_keys = inner_rows(grad_scores, first) * scale
        tile_one = jnp.where(value_lane, grad_values, grad_query).astype(BF16)
        tile_two = jnp.where(value_lane, 0.0, grad_keys).astype(BF16)
        for i, r in enumerate(runs):
            part = slice(i * share, (i + 1) * share)
            results[r][0, where, 0:TILE] = tile_one[part]
            results[r][0, where, TILE:WIDE] = tile_two[part]

    for_each_cluster(long_ref[0], count, 4, work)


def attend_back(is_long, grouped, grads):
    count = grouped[0].shape[1]
    return pl.pallas_call(
        attend_back_body,
        grid_spec=pltpu.PrefetchScalarGridSpec(
            num_scalar_prefetch=1,
            grid=(LOCAL_PAIRS,),
            in_specs=[pl.BlockSpec((1, count, WIDE), lambda p, _: (p, 0, 0))] * UNIT
            + [pl.BlockSpec((1, count, TILE), lambda p, _: (p, 0, 0))] * UNIT,
            out_specs=[pl.BlockSpec((1, count, WIDE), lambda p, _: (p, 0, 0))] * UNIT,
        ),
        out_shape=[jax.ShapeDtypeStruct((LOCAL_PAIRS, count, WIDE), BF16)] * UNIT,
        compiler_params=pltpu.CompilerParams(vmem_limit_bytes=48 << 20),
        name="attend_back",
    )(is_long, *grouped, *grads)


def unsorted(order_ref, step, rows_ref, part, chunk):
    count = rows_ref.shape[1]
    row = lax.broadcasted_iota(jnp.int32, (chunk, count), 0) + part * chunk
    total = None
    for turn in range(ROUNDS):
        pair = step * ROUNDS + turn
        picked = (order_ref[pair : pair + 1, :] == row).astype(F32).astype(BF16)
        more = jnp.dot(picked, rows_ref[turn], preferred_element_type=F32)
        total = more if total is None else total + more
    return total


def mix_body(order_ref, rows_ref, out_ref):
    count = rows_ref.shape[1]
    chunk = 256
    low = lax.broadcasted_iota(jnp.int32, (chunk, TILE), 1) < HEAD
    head = pl.program_id(0)
    for step in range(HEADS_OWN):

        @pl.when(head == step)
        def _():
            for part in range(count // chunk):
                where = pl.ds(part * chunk, chunk)
                mean = (0.5 * unsorted(order_ref, step, rows_ref, part, chunk)).astype(BF16)
                if step == 0:
                    out_ref[where, 0:TILE] = mean
                elif step == 1:
                    out_ref[where, 0:TILE] = jnp.where(
                        low, out_ref[where, 0:TILE].astype(F32), mean.astype(F32)
                    ).astype(BF16)
                else:
                    out_ref[where, TILE:WIDE] = jnp.where(low, mean.astype(F32), 0.0).astype(BF16)


def mix(order, rows):
    count = rows.shape[1]
    return pl.pallas_call(
        mix_body,
        grid=(HEADS_OWN,),
        in_specs=[
            pl.BlockSpec((8, count), lambda h: (0, 0)),
            pl.BlockSpec((ROUNDS, count, TILE), lambda h: (h, 0, 0)),
        ],
        out_specs=pl.BlockSpec((count, WIDE), lambda h: (0, 0)),
        out_shape=jax.ShapeDtypeStruct((count, WIDE), BF16),
        compiler_params=pltpu.CompilerParams(vmem_limit_bytes=48 << 20),
        name="mix",
    )(order, rows)


def gather_grads_body(order_ref, rows_ref, out_ref):
    count = rows_ref.shape[1]
    chunk = 256
    head = pl.program_id(0)
    for step in range(HEADS_OWN):

        @pl.when(head == step)
        def _():
            for part in range(count // chunk):
                where = pl.ds(part * chunk, chunk)
                out_ref[where, :] = unsorted(order_ref, step, rows_ref, part, chunk).astype(BF16)


def gather_grads(order, rows):
    count = rows.shape[1]
    return pl.pallas_call(
        gather_grads_body,
        grid=(HEADS_OWN,),
        in_specs=[
            pl.BlockSpec((8, count), lambda h: (0, 0)),
            pl.BlockSpec((ROUNDS, count, WIDE), lambda h: (h, 0, 0)),
        ],
        out_specs=pl.BlockSpec((count, WIDE), lambda h: (0, h)),
        out_shape=jax.ShapeDtypeStruct((count, HEADS_OWN * WIDE), BF16),
        compiler_params=pltpu.CompilerParams(vmem_limit_bytes=48 << 20),
        name="gather_grads",
    )(order, rows)


def swap(value, axis, bit):
    size = lax.axis_size(axis)
    return lax.ppermute(value, axis, [(i, i ^ bit) for i in range(size)])


def gather_unit(rows):
    near = swap(rows, "tok", 1)
    far = swap(rows, "tok", 2)
    half = rows.shape[0] // 2
    across = jnp.concatenate([swap(near[:half], "tok", 2), swap(far[half:], "tok", 1)], axis=0)
    return [rows, near, far, across]


def exchange_unit(parts):
    return [parts[0]] + [swap(parts[k], "tok", k) for k in range(1, UNIT)]


def starts_of(lengths):
    index = jnp.arange(lengths.shape[0])
    return jnp.sum(jnp.where(index[None, :] < index[:, None], lengths[None, :], 0), axis=1)


def pick(values, index):
    return lax.dynamic_index_in_dim(values, index, 0, keepdims=False)


def turn_rows(value, place):
    n_tok = lax.axis_size("tok")
    slots, rows, width = value.shape
    parts = jnp.transpose(value.reshape(slots, n_tok, rows // n_tok, width), (1, 0, 2, 3))
    got = lax.all_to_all(parts, "tok", split_axis=0, concat_axis=0, tiled=True)
    got = jnp.stack([got[place.index(c)] for c in range(n_tok)], axis=2)
    return got.reshape(slots, rows // n_tok, n_tok * width)


def turn_columns(value, place):
    n_tok = lax.axis_size("tok")
    slots, rows, width = value.shape
    parts = value.reshape(slots, rows, n_tok, width // n_tok)
    parts = jnp.stack([parts[:, :, place[t]] for t in range(n_tok)], axis=0)
    got = lax.all_to_all(parts, "tok", split_axis=0, concat_axis=0, tiled=True)
    return jnp.transpose(got, (1, 0, 2, 3)).reshape(slots, n_tok * rows, width // n_tok)


def split_heads(columns):
    query, keys, values = (c.reshape(*c.shape[:-1], HEADS_OWN, HEAD) for c in columns)
    zero = jnp.zeros_like(query[..., 0, :])
    tiles = []
    for h in range(HEADS_OWN):
        q, k, v = query[..., h, :], keys[..., h, :], values[..., h, :]
        tiles += [v, q, zero, k] if h % 2 == 0 else [q, v, k, zero]
    return jnp.concatenate(tiles, axis=-1)


def join_heads(tiles):
    parts = tiles.reshape(*tiles.shape[:-1], HEADS_OWN, 4, HEAD)
    query = [parts[..., h, 1 if h % 2 == 0 else 0, :] for h in range(HEADS_OWN)]
    keys = [parts[..., h, 3 if h % 2 == 0 else 2, :] for h in range(HEADS_OWN)]
    values = [parts[..., h, 0 if h % 2 == 0 else 1, :] for h in range(HEADS_OWN)]
    return tuple(jnp.concatenate(p, axis=-1) for p in (query, keys, values))


def fast(
    tokens,
    cotangent,
    lengths,
    clusters,
    owners,
    master,
    bases,
    moment_one,
    moment_two,
    vectors,
    vector_one,
    vector_two,
):
    n_tok = lax.axis_size("tok")
    n_grp = lax.axis_size("grp")
    tok = lax.axis_index("tok")
    grp = lax.axis_index("grp")
    tok_count = tokens.shape[1]
    rows_dev = master.shape[0]
    slots = master.shape[1]
    blocks_all = slots * n_grp
    member = tok % UNIT
    unit = tok // UNIT
    place = [2 * (t % UNIT) + t // UNIT for t in range(n_tok)]
    own_width = HEADS_OWN * HEAD

    slot_block = jnp.argsort(owners, stable=True).astype(jnp.int32)
    block_slot = jnp.argsort(slot_block, stable=True).astype(jnp.int32)

    by_member = jnp.transpose(
        clusters[0].reshape(ROUNDS, UNIT, HEADS_OWN, tok_count), (1, 2, 0, 3)
    ).reshape(UNIT, LOCAL_PAIRS, tok_count)
    own_clusters = exchange_unit([pick(by_member, member ^ k) for k in range(UNIT)])
    order = jnp.argsort(jnp.stack(own_clusters), axis=-1, stable=True).astype(jnp.int32)
    order = jnp.pad(order, ((0, 0), (0, 8 - LOCAL_PAIRS), (0, 0)))
    orders = [order[k] for k in range(UNIT)]
    item_starts = starts_of(lengths[0])
    unit_start = unit * UNIT * tok_count
    middle = unit_start + UNIT // 2 * tok_count
    start_of_middle = jnp.max(jnp.where(item_starts <= middle, item_starts, 0))
    is_long = (start_of_middle <= unit_start).astype(jnp.int32).reshape(1)

    inputs = tokens[0]
    unit_inputs = gather_unit(inputs)

    local = jnp.transpose(master.astype(BF16), (1, 0, 2))
    weights = lax.all_gather(local, ("tok", "grp"), axis=0, tiled=False)
    weights = weights.reshape(n_tok, n_grp * slots, rows_dev, D)
    weights = jnp.transpose(weights, (1, 0, 2, 3)).reshape(blocks_all, D, D)
    block = [pick(weights, block_slot[b]) for b in range(blocks_all)]
    w_out = block[3]
    w_up = block[4 : 4 + FFB]
    w_down = block[4 + FFB :]

    def columns_of(value, m):
        return lax.dynamic_slice_in_dim(value, m * own_width, own_width, value.ndim - 1)

    own_weights = split_heads([columns_of(block[i], member) for i in range(3)])
    own_bias = split_heads(
        [columns_of(vectors[4], member), jnp.zeros((own_width,), F32), columns_of(vectors[5], member)]
    )
    grouped = []
    for k in range(UNIT):
        qkv = (jnp.dot(unit_inputs[k], own_weights, preferred_element_type=F32) + own_bias).astype(BF16)
        grouped.append(sort_rows(orders[k], qkv, WIDE))
    sorted_out = attend(is_long, grouped)
    mixed_parts = exchange_unit([mix(orders[k], sorted_out[k]) for k in range(UNIT)])
    mixed_low = jnp.concatenate([m[:, :own_width] for m in mixed_parts], axis=1)

    def rows_relative(value):
        return jnp.concatenate(
            [
                lax.dynamic_slice_in_dim(value, (member ^ k) * own_width, own_width, 0)
                for k in range(UNIT)
            ],
            axis=0,
        )

    w_out_relative = rows_relative(w_out)
    gain_one, shift_one, gain_two, shift_two = (vectors[i] for i in range(4))
    attention = jnp.dot(mixed_low, w_out_relative, preferred_element_type=F32) + vectors[6]
    first_sum = inputs.astype(F32) + attention
    normed_one, rstd_one = normalize(first_sum)
    hidden = normed_one * gain_one + shift_one
    hidden_low = hidden.astype(BF16)
    up_proj = [
        jnp.dot(hidden_low, w_up[j], preferred_element_type=F32) + vectors[8 + j] for j in range(FFB)
    ]
    act_low = [jax.nn.gelu(u, approximate=False).astype(BF16) for u in up_proj]
    down_proj = vectors[7] + sum(
        jnp.dot(act_low[j], w_down[j], preferred_element_type=F32) for j in range(FFB)
    )
    second_sum = hidden + down_proj
    normed_two, rstd_two = normalize(second_sum)
    result = (normed_two * gain_two + shift_two).astype(BF16)
    grad_result = cotangent[0].astype(F32)
    grad_gain_two = jnp.sum(grad_result * normed_two, axis=0)
    grad_shift_two = jnp.sum(grad_result, axis=0)
    grad_second = norm_back(grad_result * gain_two, normed_two, rstd_two)
    grad_down_low = grad_second.astype(BF16)
    grad_bias_down = jnp.sum(grad_down_low.astype(F32), axis=0)
    turned_down = [inner_rows(grad_down_low, act_low[j]) for j in range(FFB)]
    grad_up_low = [
        (outer_cols(grad_down_low, w_down[j]) * gelu_slope(up_proj[j])).astype(BF16) for j in range(FFB)
    ]
    turned_up = [inner_rows(grad_up_low[j], hidden_low) for j in range(FFB)]
    grad_bias_up = [jnp.sum(g.astype(F32), axis=0) for g in grad_up_low]
    grad_hidden = grad_second + sum(outer_cols(grad_up_low[j], w_up[j]) for j in range(FFB))
    grad_gain_one = jnp.sum(grad_hidden * normed_one, axis=0)
    grad_shift_one = jnp.sum(grad_hidden, axis=0)
    grad_first = norm_back(grad_hidden * gain_one, normed_one, rstd_one)
    grad_attn_low = grad_first.astype(BF16)
    turned_out = inner_rows(grad_attn_low, mixed_low)
    grad_bias_out = jnp.sum(grad_attn_low.astype(F32), axis=0)
    grad_mixed = (0.5 * outer_cols(grad_attn_low, w_out_relative)).astype(BF16)
    zero_half = jnp.zeros((tok_count, WIDE - own_width), BF16)
    grad_parts = exchange_unit(
        [
            jnp.concatenate([grad_mixed[:, k * own_width : (k + 1) * own_width], zero_half], axis=1)
            for k in range(UNIT)
        ]
    )
    sorted_grads = [sort_grads(orders[k], grad_parts[k]) for k in range(UNIT)]
    sorted_back = attend_back(is_long, grouped, sorted_grads)
    own_grads = [gather_grads(orders[k], sorted_back[k]) for k in range(UNIT)]
    turned_qkv = sum(inner_rows(own_grads[k], unit_inputs[k]) for k in range(UNIT))
    bias_qkv = sum(jnp.sum(own_grads[k].astype(F32), axis=0) for k in range(UNIT))
    home_grads = exchange_unit(own_grads)
    all_weights = jnp.stack(
        [split_heads([b[:, m * own_width : (m + 1) * own_width] for b in block[:3]]) for m in range(UNIT)]
    )
    grad_inputs = grad_first + sum(
        outer_cols(home_grads[k], pick(all_weights, member ^ k)) for k in range(UNIT)
    )

    bias_query, _, bias_value = join_heads(bias_qkv)
    bias_rows = lax.dynamic_update_slice_in_dim(
        jnp.zeros((2, D), F32), jnp.stack([bias_query, bias_value]), member * own_width, 1
    )
    vector_grads = jnp.concatenate(
        [
            jnp.stack([grad_gain_one, grad_shift_one, grad_gain_two, grad_shift_two]),
            bias_rows,
            jnp.stack([grad_bias_out, grad_bias_down] + grad_bias_up),
        ],
        axis=0,
    )
    vector_total = lax.psum(vector_grads, ("tok", "grp"))

    piece = D // n_tok // n_grp
    turned_out = jnp.concatenate(
        [turned_out[:, (0) : own_width]]
        + [turned_out[:, k * own_width : (k + 1) * own_width] for k in range(1, UNIT)],
        axis=1,
    )
    turned_out = jnp.transpose(turned_out.reshape(D, UNIT, own_width), (1, 0, 2))
    turned_out = jnp.concatenate([pick(turned_out, member ^ m) for m in range(UNIT)], axis=1)
    rest = jnp.stack([turned_out] + turned_up + turned_down).astype(BF16)
    rest = rest.reshape(blocks_all - 3, UNIT, n_tok // UNIT, n_grp, piece, D)
    rest = jnp.transpose(rest, (2, 1, 3, 0, 4, 5)).reshape(n_tok * n_grp, blocks_all - 3, piece, D)
    rest = lax.psum_scatter(rest, ("tok", "grp"), scatter_dimension=0, tiled=True)[0]
    sent = jnp.stack(
        [pick(rest, jnp.maximum(slot_block[s] - 3, 0)) for s in range(blocks_all)]
    ).reshape(n_grp, slots, piece, D)
    got = lax.all_to_all(sent, "grp", split_axis=0, concat_axis=0, tiled=True)
    got = jnp.transpose(got, (1, 0, 2, 3)).reshape(slots, n_grp * piece, D).astype(F32)

    turned_qkv = jnp.stack(join_heads(jnp.transpose(turned_qkv)))
    turned_qkv = jnp.transpose(turned_qkv.astype(BF16).reshape(3, D, 2, own_width // 2), (2, 0, 3, 1))
    keep = pick(turned_qkv, unit).astype(F32)
    keep = (keep + swap(pick(turned_qkv, 1 - unit), "tok", UNIT).astype(F32)).astype(BF16)
    keep = jnp.sum(lax.all_gather(keep, "grp", axis=0, tiled=False).astype(F32), axis=0)

    mine = lax.dynamic_slice_in_dim(slot_block, grp * slots, slots, 0)
    reduced = jnp.stack(
        [
            jnp.where(mine[s] < 3, pick(keep, jnp.minimum(mine[s], 2)), got[s]) for s in range(slots)
        ]
    )
    left, right = bases[0], bases[1]
    high = lax.Precision.HIGHEST
    part = jnp.einsum("sia,sci->sac", left, reduced, precision=high)
    part = turn_rows(part.astype(BF16), place).astype(F32)
    rotated = jnp.einsum("sac,scb->sab", part, right, precision=high)
    rotated = jnp.transpose(rotated, (1, 0, 2))
    new_one = BETA_ONE * moment_one + (1.0 - BETA_ONE) * rotated
    new_two = BETA_TWO * moment_two + (1.0 - BETA_TWO) * rotated * rotated
    direction = new_one / (jnp.sqrt(new_two) + ADAM_EPS)
    turned = jnp.einsum("asb,scb->sac", direction, right, precision=high)
    turned = turn_columns(turned.astype(BF16), place).astype(F32)
    change = jnp.einsum("sia,sac->sic", left, turned, precision=high)
    change = turn_rows(change.astype(BF16), place).astype(F32)
    new_master = master - RATE_MATRIX * jnp.transpose(change, (1, 0, 2))
    new_vec_one = BETA_ONE * vector_one + (1.0 - BETA_ONE) * vector_total
    new_vec_two = BETA_TWO * vector_two + (1.0 - BETA_TWO) * vector_total * vector_total
    new_vectors = vectors - RATE_VECTOR * new_vec_one / (jnp.sqrt(new_vec_two) + ADAM_EPS)
    return (
        result[None],
        grad_inputs[None],
        new_one,
        new_two,
        new_master,
        new_vec_one,
        new_vec_two,
        new_vectors,
    )


def general(
    tokens,
    cotangent,
    lengths,
    clusters,
    owners,
    master,
    bases,
    moment_one,
    moment_two,
    vectors,
    vector_one,
    vector_two,
):
    n_tok = lax.axis_size("tok")
    tok_count = tokens.shape[1]
    rows_dev = master.shape[0]
    slot_block = jnp.argsort(owners, stable=True)
    block_slot = jnp.argsort(slot_block, stable=True)
    slot_part = lax.all_gather(master.astype(jnp.bfloat16), "grp", axis=1, tiled=True)
    weights = lax.all_gather(slot_part, "tok", axis=0, tiled=True)
    blocks = jnp.stack([pick(jnp.transpose(weights, (1, 0, 2)), block_slot[b]) for b in range(weights.shape[1])], axis=1)
    w_qkv = blocks[:, 0:3, :].reshape(D, 3 * D)
    w_out = blocks[:, 3, :]
    w_up = blocks[:, 4 : 4 + FF // D, :].reshape(D, FF)
    w_down = jnp.transpose(blocks[:, 4 + FF // D :, :], (1, 0, 2)).reshape(FF, D)
    inputs = tokens[0]
    gain_one = vectors[0]
    shift_one = vectors[1]
    gain_two = vectors[2]
    shift_two = vectors[3]
    bias_qkv = jnp.concatenate([vectors[4], jnp.zeros((D,), jnp.float32), vectors[5]])
    qkv = (jnp.dot(inputs, w_qkv, preferred_element_type=jnp.float32) + bias_qkv).astype(
        jnp.bfloat16
    )
    heads = jnp.transpose(qkv.reshape(tok_count, 3, H, HEAD), (2, 0, 1, 3)).reshape(
        H, tok_count, 3 * HEAD
    )
    pair_rows = jnp.broadcast_to(heads[None], (ROUNDS, H, tok_count, 3 * HEAD)).reshape(
        PAIRS * tok_count, 3 * HEAD
    )
    position = lax.axis_index("tok") * tok_count + jnp.arange(tok_count, dtype=jnp.int32)
    item_starts = starts_of(lengths[0])
    item_start = jnp.max(
        jnp.where(item_starts[None, :] <= position[:, None], item_starts[None, :], 0), axis=1
    )
    per_dev = tok_count // CLUSTER
    group_clusters = n_tok * per_dev
    pair_ids = jnp.arange(PAIRS, dtype=jnp.int32)[:, None]
    global_cluster = item_start[None, :] // CLUSTER + clusters[0]
    unit_ids = (pair_ids * group_clusters + global_cluster).reshape(-1)
    owner_ids = ((global_cluster + pair_ids * per_dev) % n_tok).reshape(-1)
    send_order = jnp.argsort(owner_ids * (PAIRS * group_clusters) + unit_ids, stable=True)
    restore = jnp.argsort(send_order, stable=True)
    slot_rows = PAIRS * tok_count // n_tok
    units_here = PAIRS * tok_count // CLUSTER
    sent_rows = pair_rows[send_order].reshape(n_tok, slot_rows // 2, 6 * HEAD)
    sent_units = unit_ids[send_order].reshape(n_tok, slot_rows)
    got_rows, got_units = (
        lax.all_to_all(sent_rows, "tok", split_axis=0, concat_axis=0, tiled=True),
        lax.all_to_all(sent_units, "tok", split_axis=0, concat_axis=0, tiled=True),
    )
    arrange = jnp.argsort(got_units.reshape(-1), stable=True)
    undo = jnp.argsort(arrange, stable=True)
    grouped = got_rows.reshape(PAIRS * tok_count, 3 * HEAD)[arrange].reshape(
        units_here, CLUSTER, 3 * HEAD
    )
    query_rows = grouped[..., :HEAD]
    key_rows = grouped[..., HEAD : 2 * HEAD]
    value_rows = grouped[..., 2 * HEAD :]
    score_scale = HEAD ** (-0.5)
    scores = (
        jnp.einsum("ucd,ued->uce", query_rows, key_rows, preferred_element_type=jnp.float32)
        * score_scale
    )
    row_max = jnp.max(scores, axis=-1, keepdims=True)
    row_total = jnp.sum(jnp.exp(scores - row_max), axis=-1, keepdims=True)
    log_total = row_max + jnp.log(row_total)
    probs = jnp.exp(scores - log_total)
    cluster_out = jnp.einsum(
        "uce,ued->ucd", probs.astype(jnp.bfloat16), value_rows, preferred_element_type=jnp.float32
    ).astype(jnp.bfloat16)
    back_rows = cluster_out.reshape(PAIRS * tok_count, HEAD)[undo].reshape(
        n_tok, slot_rows // 2, 2 * HEAD
    )
    home_rows = lax.all_to_all(back_rows, "tok", split_axis=0, concat_axis=0, tiled=True)
    home_rows = (
        home_rows.reshape(PAIRS * tok_count, HEAD)[restore]
        .reshape(ROUNDS, H, tok_count, HEAD)
        .astype(jnp.float32)
    )
    mixed_heads = 0.5 * (home_rows[0] + home_rows[1])
    mixed_low = jnp.transpose(mixed_heads, (1, 0, 2)).reshape(tok_count, D).astype(jnp.bfloat16)
    attention = jnp.dot(mixed_low, w_out, preferred_element_type=jnp.float32) + vectors[6]
    first_sum = inputs.astype(jnp.float32) + attention
    normed_one, rstd_one = normalize(first_sum)
    hidden = normed_one * gain_one + shift_one
    hidden_low = hidden.astype(jnp.bfloat16)
    up_proj = jnp.dot(hidden_low, w_up, preferred_element_type=jnp.float32) + vectors[8:].reshape(
        FF
    )
    act_low = jax.nn.gelu(up_proj, approximate=False).astype(jnp.bfloat16)
    down_proj = jnp.dot(act_low, w_down, preferred_element_type=jnp.float32) + vectors[7]
    second_sum = hidden + down_proj
    normed_two, rstd_two = normalize(second_sum)
    result = (normed_two * gain_two + shift_two).astype(jnp.bfloat16)
    grad_result = cotangent[0].astype(jnp.float32)
    grad_gain_two = jnp.sum(grad_result * normed_two, axis=0)
    grad_shift_two = jnp.sum(grad_result, axis=0)
    grad_second = norm_back(grad_result * gain_two, normed_two, rstd_two)
    grad_down_low = grad_second.astype(jnp.bfloat16)
    grad_w_down = inner_rows(act_low, grad_down_low)
    grad_bias_down = jnp.sum(grad_down_low.astype(jnp.float32), axis=0)
    grad_act = outer_cols(grad_down_low, w_down)
    grad_up_low = (grad_act * gelu_slope(up_proj)).astype(jnp.bfloat16)
    grad_w_up = inner_rows(hidden_low, grad_up_low)
    grad_bias_up = jnp.sum(grad_up_low.astype(jnp.float32), axis=0)
    grad_hidden = grad_second + outer_cols(grad_up_low, w_up)
    grad_gain_one = jnp.sum(grad_hidden * normed_one, axis=0)
    grad_shift_one = jnp.sum(grad_hidden, axis=0)
    grad_first = norm_back(grad_hidden * gain_one, normed_one, rstd_one)
    grad_attn_low = grad_first.astype(jnp.bfloat16)
    grad_w_out = inner_rows(mixed_low, grad_attn_low)
    grad_bias_out = jnp.sum(grad_attn_low.astype(jnp.float32), axis=0)
    grad_mixed = outer_cols(grad_attn_low, w_out)
    grad_heads = jnp.transpose((0.5 * grad_mixed).reshape(tok_count, H, HEAD), (1, 0, 2)).astype(
        jnp.bfloat16
    )
    grad_pairs = jnp.broadcast_to(grad_heads[None], (ROUNDS, H, tok_count, HEAD)).reshape(
        PAIRS * tok_count, HEAD
    )
    sent_grad = grad_pairs[send_order].reshape(n_tok, slot_rows // 2, 2 * HEAD)
    got_grad = lax.all_to_all(sent_grad, "tok", split_axis=0, concat_axis=0, tiled=True)
    grad_cluster = got_grad.reshape(PAIRS * tok_count, HEAD)[arrange].reshape(
        units_here, CLUSTER, HEAD
    )
    scores_again = (
        jnp.einsum("ucd,ued->uce", query_rows, key_rows, preferred_element_type=jnp.float32)
        * score_scale
    )
    probs_again = jnp.exp(scores_again - log_total)
    probs_low = probs_again.astype(jnp.bfloat16)
    grad_values = jnp.einsum(
        "uce,ucd->ued", probs_low, grad_cluster, preferred_element_type=jnp.float32
    )
    grad_probs = jnp.einsum(
        "ucd,ued->uce", grad_cluster, value_rows, preferred_element_type=jnp.float32
    )
    centre = jnp.sum(probs_again * grad_probs, axis=-1, keepdims=True)
    grad_scores = (probs_again * (grad_probs - centre)).astype(jnp.bfloat16)
    grad_query = (
        jnp.einsum("uce,ued->ucd", grad_scores, key_rows, preferred_element_type=jnp.float32)
        * score_scale
    )
    grad_keys = (
        jnp.einsum("uce,ucd->ued", grad_scores, query_rows, preferred_element_type=jnp.float32)
        * score_scale
    )
    grad_grouped = jnp.concatenate(
        [
            grad_query.astype(jnp.bfloat16),
            grad_keys.astype(jnp.bfloat16),
            grad_values.astype(jnp.bfloat16),
        ],
        axis=-1,
    )
    back_grad = grad_grouped.reshape(PAIRS * tok_count, 3 * HEAD)[undo].reshape(
        n_tok, slot_rows // 2, 6 * HEAD
    )
    home_grad = lax.all_to_all(back_grad, "tok", split_axis=0, concat_axis=0, tiled=True)
    home_grad = (
        home_grad.reshape(PAIRS * tok_count, 3 * HEAD)[restore]
        .reshape(ROUNDS, H, tok_count, 3, HEAD)
        .astype(jnp.float32)
    )
    grad_qkv = (home_grad[0] + home_grad[1]).astype(jnp.bfloat16)
    grad_qkv = jnp.transpose(grad_qkv, (1, 2, 0, 3)).reshape(tok_count, 3 * D)
    grad_w_qkv = inner_rows(inputs, grad_qkv)
    grad_bias_qkv = jnp.sum(grad_qkv.astype(jnp.float32), axis=0)
    grad_inputs = grad_first + outer_cols(grad_qkv, w_qkv)
    grad_blocks = jnp.concatenate(
        [
            grad_w_qkv.reshape(D, 3, D),
            grad_w_out[:, None, :],
            grad_w_up.reshape(D, FF // D, D),
            jnp.transpose(grad_w_down.reshape(FF // D, D, D), (1, 0, 2)),
        ],
        axis=1,
    )
    by_block = jnp.transpose(grad_blocks, (1, 0, 2))
    slot_grads = jnp.stack([pick(by_block, slot_block[s]) for s in range(by_block.shape[0])], axis=1)
    vector_grads = jnp.concatenate(
        [
            jnp.stack(
                [
                    grad_gain_one,
                    grad_shift_one,
                    grad_gain_two,
                    grad_shift_two,
                    grad_bias_qkv[:D],
                    grad_bias_qkv[2 * D :],
                    grad_bias_out,
                    grad_bias_down,
                ]
            ),
            grad_bias_up.reshape(FF // D, D),
        ],
        axis=0,
    )
    vector_total = lax.psum(vector_grads, ("tok", "grp"))
    row_total = lax.psum_scatter(slot_grads, "tok", scatter_dimension=0, tiled=True)
    reduced = lax.psum_scatter(
        row_total.astype(jnp.bfloat16), "grp", scatter_dimension=1, tiled=True
    ).astype(jnp.float32)
    left_basis = bases[0]
    right_basis = bases[1]
    first_row = lax.axis_index("tok") * rows_dev
    turned_in = jnp.einsum("rse,sef->rsf", reduced, right_basis, precision=lax.Precision.HIGHEST)
    left_rows = lax.dynamic_slice_in_dim(left_basis, first_row, rows_dev, 1)
    picked = left_rows
    rotated = lax.psum_scatter(
        jnp.einsum("sri,rsf->isf", picked, turned_in, precision=lax.Precision.HIGHEST),
        "tok",
        scatter_dimension=0,
        tiled=True,
    )
    new_one = BETA_ONE * moment_one + (1.0 - BETA_ONE) * rotated
    new_two = BETA_TWO * moment_two + (1.0 - BETA_TWO) * rotated * rotated
    direction = new_one / (jnp.sqrt(new_two) + ADAM_EPS)
    turned_out = jnp.einsum("rse,sfe->rsf", direction, right_basis, precision=lax.Precision.HIGHEST)
    left_cols = lax.dynamic_slice_in_dim(left_basis, first_row, rows_dev, 2)
    picked = left_cols
    change = lax.psum_scatter(
        jnp.einsum("sir,rsf->isf", picked, turned_out, precision=lax.Precision.HIGHEST),
        "tok",
        scatter_dimension=0,
        tiled=True,
    )
    new_master = master - RATE_MATRIX * change
    new_vec_one = BETA_ONE * vector_one + (1.0 - BETA_ONE) * vector_total
    new_vec_two = BETA_TWO * vector_two + (1.0 - BETA_TWO) * vector_total * vector_total
    new_vectors = vectors - RATE_VECTOR * new_vec_one / (jnp.sqrt(new_vec_two) + ADAM_EPS)
    return (
        result[None],
        grad_inputs[None],
        new_one,
        new_two,
        new_master,
        new_vec_one,
        new_vec_two,
        new_vectors,
    )

def solution(mesh):
    n_tok, n_grp = mesh.shape["tok"], mesh.shape["grp"]

    def on_device(*args):
        lengths, clusters = args[2], args[3]
        unit = n_tok // (lengths.shape[1] - 1)
        suits = unit == UNIT and n_tok == 2 * UNIT and n_grp == 4 and clusters.shape[2] == 1024
        return (fast if suits else general)(*args)

    return jax.shard_map(
        on_device,
        mesh=mesh,
        in_specs=(
            P("grp", "tok", None),
            P("grp", "tok", None),
            P("grp", None),
            P("grp", None, "tok"),
            P(),
            P("tok", "grp", None),
            P(None, "grp", None, None),
            P("tok", "grp", None),
            P("tok", "grp", None),
            P(),
            P(),
            P(),
        ),
        out_specs=(
            P("grp", "tok", None),
            P("grp", "tok", None),
            P("tok", "grp", None),
            P("tok", "grp", None),
            P("tok", "grp", None),
            P(),
            P(),
            P(),
        ),
        check_vma=False,
    )
```

```python
import functools

import jax
import jax.numpy as jnp
from jax import lax
from jax.experimental import pallas as pl
from jax.experimental.pallas import tpu as pltpu
from jax.sharding import PartitionSpec as P

D = 768
H = 12
FF = 3072
HEAD = 64
ROUNDS = 2
PAIRS = 24
CLUSTER = 128
FFB = FF // D

EPS_NORM = 1e-05
ADAM_EPS = 1e-08
BETA_ONE = 0.5
BETA_TWO = 0.5
RATE_MATRIX = 0.025
RATE_VECTOR = 0.15
SQRT_HALF = 0.7071067811865476
INV_ROOT_TWO_PI = 0.3989422804014327

BF16 = jnp.bfloat16
F32 = jnp.float32

UNIT = 4
HEADS_OWN = H // UNIT
LOCAL_PAIRS = ROUNDS * HEADS_OWN
TILE = 128
WIDE = 2 * TILE


def inner_rows(left, right):
    return lax.dot_general(left, right, (((0,), (0,)), ((), ())), preferred_element_type=F32)


def outer_cols(left, right):
    return lax.dot_general(left, right, (((1,), (1,)), ((), ())), preferred_element_type=F32)


def normalize(values_in):
    centre = jnp.mean(values_in, axis=-1, keepdims=True)
    offset = values_in - centre
    spread = jnp.mean(offset * offset, axis=-1, keepdims=True)
    rstd = lax.rsqrt(spread + EPS_NORM)
    return (offset * rstd, rstd)


def norm_back(grad_normed, normed, rstd):
    first_mean = jnp.mean(grad_normed, axis=-1, keepdims=True)
    second_mean = jnp.mean(grad_normed * normed, axis=-1, keepdims=True)
    return rstd * (grad_normed - first_mean - normed * second_mean)


def gelu_slope(values_in):
    return (
        0.5 * (1.0 + lax.erf(values_in * SQRT_HALF))
        + values_in * jnp.exp(-0.5 * values_in * values_in) * INV_ROOT_TWO_PI
    )


def sort_body(order_ref, rows_ref, out_ref, column_ref):
    count = rows_ref.shape[0]

    @pl.when(pl.program_id(0) == 0)
    def _():
        column_ref[...] = jnp.transpose(order_ref[...])

    head = pl.program_id(0)
    chunk = 256
    lane = lax.broadcasted_iota(jnp.int32, (chunk, count), 1)
    for step in range(HEADS_OWN):

        @pl.when(head == step)
        def _():
            for turn in range(ROUNDS):
                pair = step * ROUNDS + turn
                for part in range(count // chunk):
                    where = pl.ds(part * chunk, chunk)
                    picked = (column_ref[where, pair : pair + 1] == lane).astype(F32).astype(BF16)
                    out_ref[turn, where, :] = jnp.dot(
                        picked, rows_ref[...], preferred_element_type=F32
                    ).astype(BF16)


def sort_rows(order, rows, width):
    count = rows.shape[0]
    return pl.pallas_call(
        sort_body,
        grid=(HEADS_OWN,),
        in_specs=[
            pl.BlockSpec((8, count), lambda h: (0, 0)),
            pl.BlockSpec((count, width), lambda h: (0, h)),
        ],
        out_specs=pl.BlockSpec((ROUNDS, count, width), lambda h: (h, 0, 0)),
        out_shape=jax.ShapeDtypeStruct((LOCAL_PAIRS, count, width), BF16),
        scratch_shapes=[pltpu.VMEM((count, 8), jnp.int32)],
        compiler_params=pltpu.CompilerParams(vmem_limit_bytes=48 << 20),
        name="sort_rows",
    )(order, rows)


def sort_grads_body(order_ref, rows_ref, out_ref, column_ref):
    count = order_ref.shape[1]
    half = count // 2

    @pl.when(pl.program_id(0) == 0)
    def _():
        column_ref[...] = jnp.transpose(order_ref[...])

    head = pl.program_id(0)
    chunk = 256
    lane = lax.broadcasted_iota(jnp.int32, (chunk, count), 1)
    low = lax.broadcasted_iota(jnp.int32, (count, TILE), 1) < HEAD
    for step in range(HEADS_OWN):

        @pl.when(head == step)
        def _():
            if step < 2:
                tile = rows_ref[0:count, :].astype(F32)
                tile = jnp.where(low if step == 0 else jnp.logical_not(low), tile, 0.0).astype(BF16)
            else:
                both = rows_ref[count : count + half, :].astype(F32)
                tile = jnp.concatenate([both, turn_half(both)], axis=0)
                tile = jnp.where(low, tile, 0.0).astype(BF16)
            for turn in range(ROUNDS):
                pair = step * ROUNDS + turn
                for part in range(count // chunk):
                    where = pl.ds(part * chunk, chunk)
                    picked = (column_ref[where, pair : pair + 1] == lane).astype(F32).astype(BF16)
                    out_ref[turn, where, :] = jnp.dot(
                        picked, tile, preferred_element_type=F32
                    ).astype(BF16)


def sort_grads(order, rows):
    count = order.shape[1]
    return pl.pallas_call(
        sort_grads_body,
        grid=(HEADS_OWN,),
        in_specs=[
            pl.BlockSpec((8, count), lambda h: (0, 0)),
            pl.BlockSpec(rows.shape, lambda h: (0, 0)),
        ],
        out_specs=pl.BlockSpec((ROUNDS, count, TILE), lambda h: (h, 0, 0)),
        out_shape=jax.ShapeDtypeStruct((LOCAL_PAIRS, count, TILE), BF16),
        scratch_shapes=[pltpu.VMEM((count, 8), jnp.int32)],
        compiler_params=pltpu.CompilerParams(vmem_limit_bytes=48 << 20),
        name="sort_grads",
    )(order, rows)


def plans_of(count):
    share = CLUSTER // UNIT
    half = UNIT // 2
    return (
        [(tuple(range(UNIT)), share)],
        [(tuple(range(i * half, (i + 1) * half)), 2 * share) for i in range(2)],
    )


def for_each_batch(is_long, count, batch, work):
    for wanted, plan in zip((1, 0), plans_of(count)):

        @pl.when(is_long == wanted)
        def _(plan=plan):
            for runs, share in plan:

                def step(group, carry, runs=runs, share=share):
                    first = pl.multiple_of(group * (batch * share), batch * share)
                    work(runs, pl.ds(first, batch * share), share)
                    return carry

                lax.fori_loop(0, count // share // batch, step, 0)


def batch_of(refs, runs, where, share, width):
    parts = [refs[r][0, where, :] for r in runs]
    return jnp.concatenate([p.reshape(p.shape[0] // share, share, width) for p in parts], axis=1)


def spread(refs, runs, where, share, columns, value):
    for i, r in enumerate(runs):
        part = value[:, i * share : (i + 1) * share]
        refs[r][0, where, columns] = part.reshape(part.shape[0] * share, TILE)


def products(form, left, right):
    return jnp.einsum(form, left, right, preferred_element_type=F32)


def softmax(first, second):
    scores = products("ued,ucd->uec", second, first) * (HEAD**-0.5)
    expo = jnp.exp(scores - jnp.max(scores, axis=1, keepdims=True))
    return expo * (1.0 / jnp.sum(expo, axis=1, keepdims=True))


def attend_body(long_ref, *refs):
    grouped, results = refs[:UNIT], refs[UNIT:]

    def work(runs, where, share):
        rows = batch_of(grouped, runs, where, share, WIDE)
        first = rows[..., :TILE]
        probs = softmax(first, rows[..., TILE:]).astype(BF16)
        mixed = products("uce,ued->ucd", jnp.swapaxes(probs, 1, 2), first).astype(BF16)
        spread(results, runs, where, share, slice(0, TILE), mixed)

    for_each_batch(long_ref[0], grouped[0].shape[1], 8, work)


def attend(is_long, grouped):
    count = grouped[0].shape[1]
    return pl.pallas_call(
        attend_body,
        grid_spec=pltpu.PrefetchScalarGridSpec(
            num_scalar_prefetch=1,
            grid=(LOCAL_PAIRS,),
            in_specs=[pl.BlockSpec((1, count, WIDE), lambda p, _: (p, 0, 0))] * UNIT,
            out_specs=[pl.BlockSpec((1, count, TILE), lambda p, _: (p, 0, 0))] * UNIT,
        ),
        out_shape=[jax.ShapeDtypeStruct((LOCAL_PAIRS, count, TILE), BF16)] * UNIT,
        compiler_params=pltpu.CompilerParams(vmem_limit_bytes=48 << 20),
        name="attend",
    )(is_long, *grouped)


def attend_back_body(long_ref, *refs):
    grouped, grads, results = refs[:UNIT], refs[UNIT : 2 * UNIT], refs[2 * UNIT :]
    batch = 16
    odd = (pl.program_id(0) // ROUNDS) % 2
    lane = lax.broadcasted_iota(jnp.int32, (batch, CLUSTER, TILE), 2)
    value_lane = (lane < HEAD) == (odd == 0)
    scale = HEAD**-0.5

    def work(runs, where, share):
        rows = batch_of(grouped, runs, where, share, WIDE)
        grad = batch_of(grads, runs, where, share, TILE)
        first, second = rows[..., :TILE], rows[..., TILE:]
        probs = softmax(first, second)
        grad_probs = products("ued,ucd->uec", first, grad)
        centre = jnp.sum(probs * grad_probs, axis=1, keepdims=True)
        grad_scores = (probs * (grad_probs - centre)).astype(BF16)
        grad_values = products("uec,ucd->ued", probs.astype(BF16), grad)
        grad_keys = products("uec,ucd->ued", grad_scores, first) * scale
        grad_query = products("uce,ued->ucd", jnp.swapaxes(grad_scores, 1, 2), second) * scale
        tile_one = jnp.where(value_lane, grad_values, grad_query).astype(BF16)
        tile_two = jnp.where(value_lane, 0.0, grad_keys).astype(BF16)
        spread(results, runs, where, share, slice(0, TILE), tile_one)
        spread(results, runs, where, share, slice(TILE, WIDE), tile_two)

    for_each_batch(long_ref[0], grouped[0].shape[1], batch, work)


def attend_back(is_long, grouped, grads):
    count = grouped[0].shape[1]
    return pl.pallas_call(
        attend_back_body,
        grid_spec=pltpu.PrefetchScalarGridSpec(
            num_scalar_prefetch=1,
            grid=(LOCAL_PAIRS,),
            in_specs=[pl.BlockSpec((1, count, WIDE), lambda p, _: (p, 0, 0))] * UNIT
            + [pl.BlockSpec((1, count, TILE), lambda p, _: (p, 0, 0))] * UNIT,
            out_specs=[pl.BlockSpec((1, count, WIDE), lambda p, _: (p, 0, 0))] * UNIT,
        ),
        out_shape=[jax.ShapeDtypeStruct((LOCAL_PAIRS, count, WIDE), BF16)] * UNIT,
        compiler_params=pltpu.CompilerParams(vmem_limit_bytes=56 << 20),
        name="attend_back",
    )(is_long, *grouped, *grads)


def unsorted(order_ref, step, rows_ref, part, chunk):
    count = rows_ref.shape[1]
    row = lax.broadcasted_iota(jnp.int32, (chunk, count), 0) + part * chunk
    total = None
    for turn in range(ROUNDS):
        pair = step * ROUNDS + turn
        picked = (order_ref[pair : pair + 1, :] == row).astype(F32).astype(BF16)
        more = jnp.dot(picked, rows_ref[turn], preferred_element_type=F32)
        total = more if total is None else total + more
    return total


def mix_body(order_ref, rows_ref, out_ref):
    count = rows_ref.shape[1]
    chunk = 256
    parts = count // chunk
    low = lax.broadcasted_iota(jnp.int32, (chunk, TILE), 1) < HEAD
    head = pl.program_id(0)
    for step in range(HEADS_OWN):

        @pl.when(head == step)
        def _():
            means = [0.5 * unsorted(order_ref, step, rows_ref, part, chunk) for part in range(parts)]
            for part in range(parts):
                where = pl.ds(part * chunk, chunk)
                if step == 0:
                    out_ref[where, :] = means[part].astype(BF16)
                elif step == 1:
                    out_ref[where, :] = jnp.where(low, out_ref[where, :].astype(F32), means[part]).astype(BF16)
                elif part < parts // 2:
                    both = jnp.where(low, means[part], turn_half(means[part + parts // 2]))
                    out_ref[pl.ds(count + part * chunk, chunk), :] = both.astype(BF16)


def mix(order, rows):
    count = rows.shape[1]
    packed = (count + count // 2, TILE)
    return pl.pallas_call(
        mix_body,
        grid=(HEADS_OWN,),
        in_specs=[
            pl.BlockSpec((8, count), lambda h: (0, 0)),
            pl.BlockSpec((ROUNDS, count, TILE), lambda h: (h, 0, 0)),
        ],
        out_specs=pl.BlockSpec(packed, lambda h: (0, 0)),
        out_shape=jax.ShapeDtypeStruct(packed, BF16),
        compiler_params=pltpu.CompilerParams(vmem_limit_bytes=48 << 20),
        name="mix",
    )(order, rows)


def gather_grads_body(order_ref, rows_ref, out_ref):
    count = rows_ref.shape[1]
    chunk = 256
    head = pl.program_id(0)
    for step in range(HEADS_OWN):

        @pl.when(head == step)
        def _():
            for part in range(count // chunk):
                where = pl.ds(part * chunk, chunk)
                out_ref[where, :] = unsorted(order_ref, step, rows_ref, part, chunk).astype(BF16)


def gather_grads(order, rows):
    count = rows.shape[1]
    return pl.pallas_call(
        gather_grads_body,
        grid=(HEADS_OWN,),
        in_specs=[
            pl.BlockSpec((8, count), lambda h: (0, 0)),
            pl.BlockSpec((ROUNDS, count, WIDE), lambda h: (h, 0, 0)),
        ],
        out_specs=pl.BlockSpec((count, WIDE), lambda h: (0, h)),
        out_shape=jax.ShapeDtypeStruct((count, HEADS_OWN * WIDE), BF16),
        compiler_params=pltpu.CompilerParams(vmem_limit_bytes=48 << 20),
        name="gather_grads",
    )(order, rows)


ERF_TOP = (0.00022905065861350646, 0.0034082910107109506, 0.050955695062380861, 0.18520832239976145, 1.128379143519084)
ERF_BOTTOM = (
    -1.1791602954361697e-7,
    0.000023547966471313185,
    0.0010179625278914885,
    0.014070470171167667,
    0.11098505178285362,
    0.49746925110067538,
    1.0,
)


def polynomial(value, factors):
    total = jnp.full_like(value, factors[0])
    for factor in factors[1:]:
        total = total * value + factor
    return total


def error_function(value):
    value = jnp.clip(value, -3.832506856900711, 3.832506856900711)
    square = value * value
    return value * polynomial(square, ERF_TOP) / polynomial(square, ERF_BOTTOM)


VEC_ROWS = 16
FFN_TILE = 256


def turn_half(value):
    return pltpu.roll(value, HEAD, 1)


def layer_body(
    n_shards,
    table_ref,
    *refs,
):
    shards, refs = refs[:n_shards], refs[n_shards:]
    parts, refs = refs[:UNIT], refs[UNIT:]
    x_ref, cot_ref, vec_ref, result_ref, first_ref, back_ref, sums_ref, pieces_ref = refs[:8]
    w_ref, packed_ref, mixed_ref, hidden_ref, act_ref, down_ref, up_ref, attn_ref = refs[8:16]
    slope_ref, stage_ref, weight_sem, part_sem, stage_sem = refs[16:]
    count = x_ref.shape[0]
    half = count // 2
    n_weights, shard_rows = shards[0].shape[:2]
    member = table_ref[0]
    for k in range(UNIT):
        pltpu.make_async_copy(parts[k], packed_ref.at[member ^ k], part_sem.at[k]).start()
    for b in range(n_weights):
        for n, shard in enumerate(shards):
            row = pl.multiple_of(table_ref[6 + n], shard_rows)
            pltpu.make_async_copy(
                shard.at[b], w_ref.at[b, pl.ds(row, shard_rows), :], weight_sem.at[b]
            ).start()
    for k in range(UNIT):
        pltpu.make_async_copy(parts[k], packed_ref.at[member ^ k], part_sem.at[k]).wait()
    for b in range(n_weights):
        pltpu.make_async_copy(w_ref.at[b], w_ref.at[b], weight_sem.at[b]).wait()

    sums_ref[...] = jnp.zeros_like(sums_ref)
    low = lax.broadcasted_iota(jnp.int32, (FFN_TILE, TILE), 1) < HEAD
    vec = [vec_ref[i : i + 1, :] for i in range(8 + FFB)]
    gain_one, shift_one, gain_two, shift_two = vec[:4]
    bias_out, bias_down = vec[6], vec[7]

    def add_sum(row, value):
        sums_ref[row : row + 1, :] += jnp.sum(value, axis=0, keepdims=True)

    def tile_step(i, carry):
        rows = pl.ds(pl.multiple_of(i * FFN_TILE, FFN_TILE), FFN_TILE)
        is_first = i * FFN_TILE < half
        extra = pl.ds(pl.multiple_of(count + lax.rem(i * FFN_TILE, half), FFN_TILE), FFN_TILE)

        def pair(m):
            return packed_ref[m, rows, :].astype(F32)

        def single(m):
            value = packed_ref[m, extra, :].astype(F32)
            return jnp.where(is_first, value, turn_half(value))

        for m in (0, 2):
            at = m * (HEADS_OWN * HEAD)
            nxt = turn_half(pair(m + 1))
            mixed_ref[rows, at : at + TILE] = pair(m).astype(BF16)
            mixed_ref[rows, at + TILE : at + 2 * TILE] = jnp.where(low, single(m), nxt).astype(BF16)
            mixed_ref[rows, at + 2 * TILE : at + 3 * TILE] = jnp.where(
                low, nxt, turn_half(single(m + 1))
            ).astype(BF16)
        attention = jnp.dot(mixed_ref[rows, :], w_ref[0], preferred_element_type=F32) + bias_out
        normed_one, rstd_one = normalize(x_ref[rows, :].astype(F32) + attention)
        hidden = normed_one * gain_one + shift_one
        hidden_low = hidden.astype(BF16)
        hidden_ref[rows, :] = hidden_low
        down = jnp.broadcast_to(bias_down, hidden.shape)
        for j in range(FFB):
            up = jnp.dot(hidden_low, w_ref[1 + j], preferred_element_type=F32) + vec[8 + j]
            phi = 0.5 * (1.0 + error_function(up * SQRT_HALF))
            slope_ref[j] = phi + up * jnp.exp(-0.5 * up * up) * INV_ROOT_TWO_PI
            act = (up * phi).astype(BF16)
            act_ref[j, rows, :] = act
            down = down + jnp.dot(act, w_ref[1 + FFB + j], preferred_element_type=F32)
        normed_two, rstd_two = normalize(hidden + down)
        result_ref[rows, :] = (normed_two * gain_two + shift_two).astype(BF16)
        grad_result = cot_ref[rows, :].astype(F32)
        add_sum(2, grad_result * normed_two)
        add_sum(3, grad_result)
        grad_second = norm_back(grad_result * gain_two, normed_two, rstd_two)
        grad_down = grad_second.astype(BF16)
        down_ref[rows, :] = grad_down
        add_sum(7, grad_down.astype(F32))
        grad_hidden = grad_second
        for j in range(FFB):
            grad_up = (outer_cols(grad_down, w_ref[1 + FFB + j]) * slope_ref[j]).astype(BF16)
            up_ref[j, rows, :] = grad_up
            add_sum(8 + j, grad_up.astype(F32))
            grad_hidden = grad_hidden + outer_cols(grad_up, w_ref[1 + j])
        add_sum(0, grad_hidden * normed_one)
        add_sum(1, grad_hidden)
        grad_first = norm_back(grad_hidden * gain_one, normed_one, rstd_one)
        first_ref[rows, :] = grad_first
        grad_attn = grad_first.astype(BF16)
        attn_ref[rows, :] = grad_attn
        add_sum(6, grad_attn.astype(F32))
        grad_mixed = (0.5 * outer_cols(grad_attn, w_ref[0])).astype(BF16).astype(F32)
        for m in range(UNIT):
            at = (m // 2) * 3 * TILE
            tiles = [grad_mixed[:, at + n * TILE : at + (n + 1) * TILE] for n in range(3)]
            if m % 2 == 0:
                two, one = tiles[0], tiles[1]
            else:
                two, one = turn_half(jnp.where(low, tiles[2], tiles[1])), turn_half(tiles[2])
            back_ref[member ^ m, rows, :] = two.astype(BF16)

            @pl.when(is_first)
            def _(one=one, m=m):
                back_ref[member ^ m, extra, :] = jnp.where(low, one, 0.0).astype(BF16)

            @pl.when(jnp.logical_not(is_first))
            def _(one=one, m=m):
                old = back_ref[member ^ m, extra, :].astype(F32)
                back_ref[member ^ m, extra, :] = jnp.where(low, old, turn_half(one)).astype(BF16)

        return carry

    lax.fori_loop(0, count // FFN_TILE, tile_step, 0)

    core, bits = table_ref[1], [table_ref[2 + d] for d in range(4)]
    piece, half_columns = pieces_ref.shape[4:]
    n_parts = pieces_ref.shape[1]

    def copies(block, slot):
        part = block // (n_weights // n_parts)
        made = []
        for index in range(2 * 16):
            c = (index % 2) ^ core
            x, zh, y, zl = ((index >> s) % 2 for s in (1, 2, 3, 4))
            rel = {"x": x ^ bits[0], "y": y ^ bits[1], "zl": zl ^ bits[2], "zh": zh ^ bits[3]}
            place = 0
            for name in PART_ORDERS[part]:
                place = place * 2 + rel[name]
            made.append(
                pltpu.make_async_copy(
                    stage_ref.at[
                        slot,
                        pl.ds(index // 2 * piece, piece),
                        pl.ds(index % 2 * half_columns, half_columns),
                    ],
                    pieces_ref.at[c, part, place, block % (n_weights // n_parts)],
                    stage_sem.at[slot, index],
                )
            )
        return made

    plan = [(attn_ref, None, mixed_ref, None, 0)]
    plan += [(down_ref, None, act_ref, j, 1 + FFB + j) for j in range(FFB)]
    plan += [(up_ref, j, hidden_ref, None, 1 + j) for j in range(FFB)]
    pending = [None, None]
    for n, (left, lj, right, rj, block) in enumerate(plan):
        slot = n % 2
        if pending[slot] is not None:
            for copy in pending[slot]:
                copy.wait()
        value = inner_rows(
            left[...] if lj is None else left[lj], right[...] if rj is None else right[rj]
        )
        stage_ref[slot] = value.astype(BF16)
        pending[slot] = copies(block, slot)
        for copy in pending[slot]:
            copy.start()
    for group in pending:
        for copy in group:
            copy.wait()


PART_ORDERS = (("x", "y", "zl", "zh"), ("y", "zl", "zh", "x"), ("zl", "zh", "x", "y"))


def layer(table, shards, parts, inputs, cotangent, vectors):
    count = inputs.shape[0]
    n_weights = 1 + 2 * FFB
    n_shards = len(shards)
    anywhere = pl.BlockSpec(memory_space=pl.ANY)
    inside = pl.BlockSpec(memory_space=pltpu.VMEM)
    packed = parts[0].shape
    return pl.pallas_call(
        functools.partial(layer_body, n_shards),
        in_specs=[pl.BlockSpec(memory_space=pltpu.SMEM)] + [anywhere] * (n_shards + UNIT) + [inside] * 3,
        out_specs=[inside, inside, inside, inside, anywhere],
        out_shape=[
            jax.ShapeDtypeStruct((count, D), BF16),
            jax.ShapeDtypeStruct((count, D), F32),
            jax.ShapeDtypeStruct((UNIT, *packed), BF16),
            jax.ShapeDtypeStruct((VEC_ROWS, D), F32),
            jax.ShapeDtypeStruct((2, 3, 16, n_weights // 3, D // 16, D // 2), BF16),
        ],
        scratch_shapes=[
            pltpu.VMEM((n_weights, D, D), BF16),
            pltpu.VMEM((UNIT, *packed), BF16),
            pltpu.VMEM((count, D), BF16),
            pltpu.VMEM((count, D), BF16),
            pltpu.VMEM((FFB, count, D), BF16),
            pltpu.VMEM((count, D), BF16),
            pltpu.VMEM((FFB, count, D), BF16),
            pltpu.VMEM((count, D), BF16),
            pltpu.VMEM((FFB, FFN_TILE, D), F32),
            pltpu.VMEM((2, D, D), BF16),
            pltpu.SemaphoreType.DMA((n_weights,)),
            pltpu.SemaphoreType.DMA((UNIT,)),
            pltpu.SemaphoreType.DMA((2, 32)),
        ],
        compiler_params=pltpu.CompilerParams(vmem_limit_bytes=60 << 20),
        name="layer",
    )(table, *shards, *parts, inputs, cotangent, vectors)


def swap(value, axis, bit):
    size = lax.axis_size(axis)
    return lax.ppermute(value, axis, [(i, i ^ bit) for i in range(size)])


def gather_unit(rows):
    near = swap(rows, "tok", 1)
    far = swap(rows, "tok", 2)
    half = rows.shape[0] // 2
    across = jnp.concatenate([swap(near[:half], "tok", 2), swap(far[half:], "tok", 1)], axis=0)
    return [rows, near, far, across]


def exchange_unit(parts):
    return [parts[0]] + [swap(parts[k], "tok", k) for k in range(1, UNIT)]


LINKS = {"x": ("grp", 2), "y": ("tok", 1), "zl": ("tok", 2), "zh": ("tok", 4)}


def reduce_pieces(pieces):
    other = swap(pieces[1], "grp", 1)
    done = []
    for part, names in enumerate(PART_ORDERS):
        value = pieces[0, part].astype(F32) + other[part].astype(F32)
        for name in names:
            half = value.shape[0] // 2
            value = value[:half] + swap(value[half:].astype(BF16), *LINKS[name]).astype(F32)
        done.append(value[0].astype(BF16))
    return jnp.concatenate(done, axis=0)


def starts_of(lengths):
    index = jnp.arange(lengths.shape[0])
    return jnp.sum(jnp.where(index[None, :] < index[:, None], lengths[None, :], 0), axis=1)


def total_of(value):
    for axis in ("grp", "tok"):
        bit = 1
        while bit < lax.axis_size(axis):
            value = value + swap(value, axis, bit)
            bit *= 2
    return value


def pick(values, index):
    return lax.dynamic_index_in_dim(values, index, 0, keepdims=False)


def turn_rows(value, place):
    n_tok = lax.axis_size("tok")
    slots, rows, width = value.shape
    parts = jnp.transpose(value.reshape(slots, n_tok, rows // n_tok, width), (1, 0, 2, 3))
    got = lax.all_to_all(parts, "tok", split_axis=0, concat_axis=0, tiled=True)
    got = jnp.stack([got[place.index(c)] for c in range(n_tok)], axis=2)
    return got.reshape(slots, rows // n_tok, n_tok * width)


def turn_columns(value, place):
    n_tok = lax.axis_size("tok")
    slots, rows, width = value.shape
    parts = value.reshape(slots, rows, n_tok, width // n_tok)
    parts = jnp.stack([parts[:, :, place[t]] for t in range(n_tok)], axis=0)
    got = lax.all_to_all(parts, "tok", split_axis=0, concat_axis=0, tiled=True)
    return jnp.transpose(got, (1, 0, 2, 3)).reshape(slots, n_tok * rows, width // n_tok)


def split_heads(columns):
    query, keys, values = (c.reshape(*c.shape[:-1], HEADS_OWN, HEAD) for c in columns)
    zero = jnp.zeros_like(query[..., 0, :])
    tiles = []
    for h in range(HEADS_OWN):
        q, k, v = query[..., h, :], keys[..., h, :], values[..., h, :]
        tiles += [v, q, zero, k] if h % 2 == 0 else [q, v, k, zero]
    return jnp.concatenate(tiles, axis=-1)


def join_heads(tiles):
    parts = tiles.reshape(*tiles.shape[:-1], HEADS_OWN, 4, HEAD)
    query = [parts[..., h, 1 if h % 2 == 0 else 0, :] for h in range(HEADS_OWN)]
    keys = [parts[..., h, 3 if h % 2 == 0 else 2, :] for h in range(HEADS_OWN)]
    values = [parts[..., h, 0 if h % 2 == 0 else 1, :] for h in range(HEADS_OWN)]
    return tuple(jnp.concatenate(p, axis=-1) for p in (query, keys, values))


def fast(
    tokens,
    cotangent,
    lengths,
    clusters,
    owners,
    master,
    bases,
    moment_one,
    moment_two,
    vectors,
    vector_one,
    vector_two,
):
    n_tok = lax.axis_size("tok")
    n_grp = lax.axis_size("grp")
    tok = lax.axis_index("tok")
    grp = lax.axis_index("grp")
    tok_count = tokens.shape[1]
    rows_dev = master.shape[0]
    slots = master.shape[1]
    blocks_all = slots * n_grp
    member = tok % UNIT
    unit = tok // UNIT
    place = [2 * (t % UNIT) + t // UNIT for t in range(n_tok)]
    own_width = HEADS_OWN * HEAD

    slot_block = jnp.argsort(owners, stable=True).astype(jnp.int32)
    block_slot = jnp.argsort(slot_block, stable=True).astype(jnp.int32)

    by_member = jnp.transpose(
        clusters[0].reshape(ROUNDS, UNIT, HEADS_OWN, tok_count), (1, 2, 0, 3)
    ).reshape(UNIT, LOCAL_PAIRS, tok_count)
    own_clusters = exchange_unit([pick(by_member, member ^ k) for k in range(UNIT)])
    order = jnp.argsort(jnp.stack(own_clusters), axis=-1, stable=True).astype(jnp.int32)
    order = jnp.pad(order, ((0, 0), (0, 8 - LOCAL_PAIRS), (0, 0)))
    orders = [order[k] for k in range(UNIT)]
    item_starts = starts_of(lengths[0])
    unit_start = unit * UNIT * tok_count
    middle = unit_start + UNIT // 2 * tok_count
    start_of_middle = jnp.max(jnp.where(item_starts <= middle, item_starts, 0))
    is_long = (start_of_middle <= unit_start).astype(jnp.int32).reshape(1)

    inputs = tokens[0]
    unit_inputs = gather_unit(inputs)
    core, bit_x = grp % 2, grp // 2

    local = jnp.transpose(master.astype(BF16), (1, 0, 2))
    beside = swap(local, "grp", 1)
    over = swap(local, "grp", 2)
    by_slot = jnp.concatenate([local, beside, over, swap(over, "grp", 1)], axis=0)
    at = [((block_slot[b] // slots) ^ grp) * slots + block_slot[b] % slots for b in range(blocks_all)]
    rows_of = [pick(by_slot, at[b]) for b in range(blocks_all)]

    def columns_of(value, m):
        return lax.dynamic_slice_in_dim(value, m * own_width, own_width, value.ndim - 1)

    by_owner = jnp.stack(
        [split_heads([r[:, m * own_width : (m + 1) * own_width] for r in rows_of[:3]]) for m in range(UNIT)]
    )
    got = [pick(by_owner, member)]
    got += [swap(pick(by_owner, member ^ (k % UNIT)), "tok", k) for k in range(1, n_tok)]
    got = jnp.stack(got)
    own_weights = jnp.concatenate([pick(got, tok ^ t) for t in range(n_tok)], axis=0)

    part_rows = rows_dev // 2
    rest_rows = jnp.stack(
        [lax.dynamic_slice_in_dim(r, core * part_rows, part_rows, 0) for r in rows_of[3:]]
    )
    rest_rows, _ = lax.optimization_barrier((rest_rows, unit_inputs[3]))
    shards, firsts = [], []
    step = rest_rows
    for k in range(n_tok // 2):
        if k:
            step = lax.ppermute(step, "tok", [(i, (i + 2) % n_tok) for i in range(n_tok)])
        for flip, value in ((0, step), (1, swap(step, "tok", 1))):
            source = (tok - 2 * k) % n_tok ^ flip
            for other in range(2):
                shards.append(swap(value, "grp", 1) if other else value)
                firsts.append(source * rows_dev + (core ^ other) * part_rows)

    own_bias = split_heads(
        [columns_of(vectors[4], member), jnp.zeros((own_width,), F32), columns_of(vectors[5], member)]
    )
    grouped = []
    for k in range(UNIT):
        qkv = (jnp.dot(unit_inputs[k], own_weights, preferred_element_type=F32) + own_bias).astype(BF16)
        grouped.append(sort_rows(orders[k], qkv, WIDE))
    sorted_out = attend(is_long, grouped)
    mixed_parts = exchange_unit([mix(orders[k], sorted_out[k]) for k in range(UNIT)])
    held_weights, *mixed_parts = lax.optimization_barrier((own_weights, *mixed_parts))
    turned_weights = [swap(held_weights, "tok", k) for k in range(1, UNIT)]
    table = jnp.stack([member, core, bit_x, tok % 2, tok // 2 % 2, tok // 4, *firsts]).astype(jnp.int32)
    result, grad_first, back, sums, pieces = layer(
        table, shards, mixed_parts, inputs, cotangent[0], vectors
    )
    grad_parts = exchange_unit([back[k] for k in range(UNIT)])
    sorted_grads = [sort_grads(orders[k], grad_parts[k]) for k in range(UNIT)]
    rest = reduce_pieces(pieces)
    sorted_back = attend_back(is_long, grouped, sorted_grads)
    own_grads = [gather_grads(orders[k], sorted_back[k]) for k in range(UNIT)]
    turned_qkv = sum(inner_rows(own_grads[k], unit_inputs[k]) for k in range(UNIT))
    bias_qkv = sum(jnp.sum(own_grads[k].astype(F32), axis=0) for k in range(UNIT))
    home_grads = exchange_unit(own_grads)
    grad_inputs = grad_first + sum(
        outer_cols(home_grads[k], own_weights if k == 0 else turned_weights[k - 1]) for k in range(UNIT)
    )

    bias_query, _, bias_value = join_heads(bias_qkv)
    bias_rows = lax.dynamic_update_slice_in_dim(
        jnp.zeros((2, D), F32), jnp.stack([bias_query, bias_value]), member * own_width, 1
    )
    vector_grads = sums[: 8 + FFB] + jnp.pad(bias_rows, ((4, 2 + FFB), (0, 0)))
    vector_total = total_of(vector_grads)

    sent = jnp.stack(
        [pick(rest, jnp.maximum(slot_block[s] - 3, 0)) for s in range(blocks_all)]
    ).reshape(n_grp, slots, *rest.shape[1:])
    got = lax.all_to_all(sent, "grp", split_axis=0, concat_axis=0, tiled=True)
    got = jnp.transpose(got.reshape(2, 2, *got.shape[1:]), (2, 0, 3, 1, 4))
    got = got.reshape(slots, D // n_tok, D).astype(F32)

    turned_qkv = jnp.stack(join_heads(jnp.transpose(turned_qkv)))
    turned_qkv = jnp.transpose(turned_qkv.astype(BF16).reshape(3, D, 2, own_width // 2), (2, 0, 3, 1))
    keep = pick(turned_qkv, unit).astype(F32)
    keep = keep + swap(pick(turned_qkv, 1 - unit), "tok", UNIT).astype(F32)
    keep = keep + swap(keep.astype(BF16), "grp", 1).astype(F32)
    keep = keep + swap(keep.astype(BF16), "grp", 2).astype(F32)

    mine = lax.dynamic_slice_in_dim(slot_block, grp * slots, slots, 0)
    reduced = jnp.stack(
        [
            jnp.where(mine[s] < 3, pick(keep, jnp.minimum(mine[s], 2)), got[s]) for s in range(slots)
        ]
    )
    left, right = bases[0], bases[1]
    high = lax.Precision.HIGHEST
    part = jnp.einsum("sia,sci->sac", left, reduced, precision=high)
    part = turn_rows(part.astype(BF16), place).astype(F32)
    rotated = jnp.einsum("sac,scb->sab", part, right, precision=high)
    rotated = jnp.transpose(rotated, (1, 0, 2))
    new_one = BETA_ONE * moment_one + (1.0 - BETA_ONE) * rotated
    new_two = BETA_TWO * moment_two + (1.0 - BETA_TWO) * rotated * rotated
    direction = new_one / (jnp.sqrt(new_two) + ADAM_EPS)
    turned = jnp.einsum("asb,scb->sac", direction, right, precision=high)
    turned = turn_columns(turned.astype(BF16), place).astype(F32)
    change = jnp.einsum("sia,sac->sic", left, turned, precision=high)
    change = turn_rows(change.astype(BF16), place).astype(F32)
    new_master = master - RATE_MATRIX * jnp.transpose(change, (1, 0, 2))
    new_vec_one = BETA_ONE * vector_one + (1.0 - BETA_ONE) * vector_total
    new_vec_two = BETA_TWO * vector_two + (1.0 - BETA_TWO) * vector_total * vector_total
    new_vectors = vectors - RATE_VECTOR * new_vec_one / (jnp.sqrt(new_vec_two) + ADAM_EPS)
    return (
        result[None],
        grad_inputs[None],
        new_one,
        new_two,
        new_master,
        new_vec_one,
        new_vec_two,
        new_vectors,
    )


def general(
    tokens,
    cotangent,
    lengths,
    clusters,
    owners,
    master,
    bases,
    moment_one,
    moment_two,
    vectors,
    vector_one,
    vector_two,
):
    n_tok = lax.axis_size("tok")
    tok_count = tokens.shape[1]
    rows_dev = master.shape[0]
    slot_block = jnp.argsort(owners, stable=True)
    block_slot = jnp.argsort(slot_block, stable=True)
    slot_part = lax.all_gather(master.astype(jnp.bfloat16), "grp", axis=1, tiled=True)
    weights = lax.all_gather(slot_part, "tok", axis=0, tiled=True)
    blocks = jnp.stack([pick(jnp.transpose(weights, (1, 0, 2)), block_slot[b]) for b in range(weights.shape[1])], axis=1)
    w_qkv = blocks[:, 0:3, :].reshape(D, 3 * D)
    w_out = blocks[:, 3, :]
    w_up = blocks[:, 4 : 4 + FF // D, :].reshape(D, FF)
    w_down = jnp.transpose(blocks[:, 4 + FF // D :, :], (1, 0, 2)).reshape(FF, D)
    inputs = tokens[0]
    gain_one = vectors[0]
    shift_one = vectors[1]
    gain_two = vectors[2]
    shift_two = vectors[3]
    bias_qkv = jnp.concatenate([vectors[4], jnp.zeros((D,), jnp.float32), vectors[5]])
    qkv = (jnp.dot(inputs, w_qkv, preferred_element_type=jnp.float32) + bias_qkv).astype(
        jnp.bfloat16
    )
    heads = jnp.transpose(qkv.reshape(tok_count, 3, H, HEAD), (2, 0, 1, 3)).reshape(
        H, tok_count, 3 * HEAD
    )
    pair_rows = jnp.broadcast_to(heads[None], (ROUNDS, H, tok_count, 3 * HEAD)).reshape(
        PAIRS * tok_count, 3 * HEAD
    )
    position = lax.axis_index("tok") * tok_count + jnp.arange(tok_count, dtype=jnp.int32)
    item_starts = starts_of(lengths[0])
    item_start = jnp.max(
        jnp.where(item_starts[None, :] <= position[:, None], item_starts[None, :], 0), axis=1
    )
    per_dev = tok_count // CLUSTER
    group_clusters = n_tok * per_dev
    pair_ids = jnp.arange(PAIRS, dtype=jnp.int32)[:, None]
    global_cluster = item_start[None, :] // CLUSTER + clusters[0]
    unit_ids = (pair_ids * group_clusters + global_cluster).reshape(-1)
    owner_ids = ((global_cluster + pair_ids * per_dev) % n_tok).reshape(-1)
    send_order = jnp.argsort(owner_ids * (PAIRS * group_clusters) + unit_ids, stable=True)
    restore = jnp.argsort(send_order, stable=True)
    slot_rows = PAIRS * tok_count // n_tok
    units_here = PAIRS * tok_count // CLUSTER
    sent_rows = pair_rows[send_order].reshape(n_tok, slot_rows // 2, 6 * HEAD)
    sent_units = unit_ids[send_order].reshape(n_tok, slot_rows)
    got_rows, got_units = (
        lax.all_to_all(sent_rows, "tok", split_axis=0, concat_axis=0, tiled=True),
        lax.all_to_all(sent_units, "tok", split_axis=0, concat_axis=0, tiled=True),
    )
    arrange = jnp.argsort(got_units.reshape(-1), stable=True)
    undo = jnp.argsort(arrange, stable=True)
    grouped = got_rows.reshape(PAIRS * tok_count, 3 * HEAD)[arrange].reshape(
        units_here, CLUSTER, 3 * HEAD
    )
    query_rows = grouped[..., :HEAD]
    key_rows = grouped[..., HEAD : 2 * HEAD]
    value_rows = grouped[..., 2 * HEAD :]
    score_scale = HEAD ** (-0.5)
    scores = (
        jnp.einsum("ucd,ued->uce", query_rows, key_rows, preferred_element_type=jnp.float32)
        * score_scale
    )
    row_max = jnp.max(scores, axis=-1, keepdims=True)
    row_total = jnp.sum(jnp.exp(scores - row_max), axis=-1, keepdims=True)
    log_total = row_max + jnp.log(row_total)
    probs = jnp.exp(scores - log_total)
    cluster_out = jnp.einsum(
        "uce,ued->ucd", probs.astype(jnp.bfloat16), value_rows, preferred_element_type=jnp.float32
    ).astype(jnp.bfloat16)
    back_rows = cluster_out.reshape(PAIRS * tok_count, HEAD)[undo].reshape(
        n_tok, slot_rows // 2, 2 * HEAD
    )
    home_rows = lax.all_to_all(back_rows, "tok", split_axis=0, concat_axis=0, tiled=True)
    home_rows = (
        home_rows.reshape(PAIRS * tok_count, HEAD)[restore]
        .reshape(ROUNDS, H, tok_count, HEAD)
        .astype(jnp.float32)
    )
    mixed_heads = 0.5 * (home_rows[0] + home_rows[1])
    mixed_low = jnp.transpose(mixed_heads, (1, 0, 2)).reshape(tok_count, D).astype(jnp.bfloat16)
    attention = jnp.dot(mixed_low, w_out, preferred_element_type=jnp.float32) + vectors[6]
    first_sum = inputs.astype(jnp.float32) + attention
    normed_one, rstd_one = normalize(first_sum)
    hidden = normed_one * gain_one + shift_one
    hidden_low = hidden.astype(jnp.bfloat16)
    up_proj = jnp.dot(hidden_low, w_up, preferred_element_type=jnp.float32) + vectors[8:].reshape(
        FF
    )
    act_low = jax.nn.gelu(up_proj, approximate=False).astype(jnp.bfloat16)
    down_proj = jnp.dot(act_low, w_down, preferred_element_type=jnp.float32) + vectors[7]
    second_sum = hidden + down_proj
    normed_two, rstd_two = normalize(second_sum)
    result = (normed_two * gain_two + shift_two).astype(jnp.bfloat16)
    grad_result = cotangent[0].astype(jnp.float32)
    grad_gain_two = jnp.sum(grad_result * normed_two, axis=0)
    grad_shift_two = jnp.sum(grad_result, axis=0)
    grad_second = norm_back(grad_result * gain_two, normed_two, rstd_two)
    grad_down_low = grad_second.astype(jnp.bfloat16)
    grad_w_down = inner_rows(act_low, grad_down_low)
    grad_bias_down = jnp.sum(grad_down_low.astype(jnp.float32), axis=0)
    grad_act = outer_cols(grad_down_low, w_down)
    grad_up_low = (grad_act * gelu_slope(up_proj)).astype(jnp.bfloat16)
    grad_w_up = inner_rows(hidden_low, grad_up_low)
    grad_bias_up = jnp.sum(grad_up_low.astype(jnp.float32), axis=0)
    grad_hidden = grad_second + outer_cols(grad_up_low, w_up)
    grad_gain_one = jnp.sum(grad_hidden * normed_one, axis=0)
    grad_shift_one = jnp.sum(grad_hidden, axis=0)
    grad_first = norm_back(grad_hidden * gain_one, normed_one, rstd_one)
    grad_attn_low = grad_first.astype(jnp.bfloat16)
    grad_w_out = inner_rows(mixed_low, grad_attn_low)
    grad_bias_out = jnp.sum(grad_attn_low.astype(jnp.float32), axis=0)
    grad_mixed = outer_cols(grad_attn_low, w_out)
    grad_heads = jnp.transpose((0.5 * grad_mixed).reshape(tok_count, H, HEAD), (1, 0, 2)).astype(
        jnp.bfloat16
    )
    grad_pairs = jnp.broadcast_to(grad_heads[None], (ROUNDS, H, tok_count, HEAD)).reshape(
        PAIRS * tok_count, HEAD
    )
    sent_grad = grad_pairs[send_order].reshape(n_tok, slot_rows // 2, 2 * HEAD)
    got_grad = lax.all_to_all(sent_grad, "tok", split_axis=0, concat_axis=0, tiled=True)
    grad_cluster = got_grad.reshape(PAIRS * tok_count, HEAD)[arrange].reshape(
        units_here, CLUSTER, HEAD
    )
    scores_again = (
        jnp.einsum("ucd,ued->uce", query_rows, key_rows, preferred_element_type=jnp.float32)
        * score_scale
    )
    probs_again = jnp.exp(scores_again - log_total)
    probs_low = probs_again.astype(jnp.bfloat16)
    grad_values = jnp.einsum(
        "uce,ucd->ued", probs_low, grad_cluster, preferred_element_type=jnp.float32
    )
    grad_probs = jnp.einsum(
        "ucd,ued->uce", grad_cluster, value_rows, preferred_element_type=jnp.float32
    )
    centre = jnp.sum(probs_again * grad_probs, axis=-1, keepdims=True)
    grad_scores = (probs_again * (grad_probs - centre)).astype(jnp.bfloat16)
    grad_query = (
        jnp.einsum("uce,ued->ucd", grad_scores, key_rows, preferred_element_type=jnp.float32)
        * score_scale
    )
    grad_keys = (
        jnp.einsum("uce,ucd->ued", grad_scores, query_rows, preferred_element_type=jnp.float32)
        * score_scale
    )
    grad_grouped = jnp.concatenate(
        [
            grad_query.astype(jnp.bfloat16),
            grad_keys.astype(jnp.bfloat16),
            grad_values.astype(jnp.bfloat16),
        ],
        axis=-1,
    )
    back_grad = grad_grouped.reshape(PAIRS * tok_count, 3 * HEAD)[undo].reshape(
        n_tok, slot_rows // 2, 6 * HEAD
    )
    home_grad = lax.all_to_all(back_grad, "tok", split_axis=0, concat_axis=0, tiled=True)
    home_grad = (
        home_grad.reshape(PAIRS * tok_count, 3 * HEAD)[restore]
        .reshape(ROUNDS, H, tok_count, 3, HEAD)
        .astype(jnp.float32)
    )
    grad_qkv = (home_grad[0] + home_grad[1]).astype(jnp.bfloat16)
    grad_qkv = jnp.transpose(grad_qkv, (1, 2, 0, 3)).reshape(tok_count, 3 * D)
    grad_w_qkv = inner_rows(inputs, grad_qkv)
    grad_bias_qkv = jnp.sum(grad_qkv.astype(jnp.float32), axis=0)
    grad_inputs = grad_first + outer_cols(grad_qkv, w_qkv)
    grad_blocks = jnp.concatenate(
        [
            grad_w_qkv.reshape(D, 3, D),
            grad_w_out[:, None, :],
            grad_w_up.reshape(D, FF // D, D),
            jnp.transpose(grad_w_down.reshape(FF // D, D, D), (1, 0, 2)),
        ],
        axis=1,
    )
    by_block = jnp.transpose(grad_blocks, (1, 0, 2))
    slot_grads = jnp.stack([pick(by_block, slot_block[s]) for s in range(by_block.shape[0])], axis=1)
    vector_grads = jnp.concatenate(
        [
            jnp.stack(
                [
                    grad_gain_one,
                    grad_shift_one,
                    grad_gain_two,
                    grad_shift_two,
                    grad_bias_qkv[:D],
                    grad_bias_qkv[2 * D :],
                    grad_bias_out,
                    grad_bias_down,
                ]
            ),
            grad_bias_up.reshape(FF // D, D),
        ],
        axis=0,
    )
    vector_total = lax.psum(vector_grads, ("tok", "grp"))
    row_total = lax.psum_scatter(slot_grads, "tok", scatter_dimension=0, tiled=True)
    reduced = lax.psum_scatter(
        row_total.astype(jnp.bfloat16), "grp", scatter_dimension=1, tiled=True
    ).astype(jnp.float32)
    left_basis = bases[0]
    right_basis = bases[1]
    first_row = lax.axis_index("tok") * rows_dev
    turned_in = jnp.einsum("rse,sef->rsf", reduced, right_basis, precision=lax.Precision.HIGHEST)
    left_rows = lax.dynamic_slice_in_dim(left_basis, first_row, rows_dev, 1)
    picked = left_rows
    rotated = lax.psum_scatter(
        jnp.einsum("sri,rsf->isf", picked, turned_in, precision=lax.Precision.HIGHEST),
        "tok",
        scatter_dimension=0,
        tiled=True,
    )
    new_one = BETA_ONE * moment_one + (1.0 - BETA_ONE) * rotated
    new_two = BETA_TWO * moment_two + (1.0 - BETA_TWO) * rotated * rotated
    direction = new_one / (jnp.sqrt(new_two) + ADAM_EPS)
    turned_out = jnp.einsum("rse,sfe->rsf", direction, right_basis, precision=lax.Precision.HIGHEST)
    left_cols = lax.dynamic_slice_in_dim(left_basis, first_row, rows_dev, 2)
    picked = left_cols
    change = lax.psum_scatter(
        jnp.einsum("sir,rsf->isf", picked, turned_out, precision=lax.Precision.HIGHEST),
        "tok",
        scatter_dimension=0,
        tiled=True,
    )
    new_master = master - RATE_MATRIX * change
    new_vec_one = BETA_ONE * vector_one + (1.0 - BETA_ONE) * vector_total
    new_vec_two = BETA_TWO * vector_two + (1.0 - BETA_TWO) * vector_total * vector_total
    new_vectors = vectors - RATE_VECTOR * new_vec_one / (jnp.sqrt(new_vec_two) + ADAM_EPS)
    return (
        result[None],
        grad_inputs[None],
        new_one,
        new_two,
        new_master,
        new_vec_one,
        new_vec_two,
        new_vectors,
    )

def solution(mesh):
    n_tok, n_grp = mesh.shape["tok"], mesh.shape["grp"]

    def on_device(*args):
        lengths, clusters = args[2], args[3]
        unit = n_tok // (lengths.shape[1] - 1)
        suits = unit == UNIT and n_tok == 2 * UNIT and n_grp == 4 and clusters.shape[2] == 1024
        return (fast if suits else general)(*args)

    return jax.shard_map(
        on_device,
        mesh=mesh,
        in_specs=(
            P("grp", "tok", None),
            P("grp", "tok", None),
            P("grp", None),
            P("grp", None, "tok"),
            P(),
            P("tok", "grp", None),
            P(None, "grp", None, None),
            P("tok", "grp", None),
            P("tok", "grp", None),
            P(),
            P(),
            P(),
        ),
        out_specs=(
            P("grp", "tok", None),
            P("grp", "tok", None),
            P("tok", "grp", None),
            P("tok", "grp", None),
            P("tok", "grp", None),
            P(),
            P(),
            P(),
        ),
        check_vma=False,
    )
```

```python
import functools

import jax
import jax.numpy as jnp
from jax import lax
from jax.experimental import pallas as pl
from jax.experimental.pallas import tpu as pltpu
from jax.sharding import PartitionSpec as P

D = 768
H = 12
FF = 3072
HEAD = 64
ROUNDS = 2
PAIRS = 24
CLUSTER = 128
FFB = FF // D

EPS_NORM = 1e-05
ADAM_EPS = 1e-08
BETA_ONE = 0.5
BETA_TWO = 0.5
RATE_MATRIX = 0.025
RATE_VECTOR = 0.15
SQRT_HALF = 0.7071067811865476
INV_ROOT_TWO_PI = 0.3989422804014327

BF16 = jnp.bfloat16
F32 = jnp.float32

UNIT = 4
HEADS_OWN = H // UNIT
LOCAL_PAIRS = ROUNDS * HEADS_OWN
TILE = 128
WIDE = 2 * TILE
SMALL = pl.CostEstimate(flops=0, transcendentals=0, bytes_accessed=0)


def inner_rows(left, right):
    return lax.dot_general(left, right, (((0,), (0,)), ((), ())), preferred_element_type=F32)


def outer_cols(left, right):
    return lax.dot_general(left, right, (((1,), (1,)), ((), ())), preferred_element_type=F32)


def normalize(values_in):
    centre = jnp.mean(values_in, axis=-1, keepdims=True)
    offset = values_in - centre
    spread = jnp.mean(offset * offset, axis=-1, keepdims=True)
    rstd = lax.rsqrt(spread + EPS_NORM)
    return (offset * rstd, rstd)


def norm_back(grad_normed, normed, rstd):
    first_mean = jnp.mean(grad_normed, axis=-1, keepdims=True)
    second_mean = jnp.mean(grad_normed * normed, axis=-1, keepdims=True)
    return rstd * (grad_normed - first_mean - normed * second_mean)


def gelu_slope(values_in):
    return (
        0.5 * (1.0 + lax.erf(values_in * SQRT_HALF))
        + values_in * jnp.exp(-0.5 * values_in * values_in) * INV_ROOT_TWO_PI
    )


def turn_half(value):
    return pltpu.roll(value, HEAD, 1)


def arrange_body(rows_ref, out_ref):
    count = rows_ref.shape[1]
    low = lax.broadcasted_iota(jnp.int32, (count, TILE), 1) < HEAD

    def half(part, head, high):
        at = head // 2 * TILE
        tile = rows_ref[part, :, at : at + TILE].astype(F32)
        return tile if head % 2 == high else turn_half(tile)

    for head in range(H):
        own = head % HEADS_OWN
        odd = own % 2
        value = half(2, head, odd)
        query = half(0, head, 1 - odd)
        keys = half(1, head, 1 - odd)
        one = jnp.where(low, query, value) if odd else jnp.where(low, value, query)
        two = jnp.where(low, keys, 0.0) if odd else jnp.where(low, 0.0, keys)
        out_ref[head // HEADS_OWN, :, own * WIDE : own * WIDE + TILE] = one.astype(BF16)
        out_ref[head // HEADS_OWN, :, own * WIDE + TILE : (own + 1) * WIDE] = two.astype(BF16)


def arrange(rows):
    return pl.pallas_call(
        arrange_body,
        out_shape=jax.ShapeDtypeStruct((UNIT, rows.shape[1], HEADS_OWN * WIDE), BF16),
        cost_estimate=SMALL,
        name="arrange",
    )(rows)


def assemble_body(table_ref, *refs):
    shards, out_ref, sem = refs[:-2], refs[-2], refs[-1]
    rows = shards[0].shape[1]
    copies = []
    for shard in shards:
        for i in range(shard.shape[0]):
            n = len(copies)
            first = pl.multiple_of(table_ref[n], rows)
            copies.append(
                pltpu.make_async_copy(shard.at[i], out_ref.at[pl.ds(first, rows), :], sem.at[n])
            )
    for copy in copies:
        copy.start()
    for copy in copies:
        copy.wait()


def assemble(table, shards):
    pieces = sum(s.shape[0] for s in shards)
    anywhere = pl.BlockSpec(memory_space=pl.ANY)
    return pl.pallas_call(
        assemble_body,
        in_specs=[pl.BlockSpec(memory_space=pltpu.SMEM)] + [anywhere] * len(shards),
        out_specs=anywhere,
        out_shape=jax.ShapeDtypeStruct((pieces * shards[0].shape[1], shards[0].shape[2]), BF16),
        scratch_shapes=[pltpu.SemaphoreType.DMA((pieces,))],
        cost_estimate=SMALL,
        name="assemble",
    )(table, *shards)


def sort_body(order_ref, x_ref, weight_ref, bias_ref, out_ref, column_ref, rows_ref):
    count = x_ref.shape[0]

    @pl.when(pl.program_id(0) == 0)
    def _():
        column_ref[...] = jnp.transpose(order_ref[...])

    head = pl.program_id(0)
    chunk = 256
    lane = lax.broadcasted_iota(jnp.int32, (chunk, count), 1)
    rows_ref[...] = (
        jnp.dot(x_ref[...], weight_ref[...], preferred_element_type=F32) + bias_ref[...]
    ).astype(BF16)
    for step in range(HEADS_OWN):

        @pl.when(head == step)
        def _():
            for turn in range(ROUNDS):
                pair = step * ROUNDS + turn
                for part in range(count // chunk):
                    where = pl.ds(part * chunk, chunk)
                    picked = (column_ref[where, pair : pair + 1] == lane).astype(F32).astype(BF16)
                    out_ref[turn, where, :] = jnp.dot(
                        picked, rows_ref[...], preferred_element_type=F32
                    ).astype(BF16)


def sort_rows(order, inputs, weights, bias):
    count = inputs.shape[0]
    return pl.pallas_call(
        sort_body,
        grid=(HEADS_OWN,),
        in_specs=[
            pl.BlockSpec((8, count), lambda h: (0, 0)),
            pl.BlockSpec((count, D), lambda h: (0, 0)),
            pl.BlockSpec((D, WIDE), lambda h: (0, h)),
            pl.BlockSpec((1, WIDE), lambda h: (0, h)),
        ],
        out_specs=pl.BlockSpec((ROUNDS, count, WIDE), lambda h: (h, 0, 0)),
        out_shape=jax.ShapeDtypeStruct((LOCAL_PAIRS, count, WIDE), BF16),
        scratch_shapes=[pltpu.VMEM((count, 8), jnp.int32), pltpu.VMEM((count, WIDE), BF16)],
        compiler_params=pltpu.CompilerParams(vmem_limit_bytes=48 << 20),
        cost_estimate=SMALL,
        name="sort_rows",
    )(order, inputs, weights, bias)


def sort_grads_body(order_ref, rows_ref, out_ref, column_ref):
    count = order_ref.shape[1]
    half = count // 2

    @pl.when(pl.program_id(0) == 0)
    def _():
        column_ref[...] = jnp.transpose(order_ref[...])

    head = pl.program_id(0)
    chunk = 256
    lane = lax.broadcasted_iota(jnp.int32, (chunk, count), 1)
    low = lax.broadcasted_iota(jnp.int32, (count, TILE), 1) < HEAD
    for step in range(HEADS_OWN):

        @pl.when(head == step)
        def _():
            if step < 2:
                tile = rows_ref[0:count, :].astype(F32)
                tile = jnp.where(low if step == 0 else jnp.logical_not(low), tile, 0.0).astype(BF16)
            else:
                both = rows_ref[count : count + half, :].astype(F32)
                tile = jnp.concatenate([both, turn_half(both)], axis=0)
                tile = jnp.where(low, tile, 0.0).astype(BF16)
            for turn in range(ROUNDS):
                pair = step * ROUNDS + turn
                for part in range(count // chunk):
                    where = pl.ds(part * chunk, chunk)
                    picked = (column_ref[where, pair : pair + 1] == lane).astype(F32).astype(BF16)
                    out_ref[turn, where, :] = jnp.dot(
                        picked, tile, preferred_element_type=F32
                    ).astype(BF16)


def sort_grads(order, rows):
    count = order.shape[1]
    return pl.pallas_call(
        sort_grads_body,
        grid=(HEADS_OWN,),
        in_specs=[
            pl.BlockSpec((8, count), lambda h: (0, 0)),
            pl.BlockSpec(rows.shape, lambda h: (0, 0)),
        ],
        out_specs=pl.BlockSpec((ROUNDS, count, TILE), lambda h: (h, 0, 0)),
        out_shape=jax.ShapeDtypeStruct((LOCAL_PAIRS, count, TILE), BF16),
        scratch_shapes=[pltpu.VMEM((count, 8), jnp.int32)],
        compiler_params=pltpu.CompilerParams(vmem_limit_bytes=48 << 20),
        cost_estimate=SMALL,
        name="sort_grads",
    )(order, rows)


def plans_of(count):
    share = CLUSTER // UNIT
    half = UNIT // 2
    return (
        [(tuple(range(UNIT)), share)],
        [(tuple(range(i * half, (i + 1) * half)), 2 * share) for i in range(2)],
    )


def for_each_batch(is_long, count, batch, work):
    for wanted, plan in zip((1, 0), plans_of(count)):

        @pl.when(is_long == wanted)
        def _(plan=plan):
            for runs, share in plan:

                def step(group, carry, runs=runs, share=share):
                    first = pl.multiple_of(group * (batch * share), batch * share)
                    work(runs, pl.ds(first, batch * share), share)
                    return carry

                lax.fori_loop(0, count // share // batch, step, 0)


def batch_of(refs, runs, where, share, width):
    parts = [refs[r][0, where, :] for r in runs]
    return jnp.concatenate([p.reshape(p.shape[0] // share, share, width) for p in parts], axis=1)


def spread(refs, runs, where, share, columns, value):
    for i, r in enumerate(runs):
        part = value[:, i * share : (i + 1) * share]
        refs[r][0, where, columns] = part.reshape(part.shape[0] * share, TILE)


def products(form, left, right):
    return jnp.einsum(form, left, right, preferred_element_type=F32)


def softmax(first, second):
    scores = products("ued,ucd->uec", second, first) * (HEAD**-0.5)
    expo = jnp.exp(scores - jnp.max(scores, axis=1, keepdims=True))
    return expo * (1.0 / jnp.sum(expo, axis=1, keepdims=True))


def attend_body(long_ref, *refs):
    grouped, results = refs[:UNIT], refs[UNIT:]

    def work(runs, where, share):
        rows = batch_of(grouped, runs, where, share, WIDE)
        first = rows[..., :TILE]
        probs = softmax(first, rows[..., TILE:]).astype(BF16)
        mixed = products("uce,ued->ucd", jnp.swapaxes(probs, 1, 2), first).astype(BF16)
        spread(results, runs, where, share, slice(0, TILE), mixed)

    for_each_batch(long_ref[0], grouped[0].shape[1], 8, work)


def attend(is_long, grouped):
    count = grouped[0].shape[1]
    return pl.pallas_call(
        attend_body,
        grid_spec=pltpu.PrefetchScalarGridSpec(
            num_scalar_prefetch=1,
            grid=(LOCAL_PAIRS,),
            in_specs=[pl.BlockSpec((1, count, WIDE), lambda p, _: (p, 0, 0))] * UNIT,
            out_specs=[pl.BlockSpec((1, count, TILE), lambda p, _: (p, 0, 0))] * UNIT,
        ),
        out_shape=[jax.ShapeDtypeStruct((LOCAL_PAIRS, count, TILE), BF16)] * UNIT,
        compiler_params=pltpu.CompilerParams(vmem_limit_bytes=48 << 20),
        cost_estimate=SMALL,
        name="attend",
    )(is_long, *grouped)


def attend_back_body(long_ref, *refs):
    grouped, grads, results = refs[:UNIT], refs[UNIT : 2 * UNIT], refs[2 * UNIT :]
    batch = 16
    odd = (pl.program_id(0) // ROUNDS) % 2
    lane = lax.broadcasted_iota(jnp.int32, (batch, CLUSTER, TILE), 2)
    value_lane = (lane < HEAD) == (odd == 0)
    scale = HEAD**-0.5

    def work(runs, where, share):
        rows = batch_of(grouped, runs, where, share, WIDE)
        grad = batch_of(grads, runs, where, share, TILE)
        first, second = rows[..., :TILE], rows[..., TILE:]
        probs = softmax(first, second)
        grad_probs = products("ued,ucd->uec", first, grad)
        centre = jnp.sum(probs * grad_probs, axis=1, keepdims=True)
        grad_scores = (probs * (grad_probs - centre)).astype(BF16)
        grad_values = products("uec,ucd->ued", probs.astype(BF16), grad)
        grad_keys = products("uec,ucd->ued", grad_scores, first) * scale
        grad_query = products("uce,ued->ucd", jnp.swapaxes(grad_scores, 1, 2), second) * scale
        tile_one = jnp.where(value_lane, grad_values, grad_query).astype(BF16)
        tile_two = jnp.where(value_lane, 0.0, grad_keys).astype(BF16)
        spread(results, runs, where, share, slice(0, TILE), tile_one)
        spread(results, runs, where, share, slice(TILE, WIDE), tile_two)

    for_each_batch(long_ref[0], grouped[0].shape[1], batch, work)


def attend_back(is_long, grouped, grads):
    count = grouped[0].shape[1]
    return pl.pallas_call(
        attend_back_body,
        grid_spec=pltpu.PrefetchScalarGridSpec(
            num_scalar_prefetch=1,
            grid=(LOCAL_PAIRS,),
            in_specs=[pl.BlockSpec((1, count, WIDE), lambda p, _: (p, 0, 0))] * UNIT
            + [pl.BlockSpec((1, count, TILE), lambda p, _: (p, 0, 0))] * UNIT,
            out_specs=[pl.BlockSpec((1, count, WIDE), lambda p, _: (p, 0, 0))] * UNIT,
        ),
        out_shape=[jax.ShapeDtypeStruct((LOCAL_PAIRS, count, WIDE), BF16)] * UNIT,
        compiler_params=pltpu.CompilerParams(vmem_limit_bytes=56 << 20),
        cost_estimate=SMALL,
        name="attend_back",
    )(is_long, *grouped, *grads)


def unsorted(order_ref, step, rows_ref, part, chunk):
    count = rows_ref.shape[1]
    row = lax.broadcasted_iota(jnp.int32, (chunk, count), 0) + part * chunk
    total = None
    for turn in range(ROUNDS):
        pair = step * ROUNDS + turn
        picked = (order_ref[pair : pair + 1, :] == row).astype(F32).astype(BF16)
        more = jnp.dot(picked, rows_ref[turn], preferred_element_type=F32)
        total = more if total is None else total + more
    return total


def mix_body(order_ref, rows_ref, out_ref):
    count = rows_ref.shape[1]
    chunk = 256
    parts = count // chunk
    low = lax.broadcasted_iota(jnp.int32, (chunk, TILE), 1) < HEAD
    head = pl.program_id(0)
    for step in range(HEADS_OWN):

        @pl.when(head == step)
        def _():
            means = [0.5 * unsorted(order_ref, step, rows_ref, part, chunk) for part in range(parts)]
            for part in range(parts):
                where = pl.ds(part * chunk, chunk)
                if step == 0:
                    out_ref[where, :] = means[part].astype(BF16)
                elif step == 1:
                    out_ref[where, :] = jnp.where(low, out_ref[where, :].astype(F32), means[part]).astype(BF16)
                elif part < parts // 2:
                    both = jnp.where(low, means[part], turn_half(means[part + parts // 2]))
                    out_ref[pl.ds(count + part * chunk, chunk), :] = both.astype(BF16)


def mix(order, rows):
    count = rows.shape[1]
    packed = (count + count // 2, TILE)
    return pl.pallas_call(
        mix_body,
        grid=(HEADS_OWN,),
        in_specs=[
            pl.BlockSpec((8, count), lambda h: (0, 0)),
            pl.BlockSpec((ROUNDS, count, TILE), lambda h: (h, 0, 0)),
        ],
        out_specs=pl.BlockSpec(packed, lambda h: (0, 0)),
        out_shape=jax.ShapeDtypeStruct(packed, BF16),
        compiler_params=pltpu.CompilerParams(vmem_limit_bytes=48 << 20),
        cost_estimate=SMALL,
        name="mix",
    )(order, rows)


def gather_grads_body(order_ref, rows_ref, out_ref):
    count = rows_ref.shape[1]
    chunk = 256
    head = pl.program_id(0)
    for step in range(HEADS_OWN):

        @pl.when(head == step)
        def _():
            for part in range(count // chunk):
                where = pl.ds(part * chunk, chunk)
                out_ref[where, :] = unsorted(order_ref, step, rows_ref, part, chunk).astype(BF16)


def gather_grads(order, rows):
    count = rows.shape[1]
    return pl.pallas_call(
        gather_grads_body,
        grid=(HEADS_OWN,),
        in_specs=[
            pl.BlockSpec((8, count), lambda h: (0, 0)),
            pl.BlockSpec((ROUNDS, count, WIDE), lambda h: (h, 0, 0)),
        ],
        out_specs=pl.BlockSpec((count, WIDE), lambda h: (0, h)),
        out_shape=jax.ShapeDtypeStruct((count, HEADS_OWN * WIDE), BF16),
        compiler_params=pltpu.CompilerParams(vmem_limit_bytes=48 << 20),
        cost_estimate=SMALL,
        name="gather_grads",
    )(order, rows)


ERF_TOP = (0.00022905065861350646, 0.0034082910107109506, 0.050955695062380861, 0.18520832239976145, 1.128379143519084)
ERF_BOTTOM = (
    -1.1791602954361697e-7,
    0.000023547966471313185,
    0.0010179625278914885,
    0.014070470171167667,
    0.11098505178285362,
    0.49746925110067538,
    1.0,
)


def polynomial(value, factors):
    total = jnp.full_like(value, factors[0])
    for factor in factors[1:]:
        total = total * value + factor
    return total


def error_function(value):
    value = jnp.clip(value, -3.832506856900711, 3.832506856900711)
    square = value * value
    return value * polynomial(square, ERF_TOP) / polynomial(square, ERF_BOTTOM)


VEC_ROWS = 16
FFN_TILE = 256


def layer_body(
    n_shards,
    table_ref,
    *refs,
):
    shards, refs = refs[:n_shards], refs[n_shards:]
    parts, refs = refs[:UNIT], refs[UNIT:]
    x_ref, cot_ref, vec_ref, result_ref, first_ref, back_ref, sums_ref, kept_ref, sent_ref = refs[:9]
    w_ref, packed_ref, mixed_ref, hidden_ref, act_ref, down_ref, up_ref, attn_ref = refs[9:17]
    slope_ref, stage_ref, weight_sem, part_sem, stage_sem = refs[17:]
    count = x_ref.shape[0]
    half = count // 2
    per_shard, n_weights, shard_rows = shards[0].shape[:3]
    member = table_ref[0]
    for k in range(UNIT):
        pltpu.make_async_copy(parts[k], packed_ref.at[member ^ k], part_sem.at[k]).start()
    for b in range(n_weights):
        for n in range(n_shards * per_shard):
            row = pl.multiple_of(table_ref[6 + n], shard_rows)
            pltpu.make_async_copy(
                shards[n // per_shard].at[n % per_shard, b], w_ref.at[b, pl.ds(row, shard_rows), :], weight_sem.at[b]
            ).start()
    for k in range(UNIT):
        pltpu.make_async_copy(parts[k], packed_ref.at[member ^ k], part_sem.at[k]).wait()
    for b in range(n_weights):
        pltpu.make_async_copy(w_ref.at[b], w_ref.at[b], weight_sem.at[b]).wait()

    sums_ref[...] = jnp.zeros_like(sums_ref)
    low = lax.broadcasted_iota(jnp.int32, (FFN_TILE, TILE), 1) < HEAD
    vec = [vec_ref[i : i + 1, :] for i in range(8 + FFB)]
    gain_one, shift_one, gain_two, shift_two = vec[:4]
    bias_out, bias_down = vec[6], vec[7]

    def add_sum(row, value):
        sums_ref[row : row + 1, :] += jnp.sum(value, axis=0, keepdims=True)

    def tile_step(i, carry):
        rows = pl.ds(pl.multiple_of(i * FFN_TILE, FFN_TILE), FFN_TILE)
        is_first = i * FFN_TILE < half
        extra = pl.ds(pl.multiple_of(count + lax.rem(i * FFN_TILE, half), FFN_TILE), FFN_TILE)

        def pair(m):
            return packed_ref[m, rows, :].astype(F32)

        def single(m):
            value = packed_ref[m, extra, :].astype(F32)
            return jnp.where(is_first, value, turn_half(value))

        for m in (0, 2):
            at = m * (HEADS_OWN * HEAD)
            nxt = turn_half(pair(m + 1))
            mixed_ref[rows, at : at + TILE] = pair(m).astype(BF16)
            mixed_ref[rows, at + TILE : at + 2 * TILE] = jnp.where(low, single(m), nxt).astype(BF16)
            mixed_ref[rows, at + 2 * TILE : at + 3 * TILE] = jnp.where(
                low, nxt, turn_half(single(m + 1))
            ).astype(BF16)
        attention = jnp.dot(mixed_ref[rows, :], w_ref[0], preferred_element_type=F32) + bias_out
        normed_one, rstd_one = normalize(x_ref[rows, :].astype(F32) + attention)
        hidden = normed_one * gain_one + shift_one
        hidden_low = hidden.astype(BF16)
        hidden_ref[rows, :] = hidden_low
        down = jnp.broadcast_to(bias_down, hidden.shape)
        for j in range(FFB):
            up = jnp.dot(hidden_low, w_ref[1 + j], preferred_element_type=F32) + vec[8 + j]
            phi = 0.5 * (1.0 + error_function(up * SQRT_HALF))
            slope_ref[j] = phi + up * jnp.exp(-0.5 * up * up) * INV_ROOT_TWO_PI
            act = (up * phi).astype(BF16)
            act_ref[j, rows, :] = act
            down = down + jnp.dot(act, w_ref[1 + FFB + j], preferred_element_type=F32)
        normed_two, rstd_two = normalize(hidden + down)
        result_ref[rows, :] = (normed_two * gain_two + shift_two).astype(BF16)
        grad_result = cot_ref[rows, :].astype(F32)
        add_sum(2, grad_result * normed_two)
        add_sum(3, grad_result)
        grad_second = norm_back(grad_result * gain_two, normed_two, rstd_two)
        grad_down = grad_second.astype(BF16)
        down_ref[rows, :] = grad_down
        add_sum(7, grad_down.astype(F32))
        grad_hidden = grad_second
        for j in range(FFB):
            grad_up = (outer_cols(grad_down, w_ref[1 + FFB + j]) * slope_ref[j]).astype(BF16)
            up_ref[j, rows, :] = grad_up
            add_sum(8 + j, grad_up.astype(F32))
            grad_hidden = grad_hidden + outer_cols(grad_up, w_ref[1 + j])
        add_sum(0, grad_hidden * normed_one)
        add_sum(1, grad_hidden)
        grad_first = norm_back(grad_hidden * gain_one, normed_one, rstd_one)
        first_ref[rows, :] = grad_first
        grad_attn = grad_first.astype(BF16)
        attn_ref[rows, :] = grad_attn
        add_sum(6, grad_attn.astype(F32))
        grad_mixed = (0.5 * outer_cols(grad_attn, w_ref[0])).astype(BF16).astype(F32)
        for m in range(UNIT):
            at = (m // 2) * 3 * TILE
            tiles = [grad_mixed[:, at + n * TILE : at + (n + 1) * TILE] for n in range(3)]
            if m % 2 == 0:
                two, one = tiles[0], tiles[1]
            else:
                two, one = turn_half(jnp.where(low, tiles[2], tiles[1])), turn_half(tiles[2])
            back_ref[member ^ m, rows, :] = two.astype(BF16)

            @pl.when(is_first)
            def _(one=one, m=m):
                back_ref[member ^ m, extra, :] = jnp.where(low, one, 0.0).astype(BF16)

            @pl.when(jnp.logical_not(is_first))
            def _(one=one, m=m):
                old = back_ref[member ^ m, extra, :].astype(F32)
                back_ref[member ^ m, extra, :] = jnp.where(low, old, turn_half(one)).astype(BF16)

        return carry

    lax.fori_loop(0, count // FFN_TILE, tile_step, 0)

    core, bits = table_ref[1], [table_ref[2 + d] for d in range(4)]
    piece, half_columns = kept_ref.shape[3:]
    n_parts = kept_ref.shape[0]
    per_part = n_weights // n_parts

    def copies(block, slot, half, target):
        part = block // per_part
        made = []
        for index in range(16):
            x, zh, y, zl = ((index >> s) % 2 for s in range(4))
            rel = {"x": x ^ bits[0], "y": y ^ bits[1], "zl": zl ^ bits[2], "zh": zh ^ bits[3]}
            place = 0
            for name in PART_ORDERS[part]:
                place = place * 2 + rel[name]
            made.append(
                pltpu.make_async_copy(
                    stage_ref.at[
                        slot, pl.ds(index * piece, piece), pl.ds(half * half_columns, half_columns)
                    ],
                    target.at[part, place, block % per_part],
                    stage_sem.at[slot, half * 16 + index],
                )
            )
        return made

    def send(block, slot):
        for half in range(2):

            @pl.when(core == half)
            def _(half=half):
                for copy in copies(block, slot, half, kept_ref):
                    copy.start()

            @pl.when(core != half)
            def _(half=half):
                for copy in copies(block, slot, half, sent_ref):
                    copy.start()

    def sent(block, slot):
        for half in range(2):
            for copy in copies(block, slot, half, kept_ref):
                copy.wait()

    plan = [(attn_ref, None, mixed_ref, None, 0)]
    plan += [(down_ref, None, act_ref, j, 1 + FFB + j) for j in range(FFB)]
    plan += [(up_ref, j, hidden_ref, None, 1 + j) for j in range(FFB)]
    for n, (left, lj, right, rj, block) in enumerate(plan):
        slot = n % 2
        if n >= 2:
            sent(plan[n - 2][4], slot)
        value = inner_rows(
            left[...] if lj is None else left[lj], right[...] if rj is None else right[rj]
        )
        stage_ref[slot] = value.astype(BF16)
        send(block, slot)
    for n in (len(plan) - 2, len(plan) - 1):
        sent(plan[n][4], n % 2)


PART_ORDERS = (("x", "y", "zl", "zh"), ("y", "zl", "zh", "x"), ("zl", "zh", "x", "y"))


def layer(table, shards, parts, inputs, cotangent, vectors):
    count = inputs.shape[0]
    n_weights = 1 + 2 * FFB
    n_shards = len(shards)
    anywhere = pl.BlockSpec(memory_space=pl.ANY)
    inside = pl.BlockSpec(memory_space=pltpu.VMEM)
    packed = parts[0].shape
    return pl.pallas_call(
        functools.partial(layer_body, n_shards),
        in_specs=[pl.BlockSpec(memory_space=pltpu.SMEM)] + [anywhere] * (n_shards + UNIT) + [inside] * 3,
        out_specs=[inside, inside, inside, inside, anywhere, anywhere],
        out_shape=[
            jax.ShapeDtypeStruct((count, D), BF16),
            jax.ShapeDtypeStruct((count, D), F32),
            jax.ShapeDtypeStruct((UNIT, *packed), BF16),
            jax.ShapeDtypeStruct((VEC_ROWS, D), F32),
            jax.ShapeDtypeStruct((3, 16, n_weights // 3, D // 16, D // 2), BF16),
            jax.ShapeDtypeStruct((3, 16, n_weights // 3, D // 16, D // 2), BF16),
        ],
        scratch_shapes=[
            pltpu.VMEM((n_weights, D, D), BF16),
            pltpu.VMEM((UNIT, *packed), BF16),
            pltpu.VMEM((count, D), BF16),
            pltpu.VMEM((count, D), BF16),
            pltpu.VMEM((FFB, count, D), BF16),
            pltpu.VMEM((count, D), BF16),
            pltpu.VMEM((FFB, count, D), BF16),
            pltpu.VMEM((count, D), BF16),
            pltpu.VMEM((FFB, FFN_TILE, D), F32),
            pltpu.VMEM((2, D, D), BF16),
            pltpu.SemaphoreType.DMA((n_weights,)),
            pltpu.SemaphoreType.DMA((UNIT,)),
            pltpu.SemaphoreType.DMA((2, 32)),
        ],
        compiler_params=pltpu.CompilerParams(vmem_limit_bytes=60 << 20),
        cost_estimate=SMALL,
        name="layer",
    )(table, *shards, *parts, inputs, cotangent, vectors)


def swap(value, axis, bit):
    size = lax.axis_size(axis)
    return lax.ppermute(value, axis, [(i, i ^ bit) for i in range(size)])


def exchange_unit(parts):
    return [parts[0]] + [swap(parts[k], "tok", k) for k in range(1, UNIT)]


LINKS = {"x": ("grp", 2), "y": ("tok", 1), "zl": ("tok", 2), "zh": ("tok", 4)}


def starts_of(lengths):
    index = jnp.arange(lengths.shape[0])
    return jnp.sum(jnp.where(index[None, :] < index[:, None], lengths[None, :], 0), axis=1)


def total_of(value):
    for axis in ("grp", "tok"):
        bit = 1
        while bit < lax.axis_size(axis):
            value = value + swap(value, axis, bit)
            bit *= 2
    return value


def pick(values, index):
    return lax.dynamic_index_in_dim(values, index, 0, keepdims=False)


def turn_rows(value, place):
    n_tok = lax.axis_size("tok")
    slots, rows, width = value.shape
    parts = jnp.transpose(value.reshape(slots, n_tok, rows // n_tok, width), (1, 0, 2, 3))
    got = lax.all_to_all(parts, "tok", split_axis=0, concat_axis=0, tiled=True)
    got = jnp.stack([got[place.index(c)] for c in range(n_tok)], axis=2)
    return got.reshape(slots, rows // n_tok, n_tok * width)


def turn_columns(value, place):
    n_tok = lax.axis_size("tok")
    slots, rows, width = value.shape
    parts = value.reshape(slots, rows, n_tok, width // n_tok)
    parts = jnp.stack([parts[:, :, place[t]] for t in range(n_tok)], axis=0)
    got = lax.all_to_all(parts, "tok", split_axis=0, concat_axis=0, tiled=True)
    return jnp.transpose(got, (1, 0, 2, 3)).reshape(slots, n_tok * rows, width // n_tok)


def split_heads(columns):
    query, keys, values = (c.reshape(HEADS_OWN, HEAD) for c in columns)
    zero = jnp.zeros((HEAD,), query.dtype)
    tiles = []
    for h in range(HEADS_OWN):
        tiles += [values[h], query[h], zero, keys[h]] if h % 2 == 0 else [query[h], values[h], keys[h], zero]
    return jnp.concatenate(tiles)


def join_heads(tiles):
    parts = tiles.reshape(HEADS_OWN, 4, HEAD, *tiles.shape[1:])
    at = [(1, 0), (3, 2), (0, 1)]
    return jnp.stack(
        [jnp.concatenate([parts[h, at[i][h % 2]] for h in range(HEADS_OWN)], axis=0) for i in range(3)]
    )


def doubled(value):
    high = value.astype(BF16)
    return high, (value - high.astype(F32)).astype(BF16)


def twice(form, left, right):
    return products(form, left, right[0]) + products(form, left, right[1])


def together(*groups):
    flat, tree = jax.tree.flatten(groups)
    return jax.tree.unflatten(tree, lax.optimization_barrier(flat))


def fast(
    tokens,
    cotangent,
    lengths,
    clusters,
    owners,
    master,
    bases,
    moment_one,
    moment_two,
    vectors,
    vector_one,
    vector_two,
):
    n_tok = lax.axis_size("tok")
    n_grp = lax.axis_size("grp")
    tok = lax.axis_index("tok")
    grp = lax.axis_index("grp")
    tok_count = tokens.shape[1]
    rows_dev = master.shape[0]
    slots = master.shape[1]
    blocks_all = slots * n_grp
    member = tok % UNIT
    unit = tok // UNIT
    place = [2 * (t % UNIT) + t // UNIT for t in range(n_tok)]
    own_width = HEADS_OWN * HEAD

    slot_block = jnp.argsort(owners, stable=True).astype(jnp.int32)
    block_slot = jnp.argsort(slot_block, stable=True).astype(jnp.int32)

    core, bit_x = grp % 2, grp // 2
    inputs = tokens[0]

    near, far = swap(inputs, "tok", 1), swap(inputs, "tok", 2)
    local = jnp.transpose(master.astype(BF16), (1, 0, 2))
    beside, over = swap(local, "grp", 1), swap(local, "grp", 2)
    across = swap(over, "grp", 1)

    order = jnp.argsort(clusters[0], axis=-1, stable=True).astype(jnp.int32)
    by_member = jnp.transpose(order.reshape(ROUNDS, UNIT, HEADS_OWN, tok_count), (1, 2, 0, 3))
    by_member = by_member.reshape(UNIT, LOCAL_PAIRS, tok_count)
    orders = exchange_unit([pick(by_member, member ^ k) for k in range(UNIT)])
    orders = [jnp.pad(o, ((0, 8 - LOCAL_PAIRS), (0, 0))) for o in orders]
    item_starts = starts_of(lengths[0])
    unit_start = unit * UNIT * tok_count
    middle = unit_start + UNIT // 2 * tok_count
    start_of_middle = jnp.max(jnp.where(item_starts <= middle, item_starts, 0))
    is_long = (start_of_middle <= unit_start).astype(jnp.int32).reshape(1)

    left, right = doubled(bases[0]), doubled(bases[1])
    (near, far, beside, over, across, left, right) = together(near, far, beside, over, across, left, right)
    by_slot = jnp.concatenate([local, beside, over, across], axis=0)
    at = [((block_slot[b] // slots) ^ grp) * slots + block_slot[b] % slots for b in range(blocks_all)]
    part_rows = rows_dev // 2

    def own_half(b):
        return lax.dynamic_slice(by_slot, (at[b], core * part_rows, 0), (1, part_rows, D))[0]

    by_owner = arrange(jnp.stack([own_half(b) for b in range(3)]))
    theirs = exchange_unit([pick(by_owner, member ^ k) for k in range(UNIT)])
    half = tok_count // 2
    third = (swap(near[:half], "tok", 2), swap(far[half:], "tok", 1))
    theirs = jnp.stack(theirs)
    theirs_far = swap(theirs, "tok", UNIT)
    mine_all = jnp.concatenate([theirs, theirs_far], axis=0)
    others_all = swap(mine_all, "grp", 1)
    sources = [tok ^ k ^ (UNIT * f) for f in range(2) for k in range(UNIT)]
    firsts = [t * rows_dev + c * part_rows for c in (core, 1 - core) for t in sources]
    own_weights = assemble(jnp.stack(firsts).astype(jnp.int32), [mine_all, others_all])

    def columns_of(value, m):
        return lax.dynamic_slice_in_dim(value, m * own_width, own_width, value.ndim - 1)

    own_bias = split_heads(
        [columns_of(vectors[4], member), jnp.zeros((own_width,), F32), columns_of(vectors[5], member)]
    ).reshape(1, -1)
    grouped = [
        sort_rows(orders[k], value, own_weights, own_bias) for k, value in enumerate((inputs, near, far))
    ]
    (third, grouped) = together(third, grouped)
    unit_inputs = [inputs, near, far, jnp.concatenate(third, axis=0)]
    grouped.append(sort_rows(orders[3], unit_inputs[3], own_weights, own_bias))

    (rest_rows, _) = together(jnp.stack([own_half(b) for b in range(3, blocks_all)]), third)
    ring = [(i, (i + 2) % n_tok) for i in range(n_tok)]
    depth = n_tok // 2
    steps, flips = [rest_rows], []
    steps.append(lax.ppermute(steps[0], "tok", ring))
    flips.append(swap(steps[0], "tok", 1))
    sorted_out = attend(is_long, grouped)
    (sorted_out, steps[1], flips[0]) = together(sorted_out, steps[1], flips[0])
    mixed = [None] * UNIT
    mixed[3] = mix(orders[3], sorted_out[3])
    mixed[2] = mix(orders[2], sorted_out[2])
    mixed[1] = mix(orders[1], sorted_out[1])
    mixed_parts = exchange_unit(mixed)
    steps.append(lax.ppermute(steps[1], "tok", ring))
    flips.append(swap(steps[1], "tok", 1))
    (steps[2], flips[1], mixed_parts[1:]) = together(steps[2], flips[1], mixed_parts[1:])
    steps.append(lax.ppermute(steps[2], "tok", ring))
    flips.append(swap(steps[2], "tok", 1))
    flips.append(swap(steps[3], "tok", 1))
    mixed_parts[0] = mix(orders[0], sorted_out[0])
    mine_rest = [jnp.stack([steps[k], flips[k]]) for k in range(depth)]
    shards = mine_rest + [swap(m, "grp", 1) for m in mine_rest]
    firsts = [
        ((tok - 2 * k) % n_tok ^ flip) * rows_dev + c * part_rows
        for c in (core, 1 - core)
        for k in range(depth)
        for flip in range(2)
    ]

    held_weights, *shards = lax.optimization_barrier((own_weights, *shards))
    turned_weights = [swap(held_weights, "tok", k) for k in range(1, UNIT)]
    table = jnp.stack([member, core, bit_x, tok % 2, tok // 2 % 2, tok // 4, *firsts]).astype(jnp.int32)
    result, grad_first, back, sums, kept, sent_pieces = layer(
        table, shards, mixed_parts, inputs, cotangent[0], vectors
    )
    (turned_weights, kept, sent_pieces, back) = together(turned_weights, kept, sent_pieces, back)

    grad_parts = exchange_unit([back[k] for k in range(UNIT)])
    other = swap(sent_pieces, "grp", 1)
    sums_of = [kept[p].astype(F32) + other[p].astype(F32) for p in range(3)]

    def halves(values):
        return [v[: v.shape[0] // 2] for v in values], [v[v.shape[0] // 2 :].astype(BF16) for v in values]

    def exchanged(sent_now, stage):
        return [swap(v, *LINKS[PART_ORDERS[p][stage]]) for p, v in enumerate(sent_now)]

    def joined(kept_now, got_now):
        return [k + g.astype(F32) for k, g in zip(kept_now, got_now)]

    sorted_grads = [sort_grads(orders[0], grad_parts[0])]
    kept_now, sent_now = halves(sums_of)
    (sent_now, sorted_grads, grad_parts) = together(sent_now, sorted_grads, grad_parts)
    got_now = exchanged(sent_now, 0)
    sorted_grads += [sort_grads(orders[k], grad_parts[k]) for k in range(1, UNIT)]
    sorted_back = attend_back(is_long, grouped, sorted_grads)
    kept_now, sent_now = halves(joined(kept_now, got_now))
    (sent_now, sorted_back) = together(sent_now, sorted_back)
    got_now = exchanged(sent_now, 1)
    own_grads = [None] * UNIT
    for k in (3, 2):
        own_grads[k] = gather_grads(orders[k], sorted_back[k])
    turned_qkv = sum(inner_rows(own_grads[k], unit_inputs[k]) for k in (3, 2))
    kept_now, sent_now = halves(joined(kept_now, got_now))
    (sent_now, turned_qkv, sorted_back, own_grads[3]) = together(
        sent_now, turned_qkv, sorted_back, own_grads[3]
    )
    got_now = exchanged(sent_now, 2)
    home_grads = [None, None, None, swap(own_grads[3], "tok", 3)]
    for k in (1, 0):
        own_grads[k] = gather_grads(orders[k], sorted_back[k])
    turned_qkv = turned_qkv + sum(inner_rows(own_grads[k], unit_inputs[k]) for k in (1, 0))
    kept_now, sent_now = halves(joined(kept_now, got_now))
    turned_qkv = join_heads(turned_qkv).astype(BF16).reshape(3, 2, own_width // 2, D)
    turned_qkv = (pick(jnp.swapaxes(turned_qkv, 0, 1), unit), pick(jnp.swapaxes(turned_qkv, 0, 1), 1 - unit))
    (sent_now, turned_qkv, own_grads) = together(sent_now, turned_qkv, own_grads)
    got_now = exchanged(sent_now, 3)
    bias_qkv = sum(jnp.sum(own_grads[k].astype(F32), axis=0) for k in range(UNIT))

    bias_query, _, bias_value = join_heads(bias_qkv)
    bias_rows = lax.dynamic_update_slice_in_dim(
        jnp.zeros((2, D), F32), jnp.stack([bias_query, bias_value]), member * own_width, 1
    )
    vector_grads = sums[: 8 + FFB] + jnp.pad(bias_rows, ((4, 2 + FFB), (0, 0)))
    keep = turned_qkv[0].astype(F32) + swap(turned_qkv[1], "tok", UNIT).astype(F32)
    keep = keep + swap(keep.astype(BF16), "grp", 1).astype(F32)
    vector_total = total_of(vector_grads)
    rest = jnp.concatenate([v[0].astype(BF16) for v in joined(kept_now, got_now)], axis=0)
    (rest, home_grads[3]) = together(rest, home_grads[3])
    sent = jnp.stack(
        [pick(rest, jnp.maximum(slot_block[s] - 3, 0)) for s in range(blocks_all)]
    ).reshape(n_grp, slots, *rest.shape[1:])
    got = lax.all_to_all(sent, "grp", split_axis=0, concat_axis=0, tiled=True)
    keep = (keep + swap(keep.astype(BF16), "grp", 2).astype(F32)).astype(BF16)
    got = jnp.transpose(got.reshape(2, 2, *got.shape[1:]), (2, 0, 3, 1, 4))
    got = got.reshape(slots, D // n_tok, D)

    mine = lax.dynamic_slice_in_dim(slot_block, grp * slots, slots, 0)
    reduced = jnp.stack(
        [
            jnp.where(mine[s] < 3, pick(keep, jnp.minimum(mine[s], 2)), got[s]) for s in range(slots)
        ]
    )
    part = products("sia,sci->sac", left[0], reduced) + products("sia,sci->sac", left[1], reduced)
    part = turn_rows(part.astype(BF16), place)
    (part, own_grads[:3], vector_total) = together(part, own_grads[:3], vector_total)
    home_grads[:3] = [own_grads[0]] + [swap(own_grads[k], "tok", k) for k in (1, 2)]
    rotated = twice("sac,scb->sab", part, right)
    rotated = jnp.transpose(rotated, (1, 0, 2))
    new_one = BETA_ONE * moment_one + (1.0 - BETA_ONE) * rotated
    new_two = BETA_TWO * moment_two + (1.0 - BETA_TWO) * rotated * rotated
    direction = (new_one / (jnp.sqrt(new_two) + ADAM_EPS)).astype(BF16)
    turned = twice("asb,scb->sac", direction, right)
    (turned, home_grads[:3]) = together(turned.astype(BF16), home_grads[:3])
    turned = turn_columns(turned, place)
    change = products("sia,sac->sic", left[0], turned) + products("sia,sac->sic", left[1], turned)
    change = turn_rows(change.astype(BF16), place).astype(F32)
    grad_inputs = grad_first + sum(
        outer_cols(home_grads[k], own_weights if k == 0 else turned_weights[k - 1]) for k in range(UNIT)
    )
    new_master = master - RATE_MATRIX * jnp.transpose(change, (1, 0, 2))
    new_vec_one = BETA_ONE * vector_one + (1.0 - BETA_ONE) * vector_total
    new_vec_two = BETA_TWO * vector_two + (1.0 - BETA_TWO) * vector_total * vector_total
    new_vectors = vectors - RATE_VECTOR * new_vec_one / (jnp.sqrt(new_vec_two) + ADAM_EPS)
    return (
        result[None],
        grad_inputs[None],
        new_one,
        new_two,
        new_master,
        new_vec_one,
        new_vec_two,
        new_vectors,
    )


def general(
    tokens,
    cotangent,
    lengths,
    clusters,
    owners,
    master,
    bases,
    moment_one,
    moment_two,
    vectors,
    vector_one,
    vector_two,
):
    n_tok = lax.axis_size("tok")
    tok_count = tokens.shape[1]
    rows_dev = master.shape[0]
    slot_block = jnp.argsort(owners, stable=True)
    block_slot = jnp.argsort(slot_block, stable=True)
    slot_part = lax.all_gather(master.astype(jnp.bfloat16), "grp", axis=1, tiled=True)
    weights = lax.all_gather(slot_part, "tok", axis=0, tiled=True)
    blocks = jnp.stack([pick(jnp.transpose(weights, (1, 0, 2)), block_slot[b]) for b in range(weights.shape[1])], axis=1)
    w_qkv = blocks[:, 0:3, :].reshape(D, 3 * D)
    w_out = blocks[:, 3, :]
    w_up = blocks[:, 4 : 4 + FF // D, :].reshape(D, FF)
    w_down = jnp.transpose(blocks[:, 4 + FF // D :, :], (1, 0, 2)).reshape(FF, D)
    inputs = tokens[0]
    gain_one = vectors[0]
    shift_one = vectors[1]
    gain_two = vectors[2]
    shift_two = vectors[3]
    bias_qkv = jnp.concatenate([vectors[4], jnp.zeros((D,), jnp.float32), vectors[5]])
    qkv = (jnp.dot(inputs, w_qkv, preferred_element_type=jnp.float32) + bias_qkv).astype(
        jnp.bfloat16
    )
    heads = jnp.transpose(qkv.reshape(tok_count, 3, H, HEAD), (2, 0, 1, 3)).reshape(
        H, tok_count, 3 * HEAD
    )
    pair_rows = jnp.broadcast_to(heads[None], (ROUNDS, H, tok_count, 3 * HEAD)).reshape(
        PAIRS * tok_count, 3 * HEAD
    )
    position = lax.axis_index("tok") * tok_count + jnp.arange(tok_count, dtype=jnp.int32)
    item_starts = starts_of(lengths[0])
    item_start = jnp.max(
        jnp.where(item_starts[None, :] <= position[:, None], item_starts[None, :], 0), axis=1
    )
    per_dev = tok_count // CLUSTER
    group_clusters = n_tok * per_dev
    pair_ids = jnp.arange(PAIRS, dtype=jnp.int32)[:, None]
    global_cluster = item_start[None, :] // CLUSTER + clusters[0]
    unit_ids = (pair_ids * group_clusters + global_cluster).reshape(-1)
    owner_ids = ((global_cluster + pair_ids * per_dev) % n_tok).reshape(-1)
    send_order = jnp.argsort(owner_ids * (PAIRS * group_clusters) + unit_ids, stable=True)
    restore = jnp.argsort(send_order, stable=True)
    slot_rows = PAIRS * tok_count // n_tok
    units_here = PAIRS * tok_count // CLUSTER
    sent_rows = pair_rows[send_order].reshape(n_tok, slot_rows // 2, 6 * HEAD)
    sent_units = unit_ids[send_order].reshape(n_tok, slot_rows)
    got_rows, got_units = (
        lax.all_to_all(sent_rows, "tok", split_axis=0, concat_axis=0, tiled=True),
        lax.all_to_all(sent_units, "tok", split_axis=0, concat_axis=0, tiled=True),
    )
    arrange = jnp.argsort(got_units.reshape(-1), stable=True)
    undo = jnp.argsort(arrange, stable=True)
    grouped = got_rows.reshape(PAIRS * tok_count, 3 * HEAD)[arrange].reshape(
        units_here, CLUSTER, 3 * HEAD
    )
    query_rows = grouped[..., :HEAD]
    key_rows = grouped[..., HEAD : 2 * HEAD]
    value_rows = grouped[..., 2 * HEAD :]
    score_scale = HEAD ** (-0.5)
    scores = (
        jnp.einsum("ucd,ued->uce", query_rows, key_rows, preferred_element_type=jnp.float32)
        * score_scale
    )
    row_max = jnp.max(scores, axis=-1, keepdims=True)
    row_total = jnp.sum(jnp.exp(scores - row_max), axis=-1, keepdims=True)
    log_total = row_max + jnp.log(row_total)
    probs = jnp.exp(scores - log_total)
    cluster_out = jnp.einsum(
        "uce,ued->ucd", probs.astype(jnp.bfloat16), value_rows, preferred_element_type=jnp.float32
    ).astype(jnp.bfloat16)
    back_rows = cluster_out.reshape(PAIRS * tok_count, HEAD)[undo].reshape(
        n_tok, slot_rows // 2, 2 * HEAD
    )
    home_rows = lax.all_to_all(back_rows, "tok", split_axis=0, concat_axis=0, tiled=True)
    home_rows = (
        home_rows.reshape(PAIRS * tok_count, HEAD)[restore]
        .reshape(ROUNDS, H, tok_count, HEAD)
        .astype(jnp.float32)
    )
    mixed_heads = 0.5 * (home_rows[0] + home_rows[1])
    mixed_low = jnp.transpose(mixed_heads, (1, 0, 2)).reshape(tok_count, D).astype(jnp.bfloat16)
    attention = jnp.dot(mixed_low, w_out, preferred_element_type=jnp.float32) + vectors[6]
    first_sum = inputs.astype(jnp.float32) + attention
    normed_one, rstd_one = normalize(first_sum)
    hidden = normed_one * gain_one + shift_one
    hidden_low = hidden.astype(jnp.bfloat16)
    up_proj = jnp.dot(hidden_low, w_up, preferred_element_type=jnp.float32) + vectors[8:].reshape(
        FF
    )
    act_low = jax.nn.gelu(up_proj, approximate=False).astype(jnp.bfloat16)
    down_proj = jnp.dot(act_low, w_down, preferred_element_type=jnp.float32) + vectors[7]
    second_sum = hidden + down_proj
    normed_two, rstd_two = normalize(second_sum)
    result = (normed_two * gain_two + shift_two).astype(jnp.bfloat16)
    grad_result = cotangent[0].astype(jnp.float32)
    grad_gain_two = jnp.sum(grad_result * normed_two, axis=0)
    grad_shift_two = jnp.sum(grad_result, axis=0)
    grad_second = norm_back(grad_result * gain_two, normed_two, rstd_two)
    grad_down_low = grad_second.astype(jnp.bfloat16)
    grad_w_down = inner_rows(act_low, grad_down_low)
    grad_bias_down = jnp.sum(grad_down_low.astype(jnp.float32), axis=0)
    grad_act = outer_cols(grad_down_low, w_down)
    grad_up_low = (grad_act * gelu_slope(up_proj)).astype(jnp.bfloat16)
    grad_w_up = inner_rows(hidden_low, grad_up_low)
    grad_bias_up = jnp.sum(grad_up_low.astype(jnp.float32), axis=0)
    grad_hidden = grad_second + outer_cols(grad_up_low, w_up)
    grad_gain_one = jnp.sum(grad_hidden * normed_one, axis=0)
    grad_shift_one = jnp.sum(grad_hidden, axis=0)
    grad_first = norm_back(grad_hidden * gain_one, normed_one, rstd_one)
    grad_attn_low = grad_first.astype(jnp.bfloat16)
    grad_w_out = inner_rows(mixed_low, grad_attn_low)
    grad_bias_out = jnp.sum(grad_attn_low.astype(jnp.float32), axis=0)
    grad_mixed = outer_cols(grad_attn_low, w_out)
    grad_heads = jnp.transpose((0.5 * grad_mixed).reshape(tok_count, H, HEAD), (1, 0, 2)).astype(
        jnp.bfloat16
    )
    grad_pairs = jnp.broadcast_to(grad_heads[None], (ROUNDS, H, tok_count, HEAD)).reshape(
        PAIRS * tok_count, HEAD
    )
    sent_grad = grad_pairs[send_order].reshape(n_tok, slot_rows // 2, 2 * HEAD)
    got_grad = lax.all_to_all(sent_grad, "tok", split_axis=0, concat_axis=0, tiled=True)
    grad_cluster = got_grad.reshape(PAIRS * tok_count, HEAD)[arrange].reshape(
        units_here, CLUSTER, HEAD
    )
    scores_again = (
        jnp.einsum("ucd,ued->uce", query_rows, key_rows, preferred_element_type=jnp.float32)
        * score_scale
    )
    probs_again = jnp.exp(scores_again - log_total)
    probs_low = probs_again.astype(jnp.bfloat16)
    grad_values = jnp.einsum(
        "uce,ucd->ued", probs_low, grad_cluster, preferred_element_type=jnp.float32
    )
    grad_probs = jnp.einsum(
        "ucd,ued->uce", grad_cluster, value_rows, preferred_element_type=jnp.float32
    )
    centre = jnp.sum(probs_again * grad_probs, axis=-1, keepdims=True)
    grad_scores = (probs_again * (grad_probs - centre)).astype(jnp.bfloat16)
    grad_query = (
        jnp.einsum("uce,ued->ucd", grad_scores, key_rows, preferred_element_type=jnp.float32)
        * score_scale
    )
    grad_keys = (
        jnp.einsum("uce,ucd->ued", grad_scores, query_rows, preferred_element_type=jnp.float32)
        * score_scale
    )
    grad_grouped = jnp.concatenate(
        [
            grad_query.astype(jnp.bfloat16),
            grad_keys.astype(jnp.bfloat16),
            grad_values.astype(jnp.bfloat16),
        ],
        axis=-1,
    )
    back_grad = grad_grouped.reshape(PAIRS * tok_count, 3 * HEAD)[undo].reshape(
        n_tok, slot_rows // 2, 6 * HEAD
    )
    home_grad = lax.all_to_all(back_grad, "tok", split_axis=0, concat_axis=0, tiled=True)
    home_grad = (
        home_grad.reshape(PAIRS * tok_count, 3 * HEAD)[restore]
        .reshape(ROUNDS, H, tok_count, 3, HEAD)
        .astype(jnp.float32)
    )
    grad_qkv = (home_grad[0] + home_grad[1]).astype(jnp.bfloat16)
    grad_qkv = jnp.transpose(grad_qkv, (1, 2, 0, 3)).reshape(tok_count, 3 * D)
    grad_w_qkv = inner_rows(inputs, grad_qkv)
    grad_bias_qkv = jnp.sum(grad_qkv.astype(jnp.float32), axis=0)
    grad_inputs = grad_first + outer_cols(grad_qkv, w_qkv)
    grad_blocks = jnp.concatenate(
        [
            grad_w_qkv.reshape(D, 3, D),
            grad_w_out[:, None, :],
            grad_w_up.reshape(D, FF // D, D),
            jnp.transpose(grad_w_down.reshape(FF // D, D, D), (1, 0, 2)),
        ],
        axis=1,
    )
    by_block = jnp.transpose(grad_blocks, (1, 0, 2))
    slot_grads = jnp.stack([pick(by_block, slot_block[s]) for s in range(by_block.shape[0])], axis=1)
    vector_grads = jnp.concatenate(
        [
            jnp.stack(
                [
                    grad_gain_one,
                    grad_shift_one,
                    grad_gain_two,
                    grad_shift_two,
                    grad_bias_qkv[:D],
                    grad_bias_qkv[2 * D :],
                    grad_bias_out,
                    grad_bias_down,
                ]
            ),
            grad_bias_up.reshape(FF // D, D),
        ],
        axis=0,
    )
    vector_total = lax.psum(vector_grads, ("tok", "grp"))
    row_total = lax.psum_scatter(slot_grads, "tok", scatter_dimension=0, tiled=True)
    reduced = lax.psum_scatter(
        row_total.astype(jnp.bfloat16), "grp", scatter_dimension=1, tiled=True
    ).astype(jnp.float32)
    left_basis = bases[0]
    right_basis = bases[1]
    first_row = lax.axis_index("tok") * rows_dev
    turned_in = jnp.einsum("rse,sef->rsf", reduced, right_basis, precision=lax.Precision.HIGHEST)
    left_rows = lax.dynamic_slice_in_dim(left_basis, first_row, rows_dev, 1)
    picked = left_rows
    rotated = lax.psum_scatter(
        jnp.einsum("sri,rsf->isf", picked, turned_in, precision=lax.Precision.HIGHEST),
        "tok",
        scatter_dimension=0,
        tiled=True,
    )
    new_one = BETA_ONE * moment_one + (1.0 - BETA_ONE) * rotated
    new_two = BETA_TWO * moment_two + (1.0 - BETA_TWO) * rotated * rotated
    direction = new_one / (jnp.sqrt(new_two) + ADAM_EPS)
    turned_out = jnp.einsum("rse,sfe->rsf", direction, right_basis, precision=lax.Precision.HIGHEST)
    left_cols = lax.dynamic_slice_in_dim(left_basis, first_row, rows_dev, 2)
    picked = left_cols
    change = lax.psum_scatter(
        jnp.einsum("sir,rsf->isf", picked, turned_out, precision=lax.Precision.HIGHEST),
        "tok",
        scatter_dimension=0,
        tiled=True,
    )
    new_master = master - RATE_MATRIX * change
    new_vec_one = BETA_ONE * vector_one + (1.0 - BETA_ONE) * vector_total
    new_vec_two = BETA_TWO * vector_two + (1.0 - BETA_TWO) * vector_total * vector_total
    new_vectors = vectors - RATE_VECTOR * new_vec_one / (jnp.sqrt(new_vec_two) + ADAM_EPS)
    return (
        result[None],
        grad_inputs[None],
        new_one,
        new_two,
        new_master,
        new_vec_one,
        new_vec_two,
        new_vectors,
    )

def solution(mesh):
    n_tok, n_grp = mesh.shape["tok"], mesh.shape["grp"]

    def on_device(*args):
        lengths, clusters = args[2], args[3]
        unit = n_tok // (lengths.shape[1] - 1)
        suits = unit == UNIT and n_tok == 2 * UNIT and n_grp == 4 and clusters.shape[2] == 1024
        return (fast if suits else general)(*args)

    return jax.shard_map(
        on_device,
        mesh=mesh,
        in_specs=(
            P("grp", "tok", None),
            P("grp", "tok", None),
            P("grp", None),
            P("grp", None, "tok"),
            P(),
            P("tok", "grp", None),
            P(None, "grp", None, None),
            P("tok", "grp", None),
            P("tok", "grp", None),
            P(),
            P(),
            P(),
        ),
        out_specs=(
            P("grp", "tok", None),
            P("grp", "tok", None),
            P("tok", "grp", None),
            P("tok", "grp", None),
            P("tok", "grp", None),
            P(),
            P(),
            P(),
        ),
        check_vma=False,
    )
```

```python
import functools

import jax
import jax.numpy as jnp
from jax import lax
from jax.experimental import pallas as pl
from jax.experimental.pallas import tpu as pltpu
from jax.sharding import PartitionSpec as P

D = 768
H = 12
FF = 3072
HEAD = 64
ROUNDS = 2
PAIRS = 24
CLUSTER = 128
FFB = FF // D

EPS_NORM = 1e-05
ADAM_EPS = 1e-08
BETA_ONE = 0.5
BETA_TWO = 0.5
RATE_MATRIX = 0.025
RATE_VECTOR = 0.15
SQRT_HALF = 0.7071067811865476
INV_ROOT_TWO_PI = 0.3989422804014327

BF16 = jnp.bfloat16
F32 = jnp.float32

UNIT = 4
HEADS_OWN = H // UNIT
LOCAL_PAIRS = ROUNDS * HEADS_OWN
TILE = 128
WIDE = 2 * TILE
SMALL = pl.CostEstimate(flops=0, transcendentals=0, bytes_accessed=0)


def inner_rows(left, right):
    return lax.dot_general(left, right, (((0,), (0,)), ((), ())), preferred_element_type=F32)


def outer_cols(left, right):
    return lax.dot_general(left, right, (((1,), (1,)), ((), ())), preferred_element_type=F32)


def normalize(values_in):
    centre = jnp.mean(values_in, axis=-1, keepdims=True)
    offset = values_in - centre
    spread = jnp.mean(offset * offset, axis=-1, keepdims=True)
    rstd = lax.rsqrt(spread + EPS_NORM)
    return (offset * rstd, rstd)


def norm_back(grad_normed, normed, rstd):
    first_mean = jnp.mean(grad_normed, axis=-1, keepdims=True)
    second_mean = jnp.mean(grad_normed * normed, axis=-1, keepdims=True)
    return rstd * (grad_normed - first_mean - normed * second_mean)


def gelu_slope(values_in):
    return (
        0.5 * (1.0 + lax.erf(values_in * SQRT_HALF))
        + values_in * jnp.exp(-0.5 * values_in * values_in) * INV_ROOT_TWO_PI
    )


def turn_half(value):
    return pltpu.roll(value, HEAD, 1)


def places_body(share_ref, clusters_ref, out_ref):
    pairs, count = clusters_ref.shape
    share = share_ref[0]
    kinds = UNIT * count // CLUSTER
    kind = lax.broadcasted_iota(jnp.int32, (kinds, count), 0)
    earlier = lax.broadcasted_iota(jnp.int32, (count, count), 0) < lax.broadcasted_iota(jnp.int32, (count, count), 1)
    earlier = earlier.astype(F32).astype(BF16)
    for pair in range(pairs):
        cluster = clusters_ref[pair : pair + 1, :]
        same = (kind == cluster).astype(F32)
        before = jnp.dot(same.astype(BF16), earlier, preferred_element_type=F32)
        rank = jnp.sum(same * before, axis=0, keepdims=True).astype(jnp.int32)
        out_ref[pair : pair + 1, :] = cluster * share + rank


def places(share, clusters):
    return pl.pallas_call(
        places_body,
        in_specs=[pl.BlockSpec(memory_space=pltpu.SMEM), pl.BlockSpec(memory_space=pltpu.VMEM)],
        out_shape=jax.ShapeDtypeStruct(clusters.shape, jnp.int32),
        cost_estimate=SMALL,
        name="places",
    )(share, clusters)


def arrange_body(rows_ref, out_ref):
    count = rows_ref.shape[1]
    low = lax.broadcasted_iota(jnp.int32, (count, TILE), 1) < HEAD

    def half(part, head, high):
        at = head // 2 * TILE
        tile = rows_ref[part, :, at : at + TILE].astype(F32)
        return tile if head % 2 == high else turn_half(tile)

    for head in range(H):
        own = head % HEADS_OWN
        odd = own % 2
        value = half(2, head, odd)
        query = half(0, head, 1 - odd)
        keys = half(1, head, 1 - odd)
        one = jnp.where(low, query, value) if odd else jnp.where(low, value, query)
        two = jnp.where(low, keys, 0.0) if odd else jnp.where(low, 0.0, keys)
        out_ref[head // HEADS_OWN, :, own * WIDE : own * WIDE + TILE] = one.astype(BF16)
        out_ref[head // HEADS_OWN, :, own * WIDE + TILE : (own + 1) * WIDE] = two.astype(BF16)


def arrange(rows):
    return pl.pallas_call(
        arrange_body,
        out_shape=jax.ShapeDtypeStruct((UNIT, rows.shape[1], HEADS_OWN * WIDE), BF16),
        cost_estimate=SMALL,
        name="arrange",
    )(rows)


def assemble_body(table_ref, *refs):
    shards, out_ref, sem = refs[:-2], refs[-2], refs[-1]
    rows = shards[0].shape[1]
    copies = []
    for shard in shards:
        for i in range(shard.shape[0]):
            n = len(copies)
            first = pl.multiple_of(table_ref[n], rows)
            copies.append(
                pltpu.make_async_copy(shard.at[i], out_ref.at[pl.ds(first, rows), :], sem.at[n])
            )
    for copy in copies:
        copy.start()
    for copy in copies:
        copy.wait()


def assemble(table, shards):
    pieces = sum(s.shape[0] for s in shards)
    anywhere = pl.BlockSpec(memory_space=pl.ANY)
    return pl.pallas_call(
        assemble_body,
        in_specs=[pl.BlockSpec(memory_space=pltpu.SMEM)] + [anywhere] * len(shards),
        out_specs=pl.BlockSpec(memory_space=pltpu.VMEM),
        out_shape=jax.ShapeDtypeStruct((pieces * shards[0].shape[1], shards[0].shape[2]), BF16),
        scratch_shapes=[pltpu.SemaphoreType.DMA((pieces,))],
        cost_estimate=SMALL,
        name="assemble",
    )(table, *shards)


def sort_body(place_ref, x_ref, weight_ref, bias_ref, out_ref, rows_ref):
    count = x_ref.shape[0]
    head = pl.program_id(0)
    chunk = 256
    row = lax.broadcasted_iota(jnp.int32, (chunk, count), 0)
    rows_ref[...] = (
        jnp.dot(x_ref[...], weight_ref[...], preferred_element_type=F32) + bias_ref[...]
    ).astype(BF16)
    for step in range(HEADS_OWN):

        @pl.when(head == step)
        def _():
            for turn in range(ROUNDS):
                pair = step * ROUNDS + turn
                for part in range(count // chunk):
                    where = pl.ds(part * chunk, chunk)
                    picked = place_ref[pair : pair + 1, :] == row + part * chunk
                    picked = picked.astype(F32).astype(BF16)
                    out_ref[turn, where, :] = jnp.dot(
                        picked, rows_ref[...], preferred_element_type=F32
                    ).astype(BF16)


def sort_rows(order, inputs, weights, bias):
    count = inputs.shape[0]
    return pl.pallas_call(
        sort_body,
        grid=(HEADS_OWN,),
        in_specs=[
            pl.BlockSpec((8, count), lambda h: (0, 0)),
            pl.BlockSpec((count, D), lambda h: (0, 0)),
            pl.BlockSpec((D, WIDE), lambda h: (0, h)),
            pl.BlockSpec((1, WIDE), lambda h: (0, h)),
        ],
        out_specs=pl.BlockSpec((ROUNDS, count, WIDE), lambda h: (h, 0, 0)),
        out_shape=jax.ShapeDtypeStruct((LOCAL_PAIRS, count, WIDE), BF16),
        scratch_shapes=[pltpu.VMEM((count, WIDE), BF16)],
        compiler_params=pltpu.CompilerParams(vmem_limit_bytes=48 << 20),
        cost_estimate=SMALL,
        name="sort_rows",
    )(order, inputs, weights, bias)


def sort_grads_body(place_ref, rows_ref, out_ref):
    count = place_ref.shape[1]
    half = count // 2
    head = pl.program_id(0)
    chunk = 256
    row = lax.broadcasted_iota(jnp.int32, (chunk, count), 0)
    low = lax.broadcasted_iota(jnp.int32, (count, TILE), 1) < HEAD
    for step in range(HEADS_OWN):

        @pl.when(head == step)
        def _():
            if step < 2:
                tile = rows_ref[0:count, :].astype(F32)
                tile = jnp.where(low if step == 0 else jnp.logical_not(low), tile, 0.0).astype(BF16)
            else:
                both = rows_ref[count : count + half, :].astype(F32)
                tile = jnp.concatenate([both, turn_half(both)], axis=0)
                tile = jnp.where(low, tile, 0.0).astype(BF16)
            for turn in range(ROUNDS):
                pair = step * ROUNDS + turn
                for part in range(count // chunk):
                    where = pl.ds(part * chunk, chunk)
                    picked = place_ref[pair : pair + 1, :] == row + part * chunk
                    picked = picked.astype(F32).astype(BF16)
                    out_ref[turn, where, :] = jnp.dot(
                        picked, tile, preferred_element_type=F32
                    ).astype(BF16)


def sort_grads(order, rows):
    count = order.shape[1]
    return pl.pallas_call(
        sort_grads_body,
        grid=(HEADS_OWN,),
        in_specs=[
            pl.BlockSpec((8, count), lambda h: (0, 0)),
            pl.BlockSpec(rows.shape, lambda h: (0, 0)),
        ],
        out_specs=pl.BlockSpec((ROUNDS, count, TILE), lambda h: (h, 0, 0)),
        out_shape=jax.ShapeDtypeStruct((LOCAL_PAIRS, count, TILE), BF16),
        compiler_params=pltpu.CompilerParams(vmem_limit_bytes=48 << 20),
        cost_estimate=SMALL,
        name="sort_grads",
    )(order, rows)


def plans_of(count):
    share = CLUSTER // UNIT
    half = UNIT // 2
    return (
        [(tuple(range(UNIT)), share)],
        [(tuple(range(i * half, (i + 1) * half)), 2 * share) for i in range(2)],
    )


def for_each_batch(is_long, count, batch, work):
    for wanted, plan in zip((1, 0), plans_of(count)):

        @pl.when(is_long == wanted)
        def _(plan=plan):
            for runs, share in plan:

                def step(group, carry, runs=runs, share=share):
                    first = pl.multiple_of(group * (batch * share), batch * share)
                    work(runs, pl.ds(first, batch * share), share)
                    return carry

                lax.fori_loop(0, count // share // batch, step, 0)


def batch_of(refs, runs, where, share, width):
    parts = [refs[r][0, where, :] for r in runs]
    return jnp.concatenate([p.reshape(p.shape[0] // share, share, width) for p in parts], axis=1)


def spread(refs, runs, where, share, columns, value):
    for i, r in enumerate(runs):
        part = value[:, i * share : (i + 1) * share]
        refs[r][0, where, columns] = part.reshape(part.shape[0] * share, TILE)


def products(form, left, right):
    return jnp.einsum(form, left, right, preferred_element_type=F32)


def softmax(first, second):
    scores = products("ued,ucd->uec", second, first) * (HEAD**-0.5)
    expo = jnp.exp(scores - jnp.max(scores, axis=1, keepdims=True))
    return expo * (1.0 / jnp.sum(expo, axis=1, keepdims=True))


def attend_body(long_ref, *refs):
    grouped, results = refs[:UNIT], refs[UNIT:]

    def work(runs, where, share):
        rows = batch_of(grouped, runs, where, share, WIDE)
        first = rows[..., :TILE]
        probs = softmax(first, rows[..., TILE:]).astype(BF16)
        mixed = products("uce,ued->ucd", jnp.swapaxes(probs, 1, 2), first).astype(BF16)
        spread(results, runs, where, share, slice(0, TILE), mixed)

    for_each_batch(long_ref[0], grouped[0].shape[1], 8, work)


def attend(is_long, grouped):
    count = grouped[0].shape[1]
    return pl.pallas_call(
        attend_body,
        grid_spec=pltpu.PrefetchScalarGridSpec(
            num_scalar_prefetch=1,
            grid=(LOCAL_PAIRS,),
            in_specs=[pl.BlockSpec((1, count, WIDE), lambda p, _: (p, 0, 0))] * UNIT,
            out_specs=[pl.BlockSpec((1, count, TILE), lambda p, _: (p, 0, 0))] * UNIT,
        ),
        out_shape=[jax.ShapeDtypeStruct((LOCAL_PAIRS, count, TILE), BF16)] * UNIT,
        compiler_params=pltpu.CompilerParams(vmem_limit_bytes=48 << 20),
        cost_estimate=SMALL,
        name="attend",
    )(is_long, *grouped)


def attend_back_body(long_ref, *refs):
    grouped, grads, results = refs[:UNIT], refs[UNIT : 2 * UNIT], refs[2 * UNIT :]
    batch = 16
    odd = (pl.program_id(0) // ROUNDS) % 2
    lane = lax.broadcasted_iota(jnp.int32, (batch, CLUSTER, TILE), 2)
    value_lane = (lane < HEAD) == (odd == 0)
    scale = HEAD**-0.5

    def work(runs, where, share):
        rows = batch_of(grouped, runs, where, share, WIDE)
        grad = batch_of(grads, runs, where, share, TILE)
        first, second = rows[..., :TILE], rows[..., TILE:]
        probs = softmax(first, second)
        grad_probs = products("ued,ucd->uec", first, grad)
        centre = jnp.sum(probs * grad_probs, axis=1, keepdims=True)
        grad_scores = (probs * (grad_probs - centre)).astype(BF16)
        grad_values = products("uec,ucd->ued", probs.astype(BF16), grad)
        grad_keys = products("uec,ucd->ued", grad_scores, first) * scale
        grad_query = products("uce,ued->ucd", jnp.swapaxes(grad_scores, 1, 2), second) * scale
        tile_one = jnp.where(value_lane, grad_values, grad_query).astype(BF16)
        tile_two = jnp.where(value_lane, 0.0, grad_keys).astype(BF16)
        spread(results, runs, where, share, slice(0, TILE), tile_one)
        spread(results, runs, where, share, slice(TILE, WIDE), tile_two)

    for_each_batch(long_ref[0], grouped[0].shape[1], batch, work)


def attend_back(is_long, grouped, grads):
    count = grouped[0].shape[1]
    return pl.pallas_call(
        attend_back_body,
        grid_spec=pltpu.PrefetchScalarGridSpec(
            num_scalar_prefetch=1,
            grid=(LOCAL_PAIRS,),
            in_specs=[pl.BlockSpec((1, count, WIDE), lambda p, _: (p, 0, 0))] * UNIT
            + [pl.BlockSpec((1, count, TILE), lambda p, _: (p, 0, 0))] * UNIT,
            out_specs=[pl.BlockSpec((1, count, WIDE), lambda p, _: (p, 0, 0))] * UNIT,
        ),
        out_shape=[jax.ShapeDtypeStruct((LOCAL_PAIRS, count, WIDE), BF16)] * UNIT,
        compiler_params=pltpu.CompilerParams(vmem_limit_bytes=56 << 20),
        cost_estimate=SMALL,
        name="attend_back",
    )(is_long, *grouped, *grads)


def unsorted(column_ref, step, rows_ref, part, chunk):
    count = rows_ref.shape[1]
    where = pl.ds(part * chunk, chunk)
    lane = lax.broadcasted_iota(jnp.int32, (chunk, count), 1)
    total = None
    for turn in range(ROUNDS):
        pair = step * ROUNDS + turn
        picked = (column_ref[where, pair : pair + 1] == lane).astype(F32).astype(BF16)
        more = jnp.dot(picked, rows_ref[turn], preferred_element_type=F32)
        total = more if total is None else total + more
    return total


def mix_body(place_ref, rows_ref, out_ref, column_ref):
    @pl.when(pl.program_id(0) == 0)
    def _():
        column_ref[...] = jnp.transpose(place_ref[...])

    count = rows_ref.shape[1]
    chunk = 256
    parts = count // chunk
    low = lax.broadcasted_iota(jnp.int32, (chunk, TILE), 1) < HEAD
    head = pl.program_id(0)
    for step in range(HEADS_OWN):

        @pl.when(head == step)
        def _():
            means = [0.5 * unsorted(column_ref, step, rows_ref, part, chunk) for part in range(parts)]
            for part in range(parts):
                where = pl.ds(part * chunk, chunk)
                if step == 0:
                    out_ref[where, :] = means[part].astype(BF16)
                elif step == 1:
                    out_ref[where, :] = jnp.where(low, out_ref[where, :].astype(F32), means[part]).astype(BF16)
                elif part < parts // 2:
                    both = jnp.where(low, means[part], turn_half(means[part + parts // 2]))
                    out_ref[pl.ds(count + part * chunk, chunk), :] = both.astype(BF16)


def mix(order, rows):
    count = rows.shape[1]
    packed = (count + count // 2, TILE)
    return pl.pallas_call(
        mix_body,
        grid=(HEADS_OWN,),
        in_specs=[
            pl.BlockSpec((8, count), lambda h: (0, 0)),
            pl.BlockSpec((ROUNDS, count, TILE), lambda h: (h, 0, 0)),
        ],
        out_specs=pl.BlockSpec(packed, lambda h: (0, 0)),
        out_shape=jax.ShapeDtypeStruct(packed, BF16),
        scratch_shapes=[pltpu.VMEM((count, 8), jnp.int32)],
        compiler_params=pltpu.CompilerParams(vmem_limit_bytes=48 << 20),
        cost_estimate=SMALL,
        name="mix",
    )(order, rows)


def gather_grads_body(place_ref, rows_ref, out_ref, column_ref):
    @pl.when(pl.program_id(0) == 0)
    def _():
        column_ref[...] = jnp.transpose(place_ref[...])

    count = rows_ref.shape[1]
    chunk = 256
    head = pl.program_id(0)
    for step in range(HEADS_OWN):

        @pl.when(head == step)
        def _():
            for part in range(count // chunk):
                where = pl.ds(part * chunk, chunk)
                out_ref[where, :] = unsorted(column_ref, step, rows_ref, part, chunk).astype(BF16)


def gather_grads(order, rows):
    count = rows.shape[1]
    return pl.pallas_call(
        gather_grads_body,
        grid=(HEADS_OWN,),
        in_specs=[
            pl.BlockSpec((8, count), lambda h: (0, 0)),
            pl.BlockSpec((ROUNDS, count, WIDE), lambda h: (h, 0, 0)),
        ],
        out_specs=pl.BlockSpec((count, WIDE), lambda h: (0, h)),
        out_shape=jax.ShapeDtypeStruct((count, HEADS_OWN * WIDE), BF16),
        scratch_shapes=[pltpu.VMEM((count, 8), jnp.int32)],
        compiler_params=pltpu.CompilerParams(vmem_limit_bytes=48 << 20),
        cost_estimate=SMALL,
        name="gather_grads",
    )(order, rows)


ERF_TOP = (0.00022905065861350646, 0.0034082910107109506, 0.050955695062380861, 0.18520832239976145, 1.128379143519084)
ERF_BOTTOM = (
    -1.1791602954361697e-7,
    0.000023547966471313185,
    0.0010179625278914885,
    0.014070470171167667,
    0.11098505178285362,
    0.49746925110067538,
    1.0,
)


def polynomial(value, factors):
    total = jnp.full_like(value, factors[0])
    for factor in factors[1:]:
        total = total * value + factor
    return total


def error_function(value):
    value = jnp.clip(value, -3.832506856900711, 3.832506856900711)
    square = value * value
    return value * polynomial(square, ERF_TOP) / polynomial(square, ERF_BOTTOM)


VEC_ROWS = 16
FFN_TILE = 256


def layer_body(
    n_shards,
    table_ref,
    *refs,
):
    shards, refs = refs[:n_shards], refs[n_shards:]
    parts, refs = refs[:UNIT], refs[UNIT:]
    x_ref, cot_ref, vec_ref, result_ref, first_ref, back_ref, sums_ref, kept_ref, sent_ref = refs[:9]
    w_ref, packed_ref, mixed_ref, hidden_ref, act_ref, down_ref, up_ref, attn_ref = refs[9:17]
    slope_ref, stage_ref, weight_sem, part_sem, stage_sem = refs[17:]
    count = x_ref.shape[0]
    half = count // 2
    per_shard, n_weights, shard_rows = shards[0].shape[:3]
    member = table_ref[0]
    for k in range(UNIT):
        pltpu.make_async_copy(parts[k], packed_ref.at[member ^ k], part_sem.at[k]).start()
    for b in range(n_weights):
        for n in range(n_shards * per_shard):
            row = pl.multiple_of(table_ref[6 + n], shard_rows)
            pltpu.make_async_copy(
                shards[n // per_shard].at[n % per_shard, b], w_ref.at[b, pl.ds(row, shard_rows), :], weight_sem.at[b]
            ).start()
    for k in range(UNIT):
        pltpu.make_async_copy(parts[k], packed_ref.at[member ^ k], part_sem.at[k]).wait()
    for b in range(n_weights):
        pltpu.make_async_copy(w_ref.at[b], w_ref.at[b], weight_sem.at[b]).wait()

    sums_ref[...] = jnp.zeros_like(sums_ref)
    low = lax.broadcasted_iota(jnp.int32, (FFN_TILE, TILE), 1) < HEAD
    vec = [vec_ref[i : i + 1, :] for i in range(8 + FFB)]
    gain_one, shift_one, gain_two, shift_two = vec[:4]
    bias_out, bias_down = vec[6], vec[7]

    def add_sum(row, value):
        sums_ref[row : row + 1, :] += jnp.sum(value, axis=0, keepdims=True)

    def tile_step(i, carry):
        rows = pl.ds(pl.multiple_of(i * FFN_TILE, FFN_TILE), FFN_TILE)
        is_first = i * FFN_TILE < half
        extra = pl.ds(pl.multiple_of(count + lax.rem(i * FFN_TILE, half), FFN_TILE), FFN_TILE)

        def pair(m):
            return packed_ref[m, rows, :].astype(F32)

        def single(m):
            value = packed_ref[m, extra, :].astype(F32)
            return jnp.where(is_first, value, turn_half(value))

        for m in (0, 2):
            at = m * (HEADS_OWN * HEAD)
            nxt = turn_half(pair(m + 1))
            mixed_ref[rows, at : at + TILE] = pair(m).astype(BF16)
            mixed_ref[rows, at + TILE : at + 2 * TILE] = jnp.where(low, single(m), nxt).astype(BF16)
            mixed_ref[rows, at + 2 * TILE : at + 3 * TILE] = jnp.where(
                low, nxt, turn_half(single(m + 1))
            ).astype(BF16)
        attention = jnp.dot(mixed_ref[rows, :], w_ref[0], preferred_element_type=F32) + bias_out
        normed_one, rstd_one = normalize(x_ref[rows, :].astype(F32) + attention)
        hidden = normed_one * gain_one + shift_one
        hidden_low = hidden.astype(BF16)
        hidden_ref[rows, :] = hidden_low
        down = jnp.broadcast_to(bias_down, hidden.shape)
        for j in range(FFB):
            up = jnp.dot(hidden_low, w_ref[1 + j], preferred_element_type=F32) + vec[8 + j]
            phi = 0.5 * (1.0 + error_function(up * SQRT_HALF))
            slope_ref[j] = phi + up * jnp.exp(-0.5 * up * up) * INV_ROOT_TWO_PI
            act = (up * phi).astype(BF16)
            act_ref[j, rows, :] = act
            down = down + jnp.dot(act, w_ref[1 + FFB + j], preferred_element_type=F32)
        normed_two, rstd_two = normalize(hidden + down)
        result_ref[rows, :] = (normed_two * gain_two + shift_two).astype(BF16)
        grad_result = cot_ref[rows, :].astype(F32)
        add_sum(2, grad_result * normed_two)
        add_sum(3, grad_result)
        grad_second = norm_back(grad_result * gain_two, normed_two, rstd_two)
        grad_down = grad_second.astype(BF16)
        down_ref[rows, :] = grad_down
        add_sum(7, grad_down.astype(F32))
        grad_hidden = grad_second
        for j in range(FFB):
            grad_up = (outer_cols(grad_down, w_ref[1 + FFB + j]) * slope_ref[j]).astype(BF16)
            up_ref[j, rows, :] = grad_up
            add_sum(8 + j, grad_up.astype(F32))
            grad_hidden = grad_hidden + outer_cols(grad_up, w_ref[1 + j])
        add_sum(0, grad_hidden * normed_one)
        add_sum(1, grad_hidden)
        grad_first = norm_back(grad_hidden * gain_one, normed_one, rstd_one)
        first_ref[rows, :] = grad_first
        grad_attn = grad_first.astype(BF16)
        attn_ref[rows, :] = grad_attn
        add_sum(6, grad_attn.astype(F32))
        grad_mixed = (0.5 * outer_cols(grad_attn, w_ref[0])).astype(BF16).astype(F32)
        for m in range(UNIT):
            at = (m // 2) * 3 * TILE
            tiles = [grad_mixed[:, at + n * TILE : at + (n + 1) * TILE] for n in range(3)]
            if m % 2 == 0:
                two, one = tiles[0], tiles[1]
            else:
                two, one = turn_half(jnp.where(low, tiles[2], tiles[1])), turn_half(tiles[2])
            back_ref[member ^ m, rows, :] = two.astype(BF16)

            @pl.when(is_first)
            def _(one=one, m=m):
                back_ref[member ^ m, extra, :] = jnp.where(low, one, 0.0).astype(BF16)

            @pl.when(jnp.logical_not(is_first))
            def _(one=one, m=m):
                old = back_ref[member ^ m, extra, :].astype(F32)
                back_ref[member ^ m, extra, :] = jnp.where(low, old, turn_half(one)).astype(BF16)

        return carry

    lax.fori_loop(0, count // FFN_TILE, tile_step, 0)

    core, bits = table_ref[1], [table_ref[2 + d] for d in range(4)]
    piece, half_columns = kept_ref.shape[3:]
    n_parts = kept_ref.shape[0]
    per_part = n_weights // n_parts

    def copies(block, slot, half, target):
        part = block // per_part
        made = []
        for index in range(16):
            x, zh, y, zl = ((index >> s) % 2 for s in range(4))
            rel = {"x": x ^ bits[0], "y": y ^ bits[1], "zl": zl ^ bits[2], "zh": zh ^ bits[3]}
            place = 0
            for name in PART_ORDERS[part]:
                place = place * 2 + rel[name]
            made.append(
                pltpu.make_async_copy(
                    stage_ref.at[
                        slot, pl.ds(index * piece, piece), pl.ds(half * half_columns, half_columns)
                    ],
                    target.at[part, place, block % per_part],
                    stage_sem.at[slot, half * 16 + index],
                )
            )
        return made

    def send(block, slot):
        for half in range(2):

            @pl.when(core == half)
            def _(half=half):
                for copy in copies(block, slot, half, kept_ref):
                    copy.start()

            @pl.when(core != half)
            def _(half=half):
                for copy in copies(block, slot, half, sent_ref):
                    copy.start()

    def sent(block, slot):
        for half in range(2):
            for copy in copies(block, slot, half, kept_ref):
                copy.wait()

    plan = [(attn_ref, None, mixed_ref, None, 0)]
    plan += [(down_ref, None, act_ref, j, 1 + FFB + j) for j in range(FFB)]
    plan += [(up_ref, j, hidden_ref, None, 1 + j) for j in range(FFB)]
    for n, (left, lj, right, rj, block) in enumerate(plan):
        slot = n % 2
        if n >= 2:
            sent(plan[n - 2][4], slot)
        value = inner_rows(
            left[...] if lj is None else left[lj], right[...] if rj is None else right[rj]
        )
        stage_ref[slot] = value.astype(BF16)
        send(block, slot)
    for n in (len(plan) - 2, len(plan) - 1):
        sent(plan[n][4], n % 2)


PART_ORDERS = (("x", "y", "zl", "zh"), ("y", "zl", "zh", "x"), ("zl", "zh", "x", "y"))


def layer(table, shards, parts, inputs, cotangent, vectors):
    count = inputs.shape[0]
    n_weights = 1 + 2 * FFB
    n_shards = len(shards)
    anywhere = pl.BlockSpec(memory_space=pl.ANY)
    inside = pl.BlockSpec(memory_space=pltpu.VMEM)
    packed = parts[0].shape
    return pl.pallas_call(
        functools.partial(layer_body, n_shards),
        in_specs=[pl.BlockSpec(memory_space=pltpu.SMEM)] + [anywhere] * (n_shards + UNIT) + [inside] * 3,
        out_specs=[inside, inside, inside, inside, anywhere, anywhere],
        out_shape=[
            jax.ShapeDtypeStruct((count, D), BF16),
            jax.ShapeDtypeStruct((count, D), F32),
            jax.ShapeDtypeStruct((UNIT, *packed), BF16),
            jax.ShapeDtypeStruct((VEC_ROWS, D), F32),
            jax.ShapeDtypeStruct((3, 16, n_weights // 3, D // 16, D // 2), BF16),
            jax.ShapeDtypeStruct((3, 16, n_weights // 3, D // 16, D // 2), BF16),
        ],
        scratch_shapes=[
            pltpu.VMEM((n_weights, D, D), BF16),
            pltpu.VMEM((UNIT, *packed), BF16),
            pltpu.VMEM((count, D), BF16),
            pltpu.VMEM((count, D), BF16),
            pltpu.VMEM((FFB, count, D), BF16),
            pltpu.VMEM((count, D), BF16),
            pltpu.VMEM((FFB, count, D), BF16),
            pltpu.VMEM((count, D), BF16),
            pltpu.VMEM((FFB, FFN_TILE, D), F32),
            pltpu.VMEM((2, D, D), BF16),
            pltpu.SemaphoreType.DMA((n_weights,)),
            pltpu.SemaphoreType.DMA((UNIT,)),
            pltpu.SemaphoreType.DMA((2, 32)),
        ],
        compiler_params=pltpu.CompilerParams(vmem_limit_bytes=60 << 20),
        cost_estimate=SMALL,
        name="layer",
    )(table, *shards, *parts, inputs, cotangent, vectors)


def rotate_in_body(mine_ref, keep_ref, got_ref, high_ref, low_ref, out_ref, grad_ref):
    slots, n_tok = got_ref.shape[1], out_ref.shape[0]
    rows, columns = got_ref.shape[2:]
    width = out_ref.shape[3]
    for s in range(slots):
        block = mine_ref[s]

        @pl.when(block < 3)
        def _(s=s, block=block):
            grad_ref[...] = keep_ref[jnp.minimum(block, 2)]

        @pl.when(block >= 3)
        def _(s=s):
            for g in range(got_ref.shape[0]):
                x, c = g // 2, g % 2
                grad_ref[x * rows : (x + 1) * rows, c * columns : (c + 1) * columns] = got_ref[g, s]

        grad = grad_ref[...]
        part = jnp.dot(grad, high_ref[s], preferred_element_type=F32)
        part = jnp.transpose(part + jnp.dot(grad, low_ref[s], preferred_element_type=F32))
        for r in range(n_tok):
            out_ref[r, s] = part[r * width : (r + 1) * width].astype(BF16)


def rotate_in(mine, keep, got, left, n_tok):
    slots, width = got.shape[1], keep.shape[1]
    inside = pl.BlockSpec(memory_space=pltpu.VMEM)
    return pl.pallas_call(
        rotate_in_body,
        in_specs=[pl.BlockSpec(memory_space=pltpu.SMEM)] + [inside] * 4,
        out_specs=inside,
        out_shape=jax.ShapeDtypeStruct((n_tok, slots, width, width), BF16),
        scratch_shapes=[pltpu.VMEM(keep.shape[1:], BF16)],
        compiler_params=pltpu.CompilerParams(vmem_limit_bytes=48 << 20),
        cost_estimate=SMALL,
        name="rotate_in",
    )(mine, keep, got, *left)


def moments_body(place, got_ref, high_ref, low_ref, one_ref, two_ref, new_one_ref, new_two_ref, out_ref):
    n_tok, slots, width = got_ref.shape[:3]
    for s in range(slots):
        rotated = jnp.zeros(one_ref.shape[1:], F32)
        for t in range(n_tok):
            at = slice(place[t] * width, (place[t] + 1) * width)
            part = got_ref[t, s]
            rotated = rotated + jnp.dot(part, high_ref[s, at], preferred_element_type=F32)
            rotated = rotated + jnp.dot(part, low_ref[s, at], preferred_element_type=F32)
        new_one = BETA_ONE * one_ref[s] + (1.0 - BETA_ONE) * rotated
        new_two = BETA_TWO * two_ref[s] + (1.0 - BETA_TWO) * rotated * rotated
        new_one_ref[s] = new_one
        new_two_ref[s] = new_two
        direction = (new_one / (jnp.sqrt(new_two) + ADAM_EPS)).astype(BF16)
        for t in range(n_tok):
            at = slice(place[t] * width, (place[t] + 1) * width)
            turned = outer_cols(direction, high_ref[s, at]) + outer_cols(direction, low_ref[s, at])
            out_ref[t, s] = turned.astype(BF16)


def moments(place, got, right, one, two):
    n_tok, slots, width = got.shape[:3]
    inside = pl.BlockSpec(memory_space=pltpu.VMEM)
    return pl.pallas_call(
        functools.partial(moments_body, tuple(place)),
        in_specs=[inside] * 5,
        out_specs=[inside] * 3,
        out_shape=[
            jax.ShapeDtypeStruct(one.shape, F32),
            jax.ShapeDtypeStruct(one.shape, F32),
            jax.ShapeDtypeStruct(got.shape, BF16),
        ],
        compiler_params=pltpu.CompilerParams(vmem_limit_bytes=48 << 20),
        cost_estimate=SMALL,
        name="moments",
    )(got, *right, one, two)


def rotate_out_body(got_ref, high_ref, low_ref, out_ref, rows_ref):
    n_tok, slots, width = got_ref.shape[:3]
    for s in range(slots):
        for r in range(n_tok):
            rows_ref[r * width : (r + 1) * width, :] = got_ref[r, s]
        rows = rows_ref[...]
        change = jnp.dot(high_ref[s], rows, preferred_element_type=F32)
        change = change + jnp.dot(low_ref[s], rows, preferred_element_type=F32)
        for r in range(n_tok):
            out_ref[r, s] = change[r * width : (r + 1) * width].astype(BF16)


def rotate_out(got, left):
    n_tok, slots, width = got.shape[:3]
    inside = pl.BlockSpec(memory_space=pltpu.VMEM)
    return pl.pallas_call(
        rotate_out_body,
        in_specs=[inside] * 3,
        out_specs=inside,
        out_shape=jax.ShapeDtypeStruct(got.shape, BF16),
        scratch_shapes=[pltpu.VMEM((n_tok * width, width), BF16)],
        compiler_params=pltpu.CompilerParams(vmem_limit_bytes=48 << 20),
        cost_estimate=SMALL,
        name="rotate_out",
    )(got, *left)


def apply_body(place, got_ref, master_ref, out_ref):
    n_tok, slots, width = got_ref.shape[:3]
    for s in range(slots):
        for t in range(n_tok):
            at = slice(place[t] * width, (place[t] + 1) * width)
            out_ref[s, :, at] = master_ref[s, :, at] - RATE_MATRIX * got_ref[t, s].astype(F32)


def apply_change(place, got, master):
    inside = pl.BlockSpec(memory_space=pltpu.VMEM)
    return pl.pallas_call(
        functools.partial(apply_body, tuple(place)),
        in_specs=[inside] * 2,
        out_specs=inside,
        out_shape=jax.ShapeDtypeStruct(master.shape, F32),
        compiler_params=pltpu.CompilerParams(vmem_limit_bytes=48 << 20),
        cost_estimate=SMALL,
        name="apply_change",
    )(got, master)


def swap(value, axis, bit):
    size = lax.axis_size(axis)
    return lax.ppermute(value, axis, [(i, i ^ bit) for i in range(size)])


def exchange_unit(parts):
    return [parts[0]] + [swap(parts[k], "tok", k) for k in range(1, UNIT)]


LINKS = {"x": ("grp", 2), "y": ("tok", 1), "zl": ("tok", 2), "zh": ("tok", 4)}


def starts_of(lengths):
    index = jnp.arange(lengths.shape[0])
    return jnp.sum(jnp.where(index[None, :] < index[:, None], lengths[None, :], 0), axis=1)


LINKS = {"x": ("grp", 2), "y": ("tok", 1), "zl": ("tok", 2), "zh": ("tok", 4)}


def starts_of(lengths):
    index = jnp.arange(lengths.shape[0])
    return jnp.sum(jnp.where(index[None, :] < index[:, None], lengths[None, :], 0), axis=1)


def total_of(value):
    for axis in ("grp", "tok"):
        bit = 1
        while bit < lax.axis_size(axis):
            value = value + swap(value, axis, bit)
            bit *= 2
    return value


def pick(values, index):
    return lax.dynamic_index_in_dim(values, index, 0, keepdims=False)


def split_heads(columns):
    query, keys, values = (c.reshape(HEADS_OWN, HEAD) for c in columns)
    zero = jnp.zeros((HEAD,), query.dtype)
    tiles = []
    for h in range(HEADS_OWN):
        tiles += [values[h], query[h], zero, keys[h]] if h % 2 == 0 else [query[h], values[h], keys[h], zero]
    return jnp.concatenate(tiles)


def join_heads(tiles):
    parts = tiles.reshape(HEADS_OWN, 4, HEAD, *tiles.shape[1:])
    at = [(1, 0), (3, 2), (0, 1)]
    return jnp.stack(
        [jnp.concatenate([parts[h, at[i][h % 2]] for h in range(HEADS_OWN)], axis=0) for i in range(3)]
    )


def doubled(value):
    high = value.astype(BF16)
    return high, (value - high.astype(F32)).astype(BF16)


def together(*groups):
    flat, tree = jax.tree.flatten(groups)
    return jax.tree.unflatten(tree, lax.optimization_barrier(flat))


def fast(
    tokens,
    cotangent,
    lengths,
    clusters,
    owners,
    master,
    bases,
    moment_one,
    moment_two,
    vectors,
    vector_one,
    vector_two,
):
    n_tok = lax.axis_size("tok")
    n_grp = lax.axis_size("grp")
    tok = lax.axis_index("tok")
    grp = lax.axis_index("grp")
    tok_count = tokens.shape[1]
    rows_dev = master.shape[0]
    slots = master.shape[1]
    blocks_all = slots * n_grp
    member = tok % UNIT
    unit = tok // UNIT
    place = [2 * (t % UNIT) + t // UNIT for t in range(n_tok)]
    own_width = HEADS_OWN * HEAD

    slot_block = jnp.argsort(owners, stable=True).astype(jnp.int32)
    block_slot = jnp.argsort(slot_block, stable=True).astype(jnp.int32)

    core, bit_x = grp % 2, grp // 2
    inputs = tokens[0]

    near, far = swap(inputs, "tok", 1), swap(inputs, "tok", 2)
    local = jnp.transpose(master.astype(BF16), (1, 0, 2))
    beside, over = swap(local, "grp", 1), swap(local, "grp", 2)

    item_starts = starts_of(lengths[0])
    unit_start = unit * UNIT * tok_count
    middle = unit_start + UNIT // 2 * tok_count
    start_of_middle = jnp.max(jnp.where(item_starts <= middle, item_starts, 0))
    is_long = (start_of_middle <= unit_start).astype(jnp.int32).reshape(1)
    order = places(CLUSTER // UNIT * (2 - is_long), clusters[0])
    by_member = jnp.transpose(order.reshape(ROUNDS, UNIT, HEADS_OWN, tok_count), (1, 2, 0, 3))
    by_member = by_member.reshape(UNIT, LOCAL_PAIRS, tok_count)
    by_member = jnp.pad(by_member, ((0, 0), (0, 8 - LOCAL_PAIRS), (0, 0)))
    orders = exchange_unit([pick(by_member, member ^ k) for k in range(UNIT)])
    left, right = doubled(bases[0]), doubled(bases[1])
    (over, left, right) = together(over, left, right)
    across = swap(over, "grp", 1)

    (near, far, beside, over, across) = together(near, far, beside, over, across)
    by_slot = jnp.concatenate([local, beside, over, across], axis=0)
    at = [((block_slot[b] // slots) ^ grp) * slots + block_slot[b] % slots for b in range(blocks_all)]
    part_rows = rows_dev // 2

    def own_half(source, b):
        return lax.dynamic_slice(source, (at[b], core * part_rows, 0), (1, part_rows, D))[0]

    by_owner = arrange(jnp.stack([own_half(by_slot, b) for b in range(3)]))
    theirs = exchange_unit([pick(by_owner, member ^ k) for k in range(UNIT)])
    half = tok_count // 2
    third = (swap(near[:half], "tok", 2), swap(far[half:], "tok", 1))
    (theirs, by_slot) = together(theirs, by_slot)
    theirs = jnp.stack(theirs)
    theirs_far = swap(theirs, "tok", UNIT)
    mine_all = jnp.concatenate([theirs, theirs_far], axis=0)
    others_all = swap(mine_all, "grp", 1)
    sources = [tok ^ k ^ (UNIT * f) for f in range(2) for k in range(UNIT)]
    firsts = [t * rows_dev + c * part_rows for c in (core, 1 - core) for t in sources]
    rest_rows = jnp.stack([own_half(by_slot, b) for b in range(3, blocks_all)])
    (third, others_all, rest_rows, orders) = together(third, others_all, rest_rows, orders)
    own_weights = assemble(jnp.stack(firsts).astype(jnp.int32), [mine_all, others_all])

    def columns_of(value, m):
        return lax.dynamic_slice_in_dim(value, m * own_width, own_width, value.ndim - 1)

    own_bias = split_heads(
        [columns_of(vectors[4], member), jnp.zeros((own_width,), F32), columns_of(vectors[5], member)]
    ).reshape(1, -1)
    grouped = [
        sort_rows(orders[k], value, own_weights, own_bias) for k, value in enumerate((inputs, near, far))
    ]
    unit_inputs = [inputs, near, far, jnp.concatenate(third, axis=0)]
    grouped.append(sort_rows(orders[3], unit_inputs[3], own_weights, own_bias))

    ring = [(i, (i + 2) % n_tok) for i in range(n_tok)]
    depth = n_tok // 2
    steps, flips = [rest_rows], []
    steps.append(lax.ppermute(steps[0], "tok", ring))
    flips.append(swap(steps[0], "tok", 1))
    (grouped, steps[1], flips[0]) = together(grouped, steps[1], flips[0])
    steps.append(lax.ppermute(steps[1], "tok", ring))
    flips.append(swap(steps[1], "tok", 1))
    sorted_out = attend(is_long, grouped)
    (sorted_out, steps[2], flips[1]) = together(sorted_out, steps[2], flips[1])
    mixed = [None] * UNIT
    mixed[3] = mix(orders[3], sorted_out[3])
    mixed[2] = mix(orders[2], sorted_out[2])
    mixed[1] = mix(orders[1], sorted_out[1])
    mixed_parts = exchange_unit(mixed)
    steps.append(lax.ppermute(steps[2], "tok", ring))
    flips.append(swap(steps[2], "tok", 1))
    (steps[3], flips[2], mixed_parts[1:]) = together(steps[3], flips[2], mixed_parts[1:])
    flips.append(swap(steps[3], "tok", 1))
    mixed_parts[0] = mix(orders[0], sorted_out[0])
    mine_rest = [jnp.stack([steps[k], flips[k]]) for k in range(depth)]
    shards = mine_rest + [swap(m, "grp", 1) for m in mine_rest]
    firsts = [
        ((tok - 2 * k) % n_tok ^ flip) * rows_dev + c * part_rows
        for c in (core, 1 - core)
        for k in range(depth)
        for flip in range(2)
    ]

    held_weights, *shards = lax.optimization_barrier((own_weights, *shards))
    turned_weights = [swap(held_weights, "tok", k) for k in range(1, UNIT)]
    table = jnp.stack([member, core, bit_x, tok % 2, tok // 2 % 2, tok // 4, *firsts]).astype(jnp.int32)
    result, grad_first, back, sums, kept, sent_pieces = layer(
        table, shards, mixed_parts, inputs, cotangent[0], vectors
    )
    (turned_weights, kept, sent_pieces, back) = together(turned_weights, kept, sent_pieces, back)

    grad_parts = exchange_unit([back[k] for k in range(UNIT)])
    other = swap(sent_pieces, "grp", 1)
    sums_of = [kept[p].astype(F32) + other[p].astype(F32) for p in range(3)]

    def halves(values):
        return [v[: v.shape[0] // 2] for v in values], [v[v.shape[0] // 2 :].astype(BF16) for v in values]

    def exchanged(sent_now, stage):
        return [swap(v, *LINKS[PART_ORDERS[p][stage]]) for p, v in enumerate(sent_now)]

    def joined(kept_now, got_now):
        return [k + g.astype(F32) for k, g in zip(kept_now, got_now)]

    kept_now, sent_now = halves(sums_of)
    (sent_now, grad_parts) = together(sent_now, grad_parts)
    got_now = exchanged(sent_now, 0)
    sorted_grads = [sort_grads(orders[k], grad_parts[k]) for k in range(UNIT)]
    sorted_back = attend_back(is_long, grouped, sorted_grads)
    kept_now, sent_now = halves(joined(kept_now, got_now))
    (sent_now, sorted_back) = together(sent_now, sorted_back)
    got_now = exchanged(sent_now, 1)
    own_grads = [None] * UNIT
    for k in (3, 2):
        own_grads[k] = gather_grads(orders[k], sorted_back[k])
    turned_qkv = sum(inner_rows(own_grads[k], unit_inputs[k]) for k in (3, 2))
    kept_now, sent_now = halves(joined(kept_now, got_now))
    (sent_now, turned_qkv, sorted_back) = together(sent_now, turned_qkv, sorted_back)
    got_now = exchanged(sent_now, 2)
    for k in (1, 0):
        own_grads[k] = gather_grads(orders[k], sorted_back[k])
    turned_qkv = turned_qkv + sum(inner_rows(own_grads[k], unit_inputs[k]) for k in (1, 0))
    kept_now, sent_now = halves(joined(kept_now, got_now))
    turned_qkv = join_heads(turned_qkv).astype(BF16).reshape(3, 2, own_width // 2, 2, D // 2)
    turned_qkv = jnp.transpose(turned_qkv, (3, 1, 0, 2, 4))
    (sent_now, turned_qkv) = together(sent_now, turned_qkv)
    got_now = exchanged(sent_now, 3)

    bias_qkv = sum(jnp.sum(own_grads[k].astype(F32), axis=0) for k in range(UNIT))
    bias_query, _, bias_value = join_heads(bias_qkv)
    bias_rows = lax.dynamic_update_slice_in_dim(
        jnp.zeros((2, D), F32), jnp.stack([bias_query, bias_value]), member * own_width, 1
    )
    total = sums[: 8 + FFB] + jnp.pad(bias_rows, ((4, 2 + FFB), (0, 0)))

    core_got = swap(pick(turned_qkv, 1 - core), "grp", 1)
    more = swap(total, "grp", 1)
    keep = pick(turned_qkv, core).astype(F32) + core_got.astype(F32)
    (keep, more) = together(keep, more)
    total = total + more
    more = swap(total, "grp", 2)
    unit_got = swap(pick(keep, 1 - unit).astype(BF16), "tok", UNIT)
    home_grads = [own_grads[0], swap(own_grads[1], "tok", 1), None, None]
    rest = jnp.concatenate([v[0].astype(BF16) for v in joined(kept_now, got_now)], axis=0)
    sent = jnp.stack(
        [pick(rest, jnp.maximum(slot_block[s] - 3, 0)) for s in range(blocks_all)]
    ).reshape(n_grp, slots, *rest.shape[1:])
    got = lax.all_to_all(sent, "grp", split_axis=0, concat_axis=0, tiled=True)
    keep = pick(keep, unit) + unit_got.astype(F32)
    (keep, more, own_grads[2]) = together(keep, more, own_grads[2])
    total = total + more
    more = swap(total, "tok", 1)
    keep = keep + swap(keep.astype(BF16), "grp", 2).astype(F32)
    (keep, more) = together(keep.astype(BF16), more)
    total = total + more
    more = swap(total, "tok", 2)
    home_grads[2] = swap(own_grads[2], "tok", 2)
    kept_core = (keep, swap(keep, "grp", 1))
    keep = jnp.concatenate(
        [jnp.where(core == 0, kept_core[0], kept_core[1]), jnp.where(core == 0, kept_core[1], kept_core[0])],
        axis=-1,
    )
    mine = lax.dynamic_slice_in_dim(slot_block, grp * slots, slots, 0)

    def to_tok(value):
        return lax.all_to_all(value, "tok", split_axis=0, concat_axis=0, tiled=True)

    part = to_tok(rotate_in(mine, keep, got, left, n_tok))
    (part, more, home_grads[1], own_grads[3]) = together(part, more, home_grads[1], own_grads[3])
    total = total + more
    more = swap(total, "tok", 4)
    home_grads[3] = swap(own_grads[3], "tok", 3)
    by_slot_of = lambda value: jnp.transpose(value, (1, 0, 2))
    new_one, new_two, turned = moments(
        place, part, right, by_slot_of(moment_one), by_slot_of(moment_two)
    )
    turned = to_tok(turned)
    (turned, more, home_grads[2]) = together(turned, more, home_grads[2])
    vector_total = total + more
    change = to_tok(rotate_out(turned, left))
    new_master = by_slot_of(apply_change(place, change, by_slot_of(master)))
    new_one, new_two = by_slot_of(new_one), by_slot_of(new_two)
    grad_inputs = grad_first + sum(
        outer_cols(home_grads[k], own_weights if k == 0 else turned_weights[k - 1]) for k in range(UNIT)
    )
    new_vec_one = BETA_ONE * vector_one + (1.0 - BETA_ONE) * vector_total
    new_vec_two = BETA_TWO * vector_two + (1.0 - BETA_TWO) * vector_total * vector_total
    new_vectors = vectors - RATE_VECTOR * new_vec_one / (jnp.sqrt(new_vec_two) + ADAM_EPS)
    return (
        result[None],
        grad_inputs[None],
        new_one,
        new_two,
        new_master,
        new_vec_one,
        new_vec_two,
        new_vectors,
    )


def general(
    tokens,
    cotangent,
    lengths,
    clusters,
    owners,
    master,
    bases,
    moment_one,
    moment_two,
    vectors,
    vector_one,
    vector_two,
):
    n_tok = lax.axis_size("tok")
    tok_count = tokens.shape[1]
    rows_dev = master.shape[0]
    slot_block = jnp.argsort(owners, stable=True)
    block_slot = jnp.argsort(slot_block, stable=True)
    slot_part = lax.all_gather(master.astype(jnp.bfloat16), "grp", axis=1, tiled=True)
    weights = lax.all_gather(slot_part, "tok", axis=0, tiled=True)
    blocks = jnp.stack([pick(jnp.transpose(weights, (1, 0, 2)), block_slot[b]) for b in range(weights.shape[1])], axis=1)
    w_qkv = blocks[:, 0:3, :].reshape(D, 3 * D)
    w_out = blocks[:, 3, :]
    w_up = blocks[:, 4 : 4 + FF // D, :].reshape(D, FF)
    w_down = jnp.transpose(blocks[:, 4 + FF // D :, :], (1, 0, 2)).reshape(FF, D)
    inputs = tokens[0]
    gain_one = vectors[0]
    shift_one = vectors[1]
    gain_two = vectors[2]
    shift_two = vectors[3]
    bias_qkv = jnp.concatenate([vectors[4], jnp.zeros((D,), jnp.float32), vectors[5]])
    qkv = (jnp.dot(inputs, w_qkv, preferred_element_type=jnp.float32) + bias_qkv).astype(
        jnp.bfloat16
    )
    heads = jnp.transpose(qkv.reshape(tok_count, 3, H, HEAD), (2, 0, 1, 3)).reshape(
        H, tok_count, 3 * HEAD
    )
    pair_rows = jnp.broadcast_to(heads[None], (ROUNDS, H, tok_count, 3 * HEAD)).reshape(
        PAIRS * tok_count, 3 * HEAD
    )
    position = lax.axis_index("tok") * tok_count + jnp.arange(tok_count, dtype=jnp.int32)
    item_starts = starts_of(lengths[0])
    item_start = jnp.max(
        jnp.where(item_starts[None, :] <= position[:, None], item_starts[None, :], 0), axis=1
    )
    per_dev = tok_count // CLUSTER
    group_clusters = n_tok * per_dev
    pair_ids = jnp.arange(PAIRS, dtype=jnp.int32)[:, None]
    global_cluster = item_start[None, :] // CLUSTER + clusters[0]
    unit_ids = (pair_ids * group_clusters + global_cluster).reshape(-1)
    owner_ids = ((global_cluster + pair_ids * per_dev) % n_tok).reshape(-1)
    send_order = jnp.argsort(owner_ids * (PAIRS * group_clusters) + unit_ids, stable=True)
    restore = jnp.argsort(send_order, stable=True)
    slot_rows = PAIRS * tok_count // n_tok
    units_here = PAIRS * tok_count // CLUSTER
    sent_rows = pair_rows[send_order].reshape(n_tok, slot_rows // 2, 6 * HEAD)
    sent_units = unit_ids[send_order].reshape(n_tok, slot_rows)
    got_rows, got_units = (
        lax.all_to_all(sent_rows, "tok", split_axis=0, concat_axis=0, tiled=True),
        lax.all_to_all(sent_units, "tok", split_axis=0, concat_axis=0, tiled=True),
    )
    arrange = jnp.argsort(got_units.reshape(-1), stable=True)
    undo = jnp.argsort(arrange, stable=True)
    grouped = got_rows.reshape(PAIRS * tok_count, 3 * HEAD)[arrange].reshape(
        units_here, CLUSTER, 3 * HEAD
    )
    query_rows = grouped[..., :HEAD]
    key_rows = grouped[..., HEAD : 2 * HEAD]
    value_rows = grouped[..., 2 * HEAD :]
    score_scale = HEAD ** (-0.5)
    scores = (
        jnp.einsum("ucd,ued->uce", query_rows, key_rows, preferred_element_type=jnp.float32)
        * score_scale
    )
    row_max = jnp.max(scores, axis=-1, keepdims=True)
    row_total = jnp.sum(jnp.exp(scores - row_max), axis=-1, keepdims=True)
    log_total = row_max + jnp.log(row_total)
    probs = jnp.exp(scores - log_total)
    cluster_out = jnp.einsum(
        "uce,ued->ucd", probs.astype(jnp.bfloat16), value_rows, preferred_element_type=jnp.float32
    ).astype(jnp.bfloat16)
    back_rows = cluster_out.reshape(PAIRS * tok_count, HEAD)[undo].reshape(
        n_tok, slot_rows // 2, 2 * HEAD
    )
    home_rows = lax.all_to_all(back_rows, "tok", split_axis=0, concat_axis=0, tiled=True)
    home_rows = (
        home_rows.reshape(PAIRS * tok_count, HEAD)[restore]
        .reshape(ROUNDS, H, tok_count, HEAD)
        .astype(jnp.float32)
    )
    mixed_heads = 0.5 * (home_rows[0] + home_rows[1])
    mixed_low = jnp.transpose(mixed_heads, (1, 0, 2)).reshape(tok_count, D).astype(jnp.bfloat16)
    attention = jnp.dot(mixed_low, w_out, preferred_element_type=jnp.float32) + vectors[6]
    first_sum = inputs.astype(jnp.float32) + attention
    normed_one, rstd_one = normalize(first_sum)
    hidden = normed_one * gain_one + shift_one
    hidden_low = hidden.astype(jnp.bfloat16)
    up_proj = jnp.dot(hidden_low, w_up, preferred_element_type=jnp.float32) + vectors[8:].reshape(
        FF
    )
    act_low = jax.nn.gelu(up_proj, approximate=False).astype(jnp.bfloat16)
    down_proj = jnp.dot(act_low, w_down, preferred_element_type=jnp.float32) + vectors[7]
    second_sum = hidden + down_proj
    normed_two, rstd_two = normalize(second_sum)
    result = (normed_two * gain_two + shift_two).astype(jnp.bfloat16)
    grad_result = cotangent[0].astype(jnp.float32)
    grad_gain_two = jnp.sum(grad_result * normed_two, axis=0)
    grad_shift_two = jnp.sum(grad_result, axis=0)
    grad_second = norm_back(grad_result * gain_two, normed_two, rstd_two)
    grad_down_low = grad_second.astype(jnp.bfloat16)
    grad_w_down = inner_rows(act_low, grad_down_low)
    grad_bias_down = jnp.sum(grad_down_low.astype(jnp.float32), axis=0)
    grad_act = outer_cols(grad_down_low, w_down)
    grad_up_low = (grad_act * gelu_slope(up_proj)).astype(jnp.bfloat16)
    grad_w_up = inner_rows(hidden_low, grad_up_low)
    grad_bias_up = jnp.sum(grad_up_low.astype(jnp.float32), axis=0)
    grad_hidden = grad_second + outer_cols(grad_up_low, w_up)
    grad_gain_one = jnp.sum(grad_hidden * normed_one, axis=0)
    grad_shift_one = jnp.sum(grad_hidden, axis=0)
    grad_first = norm_back(grad_hidden * gain_one, normed_one, rstd_one)
    grad_attn_low = grad_first.astype(jnp.bfloat16)
    grad_w_out = inner_rows(mixed_low, grad_attn_low)
    grad_bias_out = jnp.sum(grad_attn_low.astype(jnp.float32), axis=0)
    grad_mixed = outer_cols(grad_attn_low, w_out)
    grad_heads = jnp.transpose((0.5 * grad_mixed).reshape(tok_count, H, HEAD), (1, 0, 2)).astype(
        jnp.bfloat16
    )
    grad_pairs = jnp.broadcast_to(grad_heads[None], (ROUNDS, H, tok_count, HEAD)).reshape(
        PAIRS * tok_count, HEAD
    )
    sent_grad = grad_pairs[send_order].reshape(n_tok, slot_rows // 2, 2 * HEAD)
    got_grad = lax.all_to_all(sent_grad, "tok", split_axis=0, concat_axis=0, tiled=True)
    grad_cluster = got_grad.reshape(PAIRS * tok_count, HEAD)[arrange].reshape(
        units_here, CLUSTER, HEAD
    )
    scores_again = (
        jnp.einsum("ucd,ued->uce", query_rows, key_rows, preferred_element_type=jnp.float32)
        * score_scale
    )
    probs_again = jnp.exp(scores_again - log_total)
    probs_low = probs_again.astype(jnp.bfloat16)
    grad_values = jnp.einsum(
        "uce,ucd->ued", probs_low, grad_cluster, preferred_element_type=jnp.float32
    )
    grad_probs = jnp.einsum(
        "ucd,ued->uce", grad_cluster, value_rows, preferred_element_type=jnp.float32
    )
    centre = jnp.sum(probs_again * grad_probs, axis=-1, keepdims=True)
    grad_scores = (probs_again * (grad_probs - centre)).astype(jnp.bfloat16)
    grad_query = (
        jnp.einsum("uce,ued->ucd", grad_scores, key_rows, preferred_element_type=jnp.float32)
        * score_scale
    )
    grad_keys = (
        jnp.einsum("uce,ucd->ued", grad_scores, query_rows, preferred_element_type=jnp.float32)
        * score_scale
    )
    grad_grouped = jnp.concatenate(
        [
            grad_query.astype(jnp.bfloat16),
            grad_keys.astype(jnp.bfloat16),
            grad_values.astype(jnp.bfloat16),
        ],
        axis=-1,
    )
    back_grad = grad_grouped.reshape(PAIRS * tok_count, 3 * HEAD)[undo].reshape(
        n_tok, slot_rows // 2, 6 * HEAD
    )
    home_grad = lax.all_to_all(back_grad, "tok", split_axis=0, concat_axis=0, tiled=True)
    home_grad = (
        home_grad.reshape(PAIRS * tok_count, 3 * HEAD)[restore]
        .reshape(ROUNDS, H, tok_count, 3, HEAD)
        .astype(jnp.float32)
    )
    grad_qkv = (home_grad[0] + home_grad[1]).astype(jnp.bfloat16)
    grad_qkv = jnp.transpose(grad_qkv, (1, 2, 0, 3)).reshape(tok_count, 3 * D)
    grad_w_qkv = inner_rows(inputs, grad_qkv)
    grad_bias_qkv = jnp.sum(grad_qkv.astype(jnp.float32), axis=0)
    grad_inputs = grad_first + outer_cols(grad_qkv, w_qkv)
    grad_blocks = jnp.concatenate(
        [
            grad_w_qkv.reshape(D, 3, D),
            grad_w_out[:, None, :],
            grad_w_up.reshape(D, FF // D, D),
            jnp.transpose(grad_w_down.reshape(FF // D, D, D), (1, 0, 2)),
        ],
        axis=1,
    )
    by_block = jnp.transpose(grad_blocks, (1, 0, 2))
    slot_grads = jnp.stack([pick(by_block, slot_block[s]) for s in range(by_block.shape[0])], axis=1)
    vector_grads = jnp.concatenate(
        [
            jnp.stack(
                [
                    grad_gain_one,
                    grad_shift_one,
                    grad_gain_two,
                    grad_shift_two,
                    grad_bias_qkv[:D],
                    grad_bias_qkv[2 * D :],
                    grad_bias_out,
                    grad_bias_down,
                ]
            ),
            grad_bias_up.reshape(FF // D, D),
        ],
        axis=0,
    )
    vector_total = lax.psum(vector_grads, ("tok", "grp"))
    row_total = lax.psum_scatter(slot_grads, "tok", scatter_dimension=0, tiled=True)
    reduced = lax.psum_scatter(
        row_total.astype(jnp.bfloat16), "grp", scatter_dimension=1, tiled=True
    ).astype(jnp.float32)
    left_basis = bases[0]
    right_basis = bases[1]
    first_row = lax.axis_index("tok") * rows_dev
    turned_in = jnp.einsum("rse,sef->rsf", reduced, right_basis, precision=lax.Precision.HIGHEST)
    left_rows = lax.dynamic_slice_in_dim(left_basis, first_row, rows_dev, 1)
    picked = left_rows
    rotated = lax.psum_scatter(
        jnp.einsum("sri,rsf->isf", picked, turned_in, precision=lax.Precision.HIGHEST),
        "tok",
        scatter_dimension=0,
        tiled=True,
    )
    new_one = BETA_ONE * moment_one + (1.0 - BETA_ONE) * rotated
    new_two = BETA_TWO * moment_two + (1.0 - BETA_TWO) * rotated * rotated
    direction = new_one / (jnp.sqrt(new_two) + ADAM_EPS)
    turned_out = jnp.einsum("rse,sfe->rsf", direction, right_basis, precision=lax.Precision.HIGHEST)
    left_cols = lax.dynamic_slice_in_dim(left_basis, first_row, rows_dev, 2)
    picked = left_cols
    change = lax.psum_scatter(
        jnp.einsum("sir,rsf->isf", picked, turned_out, precision=lax.Precision.HIGHEST),
        "tok",
        scatter_dimension=0,
        tiled=True,
    )
    new_master = master - RATE_MATRIX * change
    new_vec_one = BETA_ONE * vector_one + (1.0 - BETA_ONE) * vector_total
    new_vec_two = BETA_TWO * vector_two + (1.0 - BETA_TWO) * vector_total * vector_total
    new_vectors = vectors - RATE_VECTOR * new_vec_one / (jnp.sqrt(new_vec_two) + ADAM_EPS)
    return (
        result[None],
        grad_inputs[None],
        new_one,
        new_two,
        new_master,
        new_vec_one,
        new_vec_two,
        new_vectors,
    )

def solution(mesh):
    n_tok, n_grp = mesh.shape["tok"], mesh.shape["grp"]

    def on_device(*args):
        lengths, clusters = args[2], args[3]
        unit = n_tok // (lengths.shape[1] - 1)
        suits = unit == UNIT and n_tok == 2 * UNIT and n_grp == 4 and clusters.shape[2] == 1024
        return (fast if suits else general)(*args)

    return jax.shard_map(
        on_device,
        mesh=mesh,
        in_specs=(
            P("grp", "tok", None),
            P("grp", "tok", None),
            P("grp", None),
            P("grp", None, "tok"),
            P(),
            P("tok", "grp", None),
            P(None, "grp", None, None),
            P("tok", "grp", None),
            P("tok", "grp", None),
            P(),
            P(),
            P(),
        ),
        out_specs=(
            P("grp", "tok", None),
            P("grp", "tok", None),
            P("tok", "grp", None),
            P("tok", "grp", None),
            P("tok", "grp", None),
            P(),
            P(),
            P(),
        ),
        check_vma=False,
    )
```

```python
import functools

import jax
import jax.numpy as jnp
from jax import lax
from jax.experimental import pallas as pl
from jax.experimental.pallas import tpu as pltpu
from jax.sharding import PartitionSpec as P

D = 768
H = 12
FF = 3072
HEAD = 64
ROUNDS = 2
PAIRS = 24
CLUSTER = 128
FFB = FF // D

EPS_NORM = 1e-05
ADAM_EPS = 1e-08
BETA_ONE = 0.5
BETA_TWO = 0.5
RATE_MATRIX = 0.025
RATE_VECTOR = 0.15
SQRT_HALF = 0.7071067811865476
INV_ROOT_TWO_PI = 0.3989422804014327

BF16 = jnp.bfloat16
F32 = jnp.float32

UNIT = 4
HEADS_OWN = H // UNIT
LOCAL_PAIRS = ROUNDS * HEADS_OWN
TILE = 128
WIDE = 2 * TILE
SMALL = pl.CostEstimate(flops=0, transcendentals=0, bytes_accessed=0)


def inner_rows(left, right):
    return lax.dot_general(left, right, (((0,), (0,)), ((), ())), preferred_element_type=F32)


def outer_cols(left, right):
    return lax.dot_general(left, right, (((1,), (1,)), ((), ())), preferred_element_type=F32)


def normalize(values_in):
    centre = jnp.mean(values_in, axis=-1, keepdims=True)
    offset = values_in - centre
    spread = jnp.mean(offset * offset, axis=-1, keepdims=True)
    rstd = lax.rsqrt(spread + EPS_NORM)
    return (offset * rstd, rstd)


def norm_back(grad_normed, normed, rstd):
    first_mean = jnp.mean(grad_normed, axis=-1, keepdims=True)
    second_mean = jnp.mean(grad_normed * normed, axis=-1, keepdims=True)
    return rstd * (grad_normed - first_mean - normed * second_mean)


def gelu_slope(values_in):
    return (
        0.5 * (1.0 + lax.erf(values_in * SQRT_HALF))
        + values_in * jnp.exp(-0.5 * values_in * values_in) * INV_ROOT_TWO_PI
    )


def turn_half(value):
    return pltpu.roll(value, HEAD, 1)


def places_body(scalars_ref, clusters_ref, *refs):
    outs, all_ref = refs[:UNIT], refs[UNIT]
    pairs, count = clusters_ref.shape
    share, member = scalars_ref[0], scalars_ref[1]
    kinds = UNIT * count // CLUSTER
    kind = lax.broadcasted_iota(jnp.int32, (kinds, count), 0)
    earlier = lax.broadcasted_iota(jnp.int32, (count, count), 0) < lax.broadcasted_iota(jnp.int32, (count, count), 1)
    earlier = earlier.astype(F32).astype(BF16)
    all_ref[...] = jnp.zeros_like(all_ref)
    for pair in range(pairs):
        turn, head = pair // H, pair % H
        cluster = clusters_ref[pair : pair + 1, :]
        same = (kind == cluster).astype(F32)
        before = jnp.dot(same.astype(BF16), earlier, preferred_element_type=F32)
        rank = jnp.sum(same * before, axis=0, keepdims=True).astype(jnp.int32)
        own = head % HEADS_OWN * ROUNDS + turn
        all_ref[head // HEADS_OWN, own : own + 1, :] = cluster * share + rank
    for k in range(UNIT):
        outs[k][...] = all_ref[member ^ k]


def places(scalars, clusters):
    count = clusters.shape[1]
    inside = pl.BlockSpec(memory_space=pltpu.VMEM)
    return pl.pallas_call(
        places_body,
        in_specs=[pl.BlockSpec(memory_space=pltpu.SMEM), inside],
        out_specs=[inside] * UNIT,
        out_shape=[jax.ShapeDtypeStruct((8, count), jnp.int32)] * UNIT,
        scratch_shapes=[pltpu.VMEM((UNIT, 8, count), jnp.int32)],
        cost_estimate=SMALL,
        name="places",
    )(scalars, clusters)


def arrange_body(slots, scalars_ref, *refs):
    sources, outs, rest_ref, tiles_ref = refs[:4], refs[4 : 4 + UNIT], refs[4 + UNIT], refs[5 + UNIT]
    n_rest, count = rest_ref.shape[:2]
    n_blocks = n_rest + 3
    group, core, member = (scalars_ref[n_blocks + i] for i in range(3))
    first = pl.multiple_of(core * count, count)

    def rows_of(block):
        slot = scalars_ref[block]
        owner = lax.div(slot, slots)
        near, inner = owner ^ group, lax.rem(slot, slots)
        found = [source[inner, pl.ds(first, count), :].astype(F32) for source in sources]
        low = jnp.where(near % 2 == 0, found[0], found[1])
        high = jnp.where(near % 2 == 0, found[2], found[3])
        return jnp.where(near < 2, low, high)

    low = lax.broadcasted_iota(jnp.int32, (count, TILE), 1) < HEAD
    parts = [rows_of(i) for i in range(3)]

    def half(part, head, high):
        at = head // 2 * TILE
        tile = parts[part][:, at : at + TILE]
        return tile if head % 2 == high else turn_half(tile)

    for head in range(H):
        own = head % HEADS_OWN
        odd = own % 2
        value = half(2, head, odd)
        query = half(0, head, 1 - odd)
        keys = half(1, head, 1 - odd)
        one = jnp.where(low, query, value) if odd else jnp.where(low, value, query)
        two = jnp.where(low, keys, 0.0) if odd else jnp.where(low, 0.0, keys)
        tiles_ref[head // HEADS_OWN, :, own * WIDE : own * WIDE + TILE] = one.astype(BF16)
        tiles_ref[head // HEADS_OWN, :, own * WIDE + TILE : (own + 1) * WIDE] = two.astype(BF16)
    for k in range(UNIT):
        outs[k][...] = tiles_ref[member ^ k]
    for b in range(n_rest):
        rest_ref[b] = rows_of(3 + b).astype(BF16)


def arrange(scalars, sources, n_blocks):
    slots, rows = sources[0].shape[:2]
    count = rows // 2
    width = HEADS_OWN * WIDE
    inside = pl.BlockSpec(memory_space=pltpu.VMEM)
    return pl.pallas_call(
        functools.partial(arrange_body, slots),
        in_specs=[pl.BlockSpec(memory_space=pltpu.SMEM)] + [inside] * 4,
        out_specs=[inside] * (UNIT + 1),
        out_shape=[jax.ShapeDtypeStruct((count, width), BF16)] * UNIT
        + [jax.ShapeDtypeStruct((n_blocks - 3, count, D), BF16)],
        scratch_shapes=[pltpu.VMEM((UNIT, count, width), BF16)],
        compiler_params=pltpu.CompilerParams(vmem_limit_bytes=32 << 20),
        cost_estimate=SMALL,
        name="arrange",
    )(scalars, *sources)


def assemble_body(table_ref, *refs):
    shards, out_ref, sem = refs[:-2], refs[-2], refs[-1]
    rows = shards[0].shape[1]
    copies = []
    for shard in shards:
        for i in range(shard.shape[0]):
            n = len(copies)
            first = pl.multiple_of(table_ref[n], rows)
            copies.append(
                pltpu.make_async_copy(shard.at[i], out_ref.at[pl.ds(first, rows), :], sem.at[n])
            )
    for copy in copies:
        copy.start()
    for copy in copies:
        copy.wait()


def assemble(table, shards):
    pieces = sum(s.shape[0] for s in shards)
    anywhere = pl.BlockSpec(memory_space=pl.ANY)
    return pl.pallas_call(
        assemble_body,
        in_specs=[pl.BlockSpec(memory_space=pltpu.SMEM)] + [anywhere] * len(shards),
        out_specs=pl.BlockSpec(memory_space=pltpu.VMEM),
        out_shape=jax.ShapeDtypeStruct((pieces * shards[0].shape[1], shards[0].shape[2]), BF16),
        scratch_shapes=[pltpu.SemaphoreType.DMA((pieces,))],
        cost_estimate=SMALL,
        name="assemble",
    )(table, *shards)


def sort_body(place_ref, x_ref, weight_ref, bias_ref, out_ref, rows_ref):
    count = x_ref.shape[0]
    head = pl.program_id(0)
    chunk = 256
    row = lax.broadcasted_iota(jnp.int32, (chunk, count), 0)
    rows_ref[...] = (
        jnp.dot(x_ref[...], weight_ref[...], preferred_element_type=F32) + bias_ref[...]
    ).astype(BF16)
    for step in range(HEADS_OWN):

        @pl.when(head == step)
        def _():
            for turn in range(ROUNDS):
                pair = step * ROUNDS + turn
                for part in range(count // chunk):
                    where = pl.ds(part * chunk, chunk)
                    picked = place_ref[pair : pair + 1, :] == row + part * chunk
                    picked = picked.astype(F32).astype(BF16)
                    out_ref[turn, where, :] = jnp.dot(
                        picked, rows_ref[...], preferred_element_type=F32
                    ).astype(BF16)


def sort_rows(order, inputs, weights, bias):
    count = inputs.shape[0]
    return pl.pallas_call(
        sort_body,
        grid=(HEADS_OWN,),
        in_specs=[
            pl.BlockSpec((8, count), lambda h: (0, 0)),
            pl.BlockSpec((count, D), lambda h: (0, 0)),
            pl.BlockSpec((D, WIDE), lambda h: (0, h)),
            pl.BlockSpec((1, WIDE), lambda h: (0, h)),
        ],
        out_specs=pl.BlockSpec((ROUNDS, count, WIDE), lambda h: (h, 0, 0)),
        out_shape=jax.ShapeDtypeStruct((LOCAL_PAIRS, count, WIDE), BF16),
        scratch_shapes=[pltpu.VMEM((count, WIDE), BF16)],
        compiler_params=pltpu.CompilerParams(vmem_limit_bytes=48 << 20),
        cost_estimate=SMALL,
        name="sort_rows",
    )(order, inputs, weights, bias)


def sort_grads_body(place_ref, rows_ref, out_ref):
    count = place_ref.shape[1]
    half = count // 2
    head = pl.program_id(0)
    chunk = 256
    row = lax.broadcasted_iota(jnp.int32, (chunk, count), 0)
    low = lax.broadcasted_iota(jnp.int32, (count, TILE), 1) < HEAD
    for step in range(HEADS_OWN):

        @pl.when(head == step)
        def _():
            if step < 2:
                tile = rows_ref[0:count, :].astype(F32)
                tile = jnp.where(low if step == 0 else jnp.logical_not(low), tile, 0.0).astype(BF16)
            else:
                both = rows_ref[count : count + half, :].astype(F32)
                tile = jnp.concatenate([both, turn_half(both)], axis=0)
                tile = jnp.where(low, tile, 0.0).astype(BF16)
            for turn in range(ROUNDS):
                pair = step * ROUNDS + turn
                for part in range(count // chunk):
                    where = pl.ds(part * chunk, chunk)
                    picked = place_ref[pair : pair + 1, :] == row + part * chunk
                    picked = picked.astype(F32).astype(BF16)
                    out_ref[turn, where, :] = jnp.dot(
                        picked, tile, preferred_element_type=F32
                    ).astype(BF16)


def sort_grads(order, rows):
    count = order.shape[1]
    return pl.pallas_call(
        sort_grads_body,
        grid=(HEADS_OWN,),
        in_specs=[
            pl.BlockSpec((8, count), lambda h: (0, 0)),
            pl.BlockSpec(rows.shape, lambda h: (0, 0)),
        ],
        out_specs=pl.BlockSpec((ROUNDS, count, TILE), lambda h: (h, 0, 0)),
        out_shape=jax.ShapeDtypeStruct((LOCAL_PAIRS, count, TILE), BF16),
        compiler_params=pltpu.CompilerParams(vmem_limit_bytes=48 << 20),
        cost_estimate=SMALL,
        name="sort_grads",
    )(order, rows)


def plans_of(count):
    share = CLUSTER // UNIT
    half = UNIT // 2
    return (
        [(tuple(range(UNIT)), share)],
        [(tuple(range(i * half, (i + 1) * half)), 2 * share) for i in range(2)],
    )


def for_each_batch(is_long, count, batch, work):
    for wanted, plan in zip((1, 0), plans_of(count)):

        @pl.when(is_long == wanted)
        def _(plan=plan):
            for runs, share in plan:

                def step(group, carry, runs=runs, share=share):
                    first = pl.multiple_of(group * (batch * share), batch * share)
                    work(runs, pl.ds(first, batch * share), share)
                    return carry

                lax.fori_loop(0, count // share // batch, step, 0)


def batch_of(refs, runs, where, share, width):
    parts = [refs[r][0, where, :] for r in runs]
    return jnp.concatenate([p.reshape(p.shape[0] // share, share, width) for p in parts], axis=1)


def spread(refs, runs, where, share, columns, value):
    for i, r in enumerate(runs):
        part = value[:, i * share : (i + 1) * share]
        refs[r][0, where, columns] = part.reshape(part.shape[0] * share, TILE)


def products(form, left, right):
    return jnp.einsum(form, left, right, preferred_element_type=F32)


def softmax(first, second):
    scores = products("ued,ucd->uec", second, first) * (HEAD**-0.5)
    expo = jnp.exp(scores - jnp.max(scores, axis=1, keepdims=True))
    return expo * (1.0 / jnp.sum(expo, axis=1, keepdims=True))


def attend_body(long_ref, *refs):
    grouped, results = refs[:UNIT], refs[UNIT:]

    def work(runs, where, share):
        rows = batch_of(grouped, runs, where, share, WIDE)
        first = rows[..., :TILE]
        probs = softmax(first, rows[..., TILE:]).astype(BF16)
        mixed = products("uce,ued->ucd", jnp.swapaxes(probs, 1, 2), first).astype(BF16)
        spread(results, runs, where, share, slice(0, TILE), mixed)

    for_each_batch(long_ref[0], grouped[0].shape[1], 8, work)


def attend(is_long, grouped):
    count = grouped[0].shape[1]
    return pl.pallas_call(
        attend_body,
        grid_spec=pltpu.PrefetchScalarGridSpec(
            num_scalar_prefetch=1,
            grid=(LOCAL_PAIRS,),
            in_specs=[pl.BlockSpec((1, count, WIDE), lambda p, _: (p, 0, 0))] * UNIT,
            out_specs=[pl.BlockSpec((1, count, TILE), lambda p, _: (p, 0, 0))] * UNIT,
        ),
        out_shape=[jax.ShapeDtypeStruct((LOCAL_PAIRS, count, TILE), BF16)] * UNIT,
        compiler_params=pltpu.CompilerParams(vmem_limit_bytes=48 << 20),
        cost_estimate=SMALL,
        name="attend",
    )(is_long, *grouped)


def attend_back_body(long_ref, *refs):
    grouped, grads, results = refs[:UNIT], refs[UNIT : 2 * UNIT], refs[2 * UNIT :]
    batch = 16
    odd = (pl.program_id(0) // ROUNDS) % 2
    lane = lax.broadcasted_iota(jnp.int32, (batch, CLUSTER, TILE), 2)
    value_lane = (lane < HEAD) == (odd == 0)
    scale = HEAD**-0.5

    def work(runs, where, share):
        rows = batch_of(grouped, runs, where, share, WIDE)
        grad = batch_of(grads, runs, where, share, TILE)
        first, second = rows[..., :TILE], rows[..., TILE:]
        probs = softmax(first, second)
        grad_probs = products("ued,ucd->uec", first, grad)
        centre = jnp.sum(probs * grad_probs, axis=1, keepdims=True)
        grad_scores = (probs * (grad_probs - centre)).astype(BF16)
        grad_values = products("uec,ucd->ued", probs.astype(BF16), grad)
        grad_keys = products("uec,ucd->ued", grad_scores, first) * scale
        grad_query = products("uce,ued->ucd", jnp.swapaxes(grad_scores, 1, 2), second) * scale
        tile_one = jnp.where(value_lane, grad_values, grad_query).astype(BF16)
        tile_two = jnp.where(value_lane, 0.0, grad_keys).astype(BF16)
        spread(results, runs, where, share, slice(0, TILE), tile_one)
        spread(results, runs, where, share, slice(TILE, WIDE), tile_two)

    for_each_batch(long_ref[0], grouped[0].shape[1], batch, work)


def attend_back(is_long, grouped, grads):
    count = grouped[0].shape[1]
    return pl.pallas_call(
        attend_back_body,
        grid_spec=pltpu.PrefetchScalarGridSpec(
            num_scalar_prefetch=1,
            grid=(LOCAL_PAIRS,),
            in_specs=[pl.BlockSpec((1, count, WIDE), lambda p, _: (p, 0, 0))] * UNIT
            + [pl.BlockSpec((1, count, TILE), lambda p, _: (p, 0, 0))] * UNIT,
            out_specs=[pl.BlockSpec((1, count, WIDE), lambda p, _: (p, 0, 0))] * UNIT,
        ),
        out_shape=[jax.ShapeDtypeStruct((LOCAL_PAIRS, count, WIDE), BF16)] * UNIT,
        compiler_params=pltpu.CompilerParams(vmem_limit_bytes=56 << 20),
        cost_estimate=SMALL,
        name="attend_back",
    )(is_long, *grouped, *grads)


def unsorted(column_ref, step, rows_ref, part, chunk):
    count = rows_ref.shape[1]
    where = pl.ds(part * chunk, chunk)
    lane = lax.broadcasted_iota(jnp.int32, (chunk, count), 1)
    total = None
    for turn in range(ROUNDS):
        pair = step * ROUNDS + turn
        picked = (column_ref[where, pair : pair + 1] == lane).astype(F32).astype(BF16)
        more = jnp.dot(picked, rows_ref[turn], preferred_element_type=F32)
        total = more if total is None else total + more
    return total


def mix_body(place_ref, rows_ref, out_ref, column_ref):
    @pl.when(pl.program_id(0) == 0)
    def _():
        column_ref[...] = jnp.transpose(place_ref[...])

    count = rows_ref.shape[1]
    chunk = 256
    parts = count // chunk
    low = lax.broadcasted_iota(jnp.int32, (chunk, TILE), 1) < HEAD
    head = pl.program_id(0)
    for step in range(HEADS_OWN):

        @pl.when(head == step)
        def _():
            means = [0.5 * unsorted(column_ref, step, rows_ref, part, chunk) for part in range(parts)]
            for part in range(parts):
                where = pl.ds(part * chunk, chunk)
                if step == 0:
                    out_ref[where, :] = means[part].astype(BF16)
                elif step == 1:
                    out_ref[where, :] = jnp.where(low, out_ref[where, :].astype(F32), means[part]).astype(BF16)
                elif part < parts // 2:
                    both = jnp.where(low, means[part], turn_half(means[part + parts // 2]))
                    out_ref[pl.ds(count + part * chunk, chunk), :] = both.astype(BF16)


def mix(order, rows):
    count = rows.shape[1]
    packed = (count + count // 2, TILE)
    return pl.pallas_call(
        mix_body,
        grid=(HEADS_OWN,),
        in_specs=[
            pl.BlockSpec((8, count), lambda h: (0, 0)),
            pl.BlockSpec((ROUNDS, count, TILE), lambda h: (h, 0, 0)),
        ],
        out_specs=pl.BlockSpec(packed, lambda h: (0, 0)),
        out_shape=jax.ShapeDtypeStruct(packed, BF16),
        scratch_shapes=[pltpu.VMEM((count, 8), jnp.int32)],
        compiler_params=pltpu.CompilerParams(vmem_limit_bytes=48 << 20),
        cost_estimate=SMALL,
        name="mix",
    )(order, rows)


def gather_grads_body(place_ref, rows_ref, out_ref, column_ref):
    @pl.when(pl.program_id(0) == 0)
    def _():
        column_ref[...] = jnp.transpose(place_ref[...])

    count = rows_ref.shape[1]
    chunk = 256
    head = pl.program_id(0)
    for step in range(HEADS_OWN):

        @pl.when(head == step)
        def _():
            for part in range(count // chunk):
                where = pl.ds(part * chunk, chunk)
                out_ref[where, :] = unsorted(column_ref, step, rows_ref, part, chunk).astype(BF16)


def gather_grads(order, rows):
    count = rows.shape[1]
    return pl.pallas_call(
        gather_grads_body,
        grid=(HEADS_OWN,),
        in_specs=[
            pl.BlockSpec((8, count), lambda h: (0, 0)),
            pl.BlockSpec((ROUNDS, count, WIDE), lambda h: (h, 0, 0)),
        ],
        out_specs=pl.BlockSpec((count, WIDE), lambda h: (0, h)),
        out_shape=jax.ShapeDtypeStruct((count, HEADS_OWN * WIDE), BF16),
        scratch_shapes=[pltpu.VMEM((count, 8), jnp.int32)],
        compiler_params=pltpu.CompilerParams(vmem_limit_bytes=48 << 20),
        cost_estimate=SMALL,
        name="gather_grads",
    )(order, rows)


ERF_TOP = (0.00022905065861350646, 0.0034082910107109506, 0.050955695062380861, 0.18520832239976145, 1.128379143519084)
ERF_BOTTOM = (
    -1.1791602954361697e-7,
    0.000023547966471313185,
    0.0010179625278914885,
    0.014070470171167667,
    0.11098505178285362,
    0.49746925110067538,
    1.0,
)


def polynomial(value, factors):
    total = jnp.full_like(value, factors[0])
    for factor in factors[1:]:
        total = total * value + factor
    return total


def error_function(value):
    value = jnp.clip(value, -3.832506856900711, 3.832506856900711)
    square = value * value
    return value * polynomial(square, ERF_TOP) / polynomial(square, ERF_BOTTOM)


VEC_ROWS = 16
FFN_TILE = 256


def layer_body(
    n_shards,
    table_ref,
    *refs,
):
    shards, refs = refs[:n_shards], refs[n_shards:]
    parts, refs = refs[:UNIT], refs[UNIT:]
    x_ref, cot_ref, vec_ref, result_ref, first_ref, sums_ref, kept_ref, sent_ref = refs[:8]
    backs, refs = refs[8 : 8 + UNIT], refs[8 + UNIT :]
    w_ref, packed_ref, mixed_ref, hidden_ref, act_ref, down_ref, up_ref, attn_ref, back_ref = refs[:9]
    slope_ref, stage_ref, weight_sem, part_sem, stage_sem = refs[9:]
    count = x_ref.shape[0]
    half = count // 2
    per_shard, n_weights, shard_rows = shards[0].shape[:3]
    member = table_ref[0]
    for k in range(UNIT):
        pltpu.make_async_copy(parts[k], packed_ref.at[member ^ k], part_sem.at[k]).start()
    for b in range(n_weights):
        for n in range(n_shards * per_shard):
            row = pl.multiple_of(table_ref[6 + n], shard_rows)
            pltpu.make_async_copy(
                shards[n // per_shard].at[n % per_shard, b], w_ref.at[b, pl.ds(row, shard_rows), :], weight_sem.at[b]
            ).start()
    for k in range(UNIT):
        pltpu.make_async_copy(parts[k], packed_ref.at[member ^ k], part_sem.at[k]).wait()
    for b in range(n_weights):
        pltpu.make_async_copy(w_ref.at[b], w_ref.at[b], weight_sem.at[b]).wait()

    sums_ref[...] = jnp.zeros_like(sums_ref)
    low = lax.broadcasted_iota(jnp.int32, (FFN_TILE, TILE), 1) < HEAD
    vec = [vec_ref[i : i + 1, :] for i in range(8 + FFB)]
    gain_one, shift_one, gain_two, shift_two = vec[:4]
    bias_out, bias_down = vec[6], vec[7]

    def add_sum(row, value):
        sums_ref[row : row + 1, :] += jnp.sum(value, axis=0, keepdims=True)

    def tile_step(i, carry):
        rows = pl.ds(pl.multiple_of(i * FFN_TILE, FFN_TILE), FFN_TILE)
        is_first = i * FFN_TILE < half
        extra = pl.ds(pl.multiple_of(count + lax.rem(i * FFN_TILE, half), FFN_TILE), FFN_TILE)

        def pair(m):
            return packed_ref[m, rows, :].astype(F32)

        def single(m):
            value = packed_ref[m, extra, :].astype(F32)
            return jnp.where(is_first, value, turn_half(value))

        for m in (0, 2):
            at = m * (HEADS_OWN * HEAD)
            nxt = turn_half(pair(m + 1))
            mixed_ref[rows, at : at + TILE] = pair(m).astype(BF16)
            mixed_ref[rows, at + TILE : at + 2 * TILE] = jnp.where(low, single(m), nxt).astype(BF16)
            mixed_ref[rows, at + 2 * TILE : at + 3 * TILE] = jnp.where(
                low, nxt, turn_half(single(m + 1))
            ).astype(BF16)
        attention = jnp.dot(mixed_ref[rows, :], w_ref[0], preferred_element_type=F32) + bias_out
        normed_one, rstd_one = normalize(x_ref[rows, :].astype(F32) + attention)
        hidden = normed_one * gain_one + shift_one
        hidden_low = hidden.astype(BF16)
        hidden_ref[rows, :] = hidden_low
        down = jnp.broadcast_to(bias_down, hidden.shape)
        for j in range(FFB):
            up = jnp.dot(hidden_low, w_ref[1 + j], preferred_element_type=F32) + vec[8 + j]
            phi = 0.5 * (1.0 + error_function(up * SQRT_HALF))
            slope_ref[j] = phi + up * jnp.exp(-0.5 * up * up) * INV_ROOT_TWO_PI
            act = (up * phi).astype(BF16)
            act_ref[j, rows, :] = act
            down = down + jnp.dot(act, w_ref[1 + FFB + j], preferred_element_type=F32)
        normed_two, rstd_two = normalize(hidden + down)
        result_ref[rows, :] = (normed_two * gain_two + shift_two).astype(BF16)
        grad_result = cot_ref[rows, :].astype(F32)
        add_sum(2, grad_result * normed_two)
        add_sum(3, grad_result)
        grad_second = norm_back(grad_result * gain_two, normed_two, rstd_two)
        grad_down = grad_second.astype(BF16)
        down_ref[rows, :] = grad_down
        add_sum(7, grad_down.astype(F32))
        grad_hidden = grad_second
        for j in range(FFB):
            grad_up = (outer_cols(grad_down, w_ref[1 + FFB + j]) * slope_ref[j]).astype(BF16)
            up_ref[j, rows, :] = grad_up
            add_sum(8 + j, grad_up.astype(F32))
            grad_hidden = grad_hidden + outer_cols(grad_up, w_ref[1 + j])
        add_sum(0, grad_hidden * normed_one)
        add_sum(1, grad_hidden)
        grad_first = norm_back(grad_hidden * gain_one, normed_one, rstd_one)
        first_ref[rows, :] = grad_first
        grad_attn = grad_first.astype(BF16)
        attn_ref[rows, :] = grad_attn
        add_sum(6, grad_attn.astype(F32))
        grad_mixed = (0.5 * outer_cols(grad_attn, w_ref[0])).astype(BF16).astype(F32)
        for m in range(UNIT):
            at = (m // 2) * 3 * TILE
            tiles = [grad_mixed[:, at + n * TILE : at + (n + 1) * TILE] for n in range(3)]
            if m % 2 == 0:
                two, one = tiles[0], tiles[1]
            else:
                two, one = turn_half(jnp.where(low, tiles[2], tiles[1])), turn_half(tiles[2])
            back_ref[member ^ m, rows, :] = two.astype(BF16)

            @pl.when(is_first)
            def _(one=one, m=m):
                back_ref[member ^ m, extra, :] = jnp.where(low, one, 0.0).astype(BF16)

            @pl.when(jnp.logical_not(is_first))
            def _(one=one, m=m):
                old = back_ref[member ^ m, extra, :].astype(F32)
                back_ref[member ^ m, extra, :] = jnp.where(low, old, turn_half(one)).astype(BF16)

        return carry

    lax.fori_loop(0, count // FFN_TILE, tile_step, 0)
    for k in range(UNIT):
        backs[k][...] = back_ref[k]

    core, bits = table_ref[1], [table_ref[2 + d] for d in range(4)]
    piece, half_columns = kept_ref.shape[3:]
    n_parts = kept_ref.shape[0]
    per_part = n_weights // n_parts

    def copies(block, slot, half, target):
        part = block // per_part
        made = []
        for index in range(16):
            x, zh, y, zl = ((index >> s) % 2 for s in range(4))
            rel = {"x": x ^ bits[0], "y": y ^ bits[1], "zl": zl ^ bits[2], "zh": zh ^ bits[3]}
            place = 0
            for name in PART_ORDERS[part]:
                place = place * 2 + rel[name]
            made.append(
                pltpu.make_async_copy(
                    stage_ref.at[
                        slot, pl.ds(index * piece, piece), pl.ds(half * half_columns, half_columns)
                    ],
                    target.at[part, place, block % per_part],
                    stage_sem.at[slot, half * 16 + index],
                )
            )
        return made

    def send(block, slot):
        for half in range(2):

            @pl.when(core == half)
            def _(half=half):
                for copy in copies(block, slot, half, kept_ref):
                    copy.start()

            @pl.when(core != half)
            def _(half=half):
                for copy in copies(block, slot, half, sent_ref):
                    copy.start()

    def sent(block, slot):
        for half in range(2):
            for copy in copies(block, slot, half, kept_ref):
                copy.wait()

    plan = [(attn_ref, None, mixed_ref, None, 0)]
    plan += [(down_ref, None, act_ref, j, 1 + FFB + j) for j in range(FFB)]
    plan += [(up_ref, j, hidden_ref, None, 1 + j) for j in range(FFB)]
    for n, (left, lj, right, rj, block) in enumerate(plan):
        slot = n % 2
        if n >= 2:
            sent(plan[n - 2][4], slot)
        value = inner_rows(
            left[...] if lj is None else left[lj], right[...] if rj is None else right[rj]
        )
        stage_ref[slot] = value.astype(BF16)
        send(block, slot)
    for n in (len(plan) - 2, len(plan) - 1):
        sent(plan[n][4], n % 2)


PART_ORDERS = (("x", "y", "zl", "zh"), ("y", "zl", "zh", "x"), ("zl", "zh", "x", "y"))


def layer(table, shards, parts, inputs, cotangent, vectors):
    count = inputs.shape[0]
    n_weights = 1 + 2 * FFB
    n_shards = len(shards)
    anywhere = pl.BlockSpec(memory_space=pl.ANY)
    inside = pl.BlockSpec(memory_space=pltpu.VMEM)
    packed = parts[0].shape
    return pl.pallas_call(
        functools.partial(layer_body, n_shards),
        in_specs=[pl.BlockSpec(memory_space=pltpu.SMEM)] + [anywhere] * (n_shards + UNIT) + [inside] * 3,
        out_specs=[inside, inside, inside, anywhere, anywhere] + [inside] * UNIT,
        out_shape=[
            jax.ShapeDtypeStruct((count, D), BF16),
            jax.ShapeDtypeStruct((count, D), F32),
            jax.ShapeDtypeStruct((VEC_ROWS, D), F32),
            jax.ShapeDtypeStruct((3, 16, n_weights // 3, D // 16, D // 2), BF16),
            jax.ShapeDtypeStruct((3, 16, n_weights // 3, D // 16, D // 2), BF16),
        ]
        + [jax.ShapeDtypeStruct(packed, BF16)] * UNIT,
        scratch_shapes=[
            pltpu.VMEM((n_weights, D, D), BF16),
            pltpu.VMEM((UNIT, *packed), BF16),
            pltpu.VMEM((count, D), BF16),
            pltpu.VMEM((count, D), BF16),
            pltpu.VMEM((FFB, count, D), BF16),
            pltpu.VMEM((count, D), BF16),
            pltpu.VMEM((FFB, count, D), BF16),
            pltpu.VMEM((count, D), BF16),
            pltpu.VMEM((UNIT, *packed), BF16),
            pltpu.VMEM((FFB, FFN_TILE, D), F32),
            pltpu.VMEM((2, D, D), BF16),
            pltpu.SemaphoreType.DMA((n_weights,)),
            pltpu.SemaphoreType.DMA((UNIT,)),
            pltpu.SemaphoreType.DMA((2, 32)),
        ],
        compiler_params=pltpu.CompilerParams(vmem_limit_bytes=60 << 20),
        cost_estimate=SMALL,
        name="layer",
    )(table, *shards, *parts, inputs, cotangent, vectors)


def qkv_back_body(scalars_ref, *refs):
    grads, inputs, kept_ref, sent_ref, bias_ref, all_ref = refs[:4], refs[4:8], *refs[8:]
    core, unit = scalars_ref[0], scalars_ref[1]
    columns = all_ref.shape[4]
    step = 32
    per_unit = all_ref.shape[3]
    bias_ref[...] = jnp.zeros_like(bias_ref)
    for head in range(HEADS_OWN):
        at = slice(head * WIDE, (head + 1) * WIDE)
        total = inner_rows(grads[0][:, at], inputs[0][...])
        bias = jnp.sum(grads[0][:, at].astype(F32), axis=0, keepdims=True)
        for k in range(1, UNIT):
            total = total + inner_rows(grads[k][:, at], inputs[k][...])
            bias = bias + jnp.sum(grads[k][:, at].astype(F32), axis=0, keepdims=True)
        bias_ref[0:1, at] = bias
        firsts = (HEAD, 3 * HEAD, 0) if head % 2 == 0 else (0, 2 * HEAD, HEAD)
        for block, first in enumerate(firsts):
            for i in range(HEAD // step):
                row = head * HEAD + i * step
                rows = total[first + i * step : first + (i + 1) * step]
                for c in range(2):
                    all_ref[
                        c ^ core, row // per_unit ^ unit, block, row % per_unit : row % per_unit + step, :
                    ] = rows[:, c * columns : (c + 1) * columns].astype(BF16)
    kept_ref[...] = all_ref[0]
    sent_ref[...] = all_ref[1]


def qkv_back(scalars, grads, inputs):
    inside = pl.BlockSpec(memory_space=pltpu.VMEM)
    shape = (2, 3, HEADS_OWN * HEAD // 2, D // 2)
    return pl.pallas_call(
        qkv_back_body,
        in_specs=[pl.BlockSpec(memory_space=pltpu.SMEM)] + [inside] * (2 * UNIT),
        out_specs=[inside] * 3,
        out_shape=[
            jax.ShapeDtypeStruct(shape, BF16),
            jax.ShapeDtypeStruct(shape, BF16),
            jax.ShapeDtypeStruct((8, HEADS_OWN * WIDE), F32),
        ],
        scratch_shapes=[pltpu.VMEM((2, *shape), BF16)],
        compiler_params=pltpu.CompilerParams(vmem_limit_bytes=56 << 20),
        cost_estimate=SMALL,
        name="qkv_back",
    )(scalars, *grads, *inputs)


def pack_body(slot_block_ref, *refs):
    half = (len(refs) - 2) // 2
    kept, got, out_ref, all_ref = refs[:half], refs[half : 2 * half], refs[-2], refs[-1]
    per_part = kept[0].shape[1]
    for p in range(half):
        for b in range(per_part):
            all_ref[p * per_part + b] = (kept[p][0, b] + got[p][0, b].astype(F32)).astype(BF16)
    for s in range(out_ref.shape[0] * out_ref.shape[1]):
        out_ref[s // out_ref.shape[1], s % out_ref.shape[1]] = all_ref[jnp.maximum(slot_block_ref[s] - 3, 0)]


def pack(slot_block, kept, got, n_grp, slots):
    shape = kept[0].shape[2:]
    inside = pl.BlockSpec(memory_space=pltpu.VMEM)
    return pl.pallas_call(
        pack_body,
        in_specs=[pl.BlockSpec(memory_space=pltpu.SMEM)] + [inside] * (2 * len(kept)),
        out_specs=inside,
        out_shape=jax.ShapeDtypeStruct((n_grp, slots, *shape), BF16),
        scratch_shapes=[pltpu.VMEM((len(kept) * kept[0].shape[1], *shape), BF16)],
        compiler_params=pltpu.CompilerParams(vmem_limit_bytes=32 << 20),
        cost_estimate=SMALL,
        name="pack",
    )(slot_block, *kept, *got)


def rotate_in_body(mine_ref, keep_ref, got_ref, high_ref, low_ref, out_ref, grad_ref):
    slots, n_tok = got_ref.shape[1], out_ref.shape[0]
    rows, columns = got_ref.shape[2:]
    width = out_ref.shape[3]
    for s in range(slots):
        block = mine_ref[s]

        @pl.when(block < 3)
        def _(s=s, block=block):
            grad_ref[...] = keep_ref[jnp.minimum(block, 2)]

        @pl.when(block >= 3)
        def _(s=s):
            for g in range(got_ref.shape[0]):
                x, c = g // 2, g % 2
                grad_ref[x * rows : (x + 1) * rows, c * columns : (c + 1) * columns] = got_ref[g, s]

        grad = grad_ref[...]
        part = jnp.dot(grad, high_ref[s], preferred_element_type=F32)
        part = jnp.transpose(part + jnp.dot(grad, low_ref[s], preferred_element_type=F32))
        for r in range(n_tok):
            out_ref[r, s] = part[r * width : (r + 1) * width].astype(BF16)


def rotate_in(mine, keep, got, left, n_tok):
    slots, width = got.shape[1], keep.shape[1]
    inside = pl.BlockSpec(memory_space=pltpu.VMEM)
    return pl.pallas_call(
        rotate_in_body,
        in_specs=[pl.BlockSpec(memory_space=pltpu.SMEM)] + [inside] * 4,
        out_specs=inside,
        out_shape=jax.ShapeDtypeStruct((n_tok, slots, width, width), BF16),
        scratch_shapes=[pltpu.VMEM(keep.shape[1:], BF16)],
        compiler_params=pltpu.CompilerParams(vmem_limit_bytes=48 << 20),
        cost_estimate=SMALL,
        name="rotate_in",
    )(mine, keep, got, *left)


def moments_body(place, got_ref, high_ref, low_ref, one_ref, two_ref, new_one_ref, new_two_ref, out_ref):
    n_tok, slots, width = got_ref.shape[:3]
    for s in range(slots):
        rotated = jnp.zeros(one_ref.shape[1:], F32)
        for t in range(n_tok):
            at = slice(place[t] * width, (place[t] + 1) * width)
            part = got_ref[t, s]
            rotated = rotated + jnp.dot(part, high_ref[s, at], preferred_element_type=F32)
            rotated = rotated + jnp.dot(part, low_ref[s, at], preferred_element_type=F32)
        new_one = BETA_ONE * one_ref[s] + (1.0 - BETA_ONE) * rotated
        new_two = BETA_TWO * two_ref[s] + (1.0 - BETA_TWO) * rotated * rotated
        new_one_ref[s] = new_one
        new_two_ref[s] = new_two
        direction = (new_one / (jnp.sqrt(new_two) + ADAM_EPS)).astype(BF16)
        for t in range(n_tok):
            at = slice(place[t] * width, (place[t] + 1) * width)
            turned = outer_cols(direction, high_ref[s, at]) + outer_cols(direction, low_ref[s, at])
            out_ref[t, s] = turned.astype(BF16)


def moments(place, got, right, one, two):
    n_tok, slots, width = got.shape[:3]
    inside = pl.BlockSpec(memory_space=pltpu.VMEM)
    return pl.pallas_call(
        functools.partial(moments_body, tuple(place)),
        in_specs=[inside] * 5,
        out_specs=[inside] * 3,
        out_shape=[
            jax.ShapeDtypeStruct(one.shape, F32),
            jax.ShapeDtypeStruct(one.shape, F32),
            jax.ShapeDtypeStruct(got.shape, BF16),
        ],
        compiler_params=pltpu.CompilerParams(vmem_limit_bytes=48 << 20),
        cost_estimate=SMALL,
        name="moments",
    )(got, *right, one, two)


def rotate_out_body(got_ref, high_ref, low_ref, out_ref, rows_ref):
    n_tok, slots, width = got_ref.shape[:3]
    for s in range(slots):
        for r in range(n_tok):
            rows_ref[r * width : (r + 1) * width, :] = got_ref[r, s]
        rows = rows_ref[...]
        change = jnp.dot(high_ref[s], rows, preferred_element_type=F32)
        change = change + jnp.dot(low_ref[s], rows, preferred_element_type=F32)
        for r in range(n_tok):
            out_ref[r, s] = change[r * width : (r + 1) * width].astype(BF16)


def rotate_out(got, left):
    n_tok, slots, width = got.shape[:3]
    inside = pl.BlockSpec(memory_space=pltpu.VMEM)
    return pl.pallas_call(
        rotate_out_body,
        in_specs=[inside] * 3,
        out_specs=inside,
        out_shape=jax.ShapeDtypeStruct(got.shape, BF16),
        scratch_shapes=[pltpu.VMEM((n_tok * width, width), BF16)],
        compiler_params=pltpu.CompilerParams(vmem_limit_bytes=48 << 20),
        cost_estimate=SMALL,
        name="rotate_out",
    )(got, *left)


def apply_body(place, got_ref, master_ref, out_ref):
    n_tok, slots, width = got_ref.shape[:3]
    for s in range(slots):
        for t in range(n_tok):
            at = slice(place[t] * width, (place[t] + 1) * width)
            out_ref[s, :, at] = master_ref[s, :, at] - RATE_MATRIX * got_ref[t, s].astype(F32)


def apply_change(place, got, master):
    inside = pl.BlockSpec(memory_space=pltpu.VMEM)
    return pl.pallas_call(
        functools.partial(apply_body, tuple(place)),
        in_specs=[inside] * 2,
        out_specs=inside,
        out_shape=jax.ShapeDtypeStruct(master.shape, F32),
        compiler_params=pltpu.CompilerParams(vmem_limit_bytes=48 << 20),
        cost_estimate=SMALL,
        name="apply_change",
    )(got, master)


def swap(value, axis, bit):
    size = lax.axis_size(axis)
    return lax.ppermute(value, axis, [(i, i ^ bit) for i in range(size)])


def exchange_unit(parts):
    return [parts[0]] + [swap(parts[k], "tok", k) for k in range(1, UNIT)]


LINKS = {"x": ("grp", 2), "y": ("tok", 1), "zl": ("tok", 2), "zh": ("tok", 4)}


def starts_of(lengths):
    index = jnp.arange(lengths.shape[0])
    return jnp.sum(jnp.where(index[None, :] < index[:, None], lengths[None, :], 0), axis=1)


LINKS = {"x": ("grp", 2), "y": ("tok", 1), "zl": ("tok", 2), "zh": ("tok", 4)}


def starts_of(lengths):
    index = jnp.arange(lengths.shape[0])
    return jnp.sum(jnp.where(index[None, :] < index[:, None], lengths[None, :], 0), axis=1)


def total_of(value):
    for axis in ("grp", "tok"):
        bit = 1
        while bit < lax.axis_size(axis):
            value = value + swap(value, axis, bit)
            bit *= 2
    return value


def pick(values, index):
    return lax.dynamic_index_in_dim(values, index, 0, keepdims=False)


def split_heads(columns):
    query, keys, values = (c.reshape(HEADS_OWN, HEAD) for c in columns)
    zero = jnp.zeros((HEAD,), query.dtype)
    tiles = []
    for h in range(HEADS_OWN):
        tiles += [values[h], query[h], zero, keys[h]] if h % 2 == 0 else [query[h], values[h], keys[h], zero]
    return jnp.concatenate(tiles)


def join_heads(tiles):
    parts = tiles.reshape(HEADS_OWN, 4, HEAD, *tiles.shape[1:])
    at = [(1, 0), (3, 2), (0, 1)]
    return jnp.stack(
        [jnp.concatenate([parts[h, at[i][h % 2]] for h in range(HEADS_OWN)], axis=0) for i in range(3)]
    )


def doubled(value):
    high = value.astype(BF16)
    return high, (value - high.astype(F32)).astype(BF16)


def together(*groups):
    flat, tree = jax.tree.flatten(groups)
    return jax.tree.unflatten(tree, lax.optimization_barrier(flat))


def fast(
    tokens,
    cotangent,
    lengths,
    clusters,
    owners,
    master,
    bases,
    moment_one,
    moment_two,
    vectors,
    vector_one,
    vector_two,
):
    n_tok = lax.axis_size("tok")
    n_grp = lax.axis_size("grp")
    tok = lax.axis_index("tok")
    grp = lax.axis_index("grp")
    tok_count = tokens.shape[1]
    rows_dev = master.shape[0]
    slots = master.shape[1]
    blocks_all = slots * n_grp
    member = tok & (UNIT - 1)
    unit = tok >> 2
    place = [2 * (t % UNIT) + t // UNIT for t in range(n_tok)]
    own_width = HEADS_OWN * HEAD

    slot_block = jnp.argsort(owners, stable=True).astype(jnp.int32)
    block_slot = jnp.argsort(slot_block, stable=True).astype(jnp.int32)

    core, bit_x = grp & 1, grp >> 1
    inputs = tokens[0]

    near, far = swap(inputs, "tok", 1), swap(inputs, "tok", 2)
    local = jnp.transpose(master.astype(BF16), (1, 0, 2))
    beside, over = swap(local, "grp", 1), swap(local, "grp", 2)

    item_starts = starts_of(lengths[0])
    unit_start = unit * UNIT * tok_count
    middle = unit_start + UNIT // 2 * tok_count
    start_of_middle = jnp.max(jnp.where(item_starts <= middle, item_starts, 0))
    is_long = (start_of_middle <= unit_start).astype(jnp.int32).reshape(1)
    share = CLUSTER // UNIT * (2 - is_long)
    orders = exchange_unit(places(jnp.concatenate([share, member.reshape(1)]), clusters[0]))
    left, right = doubled(bases[0]), doubled(bases[1])
    (over, left, right) = together(over, left, right)
    across = swap(over, "grp", 1)

    (near, far, beside, over, across) = together(near, far, beside, over, across)
    part_rows = rows_dev // 2

    scalars = jnp.concatenate([block_slot, jnp.stack([grp, core, member])]).astype(jnp.int32)
    *by_owner, rest_rows = arrange(scalars, [local, beside, over, across], blocks_all)
    theirs = exchange_unit(by_owner)
    half = tok_count // 2
    third = (swap(near[:half], "tok", 2), swap(far[half:], "tok", 1))
    theirs = jnp.stack(theirs)
    theirs_far = swap(theirs, "tok", UNIT)
    mine_all = jnp.concatenate([theirs, theirs_far], axis=0)
    others_all = swap(mine_all, "grp", 1)
    sources = tok ^ jnp.arange(2 * UNIT, dtype=jnp.int32)
    cores = core ^ jnp.arange(2, dtype=jnp.int32)
    firsts = (sources[None, :] * rows_dev + cores[:, None] * part_rows).reshape(-1)
    (third, others_all, rest_rows, orders) = together(third, others_all, rest_rows, orders)
    own_weights = assemble(firsts, [mine_all, others_all])

    def columns_of(value, m):
        return lax.dynamic_slice_in_dim(value, m * own_width, own_width, value.ndim - 1)

    own_bias = split_heads(
        [columns_of(vectors[4], member), jnp.zeros((own_width,), F32), columns_of(vectors[5], member)]
    ).reshape(1, -1)
    grouped = [
        sort_rows(orders[k], value, own_weights, own_bias) for k, value in enumerate((inputs, near, far))
    ]
    unit_inputs = [inputs, near, far, jnp.concatenate(third, axis=0)]
    grouped.append(sort_rows(orders[3], unit_inputs[3], own_weights, own_bias))

    ring = [(i, (i + 2) % n_tok) for i in range(n_tok)]
    depth = n_tok // 2
    steps, flips = [rest_rows], []
    steps.append(lax.ppermute(steps[0], "tok", ring))
    flips.append(swap(steps[0], "tok", 1))
    (grouped, steps[1], flips[0]) = together(grouped, steps[1], flips[0])
    steps.append(lax.ppermute(steps[1], "tok", ring))
    flips.append(swap(steps[1], "tok", 1))
    sorted_out = attend(is_long, grouped)
    (sorted_out, steps[2], flips[1]) = together(sorted_out, steps[2], flips[1])
    mixed = [None] * UNIT
    mixed[3] = mix(orders[3], sorted_out[3])
    mixed[2] = mix(orders[2], sorted_out[2])
    mixed[1] = mix(orders[1], sorted_out[1])
    mixed_parts = exchange_unit(mixed)
    steps.append(lax.ppermute(steps[2], "tok", ring))
    flips.append(swap(steps[2], "tok", 1))
    (steps[3], flips[2], mixed_parts[1:]) = together(steps[3], flips[2], mixed_parts[1:])
    flips.append(swap(steps[3], "tok", 1))
    mixed_parts[0] = mix(orders[0], sorted_out[0])
    mine_rest = [jnp.stack([steps[k], flips[k]]) for k in range(depth)]
    shards = mine_rest + [swap(m, "grp", 1) for m in mine_rest]
    sources = (tok + n_tok - 2 * jnp.arange(depth, dtype=jnp.int32)) & (n_tok - 1)
    sources = (sources[:, None] ^ jnp.arange(2, dtype=jnp.int32)[None, :]).reshape(-1)
    firsts = (sources[None, :] * rows_dev + cores[:, None] * part_rows).reshape(-1)

    held_weights, *shards = lax.optimization_barrier((own_weights, *shards))
    turned_weights = [swap(held_weights, "tok", k) for k in range(1, UNIT)]
    place_bits = jnp.stack([member, core, bit_x, tok & 1, (tok >> 1) & 1, tok >> 2]).astype(jnp.int32)
    table = jnp.concatenate([place_bits, firsts])
    result, grad_first, sums, kept, sent_pieces, *back = layer(
        table, shards, mixed_parts, inputs, cotangent[0], vectors
    )
    (turned_weights, kept, sent_pieces, back) = together(turned_weights, kept, sent_pieces, back)

    grad_parts = exchange_unit(back)
    other = swap(sent_pieces, "grp", 1)
    sums_of = [kept[p].astype(F32) + other[p].astype(F32) for p in range(3)]

    def halves(values):
        return [v[: v.shape[0] // 2] for v in values], [v[v.shape[0] // 2 :].astype(BF16) for v in values]

    def exchanged(sent_now, stage):
        return [swap(v, *LINKS[PART_ORDERS[p][stage]]) for p, v in enumerate(sent_now)]

    def joined(kept_now, got_now):
        return [k + g.astype(F32) for k, g in zip(kept_now, got_now)]

    kept_now, sent_now = halves(sums_of)
    (sent_now, grad_parts) = together(sent_now, grad_parts)
    got_now = exchanged(sent_now, 0)
    sorted_grads = [sort_grads(orders[k], grad_parts[k]) for k in range(UNIT)]
    sorted_back = attend_back(is_long, grouped, sorted_grads)
    kept_now, sent_now = halves(joined(kept_now, got_now))
    (sent_now, sorted_back) = together(sent_now, sorted_back)
    got_now = exchanged(sent_now, 1)
    own_grads = [None] * UNIT
    own_grads[3] = gather_grads(orders[3], sorted_back[3])
    home_grads = [None, None, None, swap(own_grads[3], "tok", 3)]
    own_grads[2] = gather_grads(orders[2], sorted_back[2])
    kept_now, sent_now = halves(joined(kept_now, got_now))
    (sent_now, own_grads[2], sorted_back) = together(sent_now, own_grads[2], sorted_back)
    got_now = exchanged(sent_now, 2)
    for k in (1, 0):
        own_grads[k] = gather_grads(orders[k], sorted_back[k])
    kept_qkv, sent_qkv, bias_qkv = qkv_back(jnp.stack([core, unit]).astype(jnp.int32), own_grads, unit_inputs)
    kept_now, sent_now = halves(joined(kept_now, got_now))
    (sent_now, sent_qkv, home_grads[3]) = together(sent_now, sent_qkv, home_grads[3])
    got_now = exchanged(sent_now, 3)

    bias_query, _, bias_value = join_heads(bias_qkv[0])
    bias_rows = lax.dynamic_update_slice_in_dim(
        jnp.zeros((2, D), F32), jnp.stack([bias_query, bias_value]), member * own_width, 1
    )
    total = sums[: 8 + FFB] + jnp.pad(bias_rows, ((4, 2 + FFB), (0, 0)))

    more = swap(total, "grp", 1)
    keep = kept_qkv.astype(F32) + swap(sent_qkv, "grp", 1).astype(F32)
    (keep, more) = together(keep, more)
    total = total + more
    more = swap(total, "grp", 2)
    unit_got = swap(keep[1].astype(BF16), "tok", UNIT)
    home_grads[1] = swap(own_grads[1], "tok", 1)
    home_grads[2] = swap(own_grads[2], "tok", 2)
    sent = pack(slot_block, kept_now, got_now, n_grp, slots)
    got = lax.all_to_all(sent, "grp", split_axis=0, concat_axis=0, tiled=True)
    keep = keep[0] + unit_got.astype(F32)
    (keep, more) = together(keep, more)
    total = total + more
    more = swap(total, "tok", 1)
    keep = keep + swap(keep.astype(BF16), "grp", 2).astype(F32)
    (keep, more) = together(keep.astype(BF16), more)
    total = total + more
    more = swap(total, "tok", 2)
    kept_core = (keep, swap(keep, "grp", 1))
    keep = jnp.concatenate(
        [jnp.where(core == 0, kept_core[0], kept_core[1]), jnp.where(core == 0, kept_core[1], kept_core[0])],
        axis=-1,
    )
    mine = lax.dynamic_slice_in_dim(slot_block, grp * slots, slots, 0)

    def to_tok(value):
        return lax.all_to_all(value, "tok", split_axis=0, concat_axis=0, tiled=True)

    part = to_tok(rotate_in(mine, keep, got, left, n_tok))
    (part, more, home_grads) = together(part, more, [own_grads[0]] + home_grads[1:])
    total = total + more
    more = swap(total, "tok", 4)
    by_slot_of = lambda value: jnp.transpose(value, (1, 0, 2))
    new_one, new_two, turned = moments(
        place, part, right, by_slot_of(moment_one), by_slot_of(moment_two)
    )
    turned = to_tok(turned)
    (turned, more) = together(turned, more)
    vector_total = total + more
    change = to_tok(rotate_out(turned, left))
    new_master = by_slot_of(apply_change(place, change, by_slot_of(master)))
    new_one, new_two = by_slot_of(new_one), by_slot_of(new_two)
    grad_inputs = grad_first + sum(
        outer_cols(home_grads[k], own_weights if k == 0 else turned_weights[k - 1]) for k in range(UNIT)
    )
    new_vec_one = BETA_ONE * vector_one + (1.0 - BETA_ONE) * vector_total
    new_vec_two = BETA_TWO * vector_two + (1.0 - BETA_TWO) * vector_total * vector_total
    new_vectors = vectors - RATE_VECTOR * new_vec_one / (jnp.sqrt(new_vec_two) + ADAM_EPS)
    return (
        result[None],
        grad_inputs[None],
        new_one,
        new_two,
        new_master,
        new_vec_one,
        new_vec_two,
        new_vectors,
    )


def general(
    tokens,
    cotangent,
    lengths,
    clusters,
    owners,
    master,
    bases,
    moment_one,
    moment_two,
    vectors,
    vector_one,
    vector_two,
):
    n_tok = lax.axis_size("tok")
    tok_count = tokens.shape[1]
    rows_dev = master.shape[0]
    slot_block = jnp.argsort(owners, stable=True)
    block_slot = jnp.argsort(slot_block, stable=True)
    slot_part = lax.all_gather(master.astype(jnp.bfloat16), "grp", axis=1, tiled=True)
    weights = lax.all_gather(slot_part, "tok", axis=0, tiled=True)
    blocks = jnp.stack([pick(jnp.transpose(weights, (1, 0, 2)), block_slot[b]) for b in range(weights.shape[1])], axis=1)
    w_qkv = blocks[:, 0:3, :].reshape(D, 3 * D)
    w_out = blocks[:, 3, :]
    w_up = blocks[:, 4 : 4 + FF // D, :].reshape(D, FF)
    w_down = jnp.transpose(blocks[:, 4 + FF // D :, :], (1, 0, 2)).reshape(FF, D)
    inputs = tokens[0]
    gain_one = vectors[0]
    shift_one = vectors[1]
    gain_two = vectors[2]
    shift_two = vectors[3]
    bias_qkv = jnp.concatenate([vectors[4], jnp.zeros((D,), jnp.float32), vectors[5]])
    qkv = (jnp.dot(inputs, w_qkv, preferred_element_type=jnp.float32) + bias_qkv).astype(
        jnp.bfloat16
    )
    heads = jnp.transpose(qkv.reshape(tok_count, 3, H, HEAD), (2, 0, 1, 3)).reshape(
        H, tok_count, 3 * HEAD
    )
    pair_rows = jnp.broadcast_to(heads[None], (ROUNDS, H, tok_count, 3 * HEAD)).reshape(
        PAIRS * tok_count, 3 * HEAD
    )
    position = lax.axis_index("tok") * tok_count + jnp.arange(tok_count, dtype=jnp.int32)
    item_starts = starts_of(lengths[0])
    item_start = jnp.max(
        jnp.where(item_starts[None, :] <= position[:, None], item_starts[None, :], 0), axis=1
    )
    per_dev = tok_count // CLUSTER
    group_clusters = n_tok * per_dev
    pair_ids = jnp.arange(PAIRS, dtype=jnp.int32)[:, None]
    global_cluster = item_start[None, :] // CLUSTER + clusters[0]
    unit_ids = (pair_ids * group_clusters + global_cluster).reshape(-1)
    owner_ids = ((global_cluster + pair_ids * per_dev) % n_tok).reshape(-1)
    send_order = jnp.argsort(owner_ids * (PAIRS * group_clusters) + unit_ids, stable=True)
    restore = jnp.argsort(send_order, stable=True)
    slot_rows = PAIRS * tok_count // n_tok
    units_here = PAIRS * tok_count // CLUSTER
    sent_rows = pair_rows[send_order].reshape(n_tok, slot_rows // 2, 6 * HEAD)
    sent_units = unit_ids[send_order].reshape(n_tok, slot_rows)
    got_rows, got_units = (
        lax.all_to_all(sent_rows, "tok", split_axis=0, concat_axis=0, tiled=True),
        lax.all_to_all(sent_units, "tok", split_axis=0, concat_axis=0, tiled=True),
    )
    arrange = jnp.argsort(got_units.reshape(-1), stable=True)
    undo = jnp.argsort(arrange, stable=True)
    grouped = got_rows.reshape(PAIRS * tok_count, 3 * HEAD)[arrange].reshape(
        units_here, CLUSTER, 3 * HEAD
    )
    query_rows = grouped[..., :HEAD]
    key_rows = grouped[..., HEAD : 2 * HEAD]
    value_rows = grouped[..., 2 * HEAD :]
    score_scale = HEAD ** (-0.5)
    scores = (
        jnp.einsum("ucd,ued->uce", query_rows, key_rows, preferred_element_type=jnp.float32)
        * score_scale
    )
    row_max = jnp.max(scores, axis=-1, keepdims=True)
    row_total = jnp.sum(jnp.exp(scores - row_max), axis=-1, keepdims=True)
    log_total = row_max + jnp.log(row_total)
    probs = jnp.exp(scores - log_total)
    cluster_out = jnp.einsum(
        "uce,ued->ucd", probs.astype(jnp.bfloat16), value_rows, preferred_element_type=jnp.float32
    ).astype(jnp.bfloat16)
    back_rows = cluster_out.reshape(PAIRS * tok_count, HEAD)[undo].reshape(
        n_tok, slot_rows // 2, 2 * HEAD
    )
    home_rows = lax.all_to_all(back_rows, "tok", split_axis=0, concat_axis=0, tiled=True)
    home_rows = (
        home_rows.reshape(PAIRS * tok_count, HEAD)[restore]
        .reshape(ROUNDS, H, tok_count, HEAD)
        .astype(jnp.float32)
    )
    mixed_heads = 0.5 * (home_rows[0] + home_rows[1])
    mixed_low = jnp.transpose(mixed_heads, (1, 0, 2)).reshape(tok_count, D).astype(jnp.bfloat16)
    attention = jnp.dot(mixed_low, w_out, preferred_element_type=jnp.float32) + vectors[6]
    first_sum = inputs.astype(jnp.float32) + attention
    normed_one, rstd_one = normalize(first_sum)
    hidden = normed_one * gain_one + shift_one
    hidden_low = hidden.astype(jnp.bfloat16)
    up_proj = jnp.dot(hidden_low, w_up, preferred_element_type=jnp.float32) + vectors[8:].reshape(
        FF
    )
    act_low = jax.nn.gelu(up_proj, approximate=False).astype(jnp.bfloat16)
    down_proj = jnp.dot(act_low, w_down, preferred_element_type=jnp.float32) + vectors[7]
    second_sum = hidden + down_proj
    normed_two, rstd_two = normalize(second_sum)
    result = (normed_two * gain_two + shift_two).astype(jnp.bfloat16)
    grad_result = cotangent[0].astype(jnp.float32)
    grad_gain_two = jnp.sum(grad_result * normed_two, axis=0)
    grad_shift_two = jnp.sum(grad_result, axis=0)
    grad_second = norm_back(grad_result * gain_two, normed_two, rstd_two)
    grad_down_low = grad_second.astype(jnp.bfloat16)
    grad_w_down = inner_rows(act_low, grad_down_low)
    grad_bias_down = jnp.sum(grad_down_low.astype(jnp.float32), axis=0)
    grad_act = outer_cols(grad_down_low, w_down)
    grad_up_low = (grad_act * gelu_slope(up_proj)).astype(jnp.bfloat16)
    grad_w_up = inner_rows(hidden_low, grad_up_low)
    grad_bias_up = jnp.sum(grad_up_low.astype(jnp.float32), axis=0)
    grad_hidden = grad_second + outer_cols(grad_up_low, w_up)
    grad_gain_one = jnp.sum(grad_hidden * normed_one, axis=0)
    grad_shift_one = jnp.sum(grad_hidden, axis=0)
    grad_first = norm_back(grad_hidden * gain_one, normed_one, rstd_one)
    grad_attn_low = grad_first.astype(jnp.bfloat16)
    grad_w_out = inner_rows(mixed_low, grad_attn_low)
    grad_bias_out = jnp.sum(grad_attn_low.astype(jnp.float32), axis=0)
    grad_mixed = outer_cols(grad_attn_low, w_out)
    grad_heads = jnp.transpose((0.5 * grad_mixed).reshape(tok_count, H, HEAD), (1, 0, 2)).astype(
        jnp.bfloat16
    )
    grad_pairs = jnp.broadcast_to(grad_heads[None], (ROUNDS, H, tok_count, HEAD)).reshape(
        PAIRS * tok_count, HEAD
    )
    sent_grad = grad_pairs[send_order].reshape(n_tok, slot_rows // 2, 2 * HEAD)
    got_grad = lax.all_to_all(sent_grad, "tok", split_axis=0, concat_axis=0, tiled=True)
    grad_cluster = got_grad.reshape(PAIRS * tok_count, HEAD)[arrange].reshape(
        units_here, CLUSTER, HEAD
    )
    scores_again = (
        jnp.einsum("ucd,ued->uce", query_rows, key_rows, preferred_element_type=jnp.float32)
        * score_scale
    )
    probs_again = jnp.exp(scores_again - log_total)
    probs_low = probs_again.astype(jnp.bfloat16)
    grad_values = jnp.einsum(
        "uce,ucd->ued", probs_low, grad_cluster, preferred_element_type=jnp.float32
    )
    grad_probs = jnp.einsum(
        "ucd,ued->uce", grad_cluster, value_rows, preferred_element_type=jnp.float32
    )
    centre = jnp.sum(probs_again * grad_probs, axis=-1, keepdims=True)
    grad_scores = (probs_again * (grad_probs - centre)).astype(jnp.bfloat16)
    grad_query = (
        jnp.einsum("uce,ued->ucd", grad_scores, key_rows, preferred_element_type=jnp.float32)
        * score_scale
    )
    grad_keys = (
        jnp.einsum("uce,ucd->ued", grad_scores, query_rows, preferred_element_type=jnp.float32)
        * score_scale
    )
    grad_grouped = jnp.concatenate(
        [
            grad_query.astype(jnp.bfloat16),
            grad_keys.astype(jnp.bfloat16),
            grad_values.astype(jnp.bfloat16),
        ],
        axis=-1,
    )
    back_grad = grad_grouped.reshape(PAIRS * tok_count, 3 * HEAD)[undo].reshape(
        n_tok, slot_rows // 2, 6 * HEAD
    )
    home_grad = lax.all_to_all(back_grad, "tok", split_axis=0, concat_axis=0, tiled=True)
    home_grad = (
        home_grad.reshape(PAIRS * tok_count, 3 * HEAD)[restore]
        .reshape(ROUNDS, H, tok_count, 3, HEAD)
        .astype(jnp.float32)
    )
    grad_qkv = (home_grad[0] + home_grad[1]).astype(jnp.bfloat16)
    grad_qkv = jnp.transpose(grad_qkv, (1, 2, 0, 3)).reshape(tok_count, 3 * D)
    grad_w_qkv = inner_rows(inputs, grad_qkv)
    grad_bias_qkv = jnp.sum(grad_qkv.astype(jnp.float32), axis=0)
    grad_inputs = grad_first + outer_cols(grad_qkv, w_qkv)
    grad_blocks = jnp.concatenate(
        [
            grad_w_qkv.reshape(D, 3, D),
            grad_w_out[:, None, :],
            grad_w_up.reshape(D, FF // D, D),
            jnp.transpose(grad_w_down.reshape(FF // D, D, D), (1, 0, 2)),
        ],
        axis=1,
    )
    by_block = jnp.transpose(grad_blocks, (1, 0, 2))
    slot_grads = jnp.stack([pick(by_block, slot_block[s]) for s in range(by_block.shape[0])], axis=1)
    vector_grads = jnp.concatenate(
        [
            jnp.stack(
                [
                    grad_gain_one,
                    grad_shift_one,
                    grad_gain_two,
                    grad_shift_two,
                    grad_bias_qkv[:D],
                    grad_bias_qkv[2 * D :],
                    grad_bias_out,
                    grad_bias_down,
                ]
            ),
            grad_bias_up.reshape(FF // D, D),
        ],
        axis=0,
    )
    vector_total = lax.psum(vector_grads, ("tok", "grp"))
    row_total = lax.psum_scatter(slot_grads, "tok", scatter_dimension=0, tiled=True)
    reduced = lax.psum_scatter(
        row_total.astype(jnp.bfloat16), "grp", scatter_dimension=1, tiled=True
    ).astype(jnp.float32)
    left_basis = bases[0]
    right_basis = bases[1]
    first_row = lax.axis_index("tok") * rows_dev
    turned_in = jnp.einsum("rse,sef->rsf", reduced, right_basis, precision=lax.Precision.HIGHEST)
    left_rows = lax.dynamic_slice_in_dim(left_basis, first_row, rows_dev, 1)
    picked = left_rows
    rotated = lax.psum_scatter(
        jnp.einsum("sri,rsf->isf", picked, turned_in, precision=lax.Precision.HIGHEST),
        "tok",
        scatter_dimension=0,
        tiled=True,
    )
    new_one = BETA_ONE * moment_one + (1.0 - BETA_ONE) * rotated
    new_two = BETA_TWO * moment_two + (1.0 - BETA_TWO) * rotated * rotated
    direction = new_one / (jnp.sqrt(new_two) + ADAM_EPS)
    turned_out = jnp.einsum("rse,sfe->rsf", direction, right_basis, precision=lax.Precision.HIGHEST)
    left_cols = lax.dynamic_slice_in_dim(left_basis, first_row, rows_dev, 2)
    picked = left_cols
    change = lax.psum_scatter(
        jnp.einsum("sir,rsf->isf", picked, turned_out, precision=lax.Precision.HIGHEST),
        "tok",
        scatter_dimension=0,
        tiled=True,
    )
    new_master = master - RATE_MATRIX * change
    new_vec_one = BETA_ONE * vector_one + (1.0 - BETA_ONE) * vector_total
    new_vec_two = BETA_TWO * vector_two + (1.0 - BETA_TWO) * vector_total * vector_total
    new_vectors = vectors - RATE_VECTOR * new_vec_one / (jnp.sqrt(new_vec_two) + ADAM_EPS)
    return (
        result[None],
        grad_inputs[None],
        new_one,
        new_two,
        new_master,
        new_vec_one,
        new_vec_two,
        new_vectors,
    )

def solution(mesh):
    n_tok, n_grp = mesh.shape["tok"], mesh.shape["grp"]

    def on_device(*args):
        lengths, clusters = args[2], args[3]
        unit = n_tok // (lengths.shape[1] - 1)
        suits = unit == UNIT and n_tok == 2 * UNIT and n_grp == 4 and clusters.shape[2] == 1024
        return (fast if suits else general)(*args)

    return jax.shard_map(
        on_device,
        mesh=mesh,
        in_specs=(
            P("grp", "tok", None),
            P("grp", "tok", None),
            P("grp", None),
            P("grp", None, "tok"),
            P(),
            P("tok", "grp", None),
            P(None, "grp", None, None),
            P("tok", "grp", None),
            P("tok", "grp", None),
            P(),
            P(),
            P(),
        ),
        out_specs=(
            P("grp", "tok", None),
            P("grp", "tok", None),
            P("tok", "grp", None),
            P("tok", "grp", None),
            P("tok", "grp", None),
            P(),
            P(),
            P(),
        ),
        check_vma=False,
    )
```

```python
import functools

import jax
import jax.numpy as jnp
from jax import lax
from jax.experimental import pallas as pl
from jax.experimental.pallas import tpu as pltpu
from jax.sharding import PartitionSpec as P

D = 768
H = 12
FF = 3072
HEAD = 64
ROUNDS = 2
PAIRS = 24
CLUSTER = 128
FFB = FF // D

EPS_NORM = 1e-05
ADAM_EPS = 1e-08
BETA_ONE = 0.5
BETA_TWO = 0.5
RATE_MATRIX = 0.025
RATE_VECTOR = 0.15
SQRT_HALF = 0.7071067811865476
INV_ROOT_TWO_PI = 0.3989422804014327

BF16 = jnp.bfloat16
F32 = jnp.float32

UNIT = 4
HEADS_OWN = H // UNIT
LOCAL_PAIRS = ROUNDS * HEADS_OWN
TILE = 128
WIDE = 2 * TILE
SMALL = pl.CostEstimate(flops=0, transcendentals=0, bytes_accessed=0)


def inner_rows(left, right):
    return lax.dot_general(left, right, (((0,), (0,)), ((), ())), preferred_element_type=F32)


def outer_cols(left, right):
    return lax.dot_general(left, right, (((1,), (1,)), ((), ())), preferred_element_type=F32)


def normalize(values_in):
    centre = jnp.mean(values_in, axis=-1, keepdims=True)
    offset = values_in - centre
    spread = jnp.mean(offset * offset, axis=-1, keepdims=True)
    rstd = lax.rsqrt(spread + EPS_NORM)
    return (offset * rstd, rstd)


def norm_back(grad_normed, normed, rstd):
    first_mean = jnp.mean(grad_normed, axis=-1, keepdims=True)
    second_mean = jnp.mean(grad_normed * normed, axis=-1, keepdims=True)
    return rstd * (grad_normed - first_mean - normed * second_mean)


def gelu_slope(values_in):
    return (
        0.5 * (1.0 + lax.erf(values_in * SQRT_HALF))
        + values_in * jnp.exp(-0.5 * values_in * values_in) * INV_ROOT_TWO_PI
    )


def turn_half(value):
    return pltpu.roll(value, HEAD, 1)


def places_body(scalars_ref, clusters_ref, *refs):
    outs, all_ref = refs[:UNIT], refs[UNIT]
    pairs, count = clusters_ref.shape
    share, member = scalars_ref[0], scalars_ref[1]
    kinds = UNIT * count // CLUSTER
    kind = lax.broadcasted_iota(jnp.int32, (kinds, count), 0)
    earlier = lax.broadcasted_iota(jnp.int32, (count, count), 0) < lax.broadcasted_iota(jnp.int32, (count, count), 1)
    earlier = earlier.astype(F32).astype(BF16)
    all_ref[...] = jnp.zeros_like(all_ref)
    for pair in range(pairs):
        turn, head = pair // H, pair % H
        cluster = clusters_ref[pair : pair + 1, :]
        same = (kind == cluster).astype(F32)
        before = jnp.dot(same.astype(BF16), earlier, preferred_element_type=F32)
        rank = jnp.sum(same * before, axis=0, keepdims=True).astype(jnp.int32)
        own = head % HEADS_OWN * ROUNDS + turn
        all_ref[head // HEADS_OWN, own : own + 1, :] = cluster * share + rank
    for k in range(UNIT):
        outs[k][...] = all_ref[member ^ k]


def places(scalars, clusters):
    count = clusters.shape[1]
    inside = pl.BlockSpec(memory_space=pltpu.VMEM)
    return pl.pallas_call(
        places_body,
        in_specs=[pl.BlockSpec(memory_space=pltpu.SMEM), inside],
        out_specs=[inside] * UNIT,
        out_shape=[jax.ShapeDtypeStruct((8, count), jnp.int32)] * UNIT,
        scratch_shapes=[pltpu.VMEM((UNIT, 8, count), jnp.int32)],
        cost_estimate=SMALL,
        name="places",
    )(scalars, clusters)


def arrange_body(slots, scalars_ref, *refs):
    sources, outs, rest_ref, tiles_ref = refs[:4], refs[4 : 4 + UNIT], refs[4 + UNIT], refs[5 + UNIT]
    n_rest, count = rest_ref.shape[:2]
    n_blocks = n_rest + 3
    group, core, member = (scalars_ref[n_blocks + i] for i in range(3))
    first = pl.multiple_of(core * count, count)

    def rows_of(block):
        slot = scalars_ref[block]
        owner = lax.div(slot, slots)
        near, inner = owner ^ group, lax.rem(slot, slots)
        found = [source[inner, pl.ds(first, count), :].astype(F32) for source in sources]
        low = jnp.where(near % 2 == 0, found[0], found[1])
        high = jnp.where(near % 2 == 0, found[2], found[3])
        return jnp.where(near < 2, low, high)

    low = lax.broadcasted_iota(jnp.int32, (count, TILE), 1) < HEAD
    parts = [rows_of(i) for i in range(3)]

    def half(part, head, high):
        at = head // 2 * TILE
        tile = parts[part][:, at : at + TILE]
        return tile if head % 2 == high else turn_half(tile)

    for head in range(H):
        own = head % HEADS_OWN
        odd = own % 2
        value = half(2, head, odd)
        query = half(0, head, 1 - odd)
        keys = half(1, head, 1 - odd)
        one = jnp.where(low, query, value) if odd else jnp.where(low, value, query)
        two = jnp.where(low, keys, 0.0) if odd else jnp.where(low, 0.0, keys)
        tiles_ref[head // HEADS_OWN, :, own * WIDE : own * WIDE + TILE] = one.astype(BF16)
        tiles_ref[head // HEADS_OWN, :, own * WIDE + TILE : (own + 1) * WIDE] = two.astype(BF16)
    for k in range(UNIT):
        outs[k][...] = tiles_ref[member ^ k]
    for b in range(n_rest):
        rest_ref[b] = rows_of(3 + b).astype(BF16)


def arrange(scalars, sources, n_blocks):
    slots, rows = sources[0].shape[:2]
    count = rows // 2
    width = HEADS_OWN * WIDE
    inside = pl.BlockSpec(memory_space=pltpu.VMEM)
    return pl.pallas_call(
        functools.partial(arrange_body, slots),
        in_specs=[pl.BlockSpec(memory_space=pltpu.SMEM)] + [inside] * 4,
        out_specs=[inside] * (UNIT + 1),
        out_shape=[jax.ShapeDtypeStruct((count, width), BF16)] * UNIT
        + [jax.ShapeDtypeStruct((n_blocks - 3, count, D), BF16)],
        scratch_shapes=[pltpu.VMEM((UNIT, count, width), BF16)],
        compiler_params=pltpu.CompilerParams(vmem_limit_bytes=32 << 20),
        cost_estimate=SMALL,
        name="arrange",
    )(scalars, *sources)


def assemble_body(table_ref, *refs):
    shards, out_ref, sem = refs[:-2], refs[-2], refs[-1]
    rows = shards[0].shape[1]
    copies = []
    for shard in shards:
        for i in range(shard.shape[0]):
            n = len(copies)
            first = pl.multiple_of(table_ref[n], rows)
            copies.append(
                pltpu.make_async_copy(shard.at[i], out_ref.at[pl.ds(first, rows), :], sem.at[n])
            )
    for copy in copies:
        copy.start()
    for copy in copies:
        copy.wait()


def assemble(table, shards):
    pieces = sum(s.shape[0] for s in shards)
    anywhere = pl.BlockSpec(memory_space=pl.ANY)
    return pl.pallas_call(
        assemble_body,
        in_specs=[pl.BlockSpec(memory_space=pltpu.SMEM)] + [anywhere] * len(shards),
        out_specs=pl.BlockSpec(memory_space=pltpu.VMEM),
        out_shape=jax.ShapeDtypeStruct((pieces * shards[0].shape[1], shards[0].shape[2]), BF16),
        scratch_shapes=[pltpu.SemaphoreType.DMA((pieces,))],
        cost_estimate=SMALL,
        name="assemble",
    )(table, *shards)


def sort_body(place_ref, x_ref, weight_ref, bias_ref, out_ref, rows_ref):
    count = x_ref.shape[0]
    head = pl.program_id(0)
    chunk = 256
    row = lax.broadcasted_iota(jnp.int32, (chunk, count), 0)
    rows_ref[...] = (
        jnp.dot(x_ref[...], weight_ref[...], preferred_element_type=F32) + bias_ref[...]
    ).astype(BF16)
    for step in range(HEADS_OWN):

        @pl.when(head == step)
        def _():
            for turn in range(ROUNDS):
                pair = step * ROUNDS + turn
                for part in range(count // chunk):
                    where = pl.ds(part * chunk, chunk)
                    picked = place_ref[pair : pair + 1, :] == row + part * chunk
                    picked = picked.astype(F32).astype(BF16)
                    out_ref[turn, where, :] = jnp.dot(
                        picked, rows_ref[...], preferred_element_type=F32
                    ).astype(BF16)


def sort_rows(order, inputs, weights, bias):
    count = inputs.shape[0]
    return pl.pallas_call(
        sort_body,
        grid=(HEADS_OWN,),
        in_specs=[
            pl.BlockSpec((8, count), lambda h: (0, 0)),
            pl.BlockSpec((count, D), lambda h: (0, 0)),
            pl.BlockSpec((D, WIDE), lambda h: (0, h)),
            pl.BlockSpec((1, WIDE), lambda h: (0, h)),
        ],
        out_specs=pl.BlockSpec((ROUNDS, count, WIDE), lambda h: (h, 0, 0)),
        out_shape=jax.ShapeDtypeStruct((LOCAL_PAIRS, count, WIDE), BF16),
        scratch_shapes=[pltpu.VMEM((count, WIDE), BF16)],
        compiler_params=pltpu.CompilerParams(vmem_limit_bytes=48 << 20),
        cost_estimate=SMALL,
        name="sort_rows",
    )(order, inputs, weights, bias)


def sort_grads_body(place_ref, rows_ref, out_ref):
    count = place_ref.shape[1]
    half = count // 2
    head = pl.program_id(0)
    chunk = 256
    row = lax.broadcasted_iota(jnp.int32, (chunk, count), 0)
    low = lax.broadcasted_iota(jnp.int32, (count, TILE), 1) < HEAD
    for step in range(HEADS_OWN):

        @pl.when(head == step)
        def _():
            if step < 2:
                tile = rows_ref[0:count, :].astype(F32)
                tile = jnp.where(low if step == 0 else jnp.logical_not(low), tile, 0.0).astype(BF16)
            else:
                both = rows_ref[count : count + half, :].astype(F32)
                tile = jnp.concatenate([both, turn_half(both)], axis=0)
                tile = jnp.where(low, tile, 0.0).astype(BF16)
            for turn in range(ROUNDS):
                pair = step * ROUNDS + turn
                for part in range(count // chunk):
                    where = pl.ds(part * chunk, chunk)
                    picked = place_ref[pair : pair + 1, :] == row + part * chunk
                    picked = picked.astype(F32).astype(BF16)
                    out_ref[turn, where, :] = jnp.dot(
                        picked, tile, preferred_element_type=F32
                    ).astype(BF16)


def sort_grads(order, rows):
    count = order.shape[1]
    return pl.pallas_call(
        sort_grads_body,
        grid=(HEADS_OWN,),
        in_specs=[
            pl.BlockSpec((8, count), lambda h: (0, 0)),
            pl.BlockSpec(rows.shape, lambda h: (0, 0)),
        ],
        out_specs=pl.BlockSpec((ROUNDS, count, TILE), lambda h: (h, 0, 0)),
        out_shape=jax.ShapeDtypeStruct((LOCAL_PAIRS, count, TILE), BF16),
        compiler_params=pltpu.CompilerParams(vmem_limit_bytes=48 << 20),
        cost_estimate=SMALL,
        name="sort_grads",
    )(order, rows)


def plans_of(count):
    share = CLUSTER // UNIT
    half = UNIT // 2
    return (
        [(tuple(range(UNIT)), share)],
        [(tuple(range(i * half, (i + 1) * half)), 2 * share) for i in range(2)],
    )


def for_each_batch(is_long, count, batch, work):
    for wanted, plan in zip((1, 0), plans_of(count)):

        @pl.when(is_long == wanted)
        def _(plan=plan):
            for runs, share in plan:

                def step(group, carry, runs=runs, share=share):
                    first = pl.multiple_of(group * (batch * share), batch * share)
                    work(runs, pl.ds(first, batch * share), share)
                    return carry

                lax.fori_loop(0, count // share // batch, step, 0)


def batch_of(refs, runs, where, share, width):
    parts = [refs[r][0, where, :] for r in runs]
    return jnp.concatenate([p.reshape(p.shape[0] // share, share, width) for p in parts], axis=1)


def spread(refs, runs, where, share, columns, value):
    for i, r in enumerate(runs):
        part = value[:, i * share : (i + 1) * share]
        refs[r][0, where, columns] = part.reshape(part.shape[0] * share, TILE)


def products(form, left, right):
    return jnp.einsum(form, left, right, preferred_element_type=F32)


def softmax(first, second):
    scores = products("ued,ucd->uec", second, first) * (HEAD**-0.5)
    expo = jnp.exp(scores - jnp.max(scores, axis=1, keepdims=True))
    return expo * (1.0 / jnp.sum(expo, axis=1, keepdims=True))


def attend_body(long_ref, *refs):
    grouped, results = refs[:UNIT], refs[UNIT:]

    def work(runs, where, share):
        rows = batch_of(grouped, runs, where, share, WIDE)
        first = rows[..., :TILE]
        probs = softmax(first, rows[..., TILE:]).astype(BF16)
        mixed = products("uce,ued->ucd", jnp.swapaxes(probs, 1, 2), first).astype(BF16)
        spread(results, runs, where, share, slice(0, TILE), mixed)

    for_each_batch(long_ref[0], grouped[0].shape[1], 8, work)


def attend(is_long, grouped):
    count = grouped[0].shape[1]
    return pl.pallas_call(
        attend_body,
        grid_spec=pltpu.PrefetchScalarGridSpec(
            num_scalar_prefetch=1,
            grid=(LOCAL_PAIRS,),
            in_specs=[pl.BlockSpec((1, count, WIDE), lambda p, _: (p, 0, 0))] * UNIT,
            out_specs=[pl.BlockSpec((1, count, TILE), lambda p, _: (p, 0, 0))] * UNIT,
        ),
        out_shape=[jax.ShapeDtypeStruct((LOCAL_PAIRS, count, TILE), BF16)] * UNIT,
        compiler_params=pltpu.CompilerParams(vmem_limit_bytes=48 << 20),
        cost_estimate=SMALL,
        name="attend",
    )(is_long, *grouped)


def attend_back_body(long_ref, *refs):
    grouped, grads, results = refs[:UNIT], refs[UNIT : 2 * UNIT], refs[2 * UNIT :]
    batch = 16
    odd = (pl.program_id(0) // ROUNDS) % 2
    lane = lax.broadcasted_iota(jnp.int32, (batch, CLUSTER, TILE), 2)
    value_lane = (lane < HEAD) == (odd == 0)
    scale = HEAD**-0.5

    def work(runs, where, share):
        rows = batch_of(grouped, runs, where, share, WIDE)
        grad = batch_of(grads, runs, where, share, TILE)
        first, second = rows[..., :TILE], rows[..., TILE:]
        probs = softmax(first, second)
        grad_probs = products("ued,ucd->uec", first, grad)
        centre = jnp.sum(probs * grad_probs, axis=1, keepdims=True)
        grad_scores = (probs * (grad_probs - centre)).astype(BF16)
        grad_values = products("uec,ucd->ued", probs.astype(BF16), grad)
        grad_keys = products("uec,ucd->ued", grad_scores, first) * scale
        grad_query = products("uce,ued->ucd", jnp.swapaxes(grad_scores, 1, 2), second) * scale
        tile_one = jnp.where(value_lane, grad_values, grad_query).astype(BF16)
        tile_two = jnp.where(value_lane, 0.0, grad_keys).astype(BF16)
        spread(results, runs, where, share, slice(0, TILE), tile_one)
        spread(results, runs, where, share, slice(TILE, WIDE), tile_two)

    for_each_batch(long_ref[0], grouped[0].shape[1], batch, work)


def attend_back(is_long, grouped, grads):
    count = grouped[0].shape[1]
    return pl.pallas_call(
        attend_back_body,
        grid_spec=pltpu.PrefetchScalarGridSpec(
            num_scalar_prefetch=1,
            grid=(LOCAL_PAIRS,),
            in_specs=[pl.BlockSpec((1, count, WIDE), lambda p, _: (p, 0, 0))] * UNIT
            + [pl.BlockSpec((1, count, TILE), lambda p, _: (p, 0, 0))] * UNIT,
            out_specs=[pl.BlockSpec((1, count, WIDE), lambda p, _: (p, 0, 0))] * UNIT,
        ),
        out_shape=[jax.ShapeDtypeStruct((LOCAL_PAIRS, count, WIDE), BF16)] * UNIT,
        compiler_params=pltpu.CompilerParams(vmem_limit_bytes=56 << 20),
        cost_estimate=SMALL,
        name="attend_back",
    )(is_long, *grouped, *grads)


def unsorted(column_ref, step, rows_ref, part, chunk):
    count = rows_ref.shape[1]
    where = pl.ds(part * chunk, chunk)
    lane = lax.broadcasted_iota(jnp.int32, (chunk, count), 1)
    total = None
    for turn in range(ROUNDS):
        pair = step * ROUNDS + turn
        picked = (column_ref[where, pair : pair + 1] == lane).astype(F32).astype(BF16)
        more = jnp.dot(picked, rows_ref[turn], preferred_element_type=F32)
        total = more if total is None else total + more
    return total


def mix_body(place_ref, rows_ref, out_ref, column_ref):
    @pl.when(pl.program_id(0) == 0)
    def _():
        column_ref[...] = jnp.transpose(place_ref[...])

    count = rows_ref.shape[1]
    chunk = 256
    parts = count // chunk
    low = lax.broadcasted_iota(jnp.int32, (chunk, TILE), 1) < HEAD
    head = pl.program_id(0)
    for step in range(HEADS_OWN):

        @pl.when(head == step)
        def _():
            means = [0.5 * unsorted(column_ref, step, rows_ref, part, chunk) for part in range(parts)]
            for part in range(parts):
                where = pl.ds(part * chunk, chunk)
                if step == 0:
                    out_ref[where, :] = means[part].astype(BF16)
                elif step == 1:
                    out_ref[where, :] = jnp.where(low, out_ref[where, :].astype(F32), means[part]).astype(BF16)
                elif part < parts // 2:
                    both = jnp.where(low, means[part], turn_half(means[part + parts // 2]))
                    out_ref[pl.ds(count + part * chunk, chunk), :] = both.astype(BF16)


def mix(order, rows):
    count = rows.shape[1]
    packed = (count + count // 2, TILE)
    return pl.pallas_call(
        mix_body,
        grid=(HEADS_OWN,),
        in_specs=[
            pl.BlockSpec((8, count), lambda h: (0, 0)),
            pl.BlockSpec((ROUNDS, count, TILE), lambda h: (h, 0, 0)),
        ],
        out_specs=pl.BlockSpec(packed, lambda h: (0, 0)),
        out_shape=jax.ShapeDtypeStruct(packed, BF16),
        scratch_shapes=[pltpu.VMEM((count, 8), jnp.int32)],
        compiler_params=pltpu.CompilerParams(vmem_limit_bytes=48 << 20),
        cost_estimate=SMALL,
        name="mix",
    )(order, rows)


def gather_grads_body(place_ref, rows_ref, out_ref, column_ref):
    @pl.when(pl.program_id(0) == 0)
    def _():
        column_ref[...] = jnp.transpose(place_ref[...])

    count = rows_ref.shape[1]
    chunk = 256
    head = pl.program_id(0)
    for step in range(HEADS_OWN):

        @pl.when(head == step)
        def _():
            for part in range(count // chunk):
                where = pl.ds(part * chunk, chunk)
                out_ref[where, :] = unsorted(column_ref, step, rows_ref, part, chunk).astype(BF16)


def gather_grads(order, rows):
    count = rows.shape[1]
    return pl.pallas_call(
        gather_grads_body,
        grid=(HEADS_OWN,),
        in_specs=[
            pl.BlockSpec((8, count), lambda h: (0, 0)),
            pl.BlockSpec((ROUNDS, count, WIDE), lambda h: (h, 0, 0)),
        ],
        out_specs=pl.BlockSpec((count, WIDE), lambda h: (0, h)),
        out_shape=jax.ShapeDtypeStruct((count, HEADS_OWN * WIDE), BF16),
        scratch_shapes=[pltpu.VMEM((count, 8), jnp.int32)],
        compiler_params=pltpu.CompilerParams(vmem_limit_bytes=48 << 20),
        cost_estimate=SMALL,
        name="gather_grads",
    )(order, rows)


ERF_TOP = (0.00022905065861350646, 0.0034082910107109506, 0.050955695062380861, 0.18520832239976145, 1.128379143519084)
ERF_BOTTOM = (
    -1.1791602954361697e-7,
    0.000023547966471313185,
    0.0010179625278914885,
    0.014070470171167667,
    0.11098505178285362,
    0.49746925110067538,
    1.0,
)


def polynomial(value, factors):
    total = jnp.full_like(value, factors[0])
    for factor in factors[1:]:
        total = total * value + factor
    return total


def error_function(value):
    value = jnp.clip(value, -3.832506856900711, 3.832506856900711)
    square = value * value
    return value * polynomial(square, ERF_TOP) / polynomial(square, ERF_BOTTOM)


VEC_ROWS = 16
FFN_TILE = 256


def layer_body(
    n_shards,
    table_ref,
    *refs,
):
    shards, refs = refs[:n_shards], refs[n_shards:]
    parts, refs = refs[:UNIT], refs[UNIT:]
    x_ref, cot_ref, vec_ref, result_ref, first_ref, sums_ref, kept_ref, sent_ref = refs[:8]
    backs, refs = refs[8 : 8 + UNIT], refs[8 + UNIT :]
    w_ref, packed_ref, mixed_ref, hidden_ref, act_ref, down_ref, up_ref, attn_ref, back_ref = refs[:9]
    slope_ref, stage_ref, weight_sem, part_sem, stage_sem = refs[9:]
    count = x_ref.shape[0]
    half = count // 2
    per_shard, n_weights, shard_rows = shards[0].shape[:3]
    member = table_ref[0]
    for k in range(UNIT):
        pltpu.make_async_copy(parts[k], packed_ref.at[member ^ k], part_sem.at[k]).start()
    for b in range(n_weights):
        for n in range(n_shards * per_shard):
            row = pl.multiple_of(table_ref[6 + n], shard_rows)
            pltpu.make_async_copy(
                shards[n // per_shard].at[n % per_shard, b], w_ref.at[b, pl.ds(row, shard_rows), :], weight_sem.at[b]
            ).start()
    for k in range(UNIT):
        pltpu.make_async_copy(parts[k], packed_ref.at[member ^ k], part_sem.at[k]).wait()
    for b in range(n_weights):
        pltpu.make_async_copy(w_ref.at[b], w_ref.at[b], weight_sem.at[b]).wait()

    sums_ref[...] = jnp.zeros_like(sums_ref)
    low = lax.broadcasted_iota(jnp.int32, (FFN_TILE, TILE), 1) < HEAD
    vec = [vec_ref[i : i + 1, :] for i in range(8 + FFB)]
    gain_one, shift_one, gain_two, shift_two = vec[:4]
    bias_out, bias_down = vec[6], vec[7]

    def add_sum(row, value):
        sums_ref[row : row + 1, :] += jnp.sum(value, axis=0, keepdims=True)

    def tile_step(i, carry):
        rows = pl.ds(pl.multiple_of(i * FFN_TILE, FFN_TILE), FFN_TILE)
        is_first = i * FFN_TILE < half
        extra = pl.ds(pl.multiple_of(count + lax.rem(i * FFN_TILE, half), FFN_TILE), FFN_TILE)

        def pair(m):
            return packed_ref[m, rows, :].astype(F32)

        def single(m):
            value = packed_ref[m, extra, :].astype(F32)
            return jnp.where(is_first, value, turn_half(value))

        for m in (0, 2):
            at = m * (HEADS_OWN * HEAD)
            nxt = turn_half(pair(m + 1))
            mixed_ref[rows, at : at + TILE] = pair(m).astype(BF16)
            mixed_ref[rows, at + TILE : at + 2 * TILE] = jnp.where(low, single(m), nxt).astype(BF16)
            mixed_ref[rows, at + 2 * TILE : at + 3 * TILE] = jnp.where(
                low, nxt, turn_half(single(m + 1))
            ).astype(BF16)
        attention = jnp.dot(mixed_ref[rows, :], w_ref[0], preferred_element_type=F32) + bias_out
        normed_one, rstd_one = normalize(x_ref[rows, :].astype(F32) + attention)
        hidden = normed_one * gain_one + shift_one
        hidden_low = hidden.astype(BF16)
        hidden_ref[rows, :] = hidden_low
        down = jnp.broadcast_to(bias_down, hidden.shape)
        for j in range(FFB):
            up = jnp.dot(hidden_low, w_ref[1 + j], preferred_element_type=F32) + vec[8 + j]
            phi = 0.5 * (1.0 + error_function(up * SQRT_HALF))
            slope_ref[j] = phi + up * jnp.exp(-0.5 * up * up) * INV_ROOT_TWO_PI
            act = (up * phi).astype(BF16)
            act_ref[j, rows, :] = act
            down = down + jnp.dot(act, w_ref[1 + FFB + j], preferred_element_type=F32)
        normed_two, rstd_two = normalize(hidden + down)
        result_ref[rows, :] = (normed_two * gain_two + shift_two).astype(BF16)
        grad_result = cot_ref[rows, :].astype(F32)
        add_sum(2, grad_result * normed_two)
        add_sum(3, grad_result)
        grad_second = norm_back(grad_result * gain_two, normed_two, rstd_two)
        grad_down = grad_second.astype(BF16)
        down_ref[rows, :] = grad_down
        add_sum(7, grad_down.astype(F32))
        grad_hidden = grad_second
        for j in range(FFB):
            grad_up = (outer_cols(grad_down, w_ref[1 + FFB + j]) * slope_ref[j]).astype(BF16)
            up_ref[j, rows, :] = grad_up
            add_sum(8 + j, grad_up.astype(F32))
            grad_hidden = grad_hidden + outer_cols(grad_up, w_ref[1 + j])
        add_sum(0, grad_hidden * normed_one)
        add_sum(1, grad_hidden)
        grad_first = norm_back(grad_hidden * gain_one, normed_one, rstd_one)
        first_ref[rows, :] = grad_first
        grad_attn = grad_first.astype(BF16)
        attn_ref[rows, :] = grad_attn
        add_sum(6, grad_attn.astype(F32))
        grad_mixed = (0.5 * outer_cols(grad_attn, w_ref[0])).astype(BF16).astype(F32)
        for m in range(UNIT):
            at = (m // 2) * 3 * TILE
            tiles = [grad_mixed[:, at + n * TILE : at + (n + 1) * TILE] for n in range(3)]
            if m % 2 == 0:
                two, one = tiles[0], tiles[1]
            else:
                two, one = turn_half(jnp.where(low, tiles[2], tiles[1])), turn_half(tiles[2])
            back_ref[member ^ m, rows, :] = two.astype(BF16)

            @pl.when(is_first)
            def _(one=one, m=m):
                back_ref[member ^ m, extra, :] = jnp.where(low, one, 0.0).astype(BF16)

            @pl.when(jnp.logical_not(is_first))
            def _(one=one, m=m):
                old = back_ref[member ^ m, extra, :].astype(F32)
                back_ref[member ^ m, extra, :] = jnp.where(low, old, turn_half(one)).astype(BF16)

        return carry

    lax.fori_loop(0, count // FFN_TILE, tile_step, 0)
    for k in range(UNIT):
        backs[k][...] = back_ref[k]

    core, bits = table_ref[1], [table_ref[2 + d] for d in range(4)]
    piece, half_columns = kept_ref.shape[3:]
    n_parts = kept_ref.shape[0]
    per_part = n_weights // n_parts

    def copies(block, slot, half, target):
        part = block // per_part
        made = []
        for index in range(16):
            x, zh, y, zl = ((index >> s) % 2 for s in range(4))
            rel = {"x": x ^ bits[0], "y": y ^ bits[1], "zl": zl ^ bits[2], "zh": zh ^ bits[3]}
            place = 0
            for name in PART_ORDERS[part]:
                place = place * 2 + rel[name]
            made.append(
                pltpu.make_async_copy(
                    stage_ref.at[
                        slot, pl.ds(index * piece, piece), pl.ds(half * half_columns, half_columns)
                    ],
                    target.at[part, place, block % per_part],
                    stage_sem.at[slot, half * 16 + index],
                )
            )
        return made

    def send(block, slot):
        for half in range(2):

            @pl.when(core == half)
            def _(half=half):
                for copy in copies(block, slot, half, kept_ref):
                    copy.start()

            @pl.when(core != half)
            def _(half=half):
                for copy in copies(block, slot, half, sent_ref):
                    copy.start()

    def sent(block, slot):
        for half in range(2):
            for copy in copies(block, slot, half, kept_ref):
                copy.wait()

    plan = [(attn_ref, None, mixed_ref, None, 0)]
    plan += [(down_ref, None, act_ref, j, 1 + FFB + j) for j in range(FFB)]
    plan += [(up_ref, j, hidden_ref, None, 1 + j) for j in range(FFB)]
    for n, (left, lj, right, rj, block) in enumerate(plan):
        slot = n % 2
        if n >= 2:
            sent(plan[n - 2][4], slot)
        value = inner_rows(
            left[...] if lj is None else left[lj], right[...] if rj is None else right[rj]
        )
        stage_ref[slot] = value.astype(BF16)
        send(block, slot)
    for n in (len(plan) - 2, len(plan) - 1):
        sent(plan[n][4], n % 2)


PART_ORDERS = (("x", "y", "zl", "zh"), ("y", "zl", "zh", "x"), ("zl", "zh", "x", "y"))


def layer(table, shards, parts, inputs, cotangent, vectors):
    count = inputs.shape[0]
    n_weights = 1 + 2 * FFB
    n_shards = len(shards)
    anywhere = pl.BlockSpec(memory_space=pl.ANY)
    inside = pl.BlockSpec(memory_space=pltpu.VMEM)
    packed = parts[0].shape
    return pl.pallas_call(
        functools.partial(layer_body, n_shards),
        in_specs=[pl.BlockSpec(memory_space=pltpu.SMEM)] + [anywhere] * (n_shards + UNIT) + [inside] * 3,
        out_specs=[inside, inside, inside, anywhere, anywhere] + [inside] * UNIT,
        out_shape=[
            jax.ShapeDtypeStruct((count, D), BF16),
            jax.ShapeDtypeStruct((count, D), F32),
            jax.ShapeDtypeStruct((VEC_ROWS, D), F32),
            jax.ShapeDtypeStruct((3, 16, n_weights // 3, D // 16, D // 2), BF16),
            jax.ShapeDtypeStruct((3, 16, n_weights // 3, D // 16, D // 2), BF16),
        ]
        + [jax.ShapeDtypeStruct(packed, BF16)] * UNIT,
        scratch_shapes=[
            pltpu.VMEM((n_weights, D, D), BF16),
            pltpu.VMEM((UNIT, *packed), BF16),
            pltpu.VMEM((count, D), BF16),
            pltpu.VMEM((count, D), BF16),
            pltpu.VMEM((FFB, count, D), BF16),
            pltpu.VMEM((count, D), BF16),
            pltpu.VMEM((FFB, count, D), BF16),
            pltpu.VMEM((count, D), BF16),
            pltpu.VMEM((UNIT, *packed), BF16),
            pltpu.VMEM((FFB, FFN_TILE, D), F32),
            pltpu.VMEM((2, D, D), BF16),
            pltpu.SemaphoreType.DMA((n_weights,)),
            pltpu.SemaphoreType.DMA((UNIT,)),
            pltpu.SemaphoreType.DMA((2, 32)),
        ],
        compiler_params=pltpu.CompilerParams(vmem_limit_bytes=60 << 20),
        cost_estimate=SMALL,
        name="layer",
    )(table, *shards, *parts, inputs, cotangent, vectors)


def qkv_back_body(scalars_ref, *refs):
    grads, inputs, kept_ref, sent_ref, bias_ref, all_ref = refs[:4], refs[4:8], *refs[8:]
    core, unit = scalars_ref[0], scalars_ref[1]
    columns = all_ref.shape[4]
    step = 32
    per_unit = all_ref.shape[3]
    bias_ref[...] = jnp.zeros_like(bias_ref)
    for head in range(HEADS_OWN):
        at = slice(head * WIDE, (head + 1) * WIDE)
        total = inner_rows(grads[0][:, at], inputs[0][...])
        bias = jnp.sum(grads[0][:, at].astype(F32), axis=0, keepdims=True)
        for k in range(1, UNIT):
            total = total + inner_rows(grads[k][:, at], inputs[k][...])
            bias = bias + jnp.sum(grads[k][:, at].astype(F32), axis=0, keepdims=True)
        bias_ref[0:1, at] = bias
        firsts = (HEAD, 3 * HEAD, 0) if head % 2 == 0 else (0, 2 * HEAD, HEAD)
        for block, first in enumerate(firsts):
            for i in range(HEAD // step):
                row = head * HEAD + i * step
                rows = total[first + i * step : first + (i + 1) * step]
                for c in range(2):
                    all_ref[
                        c ^ core, row // per_unit ^ unit, block, row % per_unit : row % per_unit + step, :
                    ] = rows[:, c * columns : (c + 1) * columns].astype(BF16)
    kept_ref[...] = all_ref[0]
    sent_ref[...] = all_ref[1]


def qkv_back(scalars, grads, inputs):
    inside = pl.BlockSpec(memory_space=pltpu.VMEM)
    shape = (2, 3, HEADS_OWN * HEAD // 2, D // 2)
    return pl.pallas_call(
        qkv_back_body,
        in_specs=[pl.BlockSpec(memory_space=pltpu.SMEM)] + [inside] * (2 * UNIT),
        out_specs=[inside] * 3,
        out_shape=[
            jax.ShapeDtypeStruct(shape, BF16),
            jax.ShapeDtypeStruct(shape, BF16),
            jax.ShapeDtypeStruct((8, HEADS_OWN * WIDE), F32),
        ],
        scratch_shapes=[pltpu.VMEM((2, *shape), BF16)],
        compiler_params=pltpu.CompilerParams(vmem_limit_bytes=56 << 20),
        cost_estimate=SMALL,
        name="qkv_back",
    )(scalars, *grads, *inputs)


def pack_body(slot_block_ref, *refs):
    half = (len(refs) - 2) // 2
    kept, got, out_ref, all_ref = refs[:half], refs[half : 2 * half], refs[-2], refs[-1]
    per_part = kept[0].shape[1]
    for p in range(half):
        for b in range(per_part):
            all_ref[p * per_part + b] = (kept[p][0, b] + got[p][0, b].astype(F32)).astype(BF16)
    for s in range(out_ref.shape[0] * out_ref.shape[1]):
        out_ref[s // out_ref.shape[1], s % out_ref.shape[1]] = all_ref[jnp.maximum(slot_block_ref[s] - 3, 0)]


def pack(slot_block, kept, got, n_grp, slots):
    shape = kept[0].shape[2:]
    inside = pl.BlockSpec(memory_space=pltpu.VMEM)
    return pl.pallas_call(
        pack_body,
        in_specs=[pl.BlockSpec(memory_space=pltpu.SMEM)] + [inside] * (2 * len(kept)),
        out_specs=inside,
        out_shape=jax.ShapeDtypeStruct((n_grp, slots, *shape), BF16),
        scratch_shapes=[pltpu.VMEM((len(kept) * kept[0].shape[1], *shape), BF16)],
        compiler_params=pltpu.CompilerParams(vmem_limit_bytes=32 << 20),
        cost_estimate=SMALL,
        name="pack",
    )(slot_block, *kept, *got)


def rotate_in_body(mine_ref, keep_ref, got_ref, high_ref, low_ref, out_ref, grad_ref):
    slots, n_tok = got_ref.shape[1], out_ref.shape[0]
    rows, columns = got_ref.shape[2:]
    width = out_ref.shape[3]
    for s in range(slots):
        block = mine_ref[s]

        @pl.when(block < 3)
        def _(s=s, block=block):
            grad_ref[...] = keep_ref[jnp.minimum(block, 2)]

        @pl.when(block >= 3)
        def _(s=s):
            for g in range(got_ref.shape[0]):
                x, c = g // 2, g % 2
                grad_ref[x * rows : (x + 1) * rows, c * columns : (c + 1) * columns] = got_ref[g, s]

        grad = grad_ref[...]
        part = jnp.dot(grad, high_ref[s], preferred_element_type=F32)
        part = jnp.transpose(part + jnp.dot(grad, low_ref[s], preferred_element_type=F32))
        for r in range(n_tok):
            out_ref[r, s] = part[r * width : (r + 1) * width].astype(BF16)


def rotate_in(mine, keep, got, left, n_tok):
    slots, width = got.shape[1], keep.shape[1]
    inside = pl.BlockSpec(memory_space=pltpu.VMEM)
    return pl.pallas_call(
        rotate_in_body,
        in_specs=[pl.BlockSpec(memory_space=pltpu.SMEM)] + [inside] * 4,
        out_specs=inside,
        out_shape=jax.ShapeDtypeStruct((n_tok, slots, width, width), BF16),
        scratch_shapes=[pltpu.VMEM(keep.shape[1:], BF16)],
        compiler_params=pltpu.CompilerParams(vmem_limit_bytes=48 << 20),
        cost_estimate=SMALL,
        name="rotate_in",
    )(mine, keep, got, *left)


def moments_body(place, got_ref, high_ref, low_ref, one_ref, two_ref, new_one_ref, new_two_ref, out_ref):
    n_tok, slots, width = got_ref.shape[:3]
    for s in range(slots):
        rotated = jnp.zeros(one_ref.shape[1:], F32)
        for t in range(n_tok):
            at = slice(place[t] * width, (place[t] + 1) * width)
            part = got_ref[t, s]
            rotated = rotated + jnp.dot(part, high_ref[s, at], preferred_element_type=F32)
            rotated = rotated + jnp.dot(part, low_ref[s, at], preferred_element_type=F32)
        new_one = BETA_ONE * one_ref[s] + (1.0 - BETA_ONE) * rotated
        new_two = BETA_TWO * two_ref[s] + (1.0 - BETA_TWO) * rotated * rotated
        new_one_ref[s] = new_one
        new_two_ref[s] = new_two
        direction = (new_one / (jnp.sqrt(new_two) + ADAM_EPS)).astype(BF16)
        for t in range(n_tok):
            at = slice(place[t] * width, (place[t] + 1) * width)
            turned = outer_cols(direction, high_ref[s, at]) + outer_cols(direction, low_ref[s, at])
            out_ref[t, s] = turned.astype(BF16)


def moments(place, got, right, one, two):
    n_tok, slots, width = got.shape[:3]
    inside = pl.BlockSpec(memory_space=pltpu.VMEM)
    return pl.pallas_call(
        functools.partial(moments_body, tuple(place)),
        in_specs=[inside] * 5,
        out_specs=[inside] * 3,
        out_shape=[
            jax.ShapeDtypeStruct(one.shape, F32),
            jax.ShapeDtypeStruct(one.shape, F32),
            jax.ShapeDtypeStruct(got.shape, BF16),
        ],
        compiler_params=pltpu.CompilerParams(vmem_limit_bytes=48 << 20),
        cost_estimate=SMALL,
        name="moments",
    )(got, *right, one, two)


def rotate_out_body(got_ref, high_ref, low_ref, out_ref, rows_ref):
    n_tok, slots, width = got_ref.shape[:3]
    for s in range(slots):
        for r in range(n_tok):
            rows_ref[r * width : (r + 1) * width, :] = got_ref[r, s]
        rows = rows_ref[...]
        change = jnp.dot(high_ref[s], rows, preferred_element_type=F32)
        change = change + jnp.dot(low_ref[s], rows, preferred_element_type=F32)
        for r in range(n_tok):
            out_ref[r, s] = change[r * width : (r + 1) * width].astype(BF16)


def rotate_out(got, left):
    n_tok, slots, width = got.shape[:3]
    inside = pl.BlockSpec(memory_space=pltpu.VMEM)
    return pl.pallas_call(
        rotate_out_body,
        in_specs=[inside] * 3,
        out_specs=inside,
        out_shape=jax.ShapeDtypeStruct(got.shape, BF16),
        scratch_shapes=[pltpu.VMEM((n_tok * width, width), BF16)],
        compiler_params=pltpu.CompilerParams(vmem_limit_bytes=48 << 20),
        cost_estimate=SMALL,
        name="rotate_out",
    )(got, *left)


def apply_body(place, got_ref, master_ref, out_ref):
    n_tok, slots, width = got_ref.shape[:3]
    for s in range(slots):
        for t in range(n_tok):
            at = slice(place[t] * width, (place[t] + 1) * width)
            out_ref[s, :, at] = master_ref[s, :, at] - RATE_MATRIX * got_ref[t, s].astype(F32)


def apply_change(place, got, master):
    inside = pl.BlockSpec(memory_space=pltpu.VMEM)
    return pl.pallas_call(
        functools.partial(apply_body, tuple(place)),
        in_specs=[inside] * 2,
        out_specs=inside,
        out_shape=jax.ShapeDtypeStruct(master.shape, F32),
        compiler_params=pltpu.CompilerParams(vmem_limit_bytes=48 << 20),
        cost_estimate=SMALL,
        name="apply_change",
    )(got, master)


def swap(value, axis, bit):
    size = lax.axis_size(axis)
    return lax.ppermute(value, axis, [(i, i ^ bit) for i in range(size)])


def exchange_unit(parts):
    return [parts[0]] + [swap(parts[k], "tok", k) for k in range(1, UNIT)]


LINKS = {"x": ("grp", 2), "y": ("tok", 1), "zl": ("tok", 2), "zh": ("tok", 4)}


def starts_of(lengths):
    index = jnp.arange(lengths.shape[0])
    return jnp.sum(jnp.where(index[None, :] < index[:, None], lengths[None, :], 0), axis=1)


LINKS = {"x": ("grp", 2), "y": ("tok", 1), "zl": ("tok", 2), "zh": ("tok", 4)}


def starts_of(lengths):
    index = jnp.arange(lengths.shape[0])
    return jnp.sum(jnp.where(index[None, :] < index[:, None], lengths[None, :], 0), axis=1)


def total_of(value):
    for axis in ("grp", "tok"):
        bit = 1
        while bit < lax.axis_size(axis):
            value = value + swap(value, axis, bit)
            bit *= 2
    return value


def pick(values, index):
    return lax.dynamic_index_in_dim(values, index, 0, keepdims=False)


def split_heads(columns):
    query, keys, values = (c.reshape(HEADS_OWN, HEAD) for c in columns)
    zero = jnp.zeros((HEAD,), query.dtype)
    tiles = []
    for h in range(HEADS_OWN):
        tiles += [values[h], query[h], zero, keys[h]] if h % 2 == 0 else [query[h], values[h], keys[h], zero]
    return jnp.concatenate(tiles)


def join_heads(tiles):
    parts = tiles.reshape(HEADS_OWN, 4, HEAD, *tiles.shape[1:])
    at = [(1, 0), (3, 2), (0, 1)]
    return jnp.stack(
        [jnp.concatenate([parts[h, at[i][h % 2]] for h in range(HEADS_OWN)], axis=0) for i in range(3)]
    )


def doubled(value):
    high = value.astype(BF16)
    return high, (value - high.astype(F32)).astype(BF16)


def together(*groups):
    flat, tree = jax.tree.flatten(groups)
    return jax.tree.unflatten(tree, lax.optimization_barrier(flat))


def fast(
    tokens,
    cotangent,
    lengths,
    clusters,
    owners,
    master,
    bases,
    moment_one,
    moment_two,
    vectors,
    vector_one,
    vector_two,
):
    n_tok = lax.axis_size("tok")
    n_grp = lax.axis_size("grp")
    tok = lax.axis_index("tok")
    grp = lax.axis_index("grp")
    tok_count = tokens.shape[1]
    rows_dev = master.shape[0]
    slots = master.shape[1]
    blocks_all = slots * n_grp
    member = tok & (UNIT - 1)
    unit = tok >> 2
    place = [2 * (t % UNIT) + t // UNIT for t in range(n_tok)]
    own_width = HEADS_OWN * HEAD

    slot_block = jnp.argsort(owners, stable=True).astype(jnp.int32)
    block_slot = jnp.argsort(slot_block, stable=True).astype(jnp.int32)

    core, bit_x = grp & 1, grp >> 1
    inputs = tokens[0]

    near, far = swap(inputs, "tok", 1), swap(inputs, "tok", 2)
    local = jnp.transpose(master.astype(BF16), (1, 0, 2))
    beside, over = swap(local, "grp", 1), swap(local, "grp", 2)

    item_starts = starts_of(lengths[0])
    unit_start = unit * UNIT * tok_count
    middle = unit_start + UNIT // 2 * tok_count
    start_of_middle = jnp.max(jnp.where(item_starts <= middle, item_starts, 0))
    is_long = (start_of_middle <= unit_start).astype(jnp.int32).reshape(1)
    share = CLUSTER // UNIT * (2 - is_long)
    placed = places(jnp.concatenate([share, member.reshape(1)]), clusters[0])
    left, right = doubled(bases[0]), doubled(bases[1])
    (over, left, right, placed) = together(over, left, right, placed)
    across = swap(over, "grp", 1)

    orders = exchange_unit(placed)
    (near, far, beside, over, across, orders) = together(near, far, beside, over, across, orders)
    part_rows = rows_dev // 2

    scalars = jnp.concatenate([block_slot, jnp.stack([grp, core, member])]).astype(jnp.int32)
    *by_owner, rest_rows = arrange(scalars, [local, beside, over, across], blocks_all)
    theirs = exchange_unit(by_owner)
    half = tok_count // 2
    third = (swap(near[:half], "tok", 2), swap(far[half:], "tok", 1))
    theirs = jnp.stack(theirs)
    theirs_far = swap(theirs, "tok", UNIT)
    mine_all = jnp.concatenate([theirs, theirs_far], axis=0)
    others_all = swap(mine_all, "grp", 1)
    sources = tok ^ jnp.arange(2 * UNIT, dtype=jnp.int32)
    cores = core ^ jnp.arange(2, dtype=jnp.int32)
    firsts = (sources[None, :] * rows_dev + cores[:, None] * part_rows).reshape(-1)
    (third, others_all, rest_rows) = together(third, others_all, rest_rows)
    own_weights = assemble(firsts, [mine_all, others_all])

    def columns_of(value, m):
        return lax.dynamic_slice_in_dim(value, m * own_width, own_width, value.ndim - 1)

    own_bias = split_heads(
        [columns_of(vectors[4], member), jnp.zeros((own_width,), F32), columns_of(vectors[5], member)]
    ).reshape(1, -1)
    ring = [(i, (i + 2) % n_tok) for i in range(n_tok)]
    depth = n_tok // 2
    steps, flips, mine_rest, other_rest = [rest_rows], [], [], []

    def advance():
        if len(steps) < depth:
            steps.append(lax.ppermute(steps[-1], "tok", ring))
        flips.append(swap(steps[len(flips)], "tok", 1))

    def cross():
        k = len(mine_rest)
        mine_rest.append(jnp.stack([steps[k], flips[k]]))
        other_rest.append(swap(mine_rest[k], "grp", 1))

    advance()
    grouped = [sort_rows(orders[0], inputs, own_weights, own_bias)]
    grouped.append(sort_rows(orders[1], near, own_weights, own_bias))
    (grouped, far, third, steps[1], flips[0]) = together(grouped, far, third, steps[1], flips[0])
    advance()
    cross()
    grouped.append(sort_rows(orders[2], far, own_weights, own_bias))
    unit_inputs = [inputs, near, far, jnp.concatenate(third, axis=0)]
    grouped.append(sort_rows(orders[3], unit_inputs[3], own_weights, own_bias))
    (grouped, steps[2], flips[1], other_rest) = together(grouped, steps[2], flips[1], other_rest)
    advance()
    cross()
    sorted_out = attend(is_long, grouped)
    (sorted_out, steps[3], flips[2], other_rest) = together(sorted_out, steps[3], flips[2], other_rest)
    advance()
    cross()
    mixed = [None] * UNIT
    mixed[3] = mix(orders[3], sorted_out[3])
    mixed[2] = mix(orders[2], sorted_out[2])
    mixed[1] = mix(orders[1], sorted_out[1])
    mixed_parts = exchange_unit(mixed)
    (mixed_parts[1:], flips[-1], other_rest, held_weights) = together(
        mixed_parts[1:], flips[-1], other_rest, own_weights
    )
    cross()
    mixed_parts[0] = mix(orders[0], sorted_out[0])
    shards = mine_rest + other_rest
    sources = (tok + n_tok - 2 * jnp.arange(depth, dtype=jnp.int32)) & (n_tok - 1)
    sources = (sources[:, None] ^ jnp.arange(2, dtype=jnp.int32)[None, :]).reshape(-1)
    firsts = (sources[None, :] * rows_dev + cores[:, None] * part_rows).reshape(-1)

    turned_weights = [swap(held_weights, "tok", k) for k in range(1, UNIT)]
    place_bits = jnp.stack([member, core, bit_x, tok & 1, (tok >> 1) & 1, tok >> 2]).astype(jnp.int32)
    table = jnp.concatenate([place_bits, firsts])
    result, grad_first, sums, kept, sent_pieces, *back = layer(
        table, shards, mixed_parts, inputs, cotangent[0], vectors
    )
    (turned_weights, kept, sent_pieces, back) = together(turned_weights, kept, sent_pieces, back)

    grad_parts = exchange_unit(back)
    other = swap(sent_pieces, "grp", 1)
    sums_of = [kept[p].astype(F32) + other[p].astype(F32) for p in range(3)]

    def halves(values):
        return [v[: v.shape[0] // 2] for v in values], [v[v.shape[0] // 2 :].astype(BF16) for v in values]

    def exchanged(sent_now, stage):
        return [swap(v, *LINKS[PART_ORDERS[p][stage]]) for p, v in enumerate(sent_now)]

    def joined(kept_now, got_now):
        return [k + g.astype(F32) for k, g in zip(kept_now, got_now)]

    kept_now, sent_now = halves(sums_of)
    (sent_now, grad_parts) = together(sent_now, grad_parts)
    got_now = exchanged(sent_now, 0)
    sorted_grads = [sort_grads(orders[k], grad_parts[k]) for k in range(UNIT)]
    sorted_back = attend_back(is_long, grouped, sorted_grads)
    kept_now, sent_now = halves(joined(kept_now, got_now))
    (sent_now, sorted_back) = together(sent_now, sorted_back)
    got_now = exchanged(sent_now, 1)
    own_grads = [None] * UNIT
    own_grads[3] = gather_grads(orders[3], sorted_back[3])
    home_grads = [None, None, None, swap(own_grads[3], "tok", 3)]
    own_grads[2] = gather_grads(orders[2], sorted_back[2])
    kept_now, sent_now = halves(joined(kept_now, got_now))
    (sent_now, own_grads[2], sorted_back) = together(sent_now, own_grads[2], sorted_back)
    got_now = exchanged(sent_now, 2)
    for k in (1, 0):
        own_grads[k] = gather_grads(orders[k], sorted_back[k])
    kept_qkv, sent_qkv, bias_qkv = qkv_back(jnp.stack([core, unit]).astype(jnp.int32), own_grads, unit_inputs)
    kept_now, sent_now = halves(joined(kept_now, got_now))
    (sent_now, sent_qkv, home_grads[3]) = together(sent_now, sent_qkv, home_grads[3])
    got_now = exchanged(sent_now, 3)

    bias_query, _, bias_value = join_heads(bias_qkv[0])
    bias_rows = lax.dynamic_update_slice_in_dim(
        jnp.zeros((2, D), F32), jnp.stack([bias_query, bias_value]), member * own_width, 1
    )
    total = sums[: 8 + FFB] + jnp.pad(bias_rows, ((4, 2 + FFB), (0, 0)))

    more = swap(total, "grp", 1)
    keep = kept_qkv.astype(F32) + swap(sent_qkv, "grp", 1).astype(F32)
    (keep, more, got_now) = together(keep, more, got_now)
    total = total + more
    more = swap(total, "grp", 2)
    unit_got = swap(keep[1].astype(BF16), "tok", UNIT)
    home_grads[1] = swap(own_grads[1], "tok", 1)
    home_grads[2] = swap(own_grads[2], "tok", 2)
    sent = pack(slot_block, kept_now, got_now, n_grp, slots)
    got = lax.all_to_all(sent, "grp", split_axis=0, concat_axis=0, tiled=True)
    keep = keep[0] + unit_got.astype(F32)
    (keep, more) = together(keep, more)
    total = total + more
    keep = (keep + swap(keep.astype(BF16), "grp", 2).astype(F32)).astype(BF16)
    kept_core = (keep, swap(keep, "grp", 1))
    keep = jnp.concatenate(
        [jnp.where(core == 0, kept_core[0], kept_core[1]), jnp.where(core == 0, kept_core[1], kept_core[0])],
        axis=-1,
    )
    mine = lax.dynamic_slice_in_dim(slot_block, grp * slots, slots, 0)

    def to_tok(value):
        return lax.all_to_all(value, "tok", split_axis=0, concat_axis=0, tiled=True)

    part = to_tok(rotate_in(mine, keep, got, left, n_tok))
    grad_inputs = grad_first + outer_cols(own_grads[0], own_weights)
    (part, home_grads, grad_inputs) = together(part, home_grads[1:], grad_inputs)
    more = swap(total, "tok", 1)
    by_slot_of = lambda value: jnp.transpose(value, (1, 0, 2))
    new_one, new_two, turned = moments(
        place, part, right, by_slot_of(moment_one), by_slot_of(moment_two)
    )
    turned = to_tok(turned)
    grad_inputs = grad_inputs + outer_cols(home_grads[0], turned_weights[0])
    grad_inputs = grad_inputs + outer_cols(home_grads[1], turned_weights[1])
    (turned, more, grad_inputs, home_grads[2]) = together(turned, more, grad_inputs, home_grads[2])
    total = total + more
    total = total + swap(total, "tok", 2)
    change = to_tok(rotate_out(turned, left))
    vector_total = total + swap(total, "tok", 4)
    new_master = by_slot_of(apply_change(place, change, by_slot_of(master)))
    new_one, new_two = by_slot_of(new_one), by_slot_of(new_two)
    grad_inputs = grad_inputs + outer_cols(home_grads[2], turned_weights[2])
    new_vec_one = BETA_ONE * vector_one + (1.0 - BETA_ONE) * vector_total
    new_vec_two = BETA_TWO * vector_two + (1.0 - BETA_TWO) * vector_total * vector_total
    new_vectors = vectors - RATE_VECTOR * new_vec_one / (jnp.sqrt(new_vec_two) + ADAM_EPS)
    return (
        result[None],
        grad_inputs[None],
        new_one,
        new_two,
        new_master,
        new_vec_one,
        new_vec_two,
        new_vectors,
    )


def general(
    tokens,
    cotangent,
    lengths,
    clusters,
    owners,
    master,
    bases,
    moment_one,
    moment_two,
    vectors,
    vector_one,
    vector_two,
):
    n_tok = lax.axis_size("tok")
    tok_count = tokens.shape[1]
    rows_dev = master.shape[0]
    slot_block = jnp.argsort(owners, stable=True)
    block_slot = jnp.argsort(slot_block, stable=True)
    slot_part = lax.all_gather(master.astype(jnp.bfloat16), "grp", axis=1, tiled=True)
    weights = lax.all_gather(slot_part, "tok", axis=0, tiled=True)
    blocks = jnp.stack([pick(jnp.transpose(weights, (1, 0, 2)), block_slot[b]) for b in range(weights.shape[1])], axis=1)
    w_qkv = blocks[:, 0:3, :].reshape(D, 3 * D)
    w_out = blocks[:, 3, :]
    w_up = blocks[:, 4 : 4 + FF // D, :].reshape(D, FF)
    w_down = jnp.transpose(blocks[:, 4 + FF // D :, :], (1, 0, 2)).reshape(FF, D)
    inputs = tokens[0]
    gain_one = vectors[0]
    shift_one = vectors[1]
    gain_two = vectors[2]
    shift_two = vectors[3]
    bias_qkv = jnp.concatenate([vectors[4], jnp.zeros((D,), jnp.float32), vectors[5]])
    qkv = (jnp.dot(inputs, w_qkv, preferred_element_type=jnp.float32) + bias_qkv).astype(
        jnp.bfloat16
    )
    heads = jnp.transpose(qkv.reshape(tok_count, 3, H, HEAD), (2, 0, 1, 3)).reshape(
        H, tok_count, 3 * HEAD
    )
    pair_rows = jnp.broadcast_to(heads[None], (ROUNDS, H, tok_count, 3 * HEAD)).reshape(
        PAIRS * tok_count, 3 * HEAD
    )
    position = lax.axis_index("tok") * tok_count + jnp.arange(tok_count, dtype=jnp.int32)
    item_starts = starts_of(lengths[0])
    item_start = jnp.max(
        jnp.where(item_starts[None, :] <= position[:, None], item_starts[None, :], 0), axis=1
    )
    per_dev = tok_count // CLUSTER
    group_clusters = n_tok * per_dev
    pair_ids = jnp.arange(PAIRS, dtype=jnp.int32)[:, None]
    global_cluster = item_start[None, :] // CLUSTER + clusters[0]
    unit_ids = (pair_ids * group_clusters + global_cluster).reshape(-1)
    owner_ids = ((global_cluster + pair_ids * per_dev) % n_tok).reshape(-1)
    send_order = jnp.argsort(owner_ids * (PAIRS * group_clusters) + unit_ids, stable=True)
    restore = jnp.argsort(send_order, stable=True)
    slot_rows = PAIRS * tok_count // n_tok
    units_here = PAIRS * tok_count // CLUSTER
    sent_rows = pair_rows[send_order].reshape(n_tok, slot_rows // 2, 6 * HEAD)
    sent_units = unit_ids[send_order].reshape(n_tok, slot_rows)
    got_rows, got_units = (
        lax.all_to_all(sent_rows, "tok", split_axis=0, concat_axis=0, tiled=True),
        lax.all_to_all(sent_units, "tok", split_axis=0, concat_axis=0, tiled=True),
    )
    arrange = jnp.argsort(got_units.reshape(-1), stable=True)
    undo = jnp.argsort(arrange, stable=True)
    grouped = got_rows.reshape(PAIRS * tok_count, 3 * HEAD)[arrange].reshape(
        units_here, CLUSTER, 3 * HEAD
    )
    query_rows = grouped[..., :HEAD]
    key_rows = grouped[..., HEAD : 2 * HEAD]
    value_rows = grouped[..., 2 * HEAD :]
    score_scale = HEAD ** (-0.5)
    scores = (
        jnp.einsum("ucd,ued->uce", query_rows, key_rows, preferred_element_type=jnp.float32)
        * score_scale
    )
    row_max = jnp.max(scores, axis=-1, keepdims=True)
    row_total = jnp.sum(jnp.exp(scores - row_max), axis=-1, keepdims=True)
    log_total = row_max + jnp.log(row_total)
    probs = jnp.exp(scores - log_total)
    cluster_out = jnp.einsum(
        "uce,ued->ucd", probs.astype(jnp.bfloat16), value_rows, preferred_element_type=jnp.float32
    ).astype(jnp.bfloat16)
    back_rows = cluster_out.reshape(PAIRS * tok_count, HEAD)[undo].reshape(
        n_tok, slot_rows // 2, 2 * HEAD
    )
    home_rows = lax.all_to_all(back_rows, "tok", split_axis=0, concat_axis=0, tiled=True)
    home_rows = (
        home_rows.reshape(PAIRS * tok_count, HEAD)[restore]
        .reshape(ROUNDS, H, tok_count, HEAD)
        .astype(jnp.float32)
    )
    mixed_heads = 0.5 * (home_rows[0] + home_rows[1])
    mixed_low = jnp.transpose(mixed_heads, (1, 0, 2)).reshape(tok_count, D).astype(jnp.bfloat16)
    attention = jnp.dot(mixed_low, w_out, preferred_element_type=jnp.float32) + vectors[6]
    first_sum = inputs.astype(jnp.float32) + attention
    normed_one, rstd_one = normalize(first_sum)
    hidden = normed_one * gain_one + shift_one
    hidden_low = hidden.astype(jnp.bfloat16)
    up_proj = jnp.dot(hidden_low, w_up, preferred_element_type=jnp.float32) + vectors[8:].reshape(
        FF
    )
    act_low = jax.nn.gelu(up_proj, approximate=False).astype(jnp.bfloat16)
    down_proj = jnp.dot(act_low, w_down, preferred_element_type=jnp.float32) + vectors[7]
    second_sum = hidden + down_proj
    normed_two, rstd_two = normalize(second_sum)
    result = (normed_two * gain_two + shift_two).astype(jnp.bfloat16)
    grad_result = cotangent[0].astype(jnp.float32)
    grad_gain_two = jnp.sum(grad_result * normed_two, axis=0)
    grad_shift_two = jnp.sum(grad_result, axis=0)
    grad_second = norm_back(grad_result * gain_two, normed_two, rstd_two)
    grad_down_low = grad_second.astype(jnp.bfloat16)
    grad_w_down = inner_rows(act_low, grad_down_low)
    grad_bias_down = jnp.sum(grad_down_low.astype(jnp.float32), axis=0)
    grad_act = outer_cols(grad_down_low, w_down)
    grad_up_low = (grad_act * gelu_slope(up_proj)).astype(jnp.bfloat16)
    grad_w_up = inner_rows(hidden_low, grad_up_low)
    grad_bias_up = jnp.sum(grad_up_low.astype(jnp.float32), axis=0)
    grad_hidden = grad_second + outer_cols(grad_up_low, w_up)
    grad_gain_one = jnp.sum(grad_hidden * normed_one, axis=0)
    grad_shift_one = jnp.sum(grad_hidden, axis=0)
    grad_first = norm_back(grad_hidden * gain_one, normed_one, rstd_one)
    grad_attn_low = grad_first.astype(jnp.bfloat16)
    grad_w_out = inner_rows(mixed_low, grad_attn_low)
    grad_bias_out = jnp.sum(grad_attn_low.astype(jnp.float32), axis=0)
    grad_mixed = outer_cols(grad_attn_low, w_out)
    grad_heads = jnp.transpose((0.5 * grad_mixed).reshape(tok_count, H, HEAD), (1, 0, 2)).astype(
        jnp.bfloat16
    )
    grad_pairs = jnp.broadcast_to(grad_heads[None], (ROUNDS, H, tok_count, HEAD)).reshape(
        PAIRS * tok_count, HEAD
    )
    sent_grad = grad_pairs[send_order].reshape(n_tok, slot_rows // 2, 2 * HEAD)
    got_grad = lax.all_to_all(sent_grad, "tok", split_axis=0, concat_axis=0, tiled=True)
    grad_cluster = got_grad.reshape(PAIRS * tok_count, HEAD)[arrange].reshape(
        units_here, CLUSTER, HEAD
    )
    scores_again = (
        jnp.einsum("ucd,ued->uce", query_rows, key_rows, preferred_element_type=jnp.float32)
        * score_scale
    )
    probs_again = jnp.exp(scores_again - log_total)
    probs_low = probs_again.astype(jnp.bfloat16)
    grad_values = jnp.einsum(
        "uce,ucd->ued", probs_low, grad_cluster, preferred_element_type=jnp.float32
    )
    grad_probs = jnp.einsum(
        "ucd,ued->uce", grad_cluster, value_rows, preferred_element_type=jnp.float32
    )
    centre = jnp.sum(probs_again * grad_probs, axis=-1, keepdims=True)
    grad_scores = (probs_again * (grad_probs - centre)).astype(jnp.bfloat16)
    grad_query = (
        jnp.einsum("uce,ued->ucd", grad_scores, key_rows, preferred_element_type=jnp.float32)
        * score_scale
    )
    grad_keys = (
        jnp.einsum("uce,ucd->ued", grad_scores, query_rows, preferred_element_type=jnp.float32)
        * score_scale
    )
    grad_grouped = jnp.concatenate(
        [
            grad_query.astype(jnp.bfloat16),
            grad_keys.astype(jnp.bfloat16),
            grad_values.astype(jnp.bfloat16),
        ],
        axis=-1,
    )
    back_grad = grad_grouped.reshape(PAIRS * tok_count, 3 * HEAD)[undo].reshape(
        n_tok, slot_rows // 2, 6 * HEAD
    )
    home_grad = lax.all_to_all(back_grad, "tok", split_axis=0, concat_axis=0, tiled=True)
    home_grad = (
        home_grad.reshape(PAIRS * tok_count, 3 * HEAD)[restore]
        .reshape(ROUNDS, H, tok_count, 3, HEAD)
        .astype(jnp.float32)
    )
    grad_qkv = (home_grad[0] + home_grad[1]).astype(jnp.bfloat16)
    grad_qkv = jnp.transpose(grad_qkv, (1, 2, 0, 3)).reshape(tok_count, 3 * D)
    grad_w_qkv = inner_rows(inputs, grad_qkv)
    grad_bias_qkv = jnp.sum(grad_qkv.astype(jnp.float32), axis=0)
    grad_inputs = grad_first + outer_cols(grad_qkv, w_qkv)
    grad_blocks = jnp.concatenate(
        [
            grad_w_qkv.reshape(D, 3, D),
            grad_w_out[:, None, :],
            grad_w_up.reshape(D, FF // D, D),
            jnp.transpose(grad_w_down.reshape(FF // D, D, D), (1, 0, 2)),
        ],
        axis=1,
    )
    by_block = jnp.transpose(grad_blocks, (1, 0, 2))
    slot_grads = jnp.stack([pick(by_block, slot_block[s]) for s in range(by_block.shape[0])], axis=1)
    vector_grads = jnp.concatenate(
        [
            jnp.stack(
                [
                    grad_gain_one,
                    grad_shift_one,
                    grad_gain_two,
                    grad_shift_two,
                    grad_bias_qkv[:D],
                    grad_bias_qkv[2 * D :],
                    grad_bias_out,
                    grad_bias_down,
                ]
            ),
            grad_bias_up.reshape(FF // D, D),
        ],
        axis=0,
    )
    vector_total = lax.psum(vector_grads, ("tok", "grp"))
    row_total = lax.psum_scatter(slot_grads, "tok", scatter_dimension=0, tiled=True)
    reduced = lax.psum_scatter(
        row_total.astype(jnp.bfloat16), "grp", scatter_dimension=1, tiled=True
    ).astype(jnp.float32)
    left_basis = bases[0]
    right_basis = bases[1]
    first_row = lax.axis_index("tok") * rows_dev
    turned_in = jnp.einsum("rse,sef->rsf", reduced, right_basis, precision=lax.Precision.HIGHEST)
    left_rows = lax.dynamic_slice_in_dim(left_basis, first_row, rows_dev, 1)
    picked = left_rows
    rotated = lax.psum_scatter(
        jnp.einsum("sri,rsf->isf", picked, turned_in, precision=lax.Precision.HIGHEST),
        "tok",
        scatter_dimension=0,
        tiled=True,
    )
    new_one = BETA_ONE * moment_one + (1.0 - BETA_ONE) * rotated
    new_two = BETA_TWO * moment_two + (1.0 - BETA_TWO) * rotated * rotated
    direction = new_one / (jnp.sqrt(new_two) + ADAM_EPS)
    turned_out = jnp.einsum("rse,sfe->rsf", direction, right_basis, precision=lax.Precision.HIGHEST)
    left_cols = lax.dynamic_slice_in_dim(left_basis, first_row, rows_dev, 2)
    picked = left_cols
    change = lax.psum_scatter(
        jnp.einsum("sir,rsf->isf", picked, turned_out, precision=lax.Precision.HIGHEST),
        "tok",
        scatter_dimension=0,
        tiled=True,
    )
    new_master = master - RATE_MATRIX * change
    new_vec_one = BETA_ONE * vector_one + (1.0 - BETA_ONE) * vector_total
    new_vec_two = BETA_TWO * vector_two + (1.0 - BETA_TWO) * vector_total * vector_total
    new_vectors = vectors - RATE_VECTOR * new_vec_one / (jnp.sqrt(new_vec_two) + ADAM_EPS)
    return (
        result[None],
        grad_inputs[None],
        new_one,
        new_two,
        new_master,
        new_vec_one,
        new_vec_two,
        new_vectors,
    )

def solution(mesh):
    n_tok, n_grp = mesh.shape["tok"], mesh.shape["grp"]

    def on_device(*args):
        lengths, clusters = args[2], args[3]
        unit = n_tok // (lengths.shape[1] - 1)
        suits = unit == UNIT and n_tok == 2 * UNIT and n_grp == 4 and clusters.shape[2] == 1024
        return (fast if suits else general)(*args)

    return jax.shard_map(
        on_device,
        mesh=mesh,
        in_specs=(
            P("grp", "tok", None),
            P("grp", "tok", None),
            P("grp", None),
            P("grp", None, "tok"),
            P(),
            P("tok", "grp", None),
            P(None, "grp", None, None),
            P("tok", "grp", None),
            P("tok", "grp", None),
            P(),
            P(),
            P(),
        ),
        out_specs=(
            P("grp", "tok", None),
            P("grp", "tok", None),
            P("tok", "grp", None),
            P("tok", "grp", None),
            P("tok", "grp", None),
            P(),
            P(),
            P(),
        ),
        check_vma=False,
    )
```

```python
import functools

import jax
import jax.numpy as jnp
from jax import lax
from jax.experimental import pallas as pl
from jax.experimental.pallas import tpu as pltpu
from jax.sharding import PartitionSpec as P

D = 768
H = 12
FF = 3072
HEAD = 64
ROUNDS = 2
PAIRS = 24
CLUSTER = 128
FFB = FF // D

EPS_NORM = 1e-05
ADAM_EPS = 1e-08
BETA_ONE = 0.5
BETA_TWO = 0.5
RATE_MATRIX = 0.025
RATE_VECTOR = 0.15
SQRT_HALF = 0.7071067811865476
INV_ROOT_TWO_PI = 0.3989422804014327

BF16 = jnp.bfloat16
F32 = jnp.float32

UNIT = 4
HEADS_OWN = H // UNIT
LOCAL_PAIRS = ROUNDS * HEADS_OWN
TILE = 128
WIDE = 2 * TILE
SMALL = pl.CostEstimate(flops=0, transcendentals=0, bytes_accessed=0)


def inner_rows(left, right):
    return lax.dot_general(left, right, (((0,), (0,)), ((), ())), preferred_element_type=F32)


def outer_cols(left, right):
    return lax.dot_general(left, right, (((1,), (1,)), ((), ())), preferred_element_type=F32)


def normalize(values_in):
    centre = jnp.mean(values_in, axis=-1, keepdims=True)
    offset = values_in - centre
    spread = jnp.mean(offset * offset, axis=-1, keepdims=True)
    rstd = lax.rsqrt(spread + EPS_NORM)
    return (offset * rstd, rstd)


def norm_back(grad_normed, normed, rstd):
    first_mean = jnp.mean(grad_normed, axis=-1, keepdims=True)
    second_mean = jnp.mean(grad_normed * normed, axis=-1, keepdims=True)
    return rstd * (grad_normed - first_mean - normed * second_mean)


def gelu_slope(values_in):
    return (
        0.5 * (1.0 + lax.erf(values_in * SQRT_HALF))
        + values_in * jnp.exp(-0.5 * values_in * values_in) * INV_ROOT_TWO_PI
    )


def turn_half(value):
    return pltpu.roll(value, HEAD, 1)


def places_body(scalars_ref, clusters_ref, *refs):
    outs, all_ref = refs[:UNIT], refs[UNIT]
    pairs, count = clusters_ref.shape
    share, member = scalars_ref[0], scalars_ref[1]
    kinds = UNIT * count // CLUSTER
    kind = lax.broadcasted_iota(jnp.int32, (kinds, count), 0)
    earlier = lax.broadcasted_iota(jnp.int32, (count, count), 0) < lax.broadcasted_iota(jnp.int32, (count, count), 1)
    earlier = earlier.astype(F32).astype(BF16)
    all_ref[...] = jnp.zeros_like(all_ref)
    for pair in range(pairs):
        turn, head = pair // H, pair % H
        cluster = clusters_ref[pair : pair + 1, :]
        same = (kind == cluster).astype(F32)
        before = jnp.dot(same.astype(BF16), earlier, preferred_element_type=F32)
        rank = jnp.sum(same * before, axis=0, keepdims=True).astype(jnp.int32)
        own = head % HEADS_OWN * ROUNDS + turn
        all_ref[head // HEADS_OWN, own : own + 1, :] = cluster * share + rank
    for k in range(UNIT):
        outs[k][...] = all_ref[member ^ k]


def places(scalars, clusters):
    count = clusters.shape[1]
    inside = pl.BlockSpec(memory_space=pltpu.VMEM)
    return pl.pallas_call(
        places_body,
        in_specs=[pl.BlockSpec(memory_space=pltpu.SMEM), inside],
        out_specs=[inside] * UNIT,
        out_shape=[jax.ShapeDtypeStruct((8, count), jnp.int32)] * UNIT,
        scratch_shapes=[pltpu.VMEM((UNIT, 8, count), jnp.int32)],
        cost_estimate=SMALL,
        name="places",
    )(scalars, clusters)


def arrange_body(slots, scalars_ref, *refs):
    sources, outs, rest_ref, tiles_ref = refs[:4], refs[4 : 4 + UNIT], refs[4 + UNIT], refs[5 + UNIT]
    n_rest, count = rest_ref.shape[:2]
    n_blocks = n_rest + 3
    group, core, member = (scalars_ref[n_blocks + i] for i in range(3))
    first = pl.multiple_of(core * count, count)

    def rows_of(block):
        slot = scalars_ref[block]
        owner = lax.div(slot, slots)
        near, inner = owner ^ group, lax.rem(slot, slots)
        found = [source[inner, pl.ds(first, count), :].astype(F32) for source in sources]
        low = jnp.where(near % 2 == 0, found[0], found[1])
        high = jnp.where(near % 2 == 0, found[2], found[3])
        return jnp.where(near < 2, low, high)

    low = lax.broadcasted_iota(jnp.int32, (count, TILE), 1) < HEAD
    parts = [rows_of(i) for i in range(3)]

    def half(part, head, high):
        at = head // 2 * TILE
        tile = parts[part][:, at : at + TILE]
        return tile if head % 2 == high else turn_half(tile)

    for head in range(H):
        own = head % HEADS_OWN
        odd = own % 2
        value = half(2, head, odd)
        query = half(0, head, 1 - odd)
        keys = half(1, head, 1 - odd)
        one = jnp.where(low, query, value) if odd else jnp.where(low, value, query)
        two = jnp.where(low, keys, 0.0) if odd else jnp.where(low, 0.0, keys)
        tiles_ref[head // HEADS_OWN, :, own * WIDE : own * WIDE + TILE] = one.astype(BF16)
        tiles_ref[head // HEADS_OWN, :, own * WIDE + TILE : (own + 1) * WIDE] = two.astype(BF16)
    for k in range(UNIT):
        outs[k][...] = tiles_ref[member ^ k]
    for b in range(n_rest):
        rest_ref[b] = rows_of(3 + b).astype(BF16)


def arrange(scalars, sources, n_blocks):
    slots, rows = sources[0].shape[:2]
    count = rows // 2
    width = HEADS_OWN * WIDE
    inside = pl.BlockSpec(memory_space=pltpu.VMEM)
    return pl.pallas_call(
        functools.partial(arrange_body, slots),
        in_specs=[pl.BlockSpec(memory_space=pltpu.SMEM)] + [inside] * 4,
        out_specs=[inside] * (UNIT + 1),
        out_shape=[jax.ShapeDtypeStruct((count, width), BF16)] * UNIT
        + [jax.ShapeDtypeStruct((n_blocks - 3, count, D), BF16)],
        scratch_shapes=[pltpu.VMEM((UNIT, count, width), BF16)],
        compiler_params=pltpu.CompilerParams(vmem_limit_bytes=32 << 20),
        cost_estimate=SMALL,
        name="arrange",
    )(scalars, *sources)


def assemble_body(table_ref, *refs):
    shards, out_ref, sem = refs[:-2], refs[-2], refs[-1]
    rows = shards[0].shape[1]
    copies = []
    for shard in shards:
        for i in range(shard.shape[0]):
            n = len(copies)
            first = pl.multiple_of(table_ref[n], rows)
            copies.append(
                pltpu.make_async_copy(shard.at[i], out_ref.at[pl.ds(first, rows), :], sem.at[n])
            )
    for copy in copies:
        copy.start()
    for copy in copies:
        copy.wait()


def assemble(table, shards):
    pieces = sum(s.shape[0] for s in shards)
    anywhere = pl.BlockSpec(memory_space=pl.ANY)
    return pl.pallas_call(
        assemble_body,
        in_specs=[pl.BlockSpec(memory_space=pltpu.SMEM)] + [anywhere] * len(shards),
        out_specs=pl.BlockSpec(memory_space=pltpu.VMEM),
        out_shape=jax.ShapeDtypeStruct((pieces * shards[0].shape[1], shards[0].shape[2]), BF16),
        scratch_shapes=[pltpu.SemaphoreType.DMA((pieces,))],
        cost_estimate=SMALL,
        name="assemble",
    )(table, *shards)


def sort_body(place_ref, x_ref, weight_ref, bias_ref, out_ref, rows_ref):
    count = x_ref.shape[0]
    head = pl.program_id(0)
    chunk = 256
    row = lax.broadcasted_iota(jnp.int32, (chunk, count), 0)
    rows_ref[...] = (
        jnp.dot(x_ref[...], weight_ref[...], preferred_element_type=F32) + bias_ref[...]
    ).astype(BF16)
    for step in range(HEADS_OWN):

        @pl.when(head == step)
        def _():
            for turn in range(ROUNDS):
                pair = step * ROUNDS + turn
                for part in range(count // chunk):
                    where = pl.ds(part * chunk, chunk)
                    picked = place_ref[pair : pair + 1, :] == row + part * chunk
                    picked = picked.astype(F32).astype(BF16)
                    out_ref[turn, where, :] = jnp.dot(
                        picked, rows_ref[...], preferred_element_type=F32
                    ).astype(BF16)


def sort_rows(order, inputs, weights, bias):
    count = inputs.shape[0]
    return pl.pallas_call(
        sort_body,
        grid=(HEADS_OWN,),
        in_specs=[
            pl.BlockSpec((8, count), lambda h: (0, 0)),
            pl.BlockSpec((count, D), lambda h: (0, 0)),
            pl.BlockSpec((D, WIDE), lambda h: (0, h)),
            pl.BlockSpec((1, WIDE), lambda h: (0, h)),
        ],
        out_specs=pl.BlockSpec((ROUNDS, count, WIDE), lambda h: (h, 0, 0)),
        out_shape=jax.ShapeDtypeStruct((LOCAL_PAIRS, count, WIDE), BF16),
        scratch_shapes=[pltpu.VMEM((count, WIDE), BF16)],
        compiler_params=pltpu.CompilerParams(vmem_limit_bytes=48 << 20),
        cost_estimate=SMALL,
        name="sort_rows",
    )(order, inputs, weights, bias)


def sort_grads_body(place_ref, rows_ref, out_ref):
    count = place_ref.shape[1]
    half = count // 2
    head = pl.program_id(0)
    chunk = 256
    row = lax.broadcasted_iota(jnp.int32, (chunk, count), 0)
    low = lax.broadcasted_iota(jnp.int32, (count, TILE), 1) < HEAD
    for step in range(HEADS_OWN):

        @pl.when(head == step)
        def _():
            if step < 2:
                tile = rows_ref[0:count, :].astype(F32)
                tile = jnp.where(low if step == 0 else jnp.logical_not(low), tile, 0.0).astype(BF16)
            else:
                both = rows_ref[count : count + half, :].astype(F32)
                tile = jnp.concatenate([both, turn_half(both)], axis=0)
                tile = jnp.where(low, tile, 0.0).astype(BF16)
            for turn in range(ROUNDS):
                pair = step * ROUNDS + turn
                for part in range(count // chunk):
                    where = pl.ds(part * chunk, chunk)
                    picked = place_ref[pair : pair + 1, :] == row + part * chunk
                    picked = picked.astype(F32).astype(BF16)
                    out_ref[turn, where, :] = jnp.dot(
                        picked, tile, preferred_element_type=F32
                    ).astype(BF16)


def sort_grads(order, rows):
    count = order.shape[1]
    return pl.pallas_call(
        sort_grads_body,
        grid=(HEADS_OWN,),
        in_specs=[
            pl.BlockSpec((8, count), lambda h: (0, 0)),
            pl.BlockSpec(rows.shape, lambda h: (0, 0)),
        ],
        out_specs=pl.BlockSpec((ROUNDS, count, TILE), lambda h: (h, 0, 0)),
        out_shape=jax.ShapeDtypeStruct((LOCAL_PAIRS, count, TILE), BF16),
        compiler_params=pltpu.CompilerParams(vmem_limit_bytes=48 << 20),
        cost_estimate=SMALL,
        name="sort_grads",
    )(order, rows)


def plans_of(count):
    share = CLUSTER // UNIT
    half = UNIT // 2
    return (
        [(tuple(range(UNIT)), share)],
        [(tuple(range(i * half, (i + 1) * half)), 2 * share) for i in range(2)],
    )


def for_each_batch(is_long, count, batch, work):
    for wanted, plan in zip((1, 0), plans_of(count)):

        @pl.when(is_long == wanted)
        def _(plan=plan):
            for runs, share in plan:

                def step(group, carry, runs=runs, share=share):
                    first = pl.multiple_of(group * (batch * share), batch * share)
                    work(runs, pl.ds(first, batch * share), share)
                    return carry

                lax.fori_loop(0, count // share // batch, step, 0)


def batch_of(refs, runs, where, share, width):
    parts = [refs[r][0, where, :] for r in runs]
    return jnp.concatenate([p.reshape(p.shape[0] // share, share, width) for p in parts], axis=1)


def spread(refs, runs, where, share, columns, value):
    for i, r in enumerate(runs):
        part = value[:, i * share : (i + 1) * share]
        refs[r][0, where, columns] = part.reshape(part.shape[0] * share, TILE)


def products(form, left, right):
    return jnp.einsum(form, left, right, preferred_element_type=F32)


def softmax(first, second):
    scores = products("ued,ucd->uec", second, first) * (HEAD**-0.5)
    expo = jnp.exp(scores - jnp.max(scores, axis=1, keepdims=True))
    return expo * (1.0 / jnp.sum(expo, axis=1, keepdims=True))


def attend_body(long_ref, *refs):
    grouped, results = refs[:UNIT], refs[UNIT:]

    def work(runs, where, share):
        rows = batch_of(grouped, runs, where, share, WIDE)
        first = rows[..., :TILE]
        probs = softmax(first, rows[..., TILE:]).astype(BF16)
        mixed = products("uce,ued->ucd", jnp.swapaxes(probs, 1, 2), first).astype(BF16)
        spread(results, runs, where, share, slice(0, TILE), mixed)

    for_each_batch(long_ref[0], grouped[0].shape[1], 8, work)


def attend(is_long, grouped):
    count = grouped[0].shape[1]
    return pl.pallas_call(
        attend_body,
        grid_spec=pltpu.PrefetchScalarGridSpec(
            num_scalar_prefetch=1,
            grid=(LOCAL_PAIRS,),
            in_specs=[pl.BlockSpec((1, count, WIDE), lambda p, _: (p, 0, 0))] * UNIT,
            out_specs=[pl.BlockSpec((1, count, TILE), lambda p, _: (p, 0, 0))] * UNIT,
        ),
        out_shape=[jax.ShapeDtypeStruct((LOCAL_PAIRS, count, TILE), BF16)] * UNIT,
        compiler_params=pltpu.CompilerParams(vmem_limit_bytes=48 << 20),
        cost_estimate=SMALL,
        name="attend",
    )(is_long, *grouped)


def attend_back_body(long_ref, *refs):
    grouped, grads, results = refs[:UNIT], refs[UNIT : 2 * UNIT], refs[2 * UNIT :]
    batch = 16
    odd = (pl.program_id(0) // ROUNDS) % 2
    lane = lax.broadcasted_iota(jnp.int32, (batch, CLUSTER, TILE), 2)
    value_lane = (lane < HEAD) == (odd == 0)
    scale = HEAD**-0.5

    def work(runs, where, share):
        rows = batch_of(grouped, runs, where, share, WIDE)
        grad = batch_of(grads, runs, where, share, TILE)
        first, second = rows[..., :TILE], rows[..., TILE:]
        probs = softmax(first, second)
        grad_probs = products("ued,ucd->uec", first, grad)
        centre = jnp.sum(probs * grad_probs, axis=1, keepdims=True)
        grad_scores = (probs * (grad_probs - centre)).astype(BF16)
        grad_values = products("uec,ucd->ued", probs.astype(BF16), grad)
        grad_keys = products("uec,ucd->ued", grad_scores, first) * scale
        grad_query = products("uce,ued->ucd", jnp.swapaxes(grad_scores, 1, 2), second) * scale
        tile_one = jnp.where(value_lane, grad_values, grad_query).astype(BF16)
        tile_two = jnp.where(value_lane, 0.0, grad_keys).astype(BF16)
        spread(results, runs, where, share, slice(0, TILE), tile_one)
        spread(results, runs, where, share, slice(TILE, WIDE), tile_two)

    for_each_batch(long_ref[0], grouped[0].shape[1], batch, work)


def attend_back(is_long, grouped, grads):
    count = grouped[0].shape[1]
    return pl.pallas_call(
        attend_back_body,
        grid_spec=pltpu.PrefetchScalarGridSpec(
            num_scalar_prefetch=1,
            grid=(LOCAL_PAIRS,),
            in_specs=[pl.BlockSpec((1, count, WIDE), lambda p, _: (p, 0, 0))] * UNIT
            + [pl.BlockSpec((1, count, TILE), lambda p, _: (p, 0, 0))] * UNIT,
            out_specs=[pl.BlockSpec((1, count, WIDE), lambda p, _: (p, 0, 0))] * UNIT,
        ),
        out_shape=[jax.ShapeDtypeStruct((LOCAL_PAIRS, count, WIDE), BF16)] * UNIT,
        compiler_params=pltpu.CompilerParams(vmem_limit_bytes=56 << 20),
        cost_estimate=SMALL,
        name="attend_back",
    )(is_long, *grouped, *grads)


def unsorted(column_ref, step, rows_ref, part, chunk):
    count = rows_ref.shape[1]
    where = pl.ds(part * chunk, chunk)
    lane = lax.broadcasted_iota(jnp.int32, (chunk, count), 1)
    total = None
    for turn in range(ROUNDS):
        pair = step * ROUNDS + turn
        picked = (column_ref[where, pair : pair + 1] == lane).astype(F32).astype(BF16)
        more = jnp.dot(picked, rows_ref[turn], preferred_element_type=F32)
        total = more if total is None else total + more
    return total


def mix_body(place_ref, rows_ref, out_ref, column_ref):
    @pl.when(pl.program_id(0) == 0)
    def _():
        column_ref[...] = jnp.transpose(place_ref[...])

    count = rows_ref.shape[1]
    chunk = 256
    parts = count // chunk
    low = lax.broadcasted_iota(jnp.int32, (chunk, TILE), 1) < HEAD
    head = pl.program_id(0)
    for step in range(HEADS_OWN):

        @pl.when(head == step)
        def _():
            means = [0.5 * unsorted(column_ref, step, rows_ref, part, chunk) for part in range(parts)]
            for part in range(parts):
                where = pl.ds(part * chunk, chunk)
                if step == 0:
                    out_ref[where, :] = means[part].astype(BF16)
                elif step == 1:
                    out_ref[where, :] = jnp.where(low, out_ref[where, :].astype(F32), means[part]).astype(BF16)
                elif part < parts // 2:
                    both = jnp.where(low, means[part], turn_half(means[part + parts // 2]))
                    out_ref[pl.ds(count + part * chunk, chunk), :] = both.astype(BF16)


def mix(order, rows):
    count = rows.shape[1]
    packed = (count + count // 2, TILE)
    return pl.pallas_call(
        mix_body,
        grid=(HEADS_OWN,),
        in_specs=[
            pl.BlockSpec((8, count), lambda h: (0, 0)),
            pl.BlockSpec((ROUNDS, count, TILE), lambda h: (h, 0, 0)),
        ],
        out_specs=pl.BlockSpec(packed, lambda h: (0, 0)),
        out_shape=jax.ShapeDtypeStruct(packed, BF16),
        scratch_shapes=[pltpu.VMEM((count, 8), jnp.int32)],
        compiler_params=pltpu.CompilerParams(vmem_limit_bytes=48 << 20),
        cost_estimate=SMALL,
        name="mix",
    )(order, rows)


def gather_grads_body(place_ref, rows_ref, out_ref, column_ref):
    @pl.when(pl.program_id(0) == 0)
    def _():
        column_ref[...] = jnp.transpose(place_ref[...])

    count = rows_ref.shape[1]
    chunk = 256
    head = pl.program_id(0)
    for step in range(HEADS_OWN):

        @pl.when(head == step)
        def _():
            for part in range(count // chunk):
                where = pl.ds(part * chunk, chunk)
                out_ref[where, :] = unsorted(column_ref, step, rows_ref, part, chunk).astype(BF16)


def gather_grads(order, rows):
    count = rows.shape[1]
    return pl.pallas_call(
        gather_grads_body,
        grid=(HEADS_OWN,),
        in_specs=[
            pl.BlockSpec((8, count), lambda h: (0, 0)),
            pl.BlockSpec((ROUNDS, count, WIDE), lambda h: (h, 0, 0)),
        ],
        out_specs=pl.BlockSpec((count, WIDE), lambda h: (0, h)),
        out_shape=jax.ShapeDtypeStruct((count, HEADS_OWN * WIDE), BF16),
        scratch_shapes=[pltpu.VMEM((count, 8), jnp.int32)],
        compiler_params=pltpu.CompilerParams(vmem_limit_bytes=48 << 20),
        cost_estimate=SMALL,
        name="gather_grads",
    )(order, rows)


ERF_TOP = (0.00022905065861350646, 0.0034082910107109506, 0.050955695062380861, 0.18520832239976145, 1.128379143519084)
ERF_BOTTOM = (
    -1.1791602954361697e-7,
    0.000023547966471313185,
    0.0010179625278914885,
    0.014070470171167667,
    0.11098505178285362,
    0.49746925110067538,
    1.0,
)


def polynomial(value, factors):
    total = jnp.full_like(value, factors[0])
    for factor in factors[1:]:
        total = total * value + factor
    return total


def error_function(value):
    value = jnp.clip(value, -3.832506856900711, 3.832506856900711)
    square = value * value
    return value * polynomial(square, ERF_TOP) / polynomial(square, ERF_BOTTOM)


VEC_ROWS = 16
FFN_TILE = 256


def layer_body(
    n_shards,
    table_ref,
    *refs,
):
    shards, refs = refs[:n_shards], refs[n_shards:]
    parts, refs = refs[:UNIT], refs[UNIT:]
    x_ref, cot_ref, vec_ref, result_ref, first_ref, sums_ref, kept_ref, sent_ref = refs[:8]
    backs, refs = refs[8 : 8 + UNIT], refs[8 + UNIT :]
    w_ref, packed_ref, mixed_ref, hidden_ref, act_ref, down_ref, up_ref, attn_ref, back_ref = refs[:9]
    slope_ref, stage_ref, weight_sem, part_sem, stage_sem = refs[9:]
    count = x_ref.shape[0]
    half = count // 2
    per_shard, n_weights, shard_rows = shards[0].shape[:3]
    member = table_ref[0]
    for k in range(UNIT):
        pltpu.make_async_copy(parts[k], packed_ref.at[member ^ k], part_sem.at[k]).start()
    for b in range(n_weights):
        for n in range(n_shards * per_shard):
            row = pl.multiple_of(table_ref[6 + n], shard_rows)
            pltpu.make_async_copy(
                shards[n // per_shard].at[n % per_shard, b], w_ref.at[b, pl.ds(row, shard_rows), :], weight_sem.at[b]
            ).start()
    for k in range(UNIT):
        pltpu.make_async_copy(parts[k], packed_ref.at[member ^ k], part_sem.at[k]).wait()
    for b in range(n_weights):
        pltpu.make_async_copy(w_ref.at[b], w_ref.at[b], weight_sem.at[b]).wait()

    sums_ref[...] = jnp.zeros_like(sums_ref)
    low = lax.broadcasted_iota(jnp.int32, (FFN_TILE, TILE), 1) < HEAD
    vec = [vec_ref[i : i + 1, :] for i in range(8 + FFB)]
    gain_one, shift_one, gain_two, shift_two = vec[:4]
    bias_out, bias_down = vec[6], vec[7]

    def add_sum(row, value):
        sums_ref[row : row + 1, :] += jnp.sum(value, axis=0, keepdims=True)

    def tile_step(i, carry):
        rows = pl.ds(pl.multiple_of(i * FFN_TILE, FFN_TILE), FFN_TILE)
        is_first = i * FFN_TILE < half
        extra = pl.ds(pl.multiple_of(count + lax.rem(i * FFN_TILE, half), FFN_TILE), FFN_TILE)

        def pair(m):
            return packed_ref[m, rows, :].astype(F32)

        def single(m):
            value = packed_ref[m, extra, :].astype(F32)
            return jnp.where(is_first, value, turn_half(value))

        for m in (0, 2):
            at = m * (HEADS_OWN * HEAD)
            nxt = turn_half(pair(m + 1))
            mixed_ref[rows, at : at + TILE] = pair(m).astype(BF16)
            mixed_ref[rows, at + TILE : at + 2 * TILE] = jnp.where(low, single(m), nxt).astype(BF16)
            mixed_ref[rows, at + 2 * TILE : at + 3 * TILE] = jnp.where(
                low, nxt, turn_half(single(m + 1))
            ).astype(BF16)
        attention = jnp.dot(mixed_ref[rows, :], w_ref[0], preferred_element_type=F32) + bias_out
        normed_one, rstd_one = normalize(x_ref[rows, :].astype(F32) + attention)
        hidden = normed_one * gain_one + shift_one
        hidden_low = hidden.astype(BF16)
        hidden_ref[rows, :] = hidden_low
        down = jnp.broadcast_to(bias_down, hidden.shape)
        for j in range(FFB):
            up = jnp.dot(hidden_low, w_ref[1 + j], preferred_element_type=F32) + vec[8 + j]
            phi = 0.5 * (1.0 + error_function(up * SQRT_HALF))
            slope_ref[j] = phi + up * jnp.exp(-0.5 * up * up) * INV_ROOT_TWO_PI
            act = (up * phi).astype(BF16)
            act_ref[j, rows, :] = act
            down = down + jnp.dot(act, w_ref[1 + FFB + j], preferred_element_type=F32)
        normed_two, rstd_two = normalize(hidden + down)
        result_ref[rows, :] = (normed_two * gain_two + shift_two).astype(BF16)
        grad_result = cot_ref[rows, :].astype(F32)
        add_sum(2, grad_result * normed_two)
        add_sum(3, grad_result)
        grad_second = norm_back(grad_result * gain_two, normed_two, rstd_two)
        grad_down = grad_second.astype(BF16)
        down_ref[rows, :] = grad_down
        add_sum(7, grad_down.astype(F32))
        grad_hidden = grad_second
        for j in range(FFB):
            grad_up = (outer_cols(grad_down, w_ref[1 + FFB + j]) * slope_ref[j]).astype(BF16)
            up_ref[j, rows, :] = grad_up
            add_sum(8 + j, grad_up.astype(F32))
            grad_hidden = grad_hidden + outer_cols(grad_up, w_ref[1 + j])
        add_sum(0, grad_hidden * normed_one)
        add_sum(1, grad_hidden)
        grad_first = norm_back(grad_hidden * gain_one, normed_one, rstd_one)
        first_ref[rows, :] = grad_first
        grad_attn = grad_first.astype(BF16)
        attn_ref[rows, :] = grad_attn
        add_sum(6, grad_attn.astype(F32))
        grad_mixed = (0.5 * outer_cols(grad_attn, w_ref[0])).astype(BF16).astype(F32)
        for m in range(UNIT):
            at = (m // 2) * 3 * TILE
            tiles = [grad_mixed[:, at + n * TILE : at + (n + 1) * TILE] for n in range(3)]
            if m % 2 == 0:
                two, one = tiles[0], tiles[1]
            else:
                two, one = turn_half(jnp.where(low, tiles[2], tiles[1])), turn_half(tiles[2])
            back_ref[member ^ m, rows, :] = two.astype(BF16)

            @pl.when(is_first)
            def _(one=one, m=m):
                back_ref[member ^ m, extra, :] = jnp.where(low, one, 0.0).astype(BF16)

            @pl.when(jnp.logical_not(is_first))
            def _(one=one, m=m):
                old = back_ref[member ^ m, extra, :].astype(F32)
                back_ref[member ^ m, extra, :] = jnp.where(low, old, turn_half(one)).astype(BF16)

        return carry

    lax.fori_loop(0, count // FFN_TILE, tile_step, 0)
    for k in range(UNIT):
        backs[k][...] = back_ref[k]

    core, bits = table_ref[1], [table_ref[2 + d] for d in range(4)]
    piece, half_columns = kept_ref.shape[3:]
    n_parts = kept_ref.shape[0]
    per_part = n_weights // n_parts

    def copies(block, slot, half, target):
        part = block // per_part
        made = []
        for index in range(16):
            x, zh, y, zl = ((index >> s) % 2 for s in range(4))
            rel = {"x": x ^ bits[0], "y": y ^ bits[1], "zl": zl ^ bits[2], "zh": zh ^ bits[3]}
            place = 0
            for name in PART_ORDERS[part]:
                place = place * 2 + rel[name]
            made.append(
                pltpu.make_async_copy(
                    stage_ref.at[
                        slot, pl.ds(index * piece, piece), pl.ds(half * half_columns, half_columns)
                    ],
                    target.at[part, place, block % per_part],
                    stage_sem.at[slot, half * 16 + index],
                )
            )
        return made

    def send(block, slot):
        for half in range(2):

            @pl.when(core == half)
            def _(half=half):
                for copy in copies(block, slot, half, kept_ref):
                    copy.start()

            @pl.when(core != half)
            def _(half=half):
                for copy in copies(block, slot, half, sent_ref):
                    copy.start()

    def sent(block, slot):
        for half in range(2):
            for copy in copies(block, slot, half, kept_ref):
                copy.wait()

    plan = [(attn_ref, None, mixed_ref, None, 0)]
    plan += [(down_ref, None, act_ref, j, 1 + FFB + j) for j in range(FFB)]
    plan += [(up_ref, j, hidden_ref, None, 1 + j) for j in range(FFB)]
    for n, (left, lj, right, rj, block) in enumerate(plan):
        slot = n % 2
        if n >= 2:
            sent(plan[n - 2][4], slot)
        value = inner_rows(
            left[...] if lj is None else left[lj], right[...] if rj is None else right[rj]
        )
        stage_ref[slot] = value.astype(BF16)
        send(block, slot)
    for n in (len(plan) - 2, len(plan) - 1):
        sent(plan[n][4], n % 2)


PART_ORDERS = (("x", "y", "zl", "zh"), ("y", "zl", "zh", "x"), ("zl", "zh", "x", "y"))


def layer(table, shards, parts, inputs, cotangent, vectors):
    count = inputs.shape[0]
    n_weights = 1 + 2 * FFB
    n_shards = len(shards)
    anywhere = pl.BlockSpec(memory_space=pl.ANY)
    inside = pl.BlockSpec(memory_space=pltpu.VMEM)
    packed = parts[0].shape
    return pl.pallas_call(
        functools.partial(layer_body, n_shards),
        in_specs=[pl.BlockSpec(memory_space=pltpu.SMEM)] + [anywhere] * (n_shards + UNIT) + [inside] * 3,
        out_specs=[inside, inside, inside, anywhere, anywhere] + [inside] * UNIT,
        out_shape=[
            jax.ShapeDtypeStruct((count, D), BF16),
            jax.ShapeDtypeStruct((count, D), F32),
            jax.ShapeDtypeStruct((VEC_ROWS, D), F32),
            jax.ShapeDtypeStruct((3, 16, n_weights // 3, D // 16, D // 2), BF16),
            jax.ShapeDtypeStruct((3, 16, n_weights // 3, D // 16, D // 2), BF16),
        ]
        + [jax.ShapeDtypeStruct(packed, BF16)] * UNIT,
        scratch_shapes=[
            pltpu.VMEM((n_weights, D, D), BF16),
            pltpu.VMEM((UNIT, *packed), BF16),
            pltpu.VMEM((count, D), BF16),
            pltpu.VMEM((count, D), BF16),
            pltpu.VMEM((FFB, count, D), BF16),
            pltpu.VMEM((count, D), BF16),
            pltpu.VMEM((FFB, count, D), BF16),
            pltpu.VMEM((count, D), BF16),
            pltpu.VMEM((UNIT, *packed), BF16),
            pltpu.VMEM((FFB, FFN_TILE, D), F32),
            pltpu.VMEM((2, D, D), BF16),
            pltpu.SemaphoreType.DMA((n_weights,)),
            pltpu.SemaphoreType.DMA((UNIT,)),
            pltpu.SemaphoreType.DMA((2, 32)),
        ],
        compiler_params=pltpu.CompilerParams(vmem_limit_bytes=60 << 20),
        cost_estimate=SMALL,
        name="layer",
    )(table, *shards, *parts, inputs, cotangent, vectors)


def qkv_back_body(scalars_ref, *refs):
    grads, inputs, kept_ref, sent_ref, bias_ref, all_ref = refs[:4], refs[4:8], *refs[8:]
    core, unit = scalars_ref[0], scalars_ref[1]
    columns = all_ref.shape[4]
    step = 32
    per_unit = all_ref.shape[3]
    bias_ref[...] = jnp.zeros_like(bias_ref)
    for head in range(HEADS_OWN):
        at = slice(head * WIDE, (head + 1) * WIDE)
        total = inner_rows(grads[0][:, at], inputs[0][...])
        bias = jnp.sum(grads[0][:, at].astype(F32), axis=0, keepdims=True)
        for k in range(1, UNIT):
            total = total + inner_rows(grads[k][:, at], inputs[k][...])
            bias = bias + jnp.sum(grads[k][:, at].astype(F32), axis=0, keepdims=True)
        bias_ref[0:1, at] = bias
        firsts = (HEAD, 3 * HEAD, 0) if head % 2 == 0 else (0, 2 * HEAD, HEAD)
        for block, first in enumerate(firsts):
            for i in range(HEAD // step):
                row = head * HEAD + i * step
                rows = total[first + i * step : first + (i + 1) * step]
                for c in range(2):
                    all_ref[
                        c ^ core, row // per_unit ^ unit, block, row % per_unit : row % per_unit + step, :
                    ] = rows[:, c * columns : (c + 1) * columns].astype(BF16)
    kept_ref[...] = all_ref[0]
    sent_ref[...] = all_ref[1]


def qkv_back(scalars, grads, inputs):
    inside = pl.BlockSpec(memory_space=pltpu.VMEM)
    shape = (2, 3, HEADS_OWN * HEAD // 2, D // 2)
    return pl.pallas_call(
        qkv_back_body,
        in_specs=[pl.BlockSpec(memory_space=pltpu.SMEM)] + [inside] * (2 * UNIT),
        out_specs=[inside] * 3,
        out_shape=[
            jax.ShapeDtypeStruct(shape, BF16),
            jax.ShapeDtypeStruct(shape, BF16),
            jax.ShapeDtypeStruct((8, HEADS_OWN * WIDE), F32),
        ],
        scratch_shapes=[pltpu.VMEM((2, *shape), BF16)],
        compiler_params=pltpu.CompilerParams(vmem_limit_bytes=56 << 20),
        cost_estimate=SMALL,
        name="qkv_back",
    )(scalars, *grads, *inputs)


def pack_body(slot_block_ref, *refs):
    half = (len(refs) - 2) // 2
    kept, got, out_ref, all_ref = refs[:half], refs[half : 2 * half], refs[-2], refs[-1]
    per_part = kept[0].shape[1]
    for p in range(half):
        for b in range(per_part):
            all_ref[p * per_part + b] = (kept[p][0, b] + got[p][0, b].astype(F32)).astype(BF16)
    for s in range(out_ref.shape[0] * out_ref.shape[1]):
        out_ref[s // out_ref.shape[1], s % out_ref.shape[1]] = all_ref[jnp.maximum(slot_block_ref[s] - 3, 0)]


def pack(slot_block, kept, got, n_grp, slots):
    shape = kept[0].shape[2:]
    inside = pl.BlockSpec(memory_space=pltpu.VMEM)
    return pl.pallas_call(
        pack_body,
        in_specs=[pl.BlockSpec(memory_space=pltpu.SMEM)] + [inside] * (2 * len(kept)),
        out_specs=inside,
        out_shape=jax.ShapeDtypeStruct((n_grp, slots, *shape), BF16),
        scratch_shapes=[pltpu.VMEM((len(kept) * kept[0].shape[1], *shape), BF16)],
        compiler_params=pltpu.CompilerParams(vmem_limit_bytes=32 << 20),
        cost_estimate=SMALL,
        name="pack",
    )(slot_block, *kept, *got)


def rotate_in_body(mine_ref, keep_ref, got_ref, high_ref, low_ref, out_ref, grad_ref):
    slots, n_tok = got_ref.shape[1], out_ref.shape[0]
    rows, columns = got_ref.shape[2:]
    width = out_ref.shape[3]
    for s in range(slots):
        block = mine_ref[s]

        @pl.when(block < 3)
        def _(s=s, block=block):
            grad_ref[...] = keep_ref[jnp.minimum(block, 2)]

        @pl.when(block >= 3)
        def _(s=s):
            for g in range(got_ref.shape[0]):
                x, c = g // 2, g % 2
                grad_ref[x * rows : (x + 1) * rows, c * columns : (c + 1) * columns] = got_ref[g, s]

        grad = grad_ref[...]
        part = jnp.dot(grad, high_ref[s], preferred_element_type=F32)
        part = jnp.transpose(part + jnp.dot(grad, low_ref[s], preferred_element_type=F32))
        for r in range(n_tok):
            out_ref[r, s] = part[r * width : (r + 1) * width].astype(BF16)


def rotate_in(mine, keep, got, left, n_tok):
    slots, width = got.shape[1], keep.shape[1]
    inside = pl.BlockSpec(memory_space=pltpu.VMEM)
    return pl.pallas_call(
        rotate_in_body,
        in_specs=[pl.BlockSpec(memory_space=pltpu.SMEM)] + [inside] * 4,
        out_specs=inside,
        out_shape=jax.ShapeDtypeStruct((n_tok, slots, width, width), BF16),
        scratch_shapes=[pltpu.VMEM(keep.shape[1:], BF16)],
        compiler_params=pltpu.CompilerParams(vmem_limit_bytes=48 << 20),
        cost_estimate=SMALL,
        name="rotate_in",
    )(mine, keep, got, *left)


def moments_body(place, got_ref, high_ref, low_ref, one_ref, two_ref, new_one_ref, new_two_ref, out_ref):
    n_tok, slots, width = got_ref.shape[:3]
    for s in range(slots):
        rotated = jnp.zeros(one_ref.shape[1:], F32)
        for t in range(n_tok):
            at = slice(place[t] * width, (place[t] + 1) * width)
            part = got_ref[t, s]
            rotated = rotated + jnp.dot(part, high_ref[s, at], preferred_element_type=F32)
            rotated = rotated + jnp.dot(part, low_ref[s, at], preferred_element_type=F32)
        new_one = BETA_ONE * one_ref[s] + (1.0 - BETA_ONE) * rotated
        new_two = BETA_TWO * two_ref[s] + (1.0 - BETA_TWO) * rotated * rotated
        new_one_ref[s] = new_one
        new_two_ref[s] = new_two
        direction = (new_one / (jnp.sqrt(new_two) + ADAM_EPS)).astype(BF16)
        for t in range(n_tok):
            at = slice(place[t] * width, (place[t] + 1) * width)
            turned = outer_cols(direction, high_ref[s, at]) + outer_cols(direction, low_ref[s, at])
            out_ref[t, s] = turned.astype(BF16)


def moments(place, got, right, one, two):
    n_tok, slots, width = got.shape[:3]
    inside = pl.BlockSpec(memory_space=pltpu.VMEM)
    return pl.pallas_call(
        functools.partial(moments_body, tuple(place)),
        in_specs=[inside] * 5,
        out_specs=[inside] * 3,
        out_shape=[
            jax.ShapeDtypeStruct(one.shape, F32),
            jax.ShapeDtypeStruct(one.shape, F32),
            jax.ShapeDtypeStruct(got.shape, BF16),
        ],
        compiler_params=pltpu.CompilerParams(vmem_limit_bytes=48 << 20),
        cost_estimate=SMALL,
        name="moments",
    )(got, *right, one, two)


def rotate_out_body(got_ref, high_ref, low_ref, out_ref, rows_ref):
    n_tok, slots, width = got_ref.shape[:3]
    for s in range(slots):
        for r in range(n_tok):
            rows_ref[r * width : (r + 1) * width, :] = got_ref[r, s]
        rows = rows_ref[...]
        change = jnp.dot(high_ref[s], rows, preferred_element_type=F32)
        change = change + jnp.dot(low_ref[s], rows, preferred_element_type=F32)
        for r in range(n_tok):
            out_ref[r, s] = change[r * width : (r + 1) * width].astype(BF16)


def rotate_out(got, left):
    n_tok, slots, width = got.shape[:3]
    inside = pl.BlockSpec(memory_space=pltpu.VMEM)
    return pl.pallas_call(
        rotate_out_body,
        in_specs=[inside] * 3,
        out_specs=inside,
        out_shape=jax.ShapeDtypeStruct(got.shape, BF16),
        scratch_shapes=[pltpu.VMEM((n_tok * width, width), BF16)],
        compiler_params=pltpu.CompilerParams(vmem_limit_bytes=48 << 20),
        cost_estimate=SMALL,
        name="rotate_out",
    )(got, *left)


def apply_body(place, got_ref, master_ref, out_ref):
    n_tok, slots, width = got_ref.shape[:3]
    for s in range(slots):
        for t in range(n_tok):
            at = slice(place[t] * width, (place[t] + 1) * width)
            out_ref[s, :, at] = master_ref[s, :, at] - RATE_MATRIX * got_ref[t, s].astype(F32)


def apply_change(place, got, master):
    inside = pl.BlockSpec(memory_space=pltpu.VMEM)
    return pl.pallas_call(
        functools.partial(apply_body, tuple(place)),
        in_specs=[inside] * 2,
        out_specs=inside,
        out_shape=jax.ShapeDtypeStruct(master.shape, F32),
        compiler_params=pltpu.CompilerParams(vmem_limit_bytes=48 << 20),
        cost_estimate=SMALL,
        name="apply_change",
    )(got, master)


def swap(value, axis, bit):
    size = lax.axis_size(axis)
    return lax.ppermute(value, axis, [(i, i ^ bit) for i in range(size)])


def exchange_unit(parts):
    return [parts[0]] + [swap(parts[k], "tok", k) for k in range(1, UNIT)]


LINKS = {"x": ("grp", 2), "y": ("tok", 1), "zl": ("tok", 2), "zh": ("tok", 4)}


def starts_of(lengths):
    index = jnp.arange(lengths.shape[0])
    return jnp.sum(jnp.where(index[None, :] < index[:, None], lengths[None, :], 0), axis=1)


LINKS = {"x": ("grp", 2), "y": ("tok", 1), "zl": ("tok", 2), "zh": ("tok", 4)}


def starts_of(lengths):
    index = jnp.arange(lengths.shape[0])
    return jnp.sum(jnp.where(index[None, :] < index[:, None], lengths[None, :], 0), axis=1)


def total_of(value):
    for axis in ("grp", "tok"):
        bit = 1
        while bit < lax.axis_size(axis):
            value = value + swap(value, axis, bit)
            bit *= 2
    return value


def pick(values, index):
    return lax.dynamic_index_in_dim(values, index, 0, keepdims=False)


def split_heads(columns):
    query, keys, values = (c.reshape(HEADS_OWN, HEAD) for c in columns)
    zero = jnp.zeros((HEAD,), query.dtype)
    tiles = []
    for h in range(HEADS_OWN):
        tiles += [values[h], query[h], zero, keys[h]] if h % 2 == 0 else [query[h], values[h], keys[h], zero]
    return jnp.concatenate(tiles)


def join_heads(tiles):
    parts = tiles.reshape(HEADS_OWN, 4, HEAD, *tiles.shape[1:])
    at = [(1, 0), (3, 2), (0, 1)]
    return jnp.stack(
        [jnp.concatenate([parts[h, at[i][h % 2]] for h in range(HEADS_OWN)], axis=0) for i in range(3)]
    )


def doubled(value):
    high = value.astype(BF16)
    return high, (value - high.astype(F32)).astype(BF16)


def together(*groups):
    flat, tree = jax.tree.flatten(groups)
    return jax.tree.unflatten(tree, lax.optimization_barrier(flat))


def fast(
    tokens,
    cotangent,
    lengths,
    clusters,
    owners,
    master,
    bases,
    moment_one,
    moment_two,
    vectors,
    vector_one,
    vector_two,
):
    n_tok = lax.axis_size("tok")
    n_grp = lax.axis_size("grp")
    tok = lax.axis_index("tok")
    grp = lax.axis_index("grp")
    tok_count = tokens.shape[1]
    rows_dev = master.shape[0]
    slots = master.shape[1]
    blocks_all = slots * n_grp
    member = tok & (UNIT - 1)
    unit = tok >> 2
    place = [2 * (t % UNIT) + t // UNIT for t in range(n_tok)]
    own_width = HEADS_OWN * HEAD

    slot_block = jnp.argsort(owners, stable=True).astype(jnp.int32)
    block_slot = jnp.argsort(slot_block, stable=True).astype(jnp.int32)

    core, bit_x = grp & 1, grp >> 1
    inputs = tokens[0]

    near, far = swap(inputs, "tok", 1), swap(inputs, "tok", 2)
    local = jnp.transpose(master.astype(BF16), (1, 0, 2))
    beside, over = swap(local, "grp", 1), swap(local, "grp", 2)

    item_starts = starts_of(lengths[0])
    unit_start = unit * UNIT * tok_count
    middle = unit_start + UNIT // 2 * tok_count
    start_of_middle = jnp.max(jnp.where(item_starts <= middle, item_starts, 0))
    is_long = (start_of_middle <= unit_start).astype(jnp.int32).reshape(1)
    share = CLUSTER // UNIT * (2 - is_long)
    placed = places(jnp.concatenate([share, member.reshape(1)]), clusters[0])
    left, right = doubled(bases[0]), doubled(bases[1])
    (over, left, right, placed) = together(over, left, right, placed)
    across = swap(over, "grp", 1)

    orders = exchange_unit(placed)
    (near, far, beside, over, across) = together(near, far, beside, over, across)
    part_rows = rows_dev // 2

    scalars = jnp.concatenate([block_slot, jnp.stack([grp, core, member])]).astype(jnp.int32)
    *by_owner, rest_rows = arrange(scalars, [local, beside, over, across], blocks_all)
    theirs = exchange_unit(by_owner)
    half = tok_count // 2
    third = (swap(near[:half], "tok", 2), swap(far[half:], "tok", 1))
    (theirs, orders) = together(theirs, orders)
    theirs = jnp.stack(theirs)
    theirs_far = swap(theirs, "tok", UNIT)
    mine_all = jnp.concatenate([theirs, theirs_far], axis=0)
    others_all = swap(mine_all, "grp", 1)
    sources = tok ^ jnp.arange(2 * UNIT, dtype=jnp.int32)
    cores = core ^ jnp.arange(2, dtype=jnp.int32)
    firsts = (sources[None, :] * rows_dev + cores[:, None] * part_rows).reshape(-1)
    (third, others_all, rest_rows) = together(third, others_all, rest_rows)
    own_weights = assemble(firsts, [mine_all, others_all])

    def columns_of(value, m):
        return lax.dynamic_slice_in_dim(value, m * own_width, own_width, value.ndim - 1)

    own_bias = split_heads(
        [columns_of(vectors[4], member), jnp.zeros((own_width,), F32), columns_of(vectors[5], member)]
    ).reshape(1, -1)
    ring = [(i, (i + 2) % n_tok) for i in range(n_tok)]
    depth = n_tok // 2
    steps, flips, mine_rest, other_rest = [rest_rows], [], [], []

    def advance():
        if len(steps) < depth:
            steps.append(lax.ppermute(steps[-1], "tok", ring))
        flips.append(swap(steps[len(flips)], "tok", 1))

    def cross():
        k = len(mine_rest)
        mine_rest.append(jnp.stack([steps[k], flips[k]]))
        other_rest.append(swap(mine_rest[k], "grp", 1))

    advance()
    grouped = [sort_rows(orders[0], inputs, own_weights, own_bias)]
    grouped.append(sort_rows(orders[1], near, own_weights, own_bias))
    (grouped, far, third, steps[1], flips[0]) = together(grouped, far, third, steps[1], flips[0])
    advance()
    cross()
    grouped.append(sort_rows(orders[2], far, own_weights, own_bias))
    unit_inputs = [inputs, near, far, jnp.concatenate(third, axis=0)]
    grouped.append(sort_rows(orders[3], unit_inputs[3], own_weights, own_bias))
    (grouped, steps[2], flips[1], other_rest) = together(grouped, steps[2], flips[1], other_rest)
    advance()
    cross()
    sorted_out = attend(is_long, grouped)
    (sorted_out, steps[3], flips[2], other_rest) = together(sorted_out, steps[3], flips[2], other_rest)
    advance()
    cross()
    mixed = [None] * UNIT
    mixed[3] = mix(orders[3], sorted_out[3])
    mixed[2] = mix(orders[2], sorted_out[2])
    mixed[1] = mix(orders[1], sorted_out[1])
    mixed_parts = exchange_unit(mixed)
    (mixed_parts[1:], flips[-1], other_rest, held_weights) = together(
        mixed_parts[1:], flips[-1], other_rest, own_weights
    )
    cross()
    mixed_parts[0] = mix(orders[0], sorted_out[0])
    shards = mine_rest + other_rest
    sources = (tok + n_tok - 2 * jnp.arange(depth, dtype=jnp.int32)) & (n_tok - 1)
    sources = (sources[:, None] ^ jnp.arange(2, dtype=jnp.int32)[None, :]).reshape(-1)
    firsts = (sources[None, :] * rows_dev + cores[:, None] * part_rows).reshape(-1)

    turned_weights = [swap(held_weights, "tok", k) for k in range(1, UNIT)]
    place_bits = jnp.stack([member, core, bit_x, tok & 1, (tok >> 1) & 1, tok >> 2]).astype(jnp.int32)
    table = jnp.concatenate([place_bits, firsts])
    result, grad_first, sums, kept, sent_pieces, *back = layer(
        table, shards, mixed_parts, inputs, cotangent[0], vectors
    )
    (turned_weights, kept, sent_pieces, back) = together(turned_weights, kept, sent_pieces, back)

    grad_parts = exchange_unit(back)
    other = swap(sent_pieces, "grp", 1)
    sums_of = [kept[p].astype(F32) + other[p].astype(F32) for p in range(3)]

    def halves(values):
        return [v[: v.shape[0] // 2] for v in values], [v[v.shape[0] // 2 :].astype(BF16) for v in values]

    def exchanged(sent_now, stage):
        return [swap(v, *LINKS[PART_ORDERS[p][stage]]) for p, v in enumerate(sent_now)]

    def joined(kept_now, got_now):
        return [k + g.astype(F32) for k, g in zip(kept_now, got_now)]

    kept_now, sent_now = halves(sums_of)
    sorted_grads = [sort_grads(orders[0], grad_parts[0])]
    (sent_now, grad_parts, sorted_grads) = together(sent_now, grad_parts, sorted_grads)
    got_now = exchanged(sent_now, 0)
    sorted_grads += [sort_grads(orders[k], grad_parts[k]) for k in range(1, UNIT)]
    sorted_back = attend_back(is_long, grouped, sorted_grads)
    kept_now, sent_now = halves(joined(kept_now, got_now))
    (sent_now, sorted_back) = together(sent_now, sorted_back)
    got_now = exchanged(sent_now, 1)
    own_grads = [None] * UNIT
    own_grads[3] = gather_grads(orders[3], sorted_back[3])
    own_grads[2] = gather_grads(orders[2], sorted_back[2])
    kept_now, sent_now = halves(joined(kept_now, got_now))
    (sent_now, own_grads[2], own_grads[3], sorted_back) = together(
        sent_now, own_grads[2], own_grads[3], sorted_back
    )
    got_now = exchanged(sent_now, 2)
    home_grads = [None, None, None, swap(own_grads[3], "tok", 3)]
    for k in (1, 0):
        own_grads[k] = gather_grads(orders[k], sorted_back[k])
    kept_qkv, sent_qkv, bias_qkv = qkv_back(jnp.stack([core, unit]).astype(jnp.int32), own_grads, unit_inputs)
    (got_now, kept_qkv, sent_qkv) = together(got_now, kept_qkv, sent_qkv)
    kept_now, sent_now = halves(joined(kept_now, got_now))
    got_now = exchanged(sent_now, 3)

    bias_query, _, bias_value = join_heads(bias_qkv[0])
    bias_rows = lax.dynamic_update_slice_in_dim(
        jnp.zeros((2, D), F32), jnp.stack([bias_query, bias_value]), member * own_width, 1
    )
    total = sums[: 8 + FFB] + jnp.pad(bias_rows, ((4, 2 + FFB), (0, 0)))

    more = swap(total, "grp", 1)
    keep = kept_qkv.astype(F32) + swap(sent_qkv, "grp", 1).astype(F32)
    (keep, more) = together(keep, more)
    total = total + more
    more = swap(total, "grp", 2)
    unit_got = swap(keep[1].astype(BF16), "tok", UNIT)
    keep = keep[0] + unit_got.astype(F32)
    (keep, more, got_now, home_grads[3]) = together(keep, more, got_now, home_grads[3])
    total = total + more
    more = swap(total, "tok", 1)
    home_grads[1] = swap(own_grads[1], "tok", 1)
    home_grads[2] = swap(own_grads[2], "tok", 2)
    sent = pack(slot_block, kept_now, got_now, n_grp, slots)
    got = lax.all_to_all(sent, "grp", split_axis=0, concat_axis=0, tiled=True)
    keep = (keep + swap(keep.astype(BF16), "grp", 2).astype(F32)).astype(BF16)
    kept_core = (keep, swap(keep, "grp", 1))
    keep = jnp.concatenate(
        [jnp.where(core == 0, kept_core[0], kept_core[1]), jnp.where(core == 0, kept_core[1], kept_core[0])],
        axis=-1,
    )
    mine = lax.dynamic_slice_in_dim(slot_block, grp * slots, slots, 0)

    def to_tok(value):
        return lax.all_to_all(value, "tok", split_axis=0, concat_axis=0, tiled=True)

    part = to_tok(rotate_in(mine, keep, got, left, n_tok))
    grad_inputs = grad_first + outer_cols(own_grads[0], own_weights)
    (part, home_grads, grad_inputs, more) = together(part, home_grads[1:], grad_inputs, more)
    total = total + more
    more = swap(total, "tok", 2)
    by_slot_of = lambda value: jnp.transpose(value, (1, 0, 2))
    new_one, new_two, turned = moments(
        place, part, right, by_slot_of(moment_one), by_slot_of(moment_two)
    )
    turned = to_tok(turned)
    grad_inputs = grad_inputs + outer_cols(home_grads[0], turned_weights[0])
    grad_inputs = grad_inputs + outer_cols(home_grads[1], turned_weights[1])
    (turned, more, grad_inputs, home_grads[2]) = together(turned, more, grad_inputs, home_grads[2])
    total = total + more
    change = to_tok(rotate_out(turned, left))
    vector_total = total + swap(total, "tok", 4)
    new_master = by_slot_of(apply_change(place, change, by_slot_of(master)))
    new_one, new_two = by_slot_of(new_one), by_slot_of(new_two)
    grad_inputs = grad_inputs + outer_cols(home_grads[2], turned_weights[2])
    new_vec_one = BETA_ONE * vector_one + (1.0 - BETA_ONE) * vector_total
    new_vec_two = BETA_TWO * vector_two + (1.0 - BETA_TWO) * vector_total * vector_total
    new_vectors = vectors - RATE_VECTOR * new_vec_one / (jnp.sqrt(new_vec_two) + ADAM_EPS)
    return (
        result[None],
        grad_inputs[None],
        new_one,
        new_two,
        new_master,
        new_vec_one,
        new_vec_two,
        new_vectors,
    )


def general(
    tokens,
    cotangent,
    lengths,
    clusters,
    owners,
    master,
    bases,
    moment_one,
    moment_two,
    vectors,
    vector_one,
    vector_two,
):
    n_tok = lax.axis_size("tok")
    tok_count = tokens.shape[1]
    rows_dev = master.shape[0]
    slot_block = jnp.argsort(owners, stable=True)
    block_slot = jnp.argsort(slot_block, stable=True)
    slot_part = lax.all_gather(master.astype(jnp.bfloat16), "grp", axis=1, tiled=True)
    weights = lax.all_gather(slot_part, "tok", axis=0, tiled=True)
    blocks = jnp.stack([pick(jnp.transpose(weights, (1, 0, 2)), block_slot[b]) for b in range(weights.shape[1])], axis=1)
    w_qkv = blocks[:, 0:3, :].reshape(D, 3 * D)
    w_out = blocks[:, 3, :]
    w_up = blocks[:, 4 : 4 + FF // D, :].reshape(D, FF)
    w_down = jnp.transpose(blocks[:, 4 + FF // D :, :], (1, 0, 2)).reshape(FF, D)
    inputs = tokens[0]
    gain_one = vectors[0]
    shift_one = vectors[1]
    gain_two = vectors[2]
    shift_two = vectors[3]
    bias_qkv = jnp.concatenate([vectors[4], jnp.zeros((D,), jnp.float32), vectors[5]])
    qkv = (jnp.dot(inputs, w_qkv, preferred_element_type=jnp.float32) + bias_qkv).astype(
        jnp.bfloat16
    )
    heads = jnp.transpose(qkv.reshape(tok_count, 3, H, HEAD), (2, 0, 1, 3)).reshape(
        H, tok_count, 3 * HEAD
    )
    pair_rows = jnp.broadcast_to(heads[None], (ROUNDS, H, tok_count, 3 * HEAD)).reshape(
        PAIRS * tok_count, 3 * HEAD
    )
    position = lax.axis_index("tok") * tok_count + jnp.arange(tok_count, dtype=jnp.int32)
    item_starts = starts_of(lengths[0])
    item_start = jnp.max(
        jnp.where(item_starts[None, :] <= position[:, None], item_starts[None, :], 0), axis=1
    )
    per_dev = tok_count // CLUSTER
    group_clusters = n_tok * per_dev
    pair_ids = jnp.arange(PAIRS, dtype=jnp.int32)[:, None]
    global_cluster = item_start[None, :] // CLUSTER + clusters[0]
    unit_ids = (pair_ids * group_clusters + global_cluster).reshape(-1)
    owner_ids = ((global_cluster + pair_ids * per_dev) % n_tok).reshape(-1)
    send_order = jnp.argsort(owner_ids * (PAIRS * group_clusters) + unit_ids, stable=True)
    restore = jnp.argsort(send_order, stable=True)
    slot_rows = PAIRS * tok_count // n_tok
    units_here = PAIRS * tok_count // CLUSTER
    sent_rows = pair_rows[send_order].reshape(n_tok, slot_rows // 2, 6 * HEAD)
    sent_units = unit_ids[send_order].reshape(n_tok, slot_rows)
    got_rows, got_units = (
        lax.all_to_all(sent_rows, "tok", split_axis=0, concat_axis=0, tiled=True),
        lax.all_to_all(sent_units, "tok", split_axis=0, concat_axis=0, tiled=True),
    )
    arrange = jnp.argsort(got_units.reshape(-1), stable=True)
    undo = jnp.argsort(arrange, stable=True)
    grouped = got_rows.reshape(PAIRS * tok_count, 3 * HEAD)[arrange].reshape(
        units_here, CLUSTER, 3 * HEAD
    )
    query_rows = grouped[..., :HEAD]
    key_rows = grouped[..., HEAD : 2 * HEAD]
    value_rows = grouped[..., 2 * HEAD :]
    score_scale = HEAD ** (-0.5)
    scores = (
        jnp.einsum("ucd,ued->uce", query_rows, key_rows, preferred_element_type=jnp.float32)
        * score_scale
    )
    row_max = jnp.max(scores, axis=-1, keepdims=True)
    row_total = jnp.sum(jnp.exp(scores - row_max), axis=-1, keepdims=True)
    log_total = row_max + jnp.log(row_total)
    probs = jnp.exp(scores - log_total)
    cluster_out = jnp.einsum(
        "uce,ued->ucd", probs.astype(jnp.bfloat16), value_rows, preferred_element_type=jnp.float32
    ).astype(jnp.bfloat16)
    back_rows = cluster_out.reshape(PAIRS * tok_count, HEAD)[undo].reshape(
        n_tok, slot_rows // 2, 2 * HEAD
    )
    home_rows = lax.all_to_all(back_rows, "tok", split_axis=0, concat_axis=0, tiled=True)
    home_rows = (
        home_rows.reshape(PAIRS * tok_count, HEAD)[restore]
        .reshape(ROUNDS, H, tok_count, HEAD)
        .astype(jnp.float32)
    )
    mixed_heads = 0.5 * (home_rows[0] + home_rows[1])
    mixed_low = jnp.transpose(mixed_heads, (1, 0, 2)).reshape(tok_count, D).astype(jnp.bfloat16)
    attention = jnp.dot(mixed_low, w_out, preferred_element_type=jnp.float32) + vectors[6]
    first_sum = inputs.astype(jnp.float32) + attention
    normed_one, rstd_one = normalize(first_sum)
    hidden = normed_one * gain_one + shift_one
    hidden_low = hidden.astype(jnp.bfloat16)
    up_proj = jnp.dot(hidden_low, w_up, preferred_element_type=jnp.float32) + vectors[8:].reshape(
        FF
    )
    act_low = jax.nn.gelu(up_proj, approximate=False).astype(jnp.bfloat16)
    down_proj = jnp.dot(act_low, w_down, preferred_element_type=jnp.float32) + vectors[7]
    second_sum = hidden + down_proj
    normed_two, rstd_two = normalize(second_sum)
    result = (normed_two * gain_two + shift_two).astype(jnp.bfloat16)
    grad_result = cotangent[0].astype(jnp.float32)
    grad_gain_two = jnp.sum(grad_result * normed_two, axis=0)
    grad_shift_two = jnp.sum(grad_result, axis=0)
    grad_second = norm_back(grad_result * gain_two, normed_two, rstd_two)
    grad_down_low = grad_second.astype(jnp.bfloat16)
    grad_w_down = inner_rows(act_low, grad_down_low)
    grad_bias_down = jnp.sum(grad_down_low.astype(jnp.float32), axis=0)
    grad_act = outer_cols(grad_down_low, w_down)
    grad_up_low = (grad_act * gelu_slope(up_proj)).astype(jnp.bfloat16)
    grad_w_up = inner_rows(hidden_low, grad_up_low)
    grad_bias_up = jnp.sum(grad_up_low.astype(jnp.float32), axis=0)
    grad_hidden = grad_second + outer_cols(grad_up_low, w_up)
    grad_gain_one = jnp.sum(grad_hidden * normed_one, axis=0)
    grad_shift_one = jnp.sum(grad_hidden, axis=0)
    grad_first = norm_back(grad_hidden * gain_one, normed_one, rstd_one)
    grad_attn_low = grad_first.astype(jnp.bfloat16)
    grad_w_out = inner_rows(mixed_low, grad_attn_low)
    grad_bias_out = jnp.sum(grad_attn_low.astype(jnp.float32), axis=0)
    grad_mixed = outer_cols(grad_attn_low, w_out)
    grad_heads = jnp.transpose((0.5 * grad_mixed).reshape(tok_count, H, HEAD), (1, 0, 2)).astype(
        jnp.bfloat16
    )
    grad_pairs = jnp.broadcast_to(grad_heads[None], (ROUNDS, H, tok_count, HEAD)).reshape(
        PAIRS * tok_count, HEAD
    )
    sent_grad = grad_pairs[send_order].reshape(n_tok, slot_rows // 2, 2 * HEAD)
    got_grad = lax.all_to_all(sent_grad, "tok", split_axis=0, concat_axis=0, tiled=True)
    grad_cluster = got_grad.reshape(PAIRS * tok_count, HEAD)[arrange].reshape(
        units_here, CLUSTER, HEAD
    )
    scores_again = (
        jnp.einsum("ucd,ued->uce", query_rows, key_rows, preferred_element_type=jnp.float32)
        * score_scale
    )
    probs_again = jnp.exp(scores_again - log_total)
    probs_low = probs_again.astype(jnp.bfloat16)
    grad_values = jnp.einsum(
        "uce,ucd->ued", probs_low, grad_cluster, preferred_element_type=jnp.float32
    )
    grad_probs = jnp.einsum(
        "ucd,ued->uce", grad_cluster, value_rows, preferred_element_type=jnp.float32
    )
    centre = jnp.sum(probs_again * grad_probs, axis=-1, keepdims=True)
    grad_scores = (probs_again * (grad_probs - centre)).astype(jnp.bfloat16)
    grad_query = (
        jnp.einsum("uce,ued->ucd", grad_scores, key_rows, preferred_element_type=jnp.float32)
        * score_scale
    )
    grad_keys = (
        jnp.einsum("uce,ucd->ued", grad_scores, query_rows, preferred_element_type=jnp.float32)
        * score_scale
    )
    grad_grouped = jnp.concatenate(
        [
            grad_query.astype(jnp.bfloat16),
            grad_keys.astype(jnp.bfloat16),
            grad_values.astype(jnp.bfloat16),
        ],
        axis=-1,
    )
    back_grad = grad_grouped.reshape(PAIRS * tok_count, 3 * HEAD)[undo].reshape(
        n_tok, slot_rows // 2, 6 * HEAD
    )
    home_grad = lax.all_to_all(back_grad, "tok", split_axis=0, concat_axis=0, tiled=True)
    home_grad = (
        home_grad.reshape(PAIRS * tok_count, 3 * HEAD)[restore]
        .reshape(ROUNDS, H, tok_count, 3, HEAD)
        .astype(jnp.float32)
    )
    grad_qkv = (home_grad[0] + home_grad[1]).astype(jnp.bfloat16)
    grad_qkv = jnp.transpose(grad_qkv, (1, 2, 0, 3)).reshape(tok_count, 3 * D)
    grad_w_qkv = inner_rows(inputs, grad_qkv)
    grad_bias_qkv = jnp.sum(grad_qkv.astype(jnp.float32), axis=0)
    grad_inputs = grad_first + outer_cols(grad_qkv, w_qkv)
    grad_blocks = jnp.concatenate(
        [
            grad_w_qkv.reshape(D, 3, D),
            grad_w_out[:, None, :],
            grad_w_up.reshape(D, FF // D, D),
            jnp.transpose(grad_w_down.reshape(FF // D, D, D), (1, 0, 2)),
        ],
        axis=1,
    )
    by_block = jnp.transpose(grad_blocks, (1, 0, 2))
    slot_grads = jnp.stack([pick(by_block, slot_block[s]) for s in range(by_block.shape[0])], axis=1)
    vector_grads = jnp.concatenate(
        [
            jnp.stack(
                [
                    grad_gain_one,
                    grad_shift_one,
                    grad_gain_two,
                    grad_shift_two,
                    grad_bias_qkv[:D],
                    grad_bias_qkv[2 * D :],
                    grad_bias_out,
                    grad_bias_down,
                ]
            ),
            grad_bias_up.reshape(FF // D, D),
        ],
        axis=0,
    )
    vector_total = lax.psum(vector_grads, ("tok", "grp"))
    row_total = lax.psum_scatter(slot_grads, "tok", scatter_dimension=0, tiled=True)
    reduced = lax.psum_scatter(
        row_total.astype(jnp.bfloat16), "grp", scatter_dimension=1, tiled=True
    ).astype(jnp.float32)
    left_basis = bases[0]
    right_basis = bases[1]
    first_row = lax.axis_index("tok") * rows_dev
    turned_in = jnp.einsum("rse,sef->rsf", reduced, right_basis, precision=lax.Precision.HIGHEST)
    left_rows = lax.dynamic_slice_in_dim(left_basis, first_row, rows_dev, 1)
    picked = left_rows
    rotated = lax.psum_scatter(
        jnp.einsum("sri,rsf->isf", picked, turned_in, precision=lax.Precision.HIGHEST),
        "tok",
        scatter_dimension=0,
        tiled=True,
    )
    new_one = BETA_ONE * moment_one + (1.0 - BETA_ONE) * rotated
    new_two = BETA_TWO * moment_two + (1.0 - BETA_TWO) * rotated * rotated
    direction = new_one / (jnp.sqrt(new_two) + ADAM_EPS)
    turned_out = jnp.einsum("rse,sfe->rsf", direction, right_basis, precision=lax.Precision.HIGHEST)
    left_cols = lax.dynamic_slice_in_dim(left_basis, first_row, rows_dev, 2)
    picked = left_cols
    change = lax.psum_scatter(
        jnp.einsum("sir,rsf->isf", picked, turned_out, precision=lax.Precision.HIGHEST),
        "tok",
        scatter_dimension=0,
        tiled=True,
    )
    new_master = master - RATE_MATRIX * change
    new_vec_one = BETA_ONE * vector_one + (1.0 - BETA_ONE) * vector_total
    new_vec_two = BETA_TWO * vector_two + (1.0 - BETA_TWO) * vector_total * vector_total
    new_vectors = vectors - RATE_VECTOR * new_vec_one / (jnp.sqrt(new_vec_two) + ADAM_EPS)
    return (
        result[None],
        grad_inputs[None],
        new_one,
        new_two,
        new_master,
        new_vec_one,
        new_vec_two,
        new_vectors,
    )

def solution(mesh):
    n_tok, n_grp = mesh.shape["tok"], mesh.shape["grp"]

    def on_device(*args):
        lengths, clusters = args[2], args[3]
        unit = n_tok // (lengths.shape[1] - 1)
        suits = unit == UNIT and n_tok == 2 * UNIT and n_grp == 4 and clusters.shape[2] == 1024
        return (fast if suits else general)(*args)

    return jax.shard_map(
        on_device,
        mesh=mesh,
        in_specs=(
            P("grp", "tok", None),
            P("grp", "tok", None),
            P("grp", None),
            P("grp", None, "tok"),
            P(),
            P("tok", "grp", None),
            P(None, "grp", None, None),
            P("tok", "grp", None),
            P("tok", "grp", None),
            P(),
            P(),
            P(),
        ),
        out_specs=(
            P("grp", "tok", None),
            P("grp", "tok", None),
            P("tok", "grp", None),
            P("tok", "grp", None),
            P("tok", "grp", None),
            P(),
            P(),
            P(),
        ),
        check_vma=False,
    )
```

```python
import functools

import jax
import jax.numpy as jnp
from jax import lax
from jax.experimental import pallas as pl
from jax.experimental.pallas import tpu as pltpu
from jax.sharding import PartitionSpec as P

D = 768
H = 12
FF = 3072
HEAD = 64
ROUNDS = 2
PAIRS = 24
CLUSTER = 128
FFB = FF // D

EPS_NORM = 1e-05
ADAM_EPS = 1e-08
BETA_ONE = 0.5
BETA_TWO = 0.5
RATE_MATRIX = 0.025
RATE_VECTOR = 0.15
SQRT_HALF = 0.7071067811865476
INV_ROOT_TWO_PI = 0.3989422804014327

BF16 = jnp.bfloat16
F32 = jnp.float32

UNIT = 4
HEADS_OWN = H // UNIT
LOCAL_PAIRS = ROUNDS * HEADS_OWN
TILE = 128
WIDE = 2 * TILE
SMALL = pl.CostEstimate(flops=0, transcendentals=0, bytes_accessed=0)


def inner_rows(left, right):
    return lax.dot_general(left, right, (((0,), (0,)), ((), ())), preferred_element_type=F32)


def outer_cols(left, right):
    return lax.dot_general(left, right, (((1,), (1,)), ((), ())), preferred_element_type=F32)


def normalize(values_in):
    centre = jnp.mean(values_in, axis=-1, keepdims=True)
    offset = values_in - centre
    spread = jnp.mean(offset * offset, axis=-1, keepdims=True)
    rstd = lax.rsqrt(spread + EPS_NORM)
    return (offset * rstd, rstd)


def norm_back(grad_normed, normed, rstd):
    first_mean = jnp.mean(grad_normed, axis=-1, keepdims=True)
    second_mean = jnp.mean(grad_normed * normed, axis=-1, keepdims=True)
    return rstd * (grad_normed - first_mean - normed * second_mean)


def gelu_slope(values_in):
    return (
        0.5 * (1.0 + lax.erf(values_in * SQRT_HALF))
        + values_in * jnp.exp(-0.5 * values_in * values_in) * INV_ROOT_TWO_PI
    )


def turn_half(value):
    return pltpu.roll(value, HEAD, 1)


def places_body(scalars_ref, clusters_ref, *refs):
    outs, all_ref = refs[:UNIT], refs[UNIT]
    pairs, count = clusters_ref.shape
    share, member = scalars_ref[0], scalars_ref[1]
    kinds = UNIT * count // CLUSTER
    kind = lax.broadcasted_iota(jnp.int32, (kinds, count), 0)
    earlier = lax.broadcasted_iota(jnp.int32, (count, count), 0) < lax.broadcasted_iota(jnp.int32, (count, count), 1)
    earlier = earlier.astype(F32).astype(BF16)
    all_ref[...] = jnp.zeros_like(all_ref)
    for pair in range(pairs):
        turn, head = pair // H, pair % H
        cluster = clusters_ref[pair : pair + 1, :]
        same = (kind == cluster).astype(F32)
        before = jnp.dot(same.astype(BF16), earlier, preferred_element_type=F32)
        rank = jnp.sum(same * before, axis=0, keepdims=True).astype(jnp.int32)
        own = head % HEADS_OWN * ROUNDS + turn
        all_ref[head // HEADS_OWN, own : own + 1, :] = cluster * share + rank
    for k in range(UNIT):
        outs[k][...] = all_ref[member ^ k]


def places(scalars, clusters):
    count = clusters.shape[1]
    inside = pl.BlockSpec(memory_space=pltpu.VMEM)
    return pl.pallas_call(
        places_body,
        in_specs=[pl.BlockSpec(memory_space=pltpu.SMEM), inside],
        out_specs=[inside] * UNIT,
        out_shape=[jax.ShapeDtypeStruct((8, count), jnp.int32)] * UNIT,
        scratch_shapes=[pltpu.VMEM((UNIT, 8, count), jnp.int32)],
        cost_estimate=SMALL,
        name="places",
    )(scalars, clusters)


def arrange_body(slots, scalars_ref, *refs):
    sources, outs, rest_ref, tiles_ref = refs[:4], refs[4 : 4 + UNIT], refs[4 + UNIT], refs[5 + UNIT]
    n_rest, count = rest_ref.shape[:2]
    n_blocks = n_rest + 3
    group, core, member = (scalars_ref[n_blocks + i] for i in range(3))
    first = pl.multiple_of(core * count, count)

    def rows_of(block):
        slot = scalars_ref[block]
        owner = lax.div(slot, slots)
        near, inner = owner ^ group, lax.rem(slot, slots)
        found = [source[inner, pl.ds(first, count), :].astype(F32) for source in sources]
        low = jnp.where(near % 2 == 0, found[0], found[1])
        high = jnp.where(near % 2 == 0, found[2], found[3])
        return jnp.where(near < 2, low, high)

    low = lax.broadcasted_iota(jnp.int32, (count, TILE), 1) < HEAD
    parts = [rows_of(i) for i in range(3)]

    def half(part, head, high):
        at = head // 2 * TILE
        tile = parts[part][:, at : at + TILE]
        return tile if head % 2 == high else turn_half(tile)

    for head in range(H):
        own = head % HEADS_OWN
        odd = own % 2
        value = half(2, head, odd)
        query = half(0, head, 1 - odd)
        keys = half(1, head, 1 - odd)
        one = jnp.where(low, query, value) if odd else jnp.where(low, value, query)
        two = jnp.where(low, keys, 0.0) if odd else jnp.where(low, 0.0, keys)
        tiles_ref[head // HEADS_OWN, :, own * WIDE : own * WIDE + TILE] = one.astype(BF16)
        tiles_ref[head // HEADS_OWN, :, own * WIDE + TILE : (own + 1) * WIDE] = two.astype(BF16)
    for k in range(UNIT):
        outs[k][...] = tiles_ref[member ^ k]
    for b in range(n_rest):
        rest_ref[b] = rows_of(3 + b).astype(BF16)


def arrange(scalars, sources, n_blocks):
    slots, rows = sources[0].shape[:2]
    count = rows // 2
    width = HEADS_OWN * WIDE
    inside = pl.BlockSpec(memory_space=pltpu.VMEM)
    return pl.pallas_call(
        functools.partial(arrange_body, slots),
        in_specs=[pl.BlockSpec(memory_space=pltpu.SMEM)] + [inside] * 4,
        out_specs=[inside] * (UNIT + 1),
        out_shape=[jax.ShapeDtypeStruct((count, width), BF16)] * UNIT
        + [jax.ShapeDtypeStruct((n_blocks - 3, count, D), BF16)],
        scratch_shapes=[pltpu.VMEM((UNIT, count, width), BF16)],
        compiler_params=pltpu.CompilerParams(vmem_limit_bytes=32 << 20),
        cost_estimate=SMALL,
        name="arrange",
    )(scalars, *sources)


def assemble_body(table_ref, *refs):
    shards, out_ref, sem = refs[:-2], refs[-2], refs[-1]
    rows = shards[0].shape[1]
    copies = []
    for shard in shards:
        for i in range(shard.shape[0]):
            n = len(copies)
            first = pl.multiple_of(table_ref[n], rows)
            copies.append(
                pltpu.make_async_copy(shard.at[i], out_ref.at[pl.ds(first, rows), :], sem.at[n])
            )
    for copy in copies:
        copy.start()
    for copy in copies:
        copy.wait()


def assemble(table, shards):
    pieces = sum(s.shape[0] for s in shards)
    anywhere = pl.BlockSpec(memory_space=pl.ANY)
    return pl.pallas_call(
        assemble_body,
        in_specs=[pl.BlockSpec(memory_space=pltpu.SMEM)] + [anywhere] * len(shards),
        out_specs=pl.BlockSpec(memory_space=pltpu.VMEM),
        out_shape=jax.ShapeDtypeStruct((pieces * shards[0].shape[1], shards[0].shape[2]), BF16),
        scratch_shapes=[pltpu.SemaphoreType.DMA((pieces,))],
        cost_estimate=SMALL,
        name="assemble",
    )(table, *shards)


def sort_body(place_ref, x_ref, weight_ref, bias_ref, out_ref, rows_ref):
    count = x_ref.shape[0]
    head = pl.program_id(0)
    chunk = 256
    row = lax.broadcasted_iota(jnp.int32, (chunk, count), 0)
    rows_ref[...] = (
        jnp.dot(x_ref[...], weight_ref[...], preferred_element_type=F32) + bias_ref[...]
    ).astype(BF16)
    for step in range(HEADS_OWN):

        @pl.when(head == step)
        def _():
            for turn in range(ROUNDS):
                pair = step * ROUNDS + turn
                for part in range(count // chunk):
                    where = pl.ds(part * chunk, chunk)
                    picked = place_ref[pair : pair + 1, :] == row + part * chunk
                    picked = picked.astype(F32).astype(BF16)
                    out_ref[turn, where, :] = jnp.dot(
                        picked, rows_ref[...], preferred_element_type=F32
                    ).astype(BF16)


def sort_rows(order, inputs, weights, bias):
    count = inputs.shape[0]
    return pl.pallas_call(
        sort_body,
        grid=(HEADS_OWN,),
        in_specs=[
            pl.BlockSpec((8, count), lambda h: (0, 0)),
            pl.BlockSpec((count, D), lambda h: (0, 0)),
            pl.BlockSpec((D, WIDE), lambda h: (0, h)),
            pl.BlockSpec((1, WIDE), lambda h: (0, h)),
        ],
        out_specs=pl.BlockSpec((ROUNDS, count, WIDE), lambda h: (h, 0, 0)),
        out_shape=jax.ShapeDtypeStruct((LOCAL_PAIRS, count, WIDE), BF16),
        scratch_shapes=[pltpu.VMEM((count, WIDE), BF16)],
        compiler_params=pltpu.CompilerParams(vmem_limit_bytes=48 << 20),
        cost_estimate=SMALL,
        name="sort_rows",
    )(order, inputs, weights, bias)


def sort_grads_body(place_ref, rows_ref, out_ref):
    count = place_ref.shape[1]
    half = count // 2
    head = pl.program_id(0)
    chunk = 256
    row = lax.broadcasted_iota(jnp.int32, (chunk, count), 0)
    low = lax.broadcasted_iota(jnp.int32, (count, TILE), 1) < HEAD
    for step in range(HEADS_OWN):

        @pl.when(head == step)
        def _():
            if step < 2:
                tile = rows_ref[0:count, :].astype(F32)
                tile = jnp.where(low if step == 0 else jnp.logical_not(low), tile, 0.0).astype(BF16)
            else:
                both = rows_ref[count : count + half, :].astype(F32)
                tile = jnp.concatenate([both, turn_half(both)], axis=0)
                tile = jnp.where(low, tile, 0.0).astype(BF16)
            for turn in range(ROUNDS):
                pair = step * ROUNDS + turn
                for part in range(count // chunk):
                    where = pl.ds(part * chunk, chunk)
                    picked = place_ref[pair : pair + 1, :] == row + part * chunk
                    picked = picked.astype(F32).astype(BF16)
                    out_ref[turn, where, :] = jnp.dot(
                        picked, tile, preferred_element_type=F32
                    ).astype(BF16)


def sort_grads(order, rows):
    count = order.shape[1]
    return pl.pallas_call(
        sort_grads_body,
        grid=(HEADS_OWN,),
        in_specs=[
            pl.BlockSpec((8, count), lambda h: (0, 0)),
            pl.BlockSpec(rows.shape, lambda h: (0, 0)),
        ],
        out_specs=pl.BlockSpec((ROUNDS, count, TILE), lambda h: (h, 0, 0)),
        out_shape=jax.ShapeDtypeStruct((LOCAL_PAIRS, count, TILE), BF16),
        compiler_params=pltpu.CompilerParams(vmem_limit_bytes=48 << 20),
        cost_estimate=SMALL,
        name="sort_grads",
    )(order, rows)


def plans_of(count):
    share = CLUSTER // UNIT
    half = UNIT // 2
    return (
        [(tuple(range(UNIT)), share)],
        [(tuple(range(i * half, (i + 1) * half)), 2 * share) for i in range(2)],
    )


def for_each_batch(is_long, count, batch, work):
    for wanted, plan in zip((1, 0), plans_of(count)):

        @pl.when(is_long == wanted)
        def _(plan=plan):
            for runs, share in plan:

                def step(group, carry, runs=runs, share=share):
                    first = pl.multiple_of(group * (batch * share), batch * share)
                    work(runs, pl.ds(first, batch * share), share)
                    return carry

                lax.fori_loop(0, count // share // batch, step, 0)


def batch_of(refs, runs, where, share, width):
    parts = [refs[r][0, where, :] for r in runs]
    return jnp.concatenate([p.reshape(p.shape[0] // share, share, width) for p in parts], axis=1)


def spread(refs, runs, where, share, columns, value):
    for i, r in enumerate(runs):
        part = value[:, i * share : (i + 1) * share]
        refs[r][0, where, columns] = part.reshape(part.shape[0] * share, TILE)


def products(form, left, right):
    return jnp.einsum(form, left, right, preferred_element_type=F32)


def softmax(first, second):
    scores = products("ued,ucd->uec", second, first) * (HEAD**-0.5)
    expo = jnp.exp(scores - jnp.max(scores, axis=1, keepdims=True))
    return expo * (1.0 / jnp.sum(expo, axis=1, keepdims=True))


def attend_body(long_ref, *refs):
    grouped, results = refs[:UNIT], refs[UNIT:]

    def work(runs, where, share):
        rows = batch_of(grouped, runs, where, share, WIDE)
        first = rows[..., :TILE]
        probs = softmax(first, rows[..., TILE:]).astype(BF16)
        mixed = products("uce,ued->ucd", jnp.swapaxes(probs, 1, 2), first).astype(BF16)
        spread(results, runs, where, share, slice(0, TILE), mixed)

    for_each_batch(long_ref[0], grouped[0].shape[1], 8, work)


def attend(is_long, grouped):
    count = grouped[0].shape[1]
    return pl.pallas_call(
        attend_body,
        grid_spec=pltpu.PrefetchScalarGridSpec(
            num_scalar_prefetch=1,
            grid=(LOCAL_PAIRS,),
            in_specs=[pl.BlockSpec((1, count, WIDE), lambda p, _: (p, 0, 0))] * UNIT,
            out_specs=[pl.BlockSpec((1, count, TILE), lambda p, _: (p, 0, 0))] * UNIT,
        ),
        out_shape=[jax.ShapeDtypeStruct((LOCAL_PAIRS, count, TILE), BF16)] * UNIT,
        compiler_params=pltpu.CompilerParams(vmem_limit_bytes=48 << 20),
        cost_estimate=SMALL,
        name="attend",
    )(is_long, *grouped)


def attend_back_body(long_ref, *refs):
    grouped, grads, results = refs[:UNIT], refs[UNIT : 2 * UNIT], refs[2 * UNIT :]
    batch = 16
    odd = (pl.program_id(0) // ROUNDS) % 2
    lane = lax.broadcasted_iota(jnp.int32, (batch, CLUSTER, TILE), 2)
    value_lane = (lane < HEAD) == (odd == 0)
    scale = HEAD**-0.5

    def work(runs, where, share):
        rows = batch_of(grouped, runs, where, share, WIDE)
        grad = batch_of(grads, runs, where, share, TILE)
        first, second = rows[..., :TILE], rows[..., TILE:]
        probs = softmax(first, second)
        grad_probs = products("ued,ucd->uec", first, grad)
        centre = jnp.sum(probs * grad_probs, axis=1, keepdims=True)
        grad_scores = (probs * (grad_probs - centre)).astype(BF16)
        grad_values = products("uec,ucd->ued", probs.astype(BF16), grad)
        grad_keys = products("uec,ucd->ued", grad_scores, first) * scale
        grad_query = products("uce,ued->ucd", jnp.swapaxes(grad_scores, 1, 2), second) * scale
        tile_one = jnp.where(value_lane, grad_values, grad_query).astype(BF16)
        tile_two = jnp.where(value_lane, 0.0, grad_keys).astype(BF16)
        spread(results, runs, where, share, slice(0, TILE), tile_one)
        spread(results, runs, where, share, slice(TILE, WIDE), tile_two)

    for_each_batch(long_ref[0], grouped[0].shape[1], batch, work)


def attend_back(is_long, grouped, grads):
    count = grouped[0].shape[1]
    return pl.pallas_call(
        attend_back_body,
        grid_spec=pltpu.PrefetchScalarGridSpec(
            num_scalar_prefetch=1,
            grid=(LOCAL_PAIRS,),
            in_specs=[pl.BlockSpec((1, count, WIDE), lambda p, _: (p, 0, 0))] * UNIT
            + [pl.BlockSpec((1, count, TILE), lambda p, _: (p, 0, 0))] * UNIT,
            out_specs=[pl.BlockSpec((1, count, WIDE), lambda p, _: (p, 0, 0))] * UNIT,
        ),
        out_shape=[jax.ShapeDtypeStruct((LOCAL_PAIRS, count, WIDE), BF16)] * UNIT,
        compiler_params=pltpu.CompilerParams(vmem_limit_bytes=56 << 20),
        cost_estimate=SMALL,
        name="attend_back",
    )(is_long, *grouped, *grads)


def unsorted(column_ref, step, rows_ref, part, chunk):
    count = rows_ref.shape[1]
    where = pl.ds(part * chunk, chunk)
    lane = lax.broadcasted_iota(jnp.int32, (chunk, count), 1)
    total = None
    for turn in range(ROUNDS):
        pair = step * ROUNDS + turn
        picked = (column_ref[where, pair : pair + 1] == lane).astype(F32).astype(BF16)
        more = jnp.dot(picked, rows_ref[turn], preferred_element_type=F32)
        total = more if total is None else total + more
    return total


def mix_body(place_ref, rows_ref, out_ref, column_ref):
    @pl.when(pl.program_id(0) == 0)
    def _():
        column_ref[...] = jnp.transpose(place_ref[...])

    count = rows_ref.shape[1]
    chunk = 256
    parts = count // chunk
    low = lax.broadcasted_iota(jnp.int32, (chunk, TILE), 1) < HEAD
    head = pl.program_id(0)
    for step in range(HEADS_OWN):

        @pl.when(head == step)
        def _():
            means = [0.5 * unsorted(column_ref, step, rows_ref, part, chunk) for part in range(parts)]
            for part in range(parts):
                where = pl.ds(part * chunk, chunk)
                if step == 0:
                    out_ref[where, :] = means[part].astype(BF16)
                elif step == 1:
                    out_ref[where, :] = jnp.where(low, out_ref[where, :].astype(F32), means[part]).astype(BF16)
                elif part < parts // 2:
                    both = jnp.where(low, means[part], turn_half(means[part + parts // 2]))
                    out_ref[pl.ds(count + part * chunk, chunk), :] = both.astype(BF16)


def mix(order, rows):
    count = rows.shape[1]
    packed = (count + count // 2, TILE)
    return pl.pallas_call(
        mix_body,
        grid=(HEADS_OWN,),
        in_specs=[
            pl.BlockSpec((8, count), lambda h: (0, 0)),
            pl.BlockSpec((ROUNDS, count, TILE), lambda h: (h, 0, 0)),
        ],
        out_specs=pl.BlockSpec(packed, lambda h: (0, 0)),
        out_shape=jax.ShapeDtypeStruct(packed, BF16),
        scratch_shapes=[pltpu.VMEM((count, 8), jnp.int32)],
        compiler_params=pltpu.CompilerParams(vmem_limit_bytes=48 << 20),
        cost_estimate=SMALL,
        name="mix",
    )(order, rows)


def gather_grads_body(place_ref, rows_ref, out_ref, column_ref):
    @pl.when(pl.program_id(0) == 0)
    def _():
        column_ref[...] = jnp.transpose(place_ref[...])

    count = rows_ref.shape[1]
    chunk = 256
    head = pl.program_id(0)
    for step in range(HEADS_OWN):

        @pl.when(head == step)
        def _():
            for part in range(count // chunk):
                where = pl.ds(part * chunk, chunk)
                out_ref[where, :] = unsorted(column_ref, step, rows_ref, part, chunk).astype(BF16)


def gather_grads(order, rows):
    count = rows.shape[1]
    return pl.pallas_call(
        gather_grads_body,
        grid=(HEADS_OWN,),
        in_specs=[
            pl.BlockSpec((8, count), lambda h: (0, 0)),
            pl.BlockSpec((ROUNDS, count, WIDE), lambda h: (h, 0, 0)),
        ],
        out_specs=pl.BlockSpec((count, WIDE), lambda h: (0, h)),
        out_shape=jax.ShapeDtypeStruct((count, HEADS_OWN * WIDE), BF16),
        scratch_shapes=[pltpu.VMEM((count, 8), jnp.int32)],
        compiler_params=pltpu.CompilerParams(vmem_limit_bytes=48 << 20),
        cost_estimate=SMALL,
        name="gather_grads",
    )(order, rows)


ERF_TOP = (0.00022905065861350646, 0.0034082910107109506, 0.050955695062380861, 0.18520832239976145, 1.128379143519084)
ERF_BOTTOM = (
    -1.1791602954361697e-7,
    0.000023547966471313185,
    0.0010179625278914885,
    0.014070470171167667,
    0.11098505178285362,
    0.49746925110067538,
    1.0,
)


def polynomial(value, factors):
    total = jnp.full_like(value, factors[0])
    for factor in factors[1:]:
        total = total * value + factor
    return total


def error_function(value):
    value = jnp.clip(value, -3.832506856900711, 3.832506856900711)
    square = value * value
    return value * polynomial(square, ERF_TOP) / polynomial(square, ERF_BOTTOM)


VEC_ROWS = 16
FFN_TILE = 256


def layer_body(
    n_shards,
    table_ref,
    *refs,
):
    shards, refs = refs[:n_shards], refs[n_shards:]
    parts, refs = refs[:UNIT], refs[UNIT:]
    x_ref, cot_ref, vec_ref, result_ref, first_ref, sums_ref, kept_ref, sent_ref = refs[:8]
    backs, refs = refs[8 : 8 + UNIT], refs[8 + UNIT :]
    w_ref, packed_ref, mixed_ref, hidden_ref, act_ref, down_ref, up_ref, attn_ref, back_ref = refs[:9]
    slope_ref, stage_ref, weight_sem, part_sem, stage_sem = refs[9:]
    count = x_ref.shape[0]
    half = count // 2
    per_shard, n_weights, shard_rows = shards[0].shape[:3]
    member = table_ref[0]
    for k in range(UNIT):
        pltpu.make_async_copy(parts[k], packed_ref.at[member ^ k], part_sem.at[k]).start()
    for b in range(n_weights):
        for n in range(n_shards * per_shard):
            row = pl.multiple_of(table_ref[6 + n], shard_rows)
            pltpu.make_async_copy(
                shards[n // per_shard].at[n % per_shard, b], w_ref.at[b, pl.ds(row, shard_rows), :], weight_sem.at[b]
            ).start()
    for k in range(UNIT):
        pltpu.make_async_copy(parts[k], packed_ref.at[member ^ k], part_sem.at[k]).wait()
    for b in range(n_weights):
        pltpu.make_async_copy(w_ref.at[b], w_ref.at[b], weight_sem.at[b]).wait()

    sums_ref[...] = jnp.zeros_like(sums_ref)
    low = lax.broadcasted_iota(jnp.int32, (FFN_TILE, TILE), 1) < HEAD
    vec = [vec_ref[i : i + 1, :] for i in range(8 + FFB)]
    gain_one, shift_one, gain_two, shift_two = vec[:4]
    bias_out, bias_down = vec[6], vec[7]

    def add_sum(row, value):
        sums_ref[row : row + 1, :] += jnp.sum(value, axis=0, keepdims=True)

    def tile_step(i, carry):
        rows = pl.ds(pl.multiple_of(i * FFN_TILE, FFN_TILE), FFN_TILE)
        is_first = i * FFN_TILE < half
        extra = pl.ds(pl.multiple_of(count + lax.rem(i * FFN_TILE, half), FFN_TILE), FFN_TILE)

        def pair(m):
            return packed_ref[m, rows, :].astype(F32)

        def single(m):
            value = packed_ref[m, extra, :].astype(F32)
            return jnp.where(is_first, value, turn_half(value))

        for m in (0, 2):
            at = m * (HEADS_OWN * HEAD)
            nxt = turn_half(pair(m + 1))
            mixed_ref[rows, at : at + TILE] = pair(m).astype(BF16)
            mixed_ref[rows, at + TILE : at + 2 * TILE] = jnp.where(low, single(m), nxt).astype(BF16)
            mixed_ref[rows, at + 2 * TILE : at + 3 * TILE] = jnp.where(
                low, nxt, turn_half(single(m + 1))
            ).astype(BF16)
        attention = jnp.dot(mixed_ref[rows, :], w_ref[0], preferred_element_type=F32) + bias_out
        normed_one, rstd_one = normalize(x_ref[rows, :].astype(F32) + attention)
        hidden = normed_one * gain_one + shift_one
        hidden_low = hidden.astype(BF16)
        hidden_ref[rows, :] = hidden_low
        down = jnp.broadcast_to(bias_down, hidden.shape)
        for j in range(FFB):
            up = jnp.dot(hidden_low, w_ref[1 + j], preferred_element_type=F32) + vec[8 + j]
            phi = 0.5 * (1.0 + error_function(up * SQRT_HALF))
            slope_ref[j] = phi + up * jnp.exp(-0.5 * up * up) * INV_ROOT_TWO_PI
            act = (up * phi).astype(BF16)
            act_ref[j, rows, :] = act
            down = down + jnp.dot(act, w_ref[1 + FFB + j], preferred_element_type=F32)
        normed_two, rstd_two = normalize(hidden + down)
        result_ref[rows, :] = (normed_two * gain_two + shift_two).astype(BF16)
        grad_result = cot_ref[rows, :].astype(F32)
        add_sum(2, grad_result * normed_two)
        add_sum(3, grad_result)
        grad_second = norm_back(grad_result * gain_two, normed_two, rstd_two)
        grad_down = grad_second.astype(BF16)
        down_ref[rows, :] = grad_down
        add_sum(7, grad_down.astype(F32))
        grad_hidden = grad_second
        for j in range(FFB):
            grad_up = (outer_cols(grad_down, w_ref[1 + FFB + j]) * slope_ref[j]).astype(BF16)
            up_ref[j, rows, :] = grad_up
            add_sum(8 + j, grad_up.astype(F32))
            grad_hidden = grad_hidden + outer_cols(grad_up, w_ref[1 + j])
        add_sum(0, grad_hidden * normed_one)
        add_sum(1, grad_hidden)
        grad_first = norm_back(grad_hidden * gain_one, normed_one, rstd_one)
        first_ref[rows, :] = grad_first
        grad_attn = grad_first.astype(BF16)
        attn_ref[rows, :] = grad_attn
        add_sum(6, grad_attn.astype(F32))
        grad_mixed = (0.5 * outer_cols(grad_attn, w_ref[0])).astype(BF16).astype(F32)
        for m in range(UNIT):
            at = (m // 2) * 3 * TILE
            tiles = [grad_mixed[:, at + n * TILE : at + (n + 1) * TILE] for n in range(3)]
            if m % 2 == 0:
                two, one = tiles[0], tiles[1]
            else:
                two, one = turn_half(jnp.where(low, tiles[2], tiles[1])), turn_half(tiles[2])
            back_ref[member ^ m, rows, :] = two.astype(BF16)

            @pl.when(is_first)
            def _(one=one, m=m):
                back_ref[member ^ m, extra, :] = jnp.where(low, one, 0.0).astype(BF16)

            @pl.when(jnp.logical_not(is_first))
            def _(one=one, m=m):
                old = back_ref[member ^ m, extra, :].astype(F32)
                back_ref[member ^ m, extra, :] = jnp.where(low, old, turn_half(one)).astype(BF16)

        return carry

    lax.fori_loop(0, count // FFN_TILE, tile_step, 0)
    for k in range(UNIT):
        backs[k][...] = back_ref[k]

    core, bits = table_ref[1], [table_ref[2 + d] for d in range(4)]
    piece, half_columns = kept_ref.shape[3:]
    n_parts = kept_ref.shape[0]
    per_part = n_weights // n_parts

    def copies(block, slot, half, target):
        part = block // per_part
        made = []
        for index in range(16):
            x, zh, y, zl = ((index >> s) % 2 for s in range(4))
            rel = {"x": x ^ bits[0], "y": y ^ bits[1], "zl": zl ^ bits[2], "zh": zh ^ bits[3]}
            place = 0
            for name in PART_ORDERS[part]:
                place = place * 2 + rel[name]
            made.append(
                pltpu.make_async_copy(
                    stage_ref.at[
                        slot, pl.ds(index * piece, piece), pl.ds(half * half_columns, half_columns)
                    ],
                    target.at[part, place, block % per_part],
                    stage_sem.at[slot, half * 16 + index],
                )
            )
        return made

    def send(block, slot):
        for half in range(2):

            @pl.when(core == half)
            def _(half=half):
                for copy in copies(block, slot, half, kept_ref):
                    copy.start()

            @pl.when(core != half)
            def _(half=half):
                for copy in copies(block, slot, half, sent_ref):
                    copy.start()

    def sent(block, slot):
        for half in range(2):
            for copy in copies(block, slot, half, kept_ref):
                copy.wait()

    plan = [(attn_ref, None, mixed_ref, None, 0)]
    plan += [(down_ref, None, act_ref, j, 1 + FFB + j) for j in range(FFB)]
    plan += [(up_ref, j, hidden_ref, None, 1 + j) for j in range(FFB)]
    for n, (left, lj, right, rj, block) in enumerate(plan):
        slot = n % 2
        if n >= 2:
            sent(plan[n - 2][4], slot)
        value = inner_rows(
            left[...] if lj is None else left[lj], right[...] if rj is None else right[rj]
        )
        stage_ref[slot] = value.astype(BF16)
        send(block, slot)
    for n in (len(plan) - 2, len(plan) - 1):
        sent(plan[n][4], n % 2)


PART_ORDERS = (("x", "y", "zl", "zh"), ("y", "zl", "zh", "x"), ("zl", "zh", "x", "y"))


def layer(table, shards, parts, inputs, cotangent, vectors):
    count = inputs.shape[0]
    n_weights = 1 + 2 * FFB
    n_shards = len(shards)
    anywhere = pl.BlockSpec(memory_space=pl.ANY)
    inside = pl.BlockSpec(memory_space=pltpu.VMEM)
    packed = parts[0].shape
    return pl.pallas_call(
        functools.partial(layer_body, n_shards),
        in_specs=[pl.BlockSpec(memory_space=pltpu.SMEM)] + [anywhere] * (n_shards + UNIT) + [inside] * 3,
        out_specs=[inside, inside, inside, anywhere, anywhere] + [inside] * UNIT,
        out_shape=[
            jax.ShapeDtypeStruct((count, D), BF16),
            jax.ShapeDtypeStruct((count, D), F32),
            jax.ShapeDtypeStruct((VEC_ROWS, D), F32),
            jax.ShapeDtypeStruct((3, 16, n_weights // 3, D // 16, D // 2), BF16),
            jax.ShapeDtypeStruct((3, 16, n_weights // 3, D // 16, D // 2), BF16),
        ]
        + [jax.ShapeDtypeStruct(packed, BF16)] * UNIT,
        scratch_shapes=[
            pltpu.VMEM((n_weights, D, D), BF16),
            pltpu.VMEM((UNIT, *packed), BF16),
            pltpu.VMEM((count, D), BF16),
            pltpu.VMEM((count, D), BF16),
            pltpu.VMEM((FFB, count, D), BF16),
            pltpu.VMEM((count, D), BF16),
            pltpu.VMEM((FFB, count, D), BF16),
            pltpu.VMEM((count, D), BF16),
            pltpu.VMEM((UNIT, *packed), BF16),
            pltpu.VMEM((FFB, FFN_TILE, D), F32),
            pltpu.VMEM((2, D, D), BF16),
            pltpu.SemaphoreType.DMA((n_weights,)),
            pltpu.SemaphoreType.DMA((UNIT,)),
            pltpu.SemaphoreType.DMA((2, 32)),
        ],
        compiler_params=pltpu.CompilerParams(vmem_limit_bytes=60 << 20),
        cost_estimate=SMALL,
        name="layer",
    )(table, *shards, *parts, inputs, cotangent, vectors)


def qkv_back_body(scalars_ref, *refs):
    grads, inputs, kept_ref, sent_ref, bias_ref, all_ref = refs[:4], refs[4:8], *refs[8:]
    core, unit = scalars_ref[0], scalars_ref[1]
    columns = all_ref.shape[4]
    step = 32
    per_unit = all_ref.shape[3]
    bias_ref[...] = jnp.zeros_like(bias_ref)
    for head in range(HEADS_OWN):
        at = slice(head * WIDE, (head + 1) * WIDE)
        total = inner_rows(grads[0][:, at], inputs[0][...])
        bias = jnp.sum(grads[0][:, at].astype(F32), axis=0, keepdims=True)
        for k in range(1, UNIT):
            total = total + inner_rows(grads[k][:, at], inputs[k][...])
            bias = bias + jnp.sum(grads[k][:, at].astype(F32), axis=0, keepdims=True)
        bias_ref[0:1, at] = bias
        firsts = (HEAD, 3 * HEAD, 0) if head % 2 == 0 else (0, 2 * HEAD, HEAD)
        for block, first in enumerate(firsts):
            for i in range(HEAD // step):
                row = head * HEAD + i * step
                rows = total[first + i * step : first + (i + 1) * step]
                for c in range(2):
                    all_ref[
                        c ^ core, row // per_unit ^ unit, block, row % per_unit : row % per_unit + step, :
                    ] = rows[:, c * columns : (c + 1) * columns].astype(BF16)
    kept_ref[...] = all_ref[0]
    sent_ref[...] = all_ref[1]


def qkv_back(scalars, grads, inputs):
    inside = pl.BlockSpec(memory_space=pltpu.VMEM)
    shape = (2, 3, HEADS_OWN * HEAD // 2, D // 2)
    return pl.pallas_call(
        qkv_back_body,
        in_specs=[pl.BlockSpec(memory_space=pltpu.SMEM)] + [inside] * (2 * UNIT),
        out_specs=[inside] * 3,
        out_shape=[
            jax.ShapeDtypeStruct(shape, BF16),
            jax.ShapeDtypeStruct(shape, BF16),
            jax.ShapeDtypeStruct((8, HEADS_OWN * WIDE), F32),
        ],
        scratch_shapes=[pltpu.VMEM((2, *shape), BF16)],
        compiler_params=pltpu.CompilerParams(vmem_limit_bytes=56 << 20),
        cost_estimate=SMALL,
        name="qkv_back",
    )(scalars, *grads, *inputs)


def pack_body(slot_block_ref, *refs):
    half = (len(refs) - 2) // 2
    kept, got, out_ref, all_ref = refs[:half], refs[half : 2 * half], refs[-2], refs[-1]
    per_part = kept[0].shape[1]
    for p in range(half):
        for b in range(per_part):
            all_ref[p * per_part + b] = (kept[p][0, b] + got[p][0, b].astype(F32)).astype(BF16)
    for s in range(out_ref.shape[0] * out_ref.shape[1]):
        out_ref[s // out_ref.shape[1], s % out_ref.shape[1]] = all_ref[jnp.maximum(slot_block_ref[s] - 3, 0)]


def pack(slot_block, kept, got, n_grp, slots):
    shape = kept[0].shape[2:]
    inside = pl.BlockSpec(memory_space=pltpu.VMEM)
    return pl.pallas_call(
        pack_body,
        in_specs=[pl.BlockSpec(memory_space=pltpu.SMEM)] + [inside] * (2 * len(kept)),
        out_specs=inside,
        out_shape=jax.ShapeDtypeStruct((n_grp, slots, *shape), BF16),
        scratch_shapes=[pltpu.VMEM((len(kept) * kept[0].shape[1], *shape), BF16)],
        compiler_params=pltpu.CompilerParams(vmem_limit_bytes=32 << 20),
        cost_estimate=SMALL,
        name="pack",
    )(slot_block, *kept, *got)


def rotate_in_body(mine_ref, keep_ref, got_ref, high_ref, low_ref, out_ref, grad_ref):
    slots, n_tok = got_ref.shape[1], out_ref.shape[0]
    rows, columns = got_ref.shape[2:]
    width = out_ref.shape[3]
    for s in range(slots):
        block = mine_ref[s]

        @pl.when(block < 3)
        def _(s=s, block=block):
            grad_ref[...] = keep_ref[jnp.minimum(block, 2)]

        @pl.when(block >= 3)
        def _(s=s):
            for g in range(got_ref.shape[0]):
                x, c = g // 2, g % 2
                grad_ref[x * rows : (x + 1) * rows, c * columns : (c + 1) * columns] = got_ref[g, s]

        grad = grad_ref[...]
        part = jnp.dot(grad, high_ref[s], preferred_element_type=F32)
        part = jnp.transpose(part + jnp.dot(grad, low_ref[s], preferred_element_type=F32))
        for r in range(n_tok):
            out_ref[r, s] = part[r * width : (r + 1) * width].astype(BF16)


def rotate_in(mine, keep, got, left, n_tok):
    slots, width = got.shape[1], keep.shape[1]
    inside = pl.BlockSpec(memory_space=pltpu.VMEM)
    return pl.pallas_call(
        rotate_in_body,
        in_specs=[pl.BlockSpec(memory_space=pltpu.SMEM)] + [inside] * 4,
        out_specs=inside,
        out_shape=jax.ShapeDtypeStruct((n_tok, slots, width, width), BF16),
        scratch_shapes=[pltpu.VMEM(keep.shape[1:], BF16)],
        compiler_params=pltpu.CompilerParams(vmem_limit_bytes=48 << 20),
        cost_estimate=SMALL,
        name="rotate_in",
    )(mine, keep, got, *left)


def moments_body(place, got_ref, high_ref, low_ref, one_ref, two_ref, new_one_ref, new_two_ref, out_ref):
    n_tok, slots, width = got_ref.shape[:3]
    for s in range(slots):
        rotated = jnp.zeros(one_ref.shape[1:], F32)
        for t in range(n_tok):
            at = slice(place[t] * width, (place[t] + 1) * width)
            part = got_ref[t, s]
            rotated = rotated + jnp.dot(part, high_ref[s, at], preferred_element_type=F32)
            rotated = rotated + jnp.dot(part, low_ref[s, at], preferred_element_type=F32)
        new_one = BETA_ONE * one_ref[s] + (1.0 - BETA_ONE) * rotated
        new_two = BETA_TWO * two_ref[s] + (1.0 - BETA_TWO) * rotated * rotated
        new_one_ref[s] = new_one
        new_two_ref[s] = new_two
        direction = (new_one / (jnp.sqrt(new_two) + ADAM_EPS)).astype(BF16)
        for t in range(n_tok):
            at = slice(place[t] * width, (place[t] + 1) * width)
            turned = outer_cols(direction, high_ref[s, at]) + outer_cols(direction, low_ref[s, at])
            out_ref[t, s] = turned.astype(BF16)


def moments(place, got, right, one, two):
    n_tok, slots, width = got.shape[:3]
    inside = pl.BlockSpec(memory_space=pltpu.VMEM)
    return pl.pallas_call(
        functools.partial(moments_body, tuple(place)),
        in_specs=[inside] * 5,
        out_specs=[inside] * 3,
        out_shape=[
            jax.ShapeDtypeStruct(one.shape, F32),
            jax.ShapeDtypeStruct(one.shape, F32),
            jax.ShapeDtypeStruct(got.shape, BF16),
        ],
        compiler_params=pltpu.CompilerParams(vmem_limit_bytes=48 << 20),
        cost_estimate=SMALL,
        name="moments",
    )(got, *right, one, two)


def rotate_out_body(got_ref, high_ref, low_ref, out_ref, rows_ref):
    n_tok, slots, width = got_ref.shape[:3]
    for s in range(slots):
        for r in range(n_tok):
            rows_ref[r * width : (r + 1) * width, :] = got_ref[r, s]
        rows = rows_ref[...]
        change = jnp.dot(high_ref[s], rows, preferred_element_type=F32)
        change = change + jnp.dot(low_ref[s], rows, preferred_element_type=F32)
        for r in range(n_tok):
            out_ref[r, s] = change[r * width : (r + 1) * width].astype(BF16)


def rotate_out(got, left):
    n_tok, slots, width = got.shape[:3]
    inside = pl.BlockSpec(memory_space=pltpu.VMEM)
    return pl.pallas_call(
        rotate_out_body,
        in_specs=[inside] * 3,
        out_specs=inside,
        out_shape=jax.ShapeDtypeStruct(got.shape, BF16),
        scratch_shapes=[pltpu.VMEM((n_tok * width, width), BF16)],
        compiler_params=pltpu.CompilerParams(vmem_limit_bytes=48 << 20),
        cost_estimate=SMALL,
        name="rotate_out",
    )(got, *left)


def apply_body(place, got_ref, master_ref, out_ref):
    n_tok, slots, width = got_ref.shape[:3]
    for s in range(slots):
        for t in range(n_tok):
            at = slice(place[t] * width, (place[t] + 1) * width)
            out_ref[s, :, at] = master_ref[s, :, at] - RATE_MATRIX * got_ref[t, s].astype(F32)


def apply_change(place, got, master):
    inside = pl.BlockSpec(memory_space=pltpu.VMEM)
    return pl.pallas_call(
        functools.partial(apply_body, tuple(place)),
        in_specs=[inside] * 2,
        out_specs=inside,
        out_shape=jax.ShapeDtypeStruct(master.shape, F32),
        compiler_params=pltpu.CompilerParams(vmem_limit_bytes=48 << 20),
        cost_estimate=SMALL,
        name="apply_change",
    )(got, master)


def swap(value, axis, bit):
    size = lax.axis_size(axis)
    return lax.ppermute(value, axis, [(i, i ^ bit) for i in range(size)])


def exchange_unit(parts):
    return [parts[0]] + [swap(parts[k], "tok", k) for k in range(1, UNIT)]


LINKS = {"x": ("grp", 2), "y": ("tok", 1), "zl": ("tok", 2), "zh": ("tok", 4)}


def starts_of(lengths):
    index = jnp.arange(lengths.shape[0])
    return jnp.sum(jnp.where(index[None, :] < index[:, None], lengths[None, :], 0), axis=1)


LINKS = {"x": ("grp", 2), "y": ("tok", 1), "zl": ("tok", 2), "zh": ("tok", 4)}


def starts_of(lengths):
    index = jnp.arange(lengths.shape[0])
    return jnp.sum(jnp.where(index[None, :] < index[:, None], lengths[None, :], 0), axis=1)


def total_of(value):
    for axis in ("grp", "tok"):
        bit = 1
        while bit < lax.axis_size(axis):
            value = value + swap(value, axis, bit)
            bit *= 2
    return value


def pick(values, index):
    return lax.dynamic_index_in_dim(values, index, 0, keepdims=False)


def split_heads(columns):
    query, keys, values = (c.reshape(HEADS_OWN, HEAD) for c in columns)
    zero = jnp.zeros((HEAD,), query.dtype)
    tiles = []
    for h in range(HEADS_OWN):
        tiles += [values[h], query[h], zero, keys[h]] if h % 2 == 0 else [query[h], values[h], keys[h], zero]
    return jnp.concatenate(tiles)


def join_heads(tiles):
    parts = tiles.reshape(HEADS_OWN, 4, HEAD, *tiles.shape[1:])
    at = [(1, 0), (3, 2), (0, 1)]
    return jnp.stack(
        [jnp.concatenate([parts[h, at[i][h % 2]] for h in range(HEADS_OWN)], axis=0) for i in range(3)]
    )


def doubled(value):
    high = value.astype(BF16)
    return high, (value - high.astype(F32)).astype(BF16)


def together(*groups):
    flat, tree = jax.tree.flatten(groups)
    return jax.tree.unflatten(tree, lax.optimization_barrier(flat))


def fast(
    tokens,
    cotangent,
    lengths,
    clusters,
    owners,
    master,
    bases,
    moment_one,
    moment_two,
    vectors,
    vector_one,
    vector_two,
):
    n_tok = lax.axis_size("tok")
    n_grp = lax.axis_size("grp")
    tok = lax.axis_index("tok")
    grp = lax.axis_index("grp")
    tok_count = tokens.shape[1]
    rows_dev = master.shape[0]
    slots = master.shape[1]
    blocks_all = slots * n_grp
    member = tok & (UNIT - 1)
    unit = tok >> 2
    place = [2 * (t % UNIT) + t // UNIT for t in range(n_tok)]
    own_width = HEADS_OWN * HEAD

    slot_block = jnp.argsort(owners, stable=True).astype(jnp.int32)
    block_slot = jnp.argsort(slot_block, stable=True).astype(jnp.int32)

    core, bit_x = grp & 1, grp >> 1
    inputs = tokens[0]

    near, far = swap(inputs, "tok", 1), swap(inputs, "tok", 2)
    local = jnp.transpose(master.astype(BF16), (1, 0, 2))
    beside, over = swap(local, "grp", 1), swap(local, "grp", 2)

    item_starts = starts_of(lengths[0])
    unit_start = unit * UNIT * tok_count
    middle = unit_start + UNIT // 2 * tok_count
    start_of_middle = jnp.max(jnp.where(item_starts <= middle, item_starts, 0))
    is_long = (start_of_middle <= unit_start).astype(jnp.int32).reshape(1)
    share = CLUSTER // UNIT * (2 - is_long)
    placed = places(jnp.concatenate([share, member.reshape(1)]), clusters[0])
    left, right = doubled(bases[0]), doubled(bases[1])
    (over, left, right, placed) = together(over, left, right, placed)
    across = swap(over, "grp", 1)

    orders = exchange_unit(placed)
    (near, far, beside, over, across) = together(near, far, beside, over, across)
    part_rows = rows_dev // 2

    scalars = jnp.concatenate([block_slot, jnp.stack([grp, core, member])]).astype(jnp.int32)
    *by_owner, rest_rows = arrange(scalars, [local, beside, over, across], blocks_all)
    theirs = exchange_unit(by_owner)
    half = tok_count // 2
    third = (swap(near[:half], "tok", 2), swap(far[half:], "tok", 1))
    (theirs, orders) = together(theirs, orders)
    theirs = jnp.stack(theirs)
    theirs_far = swap(theirs, "tok", UNIT)
    mine_all = jnp.concatenate([theirs, theirs_far], axis=0)
    others_all = swap(mine_all, "grp", 1)
    sources = tok ^ jnp.arange(2 * UNIT, dtype=jnp.int32)
    cores = core ^ jnp.arange(2, dtype=jnp.int32)
    firsts = (sources[None, :] * rows_dev + cores[:, None] * part_rows).reshape(-1)
    (third, others_all, rest_rows) = together(third, others_all, rest_rows)
    own_weights = assemble(firsts, [mine_all, others_all])

    def columns_of(value, m):
        return lax.dynamic_slice_in_dim(value, m * own_width, own_width, value.ndim - 1)

    own_bias = split_heads(
        [columns_of(vectors[4], member), jnp.zeros((own_width,), F32), columns_of(vectors[5], member)]
    ).reshape(1, -1)
    ring = [(i, (i + 2) % n_tok) for i in range(n_tok)]
    depth = n_tok // 2
    steps, flips, mine_rest, other_rest = [rest_rows], [], [], []

    def advance():
        if len(steps) < depth:
            steps.append(lax.ppermute(steps[-1], "tok", ring))
        flips.append(swap(steps[len(flips)], "tok", 1))

    def cross():
        k = len(mine_rest)
        mine_rest.append(jnp.stack([steps[k], flips[k]]))
        other_rest.append(swap(mine_rest[k], "grp", 1))

    advance()
    grouped = [sort_rows(orders[0], inputs, own_weights, own_bias)]
    grouped.append(sort_rows(orders[1], near, own_weights, own_bias))
    (grouped, far, third, steps[1], flips[0]) = together(grouped, far, third, steps[1], flips[0])
    advance()
    cross()
    grouped.append(sort_rows(orders[2], far, own_weights, own_bias))
    unit_inputs = [inputs, near, far, jnp.concatenate(third, axis=0)]
    grouped.append(sort_rows(orders[3], unit_inputs[3], own_weights, own_bias))
    (grouped, steps[2], flips[1], other_rest) = together(grouped, steps[2], flips[1], other_rest)
    advance()
    cross()
    sorted_out = attend(is_long, grouped)
    (sorted_out, steps[3], flips[2], other_rest) = together(sorted_out, steps[3], flips[2], other_rest)
    advance()
    cross()
    mixed = [None] * UNIT
    mixed[3] = mix(orders[3], sorted_out[3])
    mixed[2] = mix(orders[2], sorted_out[2])
    mixed[1] = mix(orders[1], sorted_out[1])
    (mixed[3], last) = together(mixed[3], sorted_out[0])
    mixed[0] = mix(orders[0], last)
    mixed_parts = exchange_unit(mixed)
    (mixed_parts, flips[-1], other_rest, held_weights) = together(
        mixed_parts, flips[-1], other_rest, own_weights
    )
    cross()
    shards = mine_rest + other_rest
    sources = (tok + n_tok - 2 * jnp.arange(depth, dtype=jnp.int32)) & (n_tok - 1)
    sources = (sources[:, None] ^ jnp.arange(2, dtype=jnp.int32)[None, :]).reshape(-1)
    firsts = (sources[None, :] * rows_dev + cores[:, None] * part_rows).reshape(-1)

    turned_weights = [swap(held_weights, "tok", k) for k in range(1, UNIT)]
    place_bits = jnp.stack([member, core, bit_x, tok & 1, (tok >> 1) & 1, tok >> 2]).astype(jnp.int32)
    table = jnp.concatenate([place_bits, firsts])
    result, grad_first, sums, kept, sent_pieces, *back = layer(
        table, shards, mixed_parts, inputs, cotangent[0], vectors
    )
    (turned_weights, kept, sent_pieces, back) = together(turned_weights, kept, sent_pieces, back)

    grad_parts = exchange_unit(back)
    other = swap(sent_pieces, "grp", 1)
    sums_of = [kept[p].astype(F32) + other[p].astype(F32) for p in range(3)]

    def halves(values):
        return [v[: v.shape[0] // 2] for v in values], [v[v.shape[0] // 2 :].astype(BF16) for v in values]

    def exchanged(sent_now, stage):
        return [swap(v, *LINKS[PART_ORDERS[p][stage]]) for p, v in enumerate(sent_now)]

    def joined(kept_now, got_now):
        return [k + g.astype(F32) for k, g in zip(kept_now, got_now)]

    kept_now, sent_now = halves(sums_of)
    sorted_grads = [sort_grads(orders[0], grad_parts[0])]
    (sent_now, grad_parts, sorted_grads) = together(sent_now, grad_parts, sorted_grads)
    got_now = exchanged(sent_now, 0)
    sorted_grads += [sort_grads(orders[k], grad_parts[k]) for k in range(1, UNIT)]
    sorted_back = attend_back(is_long, grouped, sorted_grads)
    kept_now, sent_now = halves(joined(kept_now, got_now))
    (sent_now, sorted_back) = together(sent_now, sorted_back)
    got_now = exchanged(sent_now, 1)
    own_grads = [None] * UNIT
    own_grads[3] = gather_grads(orders[3], sorted_back[3])
    own_grads[2] = gather_grads(orders[2], sorted_back[2])
    kept_now, sent_now = halves(joined(kept_now, got_now))
    (sent_now, own_grads[2], own_grads[3], sorted_back) = together(
        sent_now, own_grads[2], own_grads[3], sorted_back
    )
    got_now = exchanged(sent_now, 2)
    home_grads = [None, None, None, swap(own_grads[3], "tok", 3)]
    for k in (1, 0):
        own_grads[k] = gather_grads(orders[k], sorted_back[k])
    kept_qkv, sent_qkv, bias_qkv = qkv_back(jnp.stack([core, unit]).astype(jnp.int32), own_grads, unit_inputs)
    (got_now, kept_qkv, sent_qkv) = together(got_now, kept_qkv, sent_qkv)
    kept_now, sent_now = halves(joined(kept_now, got_now))
    got_now = exchanged(sent_now, 3)

    bias_query, _, bias_value = join_heads(bias_qkv[0])
    bias_rows = lax.dynamic_update_slice_in_dim(
        jnp.zeros((2, D), F32), jnp.stack([bias_query, bias_value]), member * own_width, 1
    )
    total = sums[: 8 + FFB] + jnp.pad(bias_rows, ((4, 2 + FFB), (0, 0)))

    more = swap(total, "grp", 1)
    keep = kept_qkv.astype(F32) + swap(sent_qkv, "grp", 1).astype(F32)
    (keep, more) = together(keep, more)
    total = total + more
    more = swap(total, "tok", 1)
    unit_got = swap(keep[1].astype(BF16), "tok", UNIT)
    keep = keep[0] + unit_got.astype(F32)
    (keep, more, got_now, home_grads[3]) = together(keep, more, got_now, home_grads[3])
    total = total + more
    more = swap(total, "tok", 2)
    home_grads[1] = swap(own_grads[1], "tok", 1)
    home_grads[2] = swap(own_grads[2], "tok", 2)
    sent = pack(slot_block, kept_now, got_now, n_grp, slots)
    got = lax.all_to_all(sent, "grp", split_axis=0, concat_axis=0, tiled=True)
    keep = (keep + swap(keep.astype(BF16), "grp", 2).astype(F32)).astype(BF16)
    kept_core = (keep, swap(keep, "grp", 1))
    keep = jnp.concatenate(
        [jnp.where(core == 0, kept_core[0], kept_core[1]), jnp.where(core == 0, kept_core[1], kept_core[0])],
        axis=-1,
    )
    mine = lax.dynamic_slice_in_dim(slot_block, grp * slots, slots, 0)

    def to_tok(value):
        return lax.all_to_all(value, "tok", split_axis=0, concat_axis=0, tiled=True)

    part = to_tok(rotate_in(mine, keep, got, left, n_tok))
    grad_inputs = grad_first + outer_cols(own_grads[0], own_weights)
    (part, home_grads, grad_inputs, more) = together(part, home_grads[1:], grad_inputs, more)
    total = total + more
    more = swap(total, "tok", 4)
    by_slot_of = lambda value: jnp.transpose(value, (1, 0, 2))
    new_one, new_two, turned = moments(
        place, part, right, by_slot_of(moment_one), by_slot_of(moment_two)
    )
    turned = to_tok(turned)
    grad_inputs = grad_inputs + outer_cols(home_grads[0], turned_weights[0])
    grad_inputs = grad_inputs + outer_cols(home_grads[1], turned_weights[1])
    (turned, more, grad_inputs, home_grads[2]) = together(turned, more, grad_inputs, home_grads[2])
    total = total + more
    change = to_tok(rotate_out(turned, left))
    vector_total = total + swap(total, "grp", 2)
    new_master = by_slot_of(apply_change(place, change, by_slot_of(master)))
    new_one, new_two = by_slot_of(new_one), by_slot_of(new_two)
    grad_inputs = grad_inputs + outer_cols(home_grads[2], turned_weights[2])
    new_vec_one = BETA_ONE * vector_one + (1.0 - BETA_ONE) * vector_total
    new_vec_two = BETA_TWO * vector_two + (1.0 - BETA_TWO) * vector_total * vector_total
    new_vectors = vectors - RATE_VECTOR * new_vec_one / (jnp.sqrt(new_vec_two) + ADAM_EPS)
    return (
        result[None],
        grad_inputs[None],
        new_one,
        new_two,
        new_master,
        new_vec_one,
        new_vec_two,
        new_vectors,
    )


def general(
    tokens,
    cotangent,
    lengths,
    clusters,
    owners,
    master,
    bases,
    moment_one,
    moment_two,
    vectors,
    vector_one,
    vector_two,
):
    n_tok = lax.axis_size("tok")
    tok_count = tokens.shape[1]
    rows_dev = master.shape[0]
    slot_block = jnp.argsort(owners, stable=True)
    block_slot = jnp.argsort(slot_block, stable=True)
    slot_part = lax.all_gather(master.astype(jnp.bfloat16), "grp", axis=1, tiled=True)
    weights = lax.all_gather(slot_part, "tok", axis=0, tiled=True)
    blocks = jnp.stack([pick(jnp.transpose(weights, (1, 0, 2)), block_slot[b]) for b in range(weights.shape[1])], axis=1)
    w_qkv = blocks[:, 0:3, :].reshape(D, 3 * D)
    w_out = blocks[:, 3, :]
    w_up = blocks[:, 4 : 4 + FF // D, :].reshape(D, FF)
    w_down = jnp.transpose(blocks[:, 4 + FF // D :, :], (1, 0, 2)).reshape(FF, D)
    inputs = tokens[0]
    gain_one = vectors[0]
    shift_one = vectors[1]
    gain_two = vectors[2]
    shift_two = vectors[3]
    bias_qkv = jnp.concatenate([vectors[4], jnp.zeros((D,), jnp.float32), vectors[5]])
    qkv = (jnp.dot(inputs, w_qkv, preferred_element_type=jnp.float32) + bias_qkv).astype(
        jnp.bfloat16
    )
    heads = jnp.transpose(qkv.reshape(tok_count, 3, H, HEAD), (2, 0, 1, 3)).reshape(
        H, tok_count, 3 * HEAD
    )
    pair_rows = jnp.broadcast_to(heads[None], (ROUNDS, H, tok_count, 3 * HEAD)).reshape(
        PAIRS * tok_count, 3 * HEAD
    )
    position = lax.axis_index("tok") * tok_count + jnp.arange(tok_count, dtype=jnp.int32)
    item_starts = starts_of(lengths[0])
    item_start = jnp.max(
        jnp.where(item_starts[None, :] <= position[:, None], item_starts[None, :], 0), axis=1
    )
    per_dev = tok_count // CLUSTER
    group_clusters = n_tok * per_dev
    pair_ids = jnp.arange(PAIRS, dtype=jnp.int32)[:, None]
    global_cluster = item_start[None, :] // CLUSTER + clusters[0]
    unit_ids = (pair_ids * group_clusters + global_cluster).reshape(-1)
    owner_ids = ((global_cluster + pair_ids * per_dev) % n_tok).reshape(-1)
    send_order = jnp.argsort(owner_ids * (PAIRS * group_clusters) + unit_ids, stable=True)
    restore = jnp.argsort(send_order, stable=True)
    slot_rows = PAIRS * tok_count // n_tok
    units_here = PAIRS * tok_count // CLUSTER
    sent_rows = pair_rows[send_order].reshape(n_tok, slot_rows // 2, 6 * HEAD)
    sent_units = unit_ids[send_order].reshape(n_tok, slot_rows)
    got_rows, got_units = (
        lax.all_to_all(sent_rows, "tok", split_axis=0, concat_axis=0, tiled=True),
        lax.all_to_all(sent_units, "tok", split_axis=0, concat_axis=0, tiled=True),
    )
    arrange = jnp.argsort(got_units.reshape(-1), stable=True)
    undo = jnp.argsort(arrange, stable=True)
    grouped = got_rows.reshape(PAIRS * tok_count, 3 * HEAD)[arrange].reshape(
        units_here, CLUSTER, 3 * HEAD
    )
    query_rows = grouped[..., :HEAD]
    key_rows = grouped[..., HEAD : 2 * HEAD]
    value_rows = grouped[..., 2 * HEAD :]
    score_scale = HEAD ** (-0.5)
    scores = (
        jnp.einsum("ucd,ued->uce", query_rows, key_rows, preferred_element_type=jnp.float32)
        * score_scale
    )
    row_max = jnp.max(scores, axis=-1, keepdims=True)
    row_total = jnp.sum(jnp.exp(scores - row_max), axis=-1, keepdims=True)
    log_total = row_max + jnp.log(row_total)
    probs = jnp.exp(scores - log_total)
    cluster_out = jnp.einsum(
        "uce,ued->ucd", probs.astype(jnp.bfloat16), value_rows, preferred_element_type=jnp.float32
    ).astype(jnp.bfloat16)
    back_rows = cluster_out.reshape(PAIRS * tok_count, HEAD)[undo].reshape(
        n_tok, slot_rows // 2, 2 * HEAD
    )
    home_rows = lax.all_to_all(back_rows, "tok", split_axis=0, concat_axis=0, tiled=True)
    home_rows = (
        home_rows.reshape(PAIRS * tok_count, HEAD)[restore]
        .reshape(ROUNDS, H, tok_count, HEAD)
        .astype(jnp.float32)
    )
    mixed_heads = 0.5 * (home_rows[0] + home_rows[1])
    mixed_low = jnp.transpose(mixed_heads, (1, 0, 2)).reshape(tok_count, D).astype(jnp.bfloat16)
    attention = jnp.dot(mixed_low, w_out, preferred_element_type=jnp.float32) + vectors[6]
    first_sum = inputs.astype(jnp.float32) + attention
    normed_one, rstd_one = normalize(first_sum)
    hidden = normed_one * gain_one + shift_one
    hidden_low = hidden.astype(jnp.bfloat16)
    up_proj = jnp.dot(hidden_low, w_up, preferred_element_type=jnp.float32) + vectors[8:].reshape(
        FF
    )
    act_low = jax.nn.gelu(up_proj, approximate=False).astype(jnp.bfloat16)
    down_proj = jnp.dot(act_low, w_down, preferred_element_type=jnp.float32) + vectors[7]
    second_sum = hidden + down_proj
    normed_two, rstd_two = normalize(second_sum)
    result = (normed_two * gain_two + shift_two).astype(jnp.bfloat16)
    grad_result = cotangent[0].astype(jnp.float32)
    grad_gain_two = jnp.sum(grad_result * normed_two, axis=0)
    grad_shift_two = jnp.sum(grad_result, axis=0)
    grad_second = norm_back(grad_result * gain_two, normed_two, rstd_two)
    grad_down_low = grad_second.astype(jnp.bfloat16)
    grad_w_down = inner_rows(act_low, grad_down_low)
    grad_bias_down = jnp.sum(grad_down_low.astype(jnp.float32), axis=0)
    grad_act = outer_cols(grad_down_low, w_down)
    grad_up_low = (grad_act * gelu_slope(up_proj)).astype(jnp.bfloat16)
    grad_w_up = inner_rows(hidden_low, grad_up_low)
    grad_bias_up = jnp.sum(grad_up_low.astype(jnp.float32), axis=0)
    grad_hidden = grad_second + outer_cols(grad_up_low, w_up)
    grad_gain_one = jnp.sum(grad_hidden * normed_one, axis=0)
    grad_shift_one = jnp.sum(grad_hidden, axis=0)
    grad_first = norm_back(grad_hidden * gain_one, normed_one, rstd_one)
    grad_attn_low = grad_first.astype(jnp.bfloat16)
    grad_w_out = inner_rows(mixed_low, grad_attn_low)
    grad_bias_out = jnp.sum(grad_attn_low.astype(jnp.float32), axis=0)
    grad_mixed = outer_cols(grad_attn_low, w_out)
    grad_heads = jnp.transpose((0.5 * grad_mixed).reshape(tok_count, H, HEAD), (1, 0, 2)).astype(
        jnp.bfloat16
    )
    grad_pairs = jnp.broadcast_to(grad_heads[None], (ROUNDS, H, tok_count, HEAD)).reshape(
        PAIRS * tok_count, HEAD
    )
    sent_grad = grad_pairs[send_order].reshape(n_tok, slot_rows // 2, 2 * HEAD)
    got_grad = lax.all_to_all(sent_grad, "tok", split_axis=0, concat_axis=0, tiled=True)
    grad_cluster = got_grad.reshape(PAIRS * tok_count, HEAD)[arrange].reshape(
        units_here, CLUSTER, HEAD
    )
    scores_again = (
        jnp.einsum("ucd,ued->uce", query_rows, key_rows, preferred_element_type=jnp.float32)
        * score_scale
    )
    probs_again = jnp.exp(scores_again - log_total)
    probs_low = probs_again.astype(jnp.bfloat16)
    grad_values = jnp.einsum(
        "uce,ucd->ued", probs_low, grad_cluster, preferred_element_type=jnp.float32
    )
    grad_probs = jnp.einsum(
        "ucd,ued->uce", grad_cluster, value_rows, preferred_element_type=jnp.float32
    )
    centre = jnp.sum(probs_again * grad_probs, axis=-1, keepdims=True)
    grad_scores = (probs_again * (grad_probs - centre)).astype(jnp.bfloat16)
    grad_query = (
        jnp.einsum("uce,ued->ucd", grad_scores, key_rows, preferred_element_type=jnp.float32)
        * score_scale
    )
    grad_keys = (
        jnp.einsum("uce,ucd->ued", grad_scores, query_rows, preferred_element_type=jnp.float32)
        * score_scale
    )
    grad_grouped = jnp.concatenate(
        [
            grad_query.astype(jnp.bfloat16),
            grad_keys.astype(jnp.bfloat16),
            grad_values.astype(jnp.bfloat16),
        ],
        axis=-1,
    )
    back_grad = grad_grouped.reshape(PAIRS * tok_count, 3 * HEAD)[undo].reshape(
        n_tok, slot_rows // 2, 6 * HEAD
    )
    home_grad = lax.all_to_all(back_grad, "tok", split_axis=0, concat_axis=0, tiled=True)
    home_grad = (
        home_grad.reshape(PAIRS * tok_count, 3 * HEAD)[restore]
        .reshape(ROUNDS, H, tok_count, 3, HEAD)
        .astype(jnp.float32)
    )
    grad_qkv = (home_grad[0] + home_grad[1]).astype(jnp.bfloat16)
    grad_qkv = jnp.transpose(grad_qkv, (1, 2, 0, 3)).reshape(tok_count, 3 * D)
    grad_w_qkv = inner_rows(inputs, grad_qkv)
    grad_bias_qkv = jnp.sum(grad_qkv.astype(jnp.float32), axis=0)
    grad_inputs = grad_first + outer_cols(grad_qkv, w_qkv)
    grad_blocks = jnp.concatenate(
        [
            grad_w_qkv.reshape(D, 3, D),
            grad_w_out[:, None, :],
            grad_w_up.reshape(D, FF // D, D),
            jnp.transpose(grad_w_down.reshape(FF // D, D, D), (1, 0, 2)),
        ],
        axis=1,
    )
    by_block = jnp.transpose(grad_blocks, (1, 0, 2))
    slot_grads = jnp.stack([pick(by_block, slot_block[s]) for s in range(by_block.shape[0])], axis=1)
    vector_grads = jnp.concatenate(
        [
            jnp.stack(
                [
                    grad_gain_one,
                    grad_shift_one,
                    grad_gain_two,
                    grad_shift_two,
                    grad_bias_qkv[:D],
                    grad_bias_qkv[2 * D :],
                    grad_bias_out,
                    grad_bias_down,
                ]
            ),
            grad_bias_up.reshape(FF // D, D),
        ],
        axis=0,
    )
    vector_total = lax.psum(vector_grads, ("tok", "grp"))
    row_total = lax.psum_scatter(slot_grads, "tok", scatter_dimension=0, tiled=True)
    reduced = lax.psum_scatter(
        row_total.astype(jnp.bfloat16), "grp", scatter_dimension=1, tiled=True
    ).astype(jnp.float32)
    left_basis = bases[0]
    right_basis = bases[1]
    first_row = lax.axis_index("tok") * rows_dev
    turned_in = jnp.einsum("rse,sef->rsf", reduced, right_basis, precision=lax.Precision.HIGHEST)
    left_rows = lax.dynamic_slice_in_dim(left_basis, first_row, rows_dev, 1)
    picked = left_rows
    rotated = lax.psum_scatter(
        jnp.einsum("sri,rsf->isf", picked, turned_in, precision=lax.Precision.HIGHEST),
        "tok",
        scatter_dimension=0,
        tiled=True,
    )
    new_one = BETA_ONE * moment_one + (1.0 - BETA_ONE) * rotated
    new_two = BETA_TWO * moment_two + (1.0 - BETA_TWO) * rotated * rotated
    direction = new_one / (jnp.sqrt(new_two) + ADAM_EPS)
    turned_out = jnp.einsum("rse,sfe->rsf", direction, right_basis, precision=lax.Precision.HIGHEST)
    left_cols = lax.dynamic_slice_in_dim(left_basis, first_row, rows_dev, 2)
    picked = left_cols
    change = lax.psum_scatter(
        jnp.einsum("sir,rsf->isf", picked, turned_out, precision=lax.Precision.HIGHEST),
        "tok",
        scatter_dimension=0,
        tiled=True,
    )
    new_master = master - RATE_MATRIX * change
    new_vec_one = BETA_ONE * vector_one + (1.0 - BETA_ONE) * vector_total
    new_vec_two = BETA_TWO * vector_two + (1.0 - BETA_TWO) * vector_total * vector_total
    new_vectors = vectors - RATE_VECTOR * new_vec_one / (jnp.sqrt(new_vec_two) + ADAM_EPS)
    return (
        result[None],
        grad_inputs[None],
        new_one,
        new_two,
        new_master,
        new_vec_one,
        new_vec_two,
        new_vectors,
    )

def solution(mesh):
    n_tok, n_grp = mesh.shape["tok"], mesh.shape["grp"]

    def on_device(*args):
        lengths, clusters = args[2], args[3]
        unit = n_tok // (lengths.shape[1] - 1)
        suits = unit == UNIT and n_tok == 2 * UNIT and n_grp == 4 and clusters.shape[2] == 1024
        return (fast if suits else general)(*args)

    return jax.shard_map(
        on_device,
        mesh=mesh,
        in_specs=(
            P("grp", "tok", None),
            P("grp", "tok", None),
            P("grp", None),
            P("grp", None, "tok"),
            P(),
            P("tok", "grp", None),
            P(None, "grp", None, None),
            P("tok", "grp", None),
            P("tok", "grp", None),
            P(),
            P(),
            P(),
        ),
        out_specs=(
            P("grp", "tok", None),
            P("grp", "tok", None),
            P("tok", "grp", None),
            P("tok", "grp", None),
            P("tok", "grp", None),
            P(),
            P(),
            P(),
        ),
        check_vma=False,
    )
```

```python
import functools

import jax
import jax.numpy as jnp
from jax import lax
from jax.experimental import pallas as pl
from jax.experimental.pallas import tpu as pltpu
from jax.sharding import PartitionSpec as P

D = 768
H = 12
FF = 3072
HEAD = 64
ROUNDS = 2
PAIRS = 24
CLUSTER = 128
FFB = FF // D

EPS_NORM = 1e-05
ADAM_EPS = 1e-08
BETA_ONE = 0.5
BETA_TWO = 0.5
RATE_MATRIX = 0.025
RATE_VECTOR = 0.15
SQRT_HALF = 0.7071067811865476
INV_ROOT_TWO_PI = 0.3989422804014327

BF16 = jnp.bfloat16
F32 = jnp.float32

UNIT = 4
HEADS_OWN = H // UNIT
LOCAL_PAIRS = ROUNDS * HEADS_OWN
TILE = 128
WIDE = 2 * TILE
SMALL = pl.CostEstimate(flops=0, transcendentals=0, bytes_accessed=0)


def inner_rows(left, right):
    return lax.dot_general(left, right, (((0,), (0,)), ((), ())), preferred_element_type=F32)


def outer_cols(left, right):
    return lax.dot_general(left, right, (((1,), (1,)), ((), ())), preferred_element_type=F32)


def normalize(values_in):
    centre = jnp.mean(values_in, axis=-1, keepdims=True)
    offset = values_in - centre
    spread = jnp.mean(offset * offset, axis=-1, keepdims=True)
    rstd = lax.rsqrt(spread + EPS_NORM)
    return (offset * rstd, rstd)


def norm_back(grad_normed, normed, rstd):
    first_mean = jnp.mean(grad_normed, axis=-1, keepdims=True)
    second_mean = jnp.mean(grad_normed * normed, axis=-1, keepdims=True)
    return rstd * (grad_normed - first_mean - normed * second_mean)


def gelu_slope(values_in):
    return (
        0.5 * (1.0 + lax.erf(values_in * SQRT_HALF))
        + values_in * jnp.exp(-0.5 * values_in * values_in) * INV_ROOT_TWO_PI
    )


def turn_half(value):
    return pltpu.roll(value, HEAD, 1)


def places_body(scalars_ref, clusters_ref, *refs):
    outs, all_ref = refs[:UNIT], refs[UNIT]
    pairs, count = clusters_ref.shape
    share, member = scalars_ref[0], scalars_ref[1]
    kinds = UNIT * count // CLUSTER
    kind = lax.broadcasted_iota(jnp.int32, (kinds, count), 0)
    earlier = lax.broadcasted_iota(jnp.int32, (count, count), 0) < lax.broadcasted_iota(jnp.int32, (count, count), 1)
    earlier = earlier.astype(F32).astype(BF16)
    all_ref[...] = jnp.zeros_like(all_ref)
    for pair in range(pairs):
        turn, head = pair // H, pair % H
        cluster = clusters_ref[pair : pair + 1, :]
        same = (kind == cluster).astype(F32)
        before = jnp.dot(same.astype(BF16), earlier, preferred_element_type=F32)
        rank = jnp.sum(same * before, axis=0, keepdims=True).astype(jnp.int32)
        own = head % HEADS_OWN * ROUNDS + turn
        all_ref[head // HEADS_OWN, own : own + 1, :] = cluster * share + rank
    for k in range(UNIT):
        outs[k][...] = all_ref[member ^ k]


def places(scalars, clusters):
    count = clusters.shape[1]
    inside = pl.BlockSpec(memory_space=pltpu.VMEM)
    return pl.pallas_call(
        places_body,
        in_specs=[pl.BlockSpec(memory_space=pltpu.SMEM), inside],
        out_specs=[inside] * UNIT,
        out_shape=[jax.ShapeDtypeStruct((8, count), jnp.int32)] * UNIT,
        scratch_shapes=[pltpu.VMEM((UNIT, 8, count), jnp.int32)],
        cost_estimate=SMALL,
        name="places",
    )(scalars, clusters)


def arrange_body(slots, scalars_ref, *refs):
    sources, outs, rest_ref, tiles_ref = refs[:4], refs[4 : 4 + UNIT], refs[4 + UNIT], refs[5 + UNIT]
    n_rest, count = rest_ref.shape[:2]
    n_blocks = n_rest + 3
    group, core, member = (scalars_ref[n_blocks + i] for i in range(3))
    first = pl.multiple_of(core * count, count)

    def rows_of(block):
        slot = scalars_ref[block]
        owner = lax.div(slot, slots)
        near, inner = owner ^ group, lax.rem(slot, slots)
        found = [source[inner, pl.ds(first, count), :].astype(F32) for source in sources]
        low = jnp.where(near % 2 == 0, found[0], found[1])
        high = jnp.where(near % 2 == 0, found[2], found[3])
        return jnp.where(near < 2, low, high)

    low = lax.broadcasted_iota(jnp.int32, (count, TILE), 1) < HEAD
    parts = [rows_of(i) for i in range(3)]

    def half(part, head, high):
        at = head // 2 * TILE
        tile = parts[part][:, at : at + TILE]
        return tile if head % 2 == high else turn_half(tile)

    for head in range(H):
        own = head % HEADS_OWN
        odd = own % 2
        value = half(2, head, odd)
        query = half(0, head, 1 - odd)
        keys = half(1, head, 1 - odd)
        one = jnp.where(low, query, value) if odd else jnp.where(low, value, query)
        two = jnp.where(low, keys, 0.0) if odd else jnp.where(low, 0.0, keys)
        tiles_ref[head // HEADS_OWN, :, own * WIDE : own * WIDE + TILE] = one.astype(BF16)
        tiles_ref[head // HEADS_OWN, :, own * WIDE + TILE : (own + 1) * WIDE] = two.astype(BF16)
    for k in range(UNIT):
        outs[k][...] = tiles_ref[member ^ k]
    for b in range(n_rest):
        rest_ref[b] = rows_of(3 + b).astype(BF16)


def arrange(scalars, sources, n_blocks):
    slots, rows = sources[0].shape[:2]
    count = rows // 2
    width = HEADS_OWN * WIDE
    inside = pl.BlockSpec(memory_space=pltpu.VMEM)
    return pl.pallas_call(
        functools.partial(arrange_body, slots),
        in_specs=[pl.BlockSpec(memory_space=pltpu.SMEM)] + [inside] * 4,
        out_specs=[inside] * (UNIT + 1),
        out_shape=[jax.ShapeDtypeStruct((count, width), BF16)] * UNIT
        + [jax.ShapeDtypeStruct((n_blocks - 3, count, D), BF16)],
        scratch_shapes=[pltpu.VMEM((UNIT, count, width), BF16)],
        compiler_params=pltpu.CompilerParams(vmem_limit_bytes=32 << 20),
        cost_estimate=SMALL,
        name="arrange",
    )(scalars, *sources)


def assemble_body(table_ref, *refs):
    shards, out_ref, sem = refs[:-2], refs[-2], refs[-1]
    rows = shards[0].shape[1]
    copies = []
    for shard in shards:
        for i in range(shard.shape[0]):
            n = len(copies)
            first = pl.multiple_of(table_ref[n], rows)
            copies.append(
                pltpu.make_async_copy(shard.at[i], out_ref.at[pl.ds(first, rows), :], sem.at[n])
            )
    for copy in copies:
        copy.start()
    for copy in copies:
        copy.wait()


def assemble(table, shards):
    pieces = sum(s.shape[0] for s in shards)
    anywhere = pl.BlockSpec(memory_space=pl.ANY)
    return pl.pallas_call(
        assemble_body,
        in_specs=[pl.BlockSpec(memory_space=pltpu.SMEM)] + [anywhere] * len(shards),
        out_specs=pl.BlockSpec(memory_space=pltpu.VMEM),
        out_shape=jax.ShapeDtypeStruct((pieces * shards[0].shape[1], shards[0].shape[2]), BF16),
        scratch_shapes=[pltpu.SemaphoreType.DMA((pieces,))],
        cost_estimate=SMALL,
        name="assemble",
    )(table, *shards)


def sort_body(place_ref, x_ref, weight_ref, bias_ref, out_ref, rows_ref):
    count = x_ref.shape[0]
    head = pl.program_id(0)
    chunk = 256
    row = lax.broadcasted_iota(jnp.int32, (chunk, count), 0)
    rows_ref[...] = (
        jnp.dot(x_ref[...], weight_ref[...], preferred_element_type=F32) + bias_ref[...]
    ).astype(BF16)
    for step in range(HEADS_OWN):

        @pl.when(head == step)
        def _():
            for turn in range(ROUNDS):
                pair = step * ROUNDS + turn
                for part in range(count // chunk):
                    where = pl.ds(part * chunk, chunk)
                    picked = place_ref[pair : pair + 1, :] == row + part * chunk
                    picked = picked.astype(F32).astype(BF16)
                    out_ref[turn, where, :] = jnp.dot(
                        picked, rows_ref[...], preferred_element_type=F32
                    ).astype(BF16)


def sort_rows(order, inputs, weights, bias):
    count = inputs.shape[0]
    return pl.pallas_call(
        sort_body,
        grid=(HEADS_OWN,),
        in_specs=[
            pl.BlockSpec((8, count), lambda h: (0, 0)),
            pl.BlockSpec((count, D), lambda h: (0, 0)),
            pl.BlockSpec((D, WIDE), lambda h: (0, h)),
            pl.BlockSpec((1, WIDE), lambda h: (0, h)),
        ],
        out_specs=pl.BlockSpec((ROUNDS, count, WIDE), lambda h: (h, 0, 0)),
        out_shape=jax.ShapeDtypeStruct((LOCAL_PAIRS, count, WIDE), BF16),
        scratch_shapes=[pltpu.VMEM((count, WIDE), BF16)],
        compiler_params=pltpu.CompilerParams(vmem_limit_bytes=48 << 20),
        cost_estimate=SMALL,
        name="sort_rows",
    )(order, inputs, weights, bias)


def sort_grads_body(place_ref, rows_ref, out_ref):
    count = place_ref.shape[1]
    half = count // 2
    head = pl.program_id(0)
    chunk = 256
    row = lax.broadcasted_iota(jnp.int32, (chunk, count), 0)
    low = lax.broadcasted_iota(jnp.int32, (count, TILE), 1) < HEAD
    for step in range(HEADS_OWN):

        @pl.when(head == step)
        def _():
            if step < 2:
                tile = rows_ref[0:count, :].astype(F32)
                tile = jnp.where(low if step == 0 else jnp.logical_not(low), tile, 0.0).astype(BF16)
            else:
                both = rows_ref[count : count + half, :].astype(F32)
                tile = jnp.concatenate([both, turn_half(both)], axis=0)
                tile = jnp.where(low, tile, 0.0).astype(BF16)
            for turn in range(ROUNDS):
                pair = step * ROUNDS + turn
                for part in range(count // chunk):
                    where = pl.ds(part * chunk, chunk)
                    picked = place_ref[pair : pair + 1, :] == row + part * chunk
                    picked = picked.astype(F32).astype(BF16)
                    out_ref[turn, where, :] = jnp.dot(
                        picked, tile, preferred_element_type=F32
                    ).astype(BF16)


def sort_grads(order, rows):
    count = order.shape[1]
    return pl.pallas_call(
        sort_grads_body,
        grid=(HEADS_OWN,),
        in_specs=[
            pl.BlockSpec((8, count), lambda h: (0, 0)),
            pl.BlockSpec(rows.shape, lambda h: (0, 0)),
        ],
        out_specs=pl.BlockSpec((ROUNDS, count, TILE), lambda h: (h, 0, 0)),
        out_shape=jax.ShapeDtypeStruct((LOCAL_PAIRS, count, TILE), BF16),
        compiler_params=pltpu.CompilerParams(vmem_limit_bytes=48 << 20),
        cost_estimate=SMALL,
        name="sort_grads",
    )(order, rows)


def plans_of(count):
    share = CLUSTER // UNIT
    half = UNIT // 2
    return (
        [(tuple(range(UNIT)), share)],
        [(tuple(range(i * half, (i + 1) * half)), 2 * share) for i in range(2)],
    )


def for_each_batch(is_long, count, batch, work):
    for wanted, plan in zip((1, 0), plans_of(count)):

        @pl.when(is_long == wanted)
        def _(plan=plan):
            for runs, share in plan:

                def step(group, carry, runs=runs, share=share):
                    first = pl.multiple_of(group * (batch * share), batch * share)
                    work(runs, pl.ds(first, batch * share), share)
                    return carry

                lax.fori_loop(0, count // share // batch, step, 0)


def batch_of(refs, runs, where, share, width):
    parts = [refs[r][0, where, :] for r in runs]
    return jnp.concatenate([p.reshape(p.shape[0] // share, share, width) for p in parts], axis=1)


def spread(refs, runs, where, share, columns, value):
    for i, r in enumerate(runs):
        part = value[:, i * share : (i + 1) * share]
        refs[r][0, where, columns] = part.reshape(part.shape[0] * share, TILE)


def products(form, left, right):
    return jnp.einsum(form, left, right, preferred_element_type=F32)


def softmax(first, second):
    scores = products("ued,ucd->uec", second, first) * (HEAD**-0.5)
    expo = jnp.exp(scores - jnp.max(scores, axis=1, keepdims=True))
    return expo * (1.0 / jnp.sum(expo, axis=1, keepdims=True))


def attend_body(long_ref, *refs):
    grouped, results = refs[:UNIT], refs[UNIT:]

    def work(runs, where, share):
        rows = batch_of(grouped, runs, where, share, WIDE)
        first = rows[..., :TILE]
        probs = softmax(first, rows[..., TILE:]).astype(BF16)
        mixed = products("uce,ued->ucd", jnp.swapaxes(probs, 1, 2), first).astype(BF16)
        spread(results, runs, where, share, slice(0, TILE), mixed)

    for_each_batch(long_ref[0], grouped[0].shape[1], 16, work)


def attend(is_long, grouped):
    count = grouped[0].shape[1]
    return pl.pallas_call(
        attend_body,
        grid_spec=pltpu.PrefetchScalarGridSpec(
            num_scalar_prefetch=1,
            grid=(LOCAL_PAIRS,),
            in_specs=[pl.BlockSpec((1, count, WIDE), lambda p, _: (p, 0, 0))] * UNIT,
            out_specs=[pl.BlockSpec((1, count, TILE), lambda p, _: (p, 0, 0))] * UNIT,
        ),
        out_shape=[jax.ShapeDtypeStruct((LOCAL_PAIRS, count, TILE), BF16)] * UNIT,
        compiler_params=pltpu.CompilerParams(vmem_limit_bytes=48 << 20),
        cost_estimate=SMALL,
        name="attend",
    )(is_long, *grouped)


def attend_back_body(long_ref, *refs):
    grouped, grads, results = refs[:UNIT], refs[UNIT : 2 * UNIT], refs[2 * UNIT :]
    batch = 16
    odd = (pl.program_id(0) // ROUNDS) % 2
    lane = lax.broadcasted_iota(jnp.int32, (batch, CLUSTER, TILE), 2)
    value_lane = (lane < HEAD) == (odd == 0)
    scale = HEAD**-0.5

    def work(runs, where, share):
        rows = batch_of(grouped, runs, where, share, WIDE)
        grad = batch_of(grads, runs, where, share, TILE)
        first, second = rows[..., :TILE], rows[..., TILE:]
        probs = softmax(first, second)
        grad_probs = products("ued,ucd->uec", first, grad)
        centre = jnp.sum(probs * grad_probs, axis=1, keepdims=True)
        grad_scores = (probs * (grad_probs - centre)).astype(BF16)
        grad_values = products("uec,ucd->ued", probs.astype(BF16), grad)
        grad_keys = products("uec,ucd->ued", grad_scores, first) * scale
        grad_query = products("uce,ued->ucd", jnp.swapaxes(grad_scores, 1, 2), second) * scale
        tile_one = jnp.where(value_lane, grad_values, grad_query).astype(BF16)
        tile_two = jnp.where(value_lane, 0.0, grad_keys).astype(BF16)
        spread(results, runs, where, share, slice(0, TILE), tile_one)
        spread(results, runs, where, share, slice(TILE, WIDE), tile_two)

    for_each_batch(long_ref[0], grouped[0].shape[1], batch, work)


def attend_back(is_long, grouped, grads):
    count = grouped[0].shape[1]
    return pl.pallas_call(
        attend_back_body,
        grid_spec=pltpu.PrefetchScalarGridSpec(
            num_scalar_prefetch=1,
            grid=(LOCAL_PAIRS,),
            in_specs=[pl.BlockSpec((1, count, WIDE), lambda p, _: (p, 0, 0))] * UNIT
            + [pl.BlockSpec((1, count, TILE), lambda p, _: (p, 0, 0))] * UNIT,
            out_specs=[pl.BlockSpec((1, count, WIDE), lambda p, _: (p, 0, 0))] * UNIT,
        ),
        out_shape=[jax.ShapeDtypeStruct((LOCAL_PAIRS, count, WIDE), BF16)] * UNIT,
        compiler_params=pltpu.CompilerParams(vmem_limit_bytes=56 << 20),
        cost_estimate=SMALL,
        name="attend_back",
    )(is_long, *grouped, *grads)


def unsorted(column_ref, step, rows_ref, part, chunk):
    count = rows_ref.shape[1]
    where = pl.ds(part * chunk, chunk)
    lane = lax.broadcasted_iota(jnp.int32, (chunk, count), 1)
    total = None
    for turn in range(ROUNDS):
        pair = step * ROUNDS + turn
        picked = (column_ref[where, pair : pair + 1] == lane).astype(F32).astype(BF16)
        more = jnp.dot(picked, rows_ref[turn], preferred_element_type=F32)
        total = more if total is None else total + more
    return total


def mix_body(place_ref, rows_ref, out_ref, column_ref):
    @pl.when(pl.program_id(0) == 0)
    def _():
        column_ref[...] = jnp.transpose(place_ref[...])

    count = rows_ref.shape[1]
    chunk = 256
    parts = count // chunk
    low = lax.broadcasted_iota(jnp.int32, (chunk, TILE), 1) < HEAD
    head = pl.program_id(0)
    for step in range(HEADS_OWN):

        @pl.when(head == step)
        def _():
            means = [0.5 * unsorted(column_ref, step, rows_ref, part, chunk) for part in range(parts)]
            for part in range(parts):
                where = pl.ds(part * chunk, chunk)
                if step == 0:
                    out_ref[where, :] = means[part].astype(BF16)
                elif step == 1:
                    out_ref[where, :] = jnp.where(low, out_ref[where, :].astype(F32), means[part]).astype(BF16)
                elif part < parts // 2:
                    both = jnp.where(low, means[part], turn_half(means[part + parts // 2]))
                    out_ref[pl.ds(count + part * chunk, chunk), :] = both.astype(BF16)


def mix(order, rows):
    count = rows.shape[1]
    packed = (count + count // 2, TILE)
    return pl.pallas_call(
        mix_body,
        grid=(HEADS_OWN,),
        in_specs=[
            pl.BlockSpec((8, count), lambda h: (0, 0)),
            pl.BlockSpec((ROUNDS, count, TILE), lambda h: (h, 0, 0)),
        ],
        out_specs=pl.BlockSpec(packed, lambda h: (0, 0)),
        out_shape=jax.ShapeDtypeStruct(packed, BF16),
        scratch_shapes=[pltpu.VMEM((count, 8), jnp.int32)],
        compiler_params=pltpu.CompilerParams(vmem_limit_bytes=48 << 20),
        cost_estimate=SMALL,
        name="mix",
    )(order, rows)


def gather_grads_body(place_ref, rows_ref, out_ref, column_ref):
    @pl.when(pl.program_id(0) == 0)
    def _():
        column_ref[...] = jnp.transpose(place_ref[...])

    count = rows_ref.shape[1]
    chunk = 256
    head = pl.program_id(0)
    for step in range(HEADS_OWN):

        @pl.when(head == step)
        def _():
            for part in range(count // chunk):
                where = pl.ds(part * chunk, chunk)
                out_ref[where, :] = unsorted(column_ref, step, rows_ref, part, chunk).astype(BF16)


def gather_grads(order, rows):
    count = rows.shape[1]
    return pl.pallas_call(
        gather_grads_body,
        grid=(HEADS_OWN,),
        in_specs=[
            pl.BlockSpec((8, count), lambda h: (0, 0)),
            pl.BlockSpec((ROUNDS, count, WIDE), lambda h: (h, 0, 0)),
        ],
        out_specs=pl.BlockSpec((count, WIDE), lambda h: (0, h)),
        out_shape=jax.ShapeDtypeStruct((count, HEADS_OWN * WIDE), BF16),
        scratch_shapes=[pltpu.VMEM((count, 8), jnp.int32)],
        compiler_params=pltpu.CompilerParams(vmem_limit_bytes=48 << 20),
        cost_estimate=SMALL,
        name="gather_grads",
    )(order, rows)


ERF_TOP = (0.00022905065861350646, 0.0034082910107109506, 0.050955695062380861, 0.18520832239976145, 1.128379143519084)
ERF_BOTTOM = (
    -1.1791602954361697e-7,
    0.000023547966471313185,
    0.0010179625278914885,
    0.014070470171167667,
    0.11098505178285362,
    0.49746925110067538,
    1.0,
)


def polynomial(value, factors):
    total = jnp.full_like(value, factors[0])
    for factor in factors[1:]:
        total = total * value + factor
    return total


def error_function(value):
    value = jnp.clip(value, -3.832506856900711, 3.832506856900711)
    square = value * value
    return value * polynomial(square, ERF_TOP) / polynomial(square, ERF_BOTTOM)


VEC_ROWS = 16
FFN_TILE = 256


def layer_body(
    n_shards,
    table_ref,
    *refs,
):
    shards, refs = refs[:n_shards], refs[n_shards:]
    parts, refs = refs[:UNIT], refs[UNIT:]
    x_ref, cot_ref, vec_ref, result_ref, first_ref, sums_ref, kept_ref, sent_ref = refs[:8]
    backs, refs = refs[8 : 8 + UNIT], refs[8 + UNIT :]
    w_ref, packed_ref, mixed_ref, hidden_ref, act_ref, down_ref, up_ref, attn_ref, back_ref = refs[:9]
    slope_ref, stage_ref, weight_sem, part_sem, stage_sem = refs[9:]
    count = x_ref.shape[0]
    half = count // 2
    per_shard, n_weights, shard_rows = shards[0].shape[:3]
    member = table_ref[0]
    for k in range(UNIT):
        pltpu.make_async_copy(parts[k], packed_ref.at[member ^ k], part_sem.at[k]).start()
    for b in range(n_weights):
        for n in range(n_shards * per_shard):
            row = pl.multiple_of(table_ref[6 + n], shard_rows)
            pltpu.make_async_copy(
                shards[n // per_shard].at[n % per_shard, b], w_ref.at[b, pl.ds(row, shard_rows), :], weight_sem.at[b]
            ).start()
    for k in range(UNIT):
        pltpu.make_async_copy(parts[k], packed_ref.at[member ^ k], part_sem.at[k]).wait()
    for b in range(n_weights):
        pltpu.make_async_copy(w_ref.at[b], w_ref.at[b], weight_sem.at[b]).wait()

    sums_ref[...] = jnp.zeros_like(sums_ref)
    low = lax.broadcasted_iota(jnp.int32, (FFN_TILE, TILE), 1) < HEAD
    vec = [vec_ref[i : i + 1, :] for i in range(8 + FFB)]
    gain_one, shift_one, gain_two, shift_two = vec[:4]
    bias_out, bias_down = vec[6], vec[7]

    def add_sum(row, value):
        sums_ref[row : row + 1, :] += jnp.sum(value, axis=0, keepdims=True)

    def tile_step(i, carry):
        rows = pl.ds(pl.multiple_of(i * FFN_TILE, FFN_TILE), FFN_TILE)
        is_first = i * FFN_TILE < half
        extra = pl.ds(pl.multiple_of(count + lax.rem(i * FFN_TILE, half), FFN_TILE), FFN_TILE)

        def pair(m):
            return packed_ref[m, rows, :].astype(F32)

        def single(m):
            value = packed_ref[m, extra, :].astype(F32)
            return jnp.where(is_first, value, turn_half(value))

        for m in (0, 2):
            at = m * (HEADS_OWN * HEAD)
            nxt = turn_half(pair(m + 1))
            mixed_ref[rows, at : at + TILE] = pair(m).astype(BF16)
            mixed_ref[rows, at + TILE : at + 2 * TILE] = jnp.where(low, single(m), nxt).astype(BF16)
            mixed_ref[rows, at + 2 * TILE : at + 3 * TILE] = jnp.where(
                low, nxt, turn_half(single(m + 1))
            ).astype(BF16)
        attention = jnp.dot(mixed_ref[rows, :], w_ref[0], preferred_element_type=F32) + bias_out
        normed_one, rstd_one = normalize(x_ref[rows, :].astype(F32) + attention)
        hidden = normed_one * gain_one + shift_one
        hidden_low = hidden.astype(BF16)
        hidden_ref[rows, :] = hidden_low
        down = jnp.broadcast_to(bias_down, hidden.shape)
        for j in range(FFB):
            up = jnp.dot(hidden_low, w_ref[1 + j], preferred_element_type=F32) + vec[8 + j]
            phi = 0.5 * (1.0 + error_function(up * SQRT_HALF))
            slope_ref[j] = phi + up * jnp.exp(-0.5 * up * up) * INV_ROOT_TWO_PI
            act = (up * phi).astype(BF16)
            act_ref[j, rows, :] = act
            down = down + jnp.dot(act, w_ref[1 + FFB + j], preferred_element_type=F32)
        normed_two, rstd_two = normalize(hidden + down)
        result_ref[rows, :] = (normed_two * gain_two + shift_two).astype(BF16)
        grad_result = cot_ref[rows, :].astype(F32)
        add_sum(2, grad_result * normed_two)
        add_sum(3, grad_result)
        grad_second = norm_back(grad_result * gain_two, normed_two, rstd_two)
        grad_down = grad_second.astype(BF16)
        down_ref[rows, :] = grad_down
        add_sum(7, grad_down.astype(F32))
        grad_hidden = grad_second
        for j in range(FFB):
            grad_up = (outer_cols(grad_down, w_ref[1 + FFB + j]) * slope_ref[j]).astype(BF16)
            up_ref[j, rows, :] = grad_up
            add_sum(8 + j, grad_up.astype(F32))
            grad_hidden = grad_hidden + outer_cols(grad_up, w_ref[1 + j])
        add_sum(0, grad_hidden * normed_one)
        add_sum(1, grad_hidden)
        grad_first = norm_back(grad_hidden * gain_one, normed_one, rstd_one)
        first_ref[rows, :] = grad_first
        grad_attn = grad_first.astype(BF16)
        attn_ref[rows, :] = grad_attn
        add_sum(6, grad_attn.astype(F32))
        grad_mixed = (0.5 * outer_cols(grad_attn, w_ref[0])).astype(BF16).astype(F32)
        for m in range(UNIT):
            at = (m // 2) * 3 * TILE
            tiles = [grad_mixed[:, at + n * TILE : at + (n + 1) * TILE] for n in range(3)]
            if m % 2 == 0:
                two, one = tiles[0], tiles[1]
            else:
                two, one = turn_half(jnp.where(low, tiles[2], tiles[1])), turn_half(tiles[2])
            back_ref[member ^ m, rows, :] = two.astype(BF16)

            @pl.when(is_first)
            def _(one=one, m=m):
                back_ref[member ^ m, extra, :] = jnp.where(low, one, 0.0).astype(BF16)

            @pl.when(jnp.logical_not(is_first))
            def _(one=one, m=m):
                old = back_ref[member ^ m, extra, :].astype(F32)
                back_ref[member ^ m, extra, :] = jnp.where(low, old, turn_half(one)).astype(BF16)

        return carry

    lax.fori_loop(0, count // FFN_TILE, tile_step, 0)
    for k in range(UNIT):
        backs[k][...] = back_ref[k]

    core, bits = table_ref[1], [table_ref[2 + d] for d in range(4)]
    piece, half_columns = kept_ref.shape[3:]
    n_parts = kept_ref.shape[0]
    per_part = n_weights // n_parts

    def copies(block, slot, half, target):
        part = block // per_part
        made = []
        for index in range(16):
            x, zh, y, zl = ((index >> s) % 2 for s in range(4))
            rel = {"x": x ^ bits[0], "y": y ^ bits[1], "zl": zl ^ bits[2], "zh": zh ^ bits[3]}
            place = 0
            for name in PART_ORDERS[part]:
                place = place * 2 + rel[name]
            made.append(
                pltpu.make_async_copy(
                    stage_ref.at[
                        slot, pl.ds(index * piece, piece), pl.ds(half * half_columns, half_columns)
                    ],
                    target.at[part, place, block % per_part],
                    stage_sem.at[slot, half * 16 + index],
                )
            )
        return made

    def send(block, slot):
        for half in range(2):

            @pl.when(core == half)
            def _(half=half):
                for copy in copies(block, slot, half, kept_ref):
                    copy.start()

            @pl.when(core != half)
            def _(half=half):
                for copy in copies(block, slot, half, sent_ref):
                    copy.start()

    def sent(block, slot):
        for half in range(2):
            for copy in copies(block, slot, half, kept_ref):
                copy.wait()

    plan = [(attn_ref, None, mixed_ref, None, 0)]
    plan += [(down_ref, None, act_ref, j, 1 + FFB + j) for j in range(FFB)]
    plan += [(up_ref, j, hidden_ref, None, 1 + j) for j in range(FFB)]
    for n, (left, lj, right, rj, block) in enumerate(plan):
        slot = n % 2
        if n >= 2:
            sent(plan[n - 2][4], slot)
        value = inner_rows(
            left[...] if lj is None else left[lj], right[...] if rj is None else right[rj]
        )
        stage_ref[slot] = value.astype(BF16)
        send(block, slot)
    for n in (len(plan) - 2, len(plan) - 1):
        sent(plan[n][4], n % 2)


PART_ORDERS = (("x", "y", "zl", "zh"), ("y", "zl", "zh", "x"), ("zl", "zh", "x", "y"))


def layer(table, shards, parts, inputs, cotangent, vectors):
    count = inputs.shape[0]
    n_weights = 1 + 2 * FFB
    n_shards = len(shards)
    anywhere = pl.BlockSpec(memory_space=pl.ANY)
    inside = pl.BlockSpec(memory_space=pltpu.VMEM)
    packed = parts[0].shape
    return pl.pallas_call(
        functools.partial(layer_body, n_shards),
        in_specs=[pl.BlockSpec(memory_space=pltpu.SMEM)] + [anywhere] * (n_shards + UNIT) + [inside] * 3,
        out_specs=[inside, inside, inside, anywhere, anywhere] + [inside] * UNIT,
        out_shape=[
            jax.ShapeDtypeStruct((count, D), BF16),
            jax.ShapeDtypeStruct((count, D), F32),
            jax.ShapeDtypeStruct((VEC_ROWS, D), F32),
            jax.ShapeDtypeStruct((3, 16, n_weights // 3, D // 16, D // 2), BF16),
            jax.ShapeDtypeStruct((3, 16, n_weights // 3, D // 16, D // 2), BF16),
        ]
        + [jax.ShapeDtypeStruct(packed, BF16)] * UNIT,
        scratch_shapes=[
            pltpu.VMEM((n_weights, D, D), BF16),
            pltpu.VMEM((UNIT, *packed), BF16),
            pltpu.VMEM((count, D), BF16),
            pltpu.VMEM((count, D), BF16),
            pltpu.VMEM((FFB, count, D), BF16),
            pltpu.VMEM((count, D), BF16),
            pltpu.VMEM((FFB, count, D), BF16),
            pltpu.VMEM((count, D), BF16),
            pltpu.VMEM((UNIT, *packed), BF16),
            pltpu.VMEM((FFB, FFN_TILE, D), F32),
            pltpu.VMEM((2, D, D), BF16),
            pltpu.SemaphoreType.DMA((n_weights,)),
            pltpu.SemaphoreType.DMA((UNIT,)),
            pltpu.SemaphoreType.DMA((2, 32)),
        ],
        compiler_params=pltpu.CompilerParams(vmem_limit_bytes=60 << 20),
        cost_estimate=SMALL,
        name="layer",
    )(table, *shards, *parts, inputs, cotangent, vectors)


def qkv_back_body(scalars_ref, *refs):
    grads, inputs, kept_ref, sent_ref, bias_ref, all_ref = refs[:4], refs[4:8], *refs[8:]
    core, unit = scalars_ref[0], scalars_ref[1]
    columns = all_ref.shape[4]
    step = 32
    per_unit = all_ref.shape[3]
    bias_ref[...] = jnp.zeros_like(bias_ref)
    for head in range(HEADS_OWN):
        at = slice(head * WIDE, (head + 1) * WIDE)
        total = inner_rows(grads[0][:, at], inputs[0][...])
        bias = jnp.sum(grads[0][:, at].astype(F32), axis=0, keepdims=True)
        for k in range(1, UNIT):
            total = total + inner_rows(grads[k][:, at], inputs[k][...])
            bias = bias + jnp.sum(grads[k][:, at].astype(F32), axis=0, keepdims=True)
        bias_ref[0:1, at] = bias
        firsts = (HEAD, 3 * HEAD, 0) if head % 2 == 0 else (0, 2 * HEAD, HEAD)
        for block, first in enumerate(firsts):
            for i in range(HEAD // step):
                row = head * HEAD + i * step
                rows = total[first + i * step : first + (i + 1) * step]
                for c in range(2):
                    all_ref[
                        c ^ core, row // per_unit ^ unit, block, row % per_unit : row % per_unit + step, :
                    ] = rows[:, c * columns : (c + 1) * columns].astype(BF16)
    kept_ref[...] = all_ref[0]
    sent_ref[...] = all_ref[1]


def qkv_back(scalars, grads, inputs):
    inside = pl.BlockSpec(memory_space=pltpu.VMEM)
    shape = (2, 3, HEADS_OWN * HEAD // 2, D // 2)
    return pl.pallas_call(
        qkv_back_body,
        in_specs=[pl.BlockSpec(memory_space=pltpu.SMEM)] + [inside] * (2 * UNIT),
        out_specs=[inside] * 3,
        out_shape=[
            jax.ShapeDtypeStruct(shape, BF16),
            jax.ShapeDtypeStruct(shape, BF16),
            jax.ShapeDtypeStruct((8, HEADS_OWN * WIDE), F32),
        ],
        scratch_shapes=[pltpu.VMEM((2, *shape), BF16)],
        compiler_params=pltpu.CompilerParams(vmem_limit_bytes=56 << 20),
        cost_estimate=SMALL,
        name="qkv_back",
    )(scalars, *grads, *inputs)


def pack_body(slot_block_ref, *refs):
    half = (len(refs) - 2) // 2
    kept, got, out_ref, all_ref = refs[:half], refs[half : 2 * half], refs[-2], refs[-1]
    per_part = kept[0].shape[1]
    for p in range(half):
        for b in range(per_part):
            all_ref[p * per_part + b] = (kept[p][0, b] + got[p][0, b].astype(F32)).astype(BF16)
    for s in range(out_ref.shape[0] * out_ref.shape[1]):
        out_ref[s // out_ref.shape[1], s % out_ref.shape[1]] = all_ref[jnp.maximum(slot_block_ref[s] - 3, 0)]


def pack(slot_block, kept, got, n_grp, slots):
    shape = kept[0].shape[2:]
    inside = pl.BlockSpec(memory_space=pltpu.VMEM)
    return pl.pallas_call(
        pack_body,
        in_specs=[pl.BlockSpec(memory_space=pltpu.SMEM)] + [inside] * (2 * len(kept)),
        out_specs=inside,
        out_shape=jax.ShapeDtypeStruct((n_grp, slots, *shape), BF16),
        scratch_shapes=[pltpu.VMEM((len(kept) * kept[0].shape[1], *shape), BF16)],
        compiler_params=pltpu.CompilerParams(vmem_limit_bytes=32 << 20),
        cost_estimate=SMALL,
        name="pack",
    )(slot_block, *kept, *got)


def rotate_in_body(mine_ref, keep_ref, got_ref, high_ref, low_ref, out_ref, grad_ref):
    slots, n_tok = got_ref.shape[1], out_ref.shape[0]
    rows, columns = got_ref.shape[2:]
    width = out_ref.shape[3]
    for s in range(slots):
        block = mine_ref[s]

        @pl.when(block < 3)
        def _(s=s, block=block):
            grad_ref[...] = keep_ref[jnp.minimum(block, 2)]

        @pl.when(block >= 3)
        def _(s=s):
            for g in range(got_ref.shape[0]):
                x, c = g // 2, g % 2
                grad_ref[x * rows : (x + 1) * rows, c * columns : (c + 1) * columns] = got_ref[g, s]

        grad = grad_ref[...]
        part = jnp.dot(grad, high_ref[s], preferred_element_type=F32)
        part = jnp.transpose(part + jnp.dot(grad, low_ref[s], preferred_element_type=F32))
        for r in range(n_tok):
            out_ref[r, s] = part[r * width : (r + 1) * width].astype(BF16)


def rotate_in(mine, keep, got, left, n_tok):
    slots, width = got.shape[1], keep.shape[1]
    inside = pl.BlockSpec(memory_space=pltpu.VMEM)
    return pl.pallas_call(
        rotate_in_body,
        in_specs=[pl.BlockSpec(memory_space=pltpu.SMEM)] + [inside] * 4,
        out_specs=inside,
        out_shape=jax.ShapeDtypeStruct((n_tok, slots, width, width), BF16),
        scratch_shapes=[pltpu.VMEM(keep.shape[1:], BF16)],
        compiler_params=pltpu.CompilerParams(vmem_limit_bytes=48 << 20),
        cost_estimate=SMALL,
        name="rotate_in",
    )(mine, keep, got, *left)


def moments_body(place, got_ref, high_ref, low_ref, one_ref, two_ref, new_one_ref, new_two_ref, out_ref):
    n_tok, slots, width = got_ref.shape[:3]
    for s in range(slots):
        rotated = jnp.zeros(one_ref.shape[1:], F32)
        for t in range(n_tok):
            at = slice(place[t] * width, (place[t] + 1) * width)
            part = got_ref[t, s]
            rotated = rotated + jnp.dot(part, high_ref[s, at], preferred_element_type=F32)
            rotated = rotated + jnp.dot(part, low_ref[s, at], preferred_element_type=F32)
        new_one = BETA_ONE * one_ref[s] + (1.0 - BETA_ONE) * rotated
        new_two = BETA_TWO * two_ref[s] + (1.0 - BETA_TWO) * rotated * rotated
        new_one_ref[s] = new_one
        new_two_ref[s] = new_two
        direction = (new_one / (jnp.sqrt(new_two) + ADAM_EPS)).astype(BF16)
        for t in range(n_tok):
            at = slice(place[t] * width, (place[t] + 1) * width)
            turned = outer_cols(direction, high_ref[s, at]) + outer_cols(direction, low_ref[s, at])
            out_ref[t, s] = turned.astype(BF16)


def moments(place, got, right, one, two):
    n_tok, slots, width = got.shape[:3]
    inside = pl.BlockSpec(memory_space=pltpu.VMEM)
    return pl.pallas_call(
        functools.partial(moments_body, tuple(place)),
        in_specs=[inside] * 5,
        out_specs=[inside] * 3,
        out_shape=[
            jax.ShapeDtypeStruct(one.shape, F32),
            jax.ShapeDtypeStruct(one.shape, F32),
            jax.ShapeDtypeStruct(got.shape, BF16),
        ],
        compiler_params=pltpu.CompilerParams(vmem_limit_bytes=48 << 20),
        cost_estimate=SMALL,
        name="moments",
    )(got, *right, one, two)


def rotate_out_body(got_ref, high_ref, low_ref, out_ref, rows_ref):
    n_tok, slots, width = got_ref.shape[:3]
    for s in range(slots):
        for r in range(n_tok):
            rows_ref[r * width : (r + 1) * width, :] = got_ref[r, s]
        rows = rows_ref[...]
        change = jnp.dot(high_ref[s], rows, preferred_element_type=F32)
        change = change + jnp.dot(low_ref[s], rows, preferred_element_type=F32)
        for r in range(n_tok):
            out_ref[r, s] = change[r * width : (r + 1) * width].astype(BF16)


def rotate_out(got, left):
    n_tok, slots, width = got.shape[:3]
    inside = pl.BlockSpec(memory_space=pltpu.VMEM)
    return pl.pallas_call(
        rotate_out_body,
        in_specs=[inside] * 3,
        out_specs=inside,
        out_shape=jax.ShapeDtypeStruct(got.shape, BF16),
        scratch_shapes=[pltpu.VMEM((n_tok * width, width), BF16)],
        compiler_params=pltpu.CompilerParams(vmem_limit_bytes=48 << 20),
        cost_estimate=SMALL,
        name="rotate_out",
    )(got, *left)


def apply_body(place, got_ref, master_ref, out_ref):
    n_tok, slots, width = got_ref.shape[:3]
    for s in range(slots):
        for t in range(n_tok):
            at = slice(place[t] * width, (place[t] + 1) * width)
            out_ref[s, :, at] = master_ref[s, :, at] - RATE_MATRIX * got_ref[t, s].astype(F32)


def apply_change(place, got, master):
    inside = pl.BlockSpec(memory_space=pltpu.VMEM)
    return pl.pallas_call(
        functools.partial(apply_body, tuple(place)),
        in_specs=[inside] * 2,
        out_specs=inside,
        out_shape=jax.ShapeDtypeStruct(master.shape, F32),
        compiler_params=pltpu.CompilerParams(vmem_limit_bytes=48 << 20),
        cost_estimate=SMALL,
        name="apply_change",
    )(got, master)


def swap(value, axis, bit):
    size = lax.axis_size(axis)
    return lax.ppermute(value, axis, [(i, i ^ bit) for i in range(size)])


def exchange_unit(parts):
    return [parts[0]] + [swap(parts[k], "tok", k) for k in range(1, UNIT)]


LINKS = {"x": ("grp", 2), "y": ("tok", 1), "zl": ("tok", 2), "zh": ("tok", 4)}


def starts_of(lengths):
    index = jnp.arange(lengths.shape[0])
    return jnp.sum(jnp.where(index[None, :] < index[:, None], lengths[None, :], 0), axis=1)


LINKS = {"x": ("grp", 2), "y": ("tok", 1), "zl": ("tok", 2), "zh": ("tok", 4)}


def starts_of(lengths):
    index = jnp.arange(lengths.shape[0])
    return jnp.sum(jnp.where(index[None, :] < index[:, None], lengths[None, :], 0), axis=1)


def total_of(value):
    for axis in ("grp", "tok"):
        bit = 1
        while bit < lax.axis_size(axis):
            value = value + swap(value, axis, bit)
            bit *= 2
    return value


def pick(values, index):
    return lax.dynamic_index_in_dim(values, index, 0, keepdims=False)


def split_heads(columns):
    query, keys, values = (c.reshape(HEADS_OWN, HEAD) for c in columns)
    zero = jnp.zeros((HEAD,), query.dtype)
    tiles = []
    for h in range(HEADS_OWN):
        tiles += [values[h], query[h], zero, keys[h]] if h % 2 == 0 else [query[h], values[h], keys[h], zero]
    return jnp.concatenate(tiles)


def join_heads(tiles):
    parts = tiles.reshape(HEADS_OWN, 4, HEAD, *tiles.shape[1:])
    at = [(1, 0), (3, 2), (0, 1)]
    return jnp.stack(
        [jnp.concatenate([parts[h, at[i][h % 2]] for h in range(HEADS_OWN)], axis=0) for i in range(3)]
    )


def doubled(value):
    high = value.astype(BF16)
    return high, (value - high.astype(F32)).astype(BF16)


def together(*groups):
    flat, tree = jax.tree.flatten(groups)
    return jax.tree.unflatten(tree, lax.optimization_barrier(flat))


def fast(
    tokens,
    cotangent,
    lengths,
    clusters,
    owners,
    master,
    bases,
    moment_one,
    moment_two,
    vectors,
    vector_one,
    vector_two,
):
    n_tok = lax.axis_size("tok")
    n_grp = lax.axis_size("grp")
    tok = lax.axis_index("tok")
    grp = lax.axis_index("grp")
    tok_count = tokens.shape[1]
    rows_dev = master.shape[0]
    slots = master.shape[1]
    blocks_all = slots * n_grp
    member = tok & (UNIT - 1)
    unit = tok >> 2
    place = [2 * (t % UNIT) + t // UNIT for t in range(n_tok)]
    own_width = HEADS_OWN * HEAD

    slot_block = jnp.argsort(owners, stable=True).astype(jnp.int32)
    block_slot = jnp.argsort(slot_block, stable=True).astype(jnp.int32)

    core, bit_x = grp & 1, grp >> 1
    inputs = tokens[0]

    near, far = swap(inputs, "tok", 1), swap(inputs, "tok", 2)
    local = jnp.transpose(master.astype(BF16), (1, 0, 2))
    beside, over = swap(local, "grp", 1), swap(local, "grp", 2)

    item_starts = starts_of(lengths[0])
    unit_start = unit * UNIT * tok_count
    middle = unit_start + UNIT // 2 * tok_count
    start_of_middle = jnp.max(jnp.where(item_starts <= middle, item_starts, 0))
    is_long = (start_of_middle <= unit_start).astype(jnp.int32).reshape(1)
    share = CLUSTER // UNIT * (2 - is_long)
    placed = places(jnp.concatenate([share, member.reshape(1)]), clusters[0])
    left, right = doubled(bases[0]), doubled(bases[1])
    (over, left, right, placed) = together(over, left, right, placed)
    across = swap(over, "grp", 1)

    orders = exchange_unit(placed)
    (near, far, beside, over, across) = together(near, far, beside, over, across)
    part_rows = rows_dev // 2

    scalars = jnp.concatenate([block_slot, jnp.stack([grp, core, member])]).astype(jnp.int32)
    *by_owner, rest_rows = arrange(scalars, [local, beside, over, across], blocks_all)
    theirs = exchange_unit(by_owner)
    half = tok_count // 2
    third = (swap(near[:half], "tok", 2), swap(far[half:], "tok", 1))
    (theirs, orders) = together(theirs, orders)
    theirs = jnp.stack(theirs)
    theirs_far = swap(theirs, "tok", UNIT)
    mine_all = jnp.concatenate([theirs, theirs_far], axis=0)
    others_all = swap(mine_all, "grp", 1)
    sources = tok ^ jnp.arange(2 * UNIT, dtype=jnp.int32)
    cores = core ^ jnp.arange(2, dtype=jnp.int32)
    firsts = (sources[None, :] * rows_dev + cores[:, None] * part_rows).reshape(-1)
    (third, others_all, rest_rows) = together(third, others_all, rest_rows)
    own_weights = assemble(firsts, [mine_all, others_all])

    def columns_of(value, m):
        return lax.dynamic_slice_in_dim(value, m * own_width, own_width, value.ndim - 1)

    own_bias = split_heads(
        [columns_of(vectors[4], member), jnp.zeros((own_width,), F32), columns_of(vectors[5], member)]
    ).reshape(1, -1)
    ring = [(i, (i + 2) % n_tok) for i in range(n_tok)]
    depth = n_tok // 2
    steps, flips, mine_rest, other_rest = [rest_rows], [], [], []

    def advance():
        if len(steps) < depth:
            steps.append(lax.ppermute(steps[-1], "tok", ring))
        flips.append(swap(steps[len(flips)], "tok", 1))

    def cross():
        k = len(mine_rest)
        mine_rest.append(jnp.stack([steps[k], flips[k]]))
        other_rest.append(swap(mine_rest[k], "grp", 1))

    advance()
    grouped = [sort_rows(orders[0], inputs, own_weights, own_bias)]
    grouped.append(sort_rows(orders[1], near, own_weights, own_bias))
    (grouped, far, third, steps[1], flips[0]) = together(grouped, far, third, steps[1], flips[0])
    advance()
    cross()
    grouped.append(sort_rows(orders[2], far, own_weights, own_bias))
    unit_inputs = [inputs, near, far, jnp.concatenate(third, axis=0)]
    grouped.append(sort_rows(orders[3], unit_inputs[3], own_weights, own_bias))
    (grouped, steps[2], flips[1], other_rest) = together(grouped, steps[2], flips[1], other_rest)
    advance()
    cross()
    sorted_out = attend(is_long, grouped)
    (sorted_out, steps[3], flips[2], other_rest) = together(sorted_out, steps[3], flips[2], other_rest)
    advance()
    cross()
    mixed = [None] * UNIT
    mixed[3] = mix(orders[3], sorted_out[3])
    mixed[2] = mix(orders[2], sorted_out[2])
    mixed[1] = mix(orders[1], sorted_out[1])
    (mixed[3], last) = together(mixed[3], sorted_out[0])
    mixed[0] = mix(orders[0], last)
    mixed_parts = exchange_unit(mixed)
    (mixed_parts, flips[-1], other_rest, held_weights) = together(
        mixed_parts, flips[-1], other_rest, own_weights
    )
    cross()
    shards = mine_rest + other_rest
    sources = (tok + n_tok - 2 * jnp.arange(depth, dtype=jnp.int32)) & (n_tok - 1)
    sources = (sources[:, None] ^ jnp.arange(2, dtype=jnp.int32)[None, :]).reshape(-1)
    firsts = (sources[None, :] * rows_dev + cores[:, None] * part_rows).reshape(-1)

    turned_weights = [swap(held_weights, "tok", k) for k in range(1, UNIT)]
    place_bits = jnp.stack([member, core, bit_x, tok & 1, (tok >> 1) & 1, tok >> 2]).astype(jnp.int32)
    table = jnp.concatenate([place_bits, firsts])
    result, grad_first, sums, kept, sent_pieces, *back = layer(
        table, shards, mixed_parts, inputs, cotangent[0], vectors
    )
    (turned_weights, kept, sent_pieces, back) = together(turned_weights, kept, sent_pieces, back)

    grad_parts = exchange_unit(back)
    other = swap(sent_pieces, "grp", 1)
    sums_of = [kept[p].astype(F32) + other[p].astype(F32) for p in range(3)]

    def halves(values):
        return [v[: v.shape[0] // 2] for v in values], [v[v.shape[0] // 2 :].astype(BF16) for v in values]

    def exchanged(sent_now, stage):
        return [swap(v, *LINKS[PART_ORDERS[p][stage]]) for p, v in enumerate(sent_now)]

    def joined(kept_now, got_now):
        return [k + g.astype(F32) for k, g in zip(kept_now, got_now)]

    kept_now, sent_now = halves(sums_of)
    sorted_grads = [sort_grads(orders[0], grad_parts[0])]
    (sent_now, grad_parts, sorted_grads) = together(sent_now, grad_parts, sorted_grads)
    got_now = exchanged(sent_now, 0)
    sorted_grads += [sort_grads(orders[k], grad_parts[k]) for k in range(1, UNIT)]
    sorted_back = attend_back(is_long, grouped, sorted_grads)
    kept_now, sent_now = halves(joined(kept_now, got_now))
    (sent_now, sorted_back) = together(sent_now, sorted_back)
    got_now = exchanged(sent_now, 1)
    own_grads = [None] * UNIT
    own_grads[3] = gather_grads(orders[3], sorted_back[3])
    own_grads[2] = gather_grads(orders[2], sorted_back[2])
    kept_now, sent_now = halves(joined(kept_now, got_now))
    (sent_now, own_grads[2], own_grads[3], sorted_back) = together(
        sent_now, own_grads[2], own_grads[3], sorted_back
    )
    got_now = exchanged(sent_now, 2)
    home_grads = [None, None, None, swap(own_grads[3], "tok", 3)]
    for k in (1, 0):
        own_grads[k] = gather_grads(orders[k], sorted_back[k])
    kept_qkv, sent_qkv, bias_qkv = qkv_back(jnp.stack([core, unit]).astype(jnp.int32), own_grads, unit_inputs)
    (got_now, kept_qkv, sent_qkv) = together(got_now, kept_qkv, sent_qkv)
    kept_now = joined(kept_now, got_now)
    sent_now = halves(kept_now)[1]
    got_now = exchanged(sent_now, 3)

    bias_query, _, bias_value = join_heads(bias_qkv[0])
    bias_rows = lax.dynamic_update_slice_in_dim(
        jnp.zeros((2, D), F32), jnp.stack([bias_query, bias_value]), member * own_width, 1
    )
    total = sums[: 8 + FFB] + jnp.pad(bias_rows, ((4, 2 + FFB), (0, 0)))

    more = swap(total, "grp", 1)
    keep = kept_qkv.astype(F32) + swap(sent_qkv, "grp", 1).astype(F32)
    (keep, more) = together(keep, more)
    total = total + more
    more = swap(total, "tok", 1)
    unit_got = swap(keep[1].astype(BF16), "tok", UNIT)
    keep = keep[0] + unit_got.astype(F32)
    (keep, more, got_now, home_grads[3]) = together(keep, more, got_now, home_grads[3])
    total = total + more
    more = swap(total, "tok", 2)
    home_grads[1] = swap(own_grads[1], "tok", 1)
    home_grads[2] = swap(own_grads[2], "tok", 2)
    sent = pack(slot_block, kept_now, got_now, n_grp, slots)
    got = lax.all_to_all(sent, "grp", split_axis=0, concat_axis=0, tiled=True)
    keep = (keep + swap(keep.astype(BF16), "grp", 2).astype(F32)).astype(BF16)
    kept_core = (keep, swap(keep, "grp", 1))
    keep = jnp.concatenate(
        [jnp.where(core == 0, kept_core[0], kept_core[1]), jnp.where(core == 0, kept_core[1], kept_core[0])],
        axis=-1,
    )
    mine = lax.dynamic_slice_in_dim(slot_block, grp * slots, slots, 0)

    def to_tok(value):
        return lax.all_to_all(value, "tok", split_axis=0, concat_axis=0, tiled=True)

    part = to_tok(rotate_in(mine, keep, got, left, n_tok))
    grad_inputs = grad_first + outer_cols(own_grads[0], own_weights)
    (part, home_grads, grad_inputs, more) = together(part, home_grads[1:], grad_inputs, more)
    total = total + more
    more = swap(total, "tok", 4)
    by_slot_of = lambda value: jnp.transpose(value, (1, 0, 2))
    new_one, new_two, turned = moments(
        place, part, right, by_slot_of(moment_one), by_slot_of(moment_two)
    )
    turned = to_tok(turned)
    grad_inputs = grad_inputs + outer_cols(home_grads[0], turned_weights[0])
    grad_inputs = grad_inputs + outer_cols(home_grads[1], turned_weights[1])
    (turned, more, grad_inputs, home_grads[2]) = together(turned, more, grad_inputs, home_grads[2])
    total = total + more
    change = to_tok(rotate_out(turned, left))
    vector_total = total + swap(total, "grp", 2)
    new_master = by_slot_of(apply_change(place, change, by_slot_of(master)))
    new_one, new_two = by_slot_of(new_one), by_slot_of(new_two)
    grad_inputs = grad_inputs + outer_cols(home_grads[2], turned_weights[2])
    new_vec_one = BETA_ONE * vector_one + (1.0 - BETA_ONE) * vector_total
    new_vec_two = BETA_TWO * vector_two + (1.0 - BETA_TWO) * vector_total * vector_total
    new_vectors = vectors - RATE_VECTOR * new_vec_one / (jnp.sqrt(new_vec_two) + ADAM_EPS)
    return (
        result[None],
        grad_inputs[None],
        new_one,
        new_two,
        new_master,
        new_vec_one,
        new_vec_two,
        new_vectors,
    )


def general(
    tokens,
    cotangent,
    lengths,
    clusters,
    owners,
    master,
    bases,
    moment_one,
    moment_two,
    vectors,
    vector_one,
    vector_two,
):
    n_tok = lax.axis_size("tok")
    tok_count = tokens.shape[1]
    rows_dev = master.shape[0]
    slot_block = jnp.argsort(owners, stable=True)
    block_slot = jnp.argsort(slot_block, stable=True)
    slot_part = lax.all_gather(master.astype(jnp.bfloat16), "grp", axis=1, tiled=True)
    weights = lax.all_gather(slot_part, "tok", axis=0, tiled=True)
    blocks = jnp.stack([pick(jnp.transpose(weights, (1, 0, 2)), block_slot[b]) for b in range(weights.shape[1])], axis=1)
    w_qkv = blocks[:, 0:3, :].reshape(D, 3 * D)
    w_out = blocks[:, 3, :]
    w_up = blocks[:, 4 : 4 + FF // D, :].reshape(D, FF)
    w_down = jnp.transpose(blocks[:, 4 + FF // D :, :], (1, 0, 2)).reshape(FF, D)
    inputs = tokens[0]
    gain_one = vectors[0]
    shift_one = vectors[1]
    gain_two = vectors[2]
    shift_two = vectors[3]
    bias_qkv = jnp.concatenate([vectors[4], jnp.zeros((D,), jnp.float32), vectors[5]])
    qkv = (jnp.dot(inputs, w_qkv, preferred_element_type=jnp.float32) + bias_qkv).astype(
        jnp.bfloat16
    )
    heads = jnp.transpose(qkv.reshape(tok_count, 3, H, HEAD), (2, 0, 1, 3)).reshape(
        H, tok_count, 3 * HEAD
    )
    pair_rows = jnp.broadcast_to(heads[None], (ROUNDS, H, tok_count, 3 * HEAD)).reshape(
        PAIRS * tok_count, 3 * HEAD
    )
    position = lax.axis_index("tok") * tok_count + jnp.arange(tok_count, dtype=jnp.int32)
    item_starts = starts_of(lengths[0])
    item_start = jnp.max(
        jnp.where(item_starts[None, :] <= position[:, None], item_starts[None, :], 0), axis=1
    )
    per_dev = tok_count // CLUSTER
    group_clusters = n_tok * per_dev
    pair_ids = jnp.arange(PAIRS, dtype=jnp.int32)[:, None]
    global_cluster = item_start[None, :] // CLUSTER + clusters[0]
    unit_ids = (pair_ids * group_clusters + global_cluster).reshape(-1)
    owner_ids = ((global_cluster + pair_ids * per_dev) % n_tok).reshape(-1)
    send_order = jnp.argsort(owner_ids * (PAIRS * group_clusters) + unit_ids, stable=True)
    restore = jnp.argsort(send_order, stable=True)
    slot_rows = PAIRS * tok_count // n_tok
    units_here = PAIRS * tok_count // CLUSTER
    sent_rows = pair_rows[send_order].reshape(n_tok, slot_rows // 2, 6 * HEAD)
    sent_units = unit_ids[send_order].reshape(n_tok, slot_rows)
    got_rows, got_units = (
        lax.all_to_all(sent_rows, "tok", split_axis=0, concat_axis=0, tiled=True),
        lax.all_to_all(sent_units, "tok", split_axis=0, concat_axis=0, tiled=True),
    )
    arrange = jnp.argsort(got_units.reshape(-1), stable=True)
    undo = jnp.argsort(arrange, stable=True)
    grouped = got_rows.reshape(PAIRS * tok_count, 3 * HEAD)[arrange].reshape(
        units_here, CLUSTER, 3 * HEAD
    )
    query_rows = grouped[..., :HEAD]
    key_rows = grouped[..., HEAD : 2 * HEAD]
    value_rows = grouped[..., 2 * HEAD :]
    score_scale = HEAD ** (-0.5)
    scores = (
        jnp.einsum("ucd,ued->uce", query_rows, key_rows, preferred_element_type=jnp.float32)
        * score_scale
    )
    row_max = jnp.max(scores, axis=-1, keepdims=True)
    row_total = jnp.sum(jnp.exp(scores - row_max), axis=-1, keepdims=True)
    log_total = row_max + jnp.log(row_total)
    probs = jnp.exp(scores - log_total)
    cluster_out = jnp.einsum(
        "uce,ued->ucd", probs.astype(jnp.bfloat16), value_rows, preferred_element_type=jnp.float32
    ).astype(jnp.bfloat16)
    back_rows = cluster_out.reshape(PAIRS * tok_count, HEAD)[undo].reshape(
        n_tok, slot_rows // 2, 2 * HEAD
    )
    home_rows = lax.all_to_all(back_rows, "tok", split_axis=0, concat_axis=0, tiled=True)
    home_rows = (
        home_rows.reshape(PAIRS * tok_count, HEAD)[restore]
        .reshape(ROUNDS, H, tok_count, HEAD)
        .astype(jnp.float32)
    )
    mixed_heads = 0.5 * (home_rows[0] + home_rows[1])
    mixed_low = jnp.transpose(mixed_heads, (1, 0, 2)).reshape(tok_count, D).astype(jnp.bfloat16)
    attention = jnp.dot(mixed_low, w_out, preferred_element_type=jnp.float32) + vectors[6]
    first_sum = inputs.astype(jnp.float32) + attention
    normed_one, rstd_one = normalize(first_sum)
    hidden = normed_one * gain_one + shift_one
    hidden_low = hidden.astype(jnp.bfloat16)
    up_proj = jnp.dot(hidden_low, w_up, preferred_element_type=jnp.float32) + vectors[8:].reshape(
        FF
    )
    act_low = jax.nn.gelu(up_proj, approximate=False).astype(jnp.bfloat16)
    down_proj = jnp.dot(act_low, w_down, preferred_element_type=jnp.float32) + vectors[7]
    second_sum = hidden + down_proj
    normed_two, rstd_two = normalize(second_sum)
    result = (normed_two * gain_two + shift_two).astype(jnp.bfloat16)
    grad_result = cotangent[0].astype(jnp.float32)
    grad_gain_two = jnp.sum(grad_result * normed_two, axis=0)
    grad_shift_two = jnp.sum(grad_result, axis=0)
    grad_second = norm_back(grad_result * gain_two, normed_two, rstd_two)
    grad_down_low = grad_second.astype(jnp.bfloat16)
    grad_w_down = inner_rows(act_low, grad_down_low)
    grad_bias_down = jnp.sum(grad_down_low.astype(jnp.float32), axis=0)
    grad_act = outer_cols(grad_down_low, w_down)
    grad_up_low = (grad_act * gelu_slope(up_proj)).astype(jnp.bfloat16)
    grad_w_up = inner_rows(hidden_low, grad_up_low)
    grad_bias_up = jnp.sum(grad_up_low.astype(jnp.float32), axis=0)
    grad_hidden = grad_second + outer_cols(grad_up_low, w_up)
    grad_gain_one = jnp.sum(grad_hidden * normed_one, axis=0)
    grad_shift_one = jnp.sum(grad_hidden, axis=0)
    grad_first = norm_back(grad_hidden * gain_one, normed_one, rstd_one)
    grad_attn_low = grad_first.astype(jnp.bfloat16)
    grad_w_out = inner_rows(mixed_low, grad_attn_low)
    grad_bias_out = jnp.sum(grad_attn_low.astype(jnp.float32), axis=0)
    grad_mixed = outer_cols(grad_attn_low, w_out)
    grad_heads = jnp.transpose((0.5 * grad_mixed).reshape(tok_count, H, HEAD), (1, 0, 2)).astype(
        jnp.bfloat16
    )
    grad_pairs = jnp.broadcast_to(grad_heads[None], (ROUNDS, H, tok_count, HEAD)).reshape(
        PAIRS * tok_count, HEAD
    )
    sent_grad = grad_pairs[send_order].reshape(n_tok, slot_rows // 2, 2 * HEAD)
    got_grad = lax.all_to_all(sent_grad, "tok", split_axis=0, concat_axis=0, tiled=True)
    grad_cluster = got_grad.reshape(PAIRS * tok_count, HEAD)[arrange].reshape(
        units_here, CLUSTER, HEAD
    )
    scores_again = (
        jnp.einsum("ucd,ued->uce", query_rows, key_rows, preferred_element_type=jnp.float32)
        * score_scale
    )
    probs_again = jnp.exp(scores_again - log_total)
    probs_low = probs_again.astype(jnp.bfloat16)
    grad_values = jnp.einsum(
        "uce,ucd->ued", probs_low, grad_cluster, preferred_element_type=jnp.float32
    )
    grad_probs = jnp.einsum(
        "ucd,ued->uce", grad_cluster, value_rows, preferred_element_type=jnp.float32
    )
    centre = jnp.sum(probs_again * grad_probs, axis=-1, keepdims=True)
    grad_scores = (probs_again * (grad_probs - centre)).astype(jnp.bfloat16)
    grad_query = (
        jnp.einsum("uce,ued->ucd", grad_scores, key_rows, preferred_element_type=jnp.float32)
        * score_scale
    )
    grad_keys = (
        jnp.einsum("uce,ucd->ued", grad_scores, query_rows, preferred_element_type=jnp.float32)
        * score_scale
    )
    grad_grouped = jnp.concatenate(
        [
            grad_query.astype(jnp.bfloat16),
            grad_keys.astype(jnp.bfloat16),
            grad_values.astype(jnp.bfloat16),
        ],
        axis=-1,
    )
    back_grad = grad_grouped.reshape(PAIRS * tok_count, 3 * HEAD)[undo].reshape(
        n_tok, slot_rows // 2, 6 * HEAD
    )
    home_grad = lax.all_to_all(back_grad, "tok", split_axis=0, concat_axis=0, tiled=True)
    home_grad = (
        home_grad.reshape(PAIRS * tok_count, 3 * HEAD)[restore]
        .reshape(ROUNDS, H, tok_count, 3, HEAD)
        .astype(jnp.float32)
    )
    grad_qkv = (home_grad[0] + home_grad[1]).astype(jnp.bfloat16)
    grad_qkv = jnp.transpose(grad_qkv, (1, 2, 0, 3)).reshape(tok_count, 3 * D)
    grad_w_qkv = inner_rows(inputs, grad_qkv)
    grad_bias_qkv = jnp.sum(grad_qkv.astype(jnp.float32), axis=0)
    grad_inputs = grad_first + outer_cols(grad_qkv, w_qkv)
    grad_blocks = jnp.concatenate(
        [
            grad_w_qkv.reshape(D, 3, D),
            grad_w_out[:, None, :],
            grad_w_up.reshape(D, FF // D, D),
            jnp.transpose(grad_w_down.reshape(FF // D, D, D), (1, 0, 2)),
        ],
        axis=1,
    )
    by_block = jnp.transpose(grad_blocks, (1, 0, 2))
    slot_grads = jnp.stack([pick(by_block, slot_block[s]) for s in range(by_block.shape[0])], axis=1)
    vector_grads = jnp.concatenate(
        [
            jnp.stack(
                [
                    grad_gain_one,
                    grad_shift_one,
                    grad_gain_two,
                    grad_shift_two,
                    grad_bias_qkv[:D],
                    grad_bias_qkv[2 * D :],
                    grad_bias_out,
                    grad_bias_down,
                ]
            ),
            grad_bias_up.reshape(FF // D, D),
        ],
        axis=0,
    )
    vector_total = lax.psum(vector_grads, ("tok", "grp"))
    row_total = lax.psum_scatter(slot_grads, "tok", scatter_dimension=0, tiled=True)
    reduced = lax.psum_scatter(
        row_total.astype(jnp.bfloat16), "grp", scatter_dimension=1, tiled=True
    ).astype(jnp.float32)
    left_basis = bases[0]
    right_basis = bases[1]
    first_row = lax.axis_index("tok") * rows_dev
    turned_in = jnp.einsum("rse,sef->rsf", reduced, right_basis, precision=lax.Precision.HIGHEST)
    left_rows = lax.dynamic_slice_in_dim(left_basis, first_row, rows_dev, 1)
    picked = left_rows
    rotated = lax.psum_scatter(
        jnp.einsum("sri,rsf->isf", picked, turned_in, precision=lax.Precision.HIGHEST),
        "tok",
        scatter_dimension=0,
        tiled=True,
    )
    new_one = BETA_ONE * moment_one + (1.0 - BETA_ONE) * rotated
    new_two = BETA_TWO * moment_two + (1.0 - BETA_TWO) * rotated * rotated
    direction = new_one / (jnp.sqrt(new_two) + ADAM_EPS)
    turned_out = jnp.einsum("rse,sfe->rsf", direction, right_basis, precision=lax.Precision.HIGHEST)
    left_cols = lax.dynamic_slice_in_dim(left_basis, first_row, rows_dev, 2)
    picked = left_cols
    change = lax.psum_scatter(
        jnp.einsum("sir,rsf->isf", picked, turned_out, precision=lax.Precision.HIGHEST),
        "tok",
        scatter_dimension=0,
        tiled=True,
    )
    new_master = master - RATE_MATRIX * change
    new_vec_one = BETA_ONE * vector_one + (1.0 - BETA_ONE) * vector_total
    new_vec_two = BETA_TWO * vector_two + (1.0 - BETA_TWO) * vector_total * vector_total
    new_vectors = vectors - RATE_VECTOR * new_vec_one / (jnp.sqrt(new_vec_two) + ADAM_EPS)
    return (
        result[None],
        grad_inputs[None],
        new_one,
        new_two,
        new_master,
        new_vec_one,
        new_vec_two,
        new_vectors,
    )

def solution(mesh):
    n_tok, n_grp = mesh.shape["tok"], mesh.shape["grp"]

    def on_device(*args):
        lengths, clusters = args[2], args[3]
        unit = n_tok // (lengths.shape[1] - 1)
        suits = unit == UNIT and n_tok == 2 * UNIT and n_grp == 4 and clusters.shape[2] == 1024
        return (fast if suits else general)(*args)

    return jax.shard_map(
        on_device,
        mesh=mesh,
        in_specs=(
            P("grp", "tok", None),
            P("grp", "tok", None),
            P("grp", None),
            P("grp", None, "tok"),
            P(),
            P("tok", "grp", None),
            P(None, "grp", None, None),
            P("tok", "grp", None),
            P("tok", "grp", None),
            P(),
            P(),
            P(),
        ),
        out_specs=(
            P("grp", "tok", None),
            P("grp", "tok", None),
            P("tok", "grp", None),
            P("tok", "grp", None),
            P("tok", "grp", None),
            P(),
            P(),
            P(),
        ),
        check_vma=False,
    )
```

```python
import functools

import jax
import jax.numpy as jnp
from jax import lax
from jax.experimental import pallas as pl
from jax.experimental.pallas import tpu as pltpu
from jax.sharding import PartitionSpec as P

D = 768
H = 12
FF = 3072
HEAD = 64
ROUNDS = 2
PAIRS = 24
CLUSTER = 128
FFB = FF // D

EPS_NORM = 1e-05
ADAM_EPS = 1e-08
BETA_ONE = 0.5
BETA_TWO = 0.5
RATE_MATRIX = 0.025
RATE_VECTOR = 0.15
SQRT_HALF = 0.7071067811865476
INV_ROOT_TWO_PI = 0.3989422804014327

BF16 = jnp.bfloat16
F32 = jnp.float32

UNIT = 4
HEADS_OWN = H // UNIT
LOCAL_PAIRS = ROUNDS * HEADS_OWN
TILE = 128
WIDE = 2 * TILE
SMALL = pl.CostEstimate(flops=0, transcendentals=0, bytes_accessed=0)


def inner_rows(left, right):
    return lax.dot_general(left, right, (((0,), (0,)), ((), ())), preferred_element_type=F32)


def outer_cols(left, right):
    return lax.dot_general(left, right, (((1,), (1,)), ((), ())), preferred_element_type=F32)


def normalize(values_in):
    centre = jnp.mean(values_in, axis=-1, keepdims=True)
    offset = values_in - centre
    spread = jnp.mean(offset * offset, axis=-1, keepdims=True)
    rstd = lax.rsqrt(spread + EPS_NORM)
    return (offset * rstd, rstd)


def norm_back(grad_normed, normed, rstd):
    first_mean = jnp.mean(grad_normed, axis=-1, keepdims=True)
    second_mean = jnp.mean(grad_normed * normed, axis=-1, keepdims=True)
    return rstd * (grad_normed - first_mean - normed * second_mean)


def gelu_slope(values_in):
    return (
        0.5 * (1.0 + lax.erf(values_in * SQRT_HALF))
        + values_in * jnp.exp(-0.5 * values_in * values_in) * INV_ROOT_TWO_PI
    )


def turn_half(value):
    return pltpu.roll(value, HEAD, 1)


def places_body(scalars_ref, clusters_ref, *refs):
    outs, all_ref = refs[:UNIT], refs[UNIT]
    pairs, count = clusters_ref.shape
    share, member = scalars_ref[0], scalars_ref[1]
    kinds = UNIT * count // CLUSTER
    kind = lax.broadcasted_iota(jnp.int32, (kinds, count), 0)
    earlier = lax.broadcasted_iota(jnp.int32, (count, count), 0) < lax.broadcasted_iota(jnp.int32, (count, count), 1)
    earlier = earlier.astype(F32).astype(BF16)
    all_ref[...] = jnp.zeros_like(all_ref)
    for pair in range(pairs):
        turn, head = pair // H, pair % H
        cluster = clusters_ref[pair : pair + 1, :]
        same = (kind == cluster).astype(F32)
        before = jnp.dot(same.astype(BF16), earlier, preferred_element_type=F32)
        rank = jnp.sum(same * before, axis=0, keepdims=True).astype(jnp.int32)
        own = head % HEADS_OWN * ROUNDS + turn
        all_ref[head // HEADS_OWN, own : own + 1, :] = cluster * share + rank
    for k in range(UNIT):
        outs[k][...] = all_ref[member ^ k]


def places(scalars, clusters):
    count = clusters.shape[1]
    inside = pl.BlockSpec(memory_space=pltpu.VMEM)
    return pl.pallas_call(
        places_body,
        in_specs=[pl.BlockSpec(memory_space=pltpu.SMEM), inside],
        out_specs=[inside] * UNIT,
        out_shape=[jax.ShapeDtypeStruct((8, count), jnp.int32)] * UNIT,
        scratch_shapes=[pltpu.VMEM((UNIT, 8, count), jnp.int32)],
        cost_estimate=SMALL,
        name="places",
    )(scalars, clusters)


def arrange_body(slots, scalars_ref, *refs):
    sources, outs, rest_ref, tiles_ref = refs[:4], refs[4 : 4 + UNIT], refs[4 + UNIT], refs[5 + UNIT]
    n_rest, count = rest_ref.shape[:2]
    n_blocks = n_rest + 3
    group, core, member = (scalars_ref[n_blocks + i] for i in range(3))
    first = pl.multiple_of(core * count, count)

    def rows_of(block):
        slot = scalars_ref[block]
        owner = lax.div(slot, slots)
        near, inner = owner ^ group, lax.rem(slot, slots)
        found = [source[inner, pl.ds(first, count), :].astype(F32) for source in sources]
        low = jnp.where(near % 2 == 0, found[0], found[1])
        high = jnp.where(near % 2 == 0, found[2], found[3])
        return jnp.where(near < 2, low, high)

    low = lax.broadcasted_iota(jnp.int32, (count, TILE), 1) < HEAD
    parts = [rows_of(i) for i in range(3)]

    def half(part, head, high):
        at = head // 2 * TILE
        tile = parts[part][:, at : at + TILE]
        return tile if head % 2 == high else turn_half(tile)

    for head in range(H):
        own = head % HEADS_OWN
        odd = own % 2
        value = half(2, head, odd)
        query = half(0, head, 1 - odd)
        keys = half(1, head, 1 - odd)
        one = jnp.where(low, query, value) if odd else jnp.where(low, value, query)
        two = jnp.where(low, keys, 0.0) if odd else jnp.where(low, 0.0, keys)
        tiles_ref[head // HEADS_OWN, :, own * WIDE : own * WIDE + TILE] = one.astype(BF16)
        tiles_ref[head // HEADS_OWN, :, own * WIDE + TILE : (own + 1) * WIDE] = two.astype(BF16)
    for k in range(UNIT):
        outs[k][...] = tiles_ref[member ^ k]
    for b in range(n_rest):
        rest_ref[b] = rows_of(3 + b).astype(BF16)


def arrange(scalars, sources, n_blocks):
    slots, rows = sources[0].shape[:2]
    count = rows // 2
    width = HEADS_OWN * WIDE
    inside = pl.BlockSpec(memory_space=pltpu.VMEM)
    return pl.pallas_call(
        functools.partial(arrange_body, slots),
        in_specs=[pl.BlockSpec(memory_space=pltpu.SMEM)] + [inside] * 4,
        out_specs=[inside] * (UNIT + 1),
        out_shape=[jax.ShapeDtypeStruct((count, width), BF16)] * UNIT
        + [jax.ShapeDtypeStruct((n_blocks - 3, count, D), BF16)],
        scratch_shapes=[pltpu.VMEM((UNIT, count, width), BF16)],
        compiler_params=pltpu.CompilerParams(vmem_limit_bytes=32 << 20),
        cost_estimate=SMALL,
        name="arrange",
    )(scalars, *sources)


def assemble_body(table_ref, *refs):
    shards, out_ref, sem = refs[:-2], refs[-2], refs[-1]
    rows = shards[0].shape[1]
    copies = []
    for shard in shards:
        for i in range(shard.shape[0]):
            n = len(copies)
            first = pl.multiple_of(table_ref[n], rows)
            copies.append(
                pltpu.make_async_copy(shard.at[i], out_ref.at[pl.ds(first, rows), :], sem.at[n])
            )
    for copy in copies:
        copy.start()
    for copy in copies:
        copy.wait()


def assemble(table, shards):
    pieces = sum(s.shape[0] for s in shards)
    anywhere = pl.BlockSpec(memory_space=pl.ANY)
    return pl.pallas_call(
        assemble_body,
        in_specs=[pl.BlockSpec(memory_space=pltpu.SMEM)] + [anywhere] * len(shards),
        out_specs=pl.BlockSpec(memory_space=pltpu.VMEM),
        out_shape=jax.ShapeDtypeStruct((pieces * shards[0].shape[1], shards[0].shape[2]), BF16),
        scratch_shapes=[pltpu.SemaphoreType.DMA((pieces,))],
        cost_estimate=SMALL,
        name="assemble",
    )(table, *shards)


def sort_body(place_ref, x_ref, weight_ref, bias_ref, out_ref, rows_ref):
    count = x_ref.shape[0]
    head = pl.program_id(0)
    chunk = 256
    row = lax.broadcasted_iota(jnp.int32, (chunk, count), 0)
    rows_ref[...] = (
        jnp.dot(x_ref[...], weight_ref[...], preferred_element_type=F32) + bias_ref[...]
    ).astype(BF16)
    for step in range(HEADS_OWN):

        @pl.when(head == step)
        def _():
            for turn in range(ROUNDS):
                pair = step * ROUNDS + turn
                for part in range(count // chunk):
                    where = pl.ds(part * chunk, chunk)
                    picked = place_ref[pair : pair + 1, :] == row + part * chunk
                    picked = picked.astype(F32).astype(BF16)
                    out_ref[turn, where, :] = jnp.dot(
                        picked, rows_ref[...], preferred_element_type=F32
                    ).astype(BF16)


def sort_rows(order, inputs, weights, bias):
    count = inputs.shape[0]
    return pl.pallas_call(
        sort_body,
        grid=(HEADS_OWN,),
        in_specs=[
            pl.BlockSpec((8, count), lambda h: (0, 0)),
            pl.BlockSpec((count, D), lambda h: (0, 0)),
            pl.BlockSpec((D, WIDE), lambda h: (0, h)),
            pl.BlockSpec((1, WIDE), lambda h: (0, h)),
        ],
        out_specs=pl.BlockSpec((ROUNDS, count, WIDE), lambda h: (h, 0, 0)),
        out_shape=jax.ShapeDtypeStruct((LOCAL_PAIRS, count, WIDE), BF16),
        scratch_shapes=[pltpu.VMEM((count, WIDE), BF16)],
        compiler_params=pltpu.CompilerParams(vmem_limit_bytes=48 << 20),
        cost_estimate=SMALL,
        name="sort_rows",
    )(order, inputs, weights, bias)


def sort_grads_body(place_ref, rows_ref, out_ref):
    count = place_ref.shape[1]
    half = count // 2
    head = pl.program_id(0)
    chunk = 256
    row = lax.broadcasted_iota(jnp.int32, (chunk, count), 0)
    low = lax.broadcasted_iota(jnp.int32, (count, TILE), 1) < HEAD
    for step in range(HEADS_OWN):

        @pl.when(head == step)
        def _():
            if step < 2:
                tile = rows_ref[0:count, :].astype(F32)
                tile = jnp.where(low if step == 0 else jnp.logical_not(low), tile, 0.0).astype(BF16)
            else:
                both = rows_ref[count : count + half, :].astype(F32)
                tile = jnp.concatenate([both, turn_half(both)], axis=0)
                tile = jnp.where(low, tile, 0.0).astype(BF16)
            for turn in range(ROUNDS):
                pair = step * ROUNDS + turn
                for part in range(count // chunk):
                    where = pl.ds(part * chunk, chunk)
                    picked = place_ref[pair : pair + 1, :] == row + part * chunk
                    picked = picked.astype(F32).astype(BF16)
                    out_ref[turn, where, :] = jnp.dot(
                        picked, tile, preferred_element_type=F32
                    ).astype(BF16)


def sort_grads(order, rows):
    count = order.shape[1]
    return pl.pallas_call(
        sort_grads_body,
        grid=(HEADS_OWN,),
        in_specs=[
            pl.BlockSpec((8, count), lambda h: (0, 0)),
            pl.BlockSpec(rows.shape, lambda h: (0, 0)),
        ],
        out_specs=pl.BlockSpec((ROUNDS, count, TILE), lambda h: (h, 0, 0)),
        out_shape=jax.ShapeDtypeStruct((LOCAL_PAIRS, count, TILE), BF16),
        compiler_params=pltpu.CompilerParams(vmem_limit_bytes=48 << 20),
        cost_estimate=SMALL,
        name="sort_grads",
    )(order, rows)


def plans_of(count):
    share = CLUSTER // UNIT
    half = UNIT // 2
    return (
        [(tuple(range(UNIT)), share)],
        [(tuple(range(i * half, (i + 1) * half)), 2 * share) for i in range(2)],
    )


def for_each_batch(is_long, count, batch, work):
    for wanted, plan in zip((1, 0), plans_of(count)):

        @pl.when(is_long == wanted)
        def _(plan=plan):
            for runs, share in plan:

                def step(group, carry, runs=runs, share=share):
                    first = pl.multiple_of(group * (batch * share), batch * share)
                    work(runs, pl.ds(first, batch * share), share)
                    return carry

                lax.fori_loop(0, count // share // batch, step, 0)


def batch_of(refs, runs, where, share, width):
    parts = [refs[r][0, where, :] for r in runs]
    return jnp.concatenate([p.reshape(p.shape[0] // share, share, width) for p in parts], axis=1)


def spread(refs, runs, where, share, columns, value):
    for i, r in enumerate(runs):
        part = value[:, i * share : (i + 1) * share]
        refs[r][0, where, columns] = part.reshape(part.shape[0] * share, TILE)


def products(form, left, right):
    return jnp.einsum(form, left, right, preferred_element_type=F32)


def softmax(first, second):
    scores = products("ued,ucd->uec", second, first) * (HEAD**-0.5)
    expo = jnp.exp(scores - jnp.max(scores, axis=1, keepdims=True))
    return expo * (1.0 / jnp.sum(expo, axis=1, keepdims=True))


def attend_body(long_ref, *refs):
    grouped, results = refs[:UNIT], refs[UNIT:]

    def work(runs, where, share):
        rows = batch_of(grouped, runs, where, share, WIDE)
        first = rows[..., :TILE]
        probs = softmax(first, rows[..., TILE:]).astype(BF16)
        mixed = products("uce,ued->ucd", jnp.swapaxes(probs, 1, 2), first).astype(BF16)
        spread(results, runs, where, share, slice(0, TILE), mixed)

    for_each_batch(long_ref[0], grouped[0].shape[1], 16, work)


def attend(is_long, grouped):
    count = grouped[0].shape[1]
    return pl.pallas_call(
        attend_body,
        grid_spec=pltpu.PrefetchScalarGridSpec(
            num_scalar_prefetch=1,
            grid=(LOCAL_PAIRS,),
            in_specs=[pl.BlockSpec((1, count, WIDE), lambda p, _: (p, 0, 0))] * UNIT,
            out_specs=[pl.BlockSpec((1, count, TILE), lambda p, _: (p, 0, 0))] * UNIT,
        ),
        out_shape=[jax.ShapeDtypeStruct((LOCAL_PAIRS, count, TILE), BF16)] * UNIT,
        compiler_params=pltpu.CompilerParams(vmem_limit_bytes=48 << 20),
        cost_estimate=SMALL,
        name="attend",
    )(is_long, *grouped)


def attend_back_body(long_ref, *refs):
    grouped, grads, results = refs[:UNIT], refs[UNIT : 2 * UNIT], refs[2 * UNIT :]
    batch = 16
    odd = (pl.program_id(0) // ROUNDS) % 2
    lane = lax.broadcasted_iota(jnp.int32, (batch, CLUSTER, TILE), 2)
    value_lane = (lane < HEAD) == (odd == 0)
    scale = HEAD**-0.5

    def work(runs, where, share):
        rows = batch_of(grouped, runs, where, share, WIDE)
        grad = batch_of(grads, runs, where, share, TILE)
        first, second = rows[..., :TILE], rows[..., TILE:]
        probs = softmax(first, second)
        grad_probs = products("ued,ucd->uec", first, grad)
        centre = jnp.sum(probs * grad_probs, axis=1, keepdims=True)
        grad_scores = (probs * (grad_probs - centre)).astype(BF16)
        grad_values = products("uec,ucd->ued", probs.astype(BF16), grad)
        grad_keys = products("uec,ucd->ued", grad_scores, first) * scale
        grad_query = products("uce,ued->ucd", jnp.swapaxes(grad_scores, 1, 2), second) * scale
        tile_one = jnp.where(value_lane, grad_values, grad_query).astype(BF16)
        tile_two = jnp.where(value_lane, 0.0, grad_keys).astype(BF16)
        spread(results, runs, where, share, slice(0, TILE), tile_one)
        spread(results, runs, where, share, slice(TILE, WIDE), tile_two)

    for_each_batch(long_ref[0], grouped[0].shape[1], batch, work)


def attend_back(is_long, grouped, grads):
    count = grouped[0].shape[1]
    return pl.pallas_call(
        attend_back_body,
        grid_spec=pltpu.PrefetchScalarGridSpec(
            num_scalar_prefetch=1,
            grid=(LOCAL_PAIRS,),
            in_specs=[pl.BlockSpec((1, count, WIDE), lambda p, _: (p, 0, 0))] * UNIT
            + [pl.BlockSpec((1, count, TILE), lambda p, _: (p, 0, 0))] * UNIT,
            out_specs=[pl.BlockSpec((1, count, WIDE), lambda p, _: (p, 0, 0))] * UNIT,
        ),
        out_shape=[jax.ShapeDtypeStruct((LOCAL_PAIRS, count, WIDE), BF16)] * UNIT,
        compiler_params=pltpu.CompilerParams(vmem_limit_bytes=56 << 20),
        cost_estimate=SMALL,
        name="attend_back",
    )(is_long, *grouped, *grads)


def unsorted(column_ref, step, rows_ref, part, chunk):
    count = rows_ref.shape[1]
    where = pl.ds(part * chunk, chunk)
    lane = lax.broadcasted_iota(jnp.int32, (chunk, count), 1)
    total = None
    for turn in range(ROUNDS):
        pair = step * ROUNDS + turn
        picked = (column_ref[where, pair : pair + 1] == lane).astype(F32).astype(BF16)
        more = jnp.dot(picked, rows_ref[turn], preferred_element_type=F32)
        total = more if total is None else total + more
    return total


def mix_body(place_ref, rows_ref, out_ref, column_ref):
    @pl.when(pl.program_id(0) == 0)
    def _():
        column_ref[...] = jnp.transpose(place_ref[...])

    count = rows_ref.shape[1]
    chunk = 256
    parts = count // chunk
    low = lax.broadcasted_iota(jnp.int32, (chunk, TILE), 1) < HEAD
    head = pl.program_id(0)
    for step in range(HEADS_OWN):

        @pl.when(head == step)
        def _():
            means = [0.5 * unsorted(column_ref, step, rows_ref, part, chunk) for part in range(parts)]
            for part in range(parts):
                where = pl.ds(part * chunk, chunk)
                if step == 0:
                    out_ref[where, :] = means[part].astype(BF16)
                elif step == 1:
                    out_ref[where, :] = jnp.where(low, out_ref[where, :].astype(F32), means[part]).astype(BF16)
                elif part < parts // 2:
                    both = jnp.where(low, means[part], turn_half(means[part + parts // 2]))
                    out_ref[pl.ds(count + part * chunk, chunk), :] = both.astype(BF16)


def mix(order, rows):
    count = rows.shape[1]
    packed = (count + count // 2, TILE)
    return pl.pallas_call(
        mix_body,
        grid=(HEADS_OWN,),
        in_specs=[
            pl.BlockSpec((8, count), lambda h: (0, 0)),
            pl.BlockSpec((ROUNDS, count, TILE), lambda h: (h, 0, 0)),
        ],
        out_specs=pl.BlockSpec(packed, lambda h: (0, 0)),
        out_shape=jax.ShapeDtypeStruct(packed, BF16),
        scratch_shapes=[pltpu.VMEM((count, 8), jnp.int32)],
        compiler_params=pltpu.CompilerParams(vmem_limit_bytes=48 << 20),
        cost_estimate=SMALL,
        name="mix",
    )(order, rows)


def gather_grads_body(place_ref, rows_ref, out_ref, column_ref):
    @pl.when(pl.program_id(0) == 0)
    def _():
        column_ref[...] = jnp.transpose(place_ref[...])

    count = rows_ref.shape[1]
    chunk = 256
    head = pl.program_id(0)
    for step in range(HEADS_OWN):

        @pl.when(head == step)
        def _():
            for part in range(count // chunk):
                where = pl.ds(part * chunk, chunk)
                out_ref[where, :] = unsorted(column_ref, step, rows_ref, part, chunk).astype(BF16)


def gather_grads(order, rows):
    count = rows.shape[1]
    return pl.pallas_call(
        gather_grads_body,
        grid=(HEADS_OWN,),
        in_specs=[
            pl.BlockSpec((8, count), lambda h: (0, 0)),
            pl.BlockSpec((ROUNDS, count, WIDE), lambda h: (h, 0, 0)),
        ],
        out_specs=pl.BlockSpec((count, WIDE), lambda h: (0, h)),
        out_shape=jax.ShapeDtypeStruct((count, HEADS_OWN * WIDE), BF16),
        scratch_shapes=[pltpu.VMEM((count, 8), jnp.int32)],
        compiler_params=pltpu.CompilerParams(vmem_limit_bytes=48 << 20),
        cost_estimate=SMALL,
        name="gather_grads",
    )(order, rows)


ERF_TOP = (0.00022905065861350646, 0.0034082910107109506, 0.050955695062380861, 0.18520832239976145, 1.128379143519084)
ERF_BOTTOM = (
    -1.1791602954361697e-7,
    0.000023547966471313185,
    0.0010179625278914885,
    0.014070470171167667,
    0.11098505178285362,
    0.49746925110067538,
    1.0,
)


def polynomial(value, factors):
    total = jnp.full_like(value, factors[0])
    for factor in factors[1:]:
        total = total * value + factor
    return total


def error_function(value):
    value = jnp.clip(value, -3.832506856900711, 3.832506856900711)
    square = value * value
    return value * polynomial(square, ERF_TOP) / polynomial(square, ERF_BOTTOM)


VEC_ROWS = 16
FFN_TILE = 256


def layer_body(
    n_shards,
    table_ref,
    *refs,
):
    shards, refs = refs[:n_shards], refs[n_shards:]
    parts, refs = refs[:UNIT], refs[UNIT:]
    x_ref, cot_ref, vec_ref, result_ref, first_ref, sums_ref, kept_ref, sent_ref = refs[:8]
    backs, refs = refs[8 : 8 + UNIT], refs[8 + UNIT :]
    w_ref, packed_ref, mixed_ref, hidden_ref, act_ref, down_ref, up_ref, attn_ref, back_ref = refs[:9]
    slope_ref, stage_ref, weight_sem, part_sem, stage_sem = refs[9:]
    count = x_ref.shape[0]
    half = count // 2
    per_shard, n_weights, shard_rows = shards[0].shape[:3]
    member = table_ref[0]
    for k in range(UNIT):
        pltpu.make_async_copy(parts[k], packed_ref.at[member ^ k], part_sem.at[k]).start()
    for b in range(n_weights):
        for n in range(n_shards * per_shard):
            row = pl.multiple_of(table_ref[6 + n], shard_rows)
            pltpu.make_async_copy(
                shards[n // per_shard].at[n % per_shard, b], w_ref.at[b, pl.ds(row, shard_rows), :], weight_sem.at[b]
            ).start()
    for k in range(UNIT):
        pltpu.make_async_copy(parts[k], packed_ref.at[member ^ k], part_sem.at[k]).wait()
    for b in range(n_weights):
        pltpu.make_async_copy(w_ref.at[b], w_ref.at[b], weight_sem.at[b]).wait()

    sums_ref[...] = jnp.zeros_like(sums_ref)
    low = lax.broadcasted_iota(jnp.int32, (FFN_TILE, TILE), 1) < HEAD
    vec = [vec_ref[i : i + 1, :] for i in range(8 + FFB)]
    gain_one, shift_one, gain_two, shift_two = vec[:4]
    bias_out, bias_down = vec[6], vec[7]

    def add_sum(row, value):
        sums_ref[row : row + 1, :] += jnp.sum(value, axis=0, keepdims=True)

    def tile_step(i, carry):
        rows = pl.ds(pl.multiple_of(i * FFN_TILE, FFN_TILE), FFN_TILE)
        is_first = i * FFN_TILE < half
        extra = pl.ds(pl.multiple_of(count + lax.rem(i * FFN_TILE, half), FFN_TILE), FFN_TILE)

        def pair(m):
            return packed_ref[m, rows, :].astype(F32)

        def single(m):
            value = packed_ref[m, extra, :].astype(F32)
            return jnp.where(is_first, value, turn_half(value))

        for m in (0, 2):
            at = m * (HEADS_OWN * HEAD)
            nxt = turn_half(pair(m + 1))
            mixed_ref[rows, at : at + TILE] = pair(m).astype(BF16)
            mixed_ref[rows, at + TILE : at + 2 * TILE] = jnp.where(low, single(m), nxt).astype(BF16)
            mixed_ref[rows, at + 2 * TILE : at + 3 * TILE] = jnp.where(
                low, nxt, turn_half(single(m + 1))
            ).astype(BF16)
        attention = jnp.dot(mixed_ref[rows, :], w_ref[0], preferred_element_type=F32) + bias_out
        normed_one, rstd_one = normalize(x_ref[rows, :].astype(F32) + attention)
        hidden = normed_one * gain_one + shift_one
        hidden_low = hidden.astype(BF16)
        hidden_ref[rows, :] = hidden_low
        down = jnp.broadcast_to(bias_down, hidden.shape)
        for j in range(FFB):
            up = jnp.dot(hidden_low, w_ref[1 + j], preferred_element_type=F32) + vec[8 + j]
            phi = 0.5 * (1.0 + error_function(up * SQRT_HALF))
            slope_ref[j] = phi + up * jnp.exp(-0.5 * up * up) * INV_ROOT_TWO_PI
            act = (up * phi).astype(BF16)
            act_ref[j, rows, :] = act
            down = down + jnp.dot(act, w_ref[1 + FFB + j], preferred_element_type=F32)
        normed_two, rstd_two = normalize(hidden + down)
        result_ref[rows, :] = (normed_two * gain_two + shift_two).astype(BF16)
        grad_result = cot_ref[rows, :].astype(F32)
        add_sum(2, grad_result * normed_two)
        add_sum(3, grad_result)
        grad_second = norm_back(grad_result * gain_two, normed_two, rstd_two)
        grad_down = grad_second.astype(BF16)
        down_ref[rows, :] = grad_down
        add_sum(7, grad_down.astype(F32))
        grad_hidden = grad_second
        for j in range(FFB):
            grad_up = (outer_cols(grad_down, w_ref[1 + FFB + j]) * slope_ref[j]).astype(BF16)
            up_ref[j, rows, :] = grad_up
            add_sum(8 + j, grad_up.astype(F32))
            grad_hidden = grad_hidden + outer_cols(grad_up, w_ref[1 + j])
        add_sum(0, grad_hidden * normed_one)
        add_sum(1, grad_hidden)
        grad_first = norm_back(grad_hidden * gain_one, normed_one, rstd_one)
        first_ref[rows, :] = grad_first
        grad_attn = grad_first.astype(BF16)
        attn_ref[rows, :] = grad_attn
        add_sum(6, grad_attn.astype(F32))
        grad_mixed = (0.5 * outer_cols(grad_attn, w_ref[0])).astype(BF16).astype(F32)
        for m in range(UNIT):
            at = (m // 2) * 3 * TILE
            tiles = [grad_mixed[:, at + n * TILE : at + (n + 1) * TILE] for n in range(3)]
            if m % 2 == 0:
                two, one = tiles[0], tiles[1]
            else:
                two, one = turn_half(jnp.where(low, tiles[2], tiles[1])), turn_half(tiles[2])
            back_ref[member ^ m, rows, :] = two.astype(BF16)

            @pl.when(is_first)
            def _(one=one, m=m):
                back_ref[member ^ m, extra, :] = jnp.where(low, one, 0.0).astype(BF16)

            @pl.when(jnp.logical_not(is_first))
            def _(one=one, m=m):
                old = back_ref[member ^ m, extra, :].astype(F32)
                back_ref[member ^ m, extra, :] = jnp.where(low, old, turn_half(one)).astype(BF16)

        return carry

    lax.fori_loop(0, count // FFN_TILE, tile_step, 0)
    for k in range(UNIT):
        backs[k][...] = back_ref[k]

    core, bits = table_ref[1], [table_ref[2 + d] for d in range(4)]
    piece, half_columns = kept_ref.shape[3:]
    n_parts = kept_ref.shape[0]
    per_part = n_weights // n_parts

    def copies(block, slot, half, target):
        part = block // per_part
        made = []
        for index in range(16):
            x, zh, y, zl = ((index >> s) % 2 for s in range(4))
            rel = {"x": x ^ bits[0], "y": y ^ bits[1], "zl": zl ^ bits[2], "zh": zh ^ bits[3]}
            place = 0
            for name in PART_ORDERS[part]:
                place = place * 2 + rel[name]
            made.append(
                pltpu.make_async_copy(
                    stage_ref.at[
                        slot, pl.ds(index * piece, piece), pl.ds(half * half_columns, half_columns)
                    ],
                    target.at[part, place, block % per_part],
                    stage_sem.at[slot, half * 16 + index],
                )
            )
        return made

    def send(block, slot):
        for half in range(2):

            @pl.when(core == half)
            def _(half=half):
                for copy in copies(block, slot, half, kept_ref):
                    copy.start()

            @pl.when(core != half)
            def _(half=half):
                for copy in copies(block, slot, half, sent_ref):
                    copy.start()

    def sent(block, slot):
        for half in range(2):
            for copy in copies(block, slot, half, kept_ref):
                copy.wait()

    plan = [(attn_ref, None, mixed_ref, None, 0)]
    plan += [(down_ref, None, act_ref, j, 1 + FFB + j) for j in range(FFB)]
    plan += [(up_ref, j, hidden_ref, None, 1 + j) for j in range(FFB)]
    for n, (left, lj, right, rj, block) in enumerate(plan):
        slot = n % 2
        if n >= 2:
            sent(plan[n - 2][4], slot)
        value = inner_rows(
            left[...] if lj is None else left[lj], right[...] if rj is None else right[rj]
        )
        stage_ref[slot] = value.astype(BF16)
        send(block, slot)
    for n in (len(plan) - 2, len(plan) - 1):
        sent(plan[n][4], n % 2)


PART_ORDERS = (("x", "y", "zl", "zh"), ("y", "zl", "zh", "x"), ("zl", "zh", "x", "y"))


def layer(table, shards, parts, inputs, cotangent, vectors):
    count = inputs.shape[0]
    n_weights = 1 + 2 * FFB
    n_shards = len(shards)
    anywhere = pl.BlockSpec(memory_space=pl.ANY)
    inside = pl.BlockSpec(memory_space=pltpu.VMEM)
    packed = parts[0].shape
    return pl.pallas_call(
        functools.partial(layer_body, n_shards),
        in_specs=[pl.BlockSpec(memory_space=pltpu.SMEM)] + [anywhere] * (n_shards + UNIT) + [inside] * 3,
        out_specs=[inside, inside, inside, anywhere, anywhere] + [inside] * UNIT,
        out_shape=[
            jax.ShapeDtypeStruct((count, D), BF16),
            jax.ShapeDtypeStruct((count, D), F32),
            jax.ShapeDtypeStruct((VEC_ROWS, D), F32),
            jax.ShapeDtypeStruct((3, 16, n_weights // 3, D // 16, D // 2), BF16),
            jax.ShapeDtypeStruct((3, 16, n_weights // 3, D // 16, D // 2), BF16),
        ]
        + [jax.ShapeDtypeStruct(packed, BF16)] * UNIT,
        scratch_shapes=[
            pltpu.VMEM((n_weights, D, D), BF16),
            pltpu.VMEM((UNIT, *packed), BF16),
            pltpu.VMEM((count, D), BF16),
            pltpu.VMEM((count, D), BF16),
            pltpu.VMEM((FFB, count, D), BF16),
            pltpu.VMEM((count, D), BF16),
            pltpu.VMEM((FFB, count, D), BF16),
            pltpu.VMEM((count, D), BF16),
            pltpu.VMEM((UNIT, *packed), BF16),
            pltpu.VMEM((FFB, FFN_TILE, D), F32),
            pltpu.VMEM((2, D, D), BF16),
            pltpu.SemaphoreType.DMA((n_weights,)),
            pltpu.SemaphoreType.DMA((UNIT,)),
            pltpu.SemaphoreType.DMA((2, 32)),
        ],
        compiler_params=pltpu.CompilerParams(vmem_limit_bytes=60 << 20),
        cost_estimate=SMALL,
        name="layer",
    )(table, *shards, *parts, inputs, cotangent, vectors)


def qkv_back_body(scalars_ref, *refs):
    grads, inputs, kept_ref, sent_ref, bias_ref, all_ref = refs[:4], refs[4:8], *refs[8:]
    core, unit = scalars_ref[0], scalars_ref[1]
    columns = all_ref.shape[4]
    step = 32
    per_unit = all_ref.shape[3]
    bias_ref[...] = jnp.zeros_like(bias_ref)
    for head in range(HEADS_OWN):
        at = slice(head * WIDE, (head + 1) * WIDE)
        total = inner_rows(grads[0][:, at], inputs[0][...])
        bias = jnp.sum(grads[0][:, at].astype(F32), axis=0, keepdims=True)
        for k in range(1, UNIT):
            total = total + inner_rows(grads[k][:, at], inputs[k][...])
            bias = bias + jnp.sum(grads[k][:, at].astype(F32), axis=0, keepdims=True)
        bias_ref[0:1, at] = bias
        firsts = (HEAD, 3 * HEAD, 0) if head % 2 == 0 else (0, 2 * HEAD, HEAD)
        for block, first in enumerate(firsts):
            for i in range(HEAD // step):
                row = head * HEAD + i * step
                rows = total[first + i * step : first + (i + 1) * step]
                for c in range(2):
                    all_ref[
                        c ^ core, row // per_unit ^ unit, block, row % per_unit : row % per_unit + step, :
                    ] = rows[:, c * columns : (c + 1) * columns].astype(BF16)
    kept_ref[...] = all_ref[0]
    sent_ref[...] = all_ref[1]


def qkv_back(scalars, grads, inputs):
    inside = pl.BlockSpec(memory_space=pltpu.VMEM)
    shape = (2, 3, HEADS_OWN * HEAD // 2, D // 2)
    return pl.pallas_call(
        qkv_back_body,
        in_specs=[pl.BlockSpec(memory_space=pltpu.SMEM)] + [inside] * (2 * UNIT),
        out_specs=[inside] * 3,
        out_shape=[
            jax.ShapeDtypeStruct(shape, BF16),
            jax.ShapeDtypeStruct(shape, BF16),
            jax.ShapeDtypeStruct((8, HEADS_OWN * WIDE), F32),
        ],
        scratch_shapes=[pltpu.VMEM((2, *shape), BF16)],
        compiler_params=pltpu.CompilerParams(vmem_limit_bytes=56 << 20),
        cost_estimate=SMALL,
        name="qkv_back",
    )(scalars, *grads, *inputs)


def pack_body(slot_block_ref, *refs):
    half = (len(refs) - 2) // 2
    kept, got, out_ref, all_ref = refs[:half], refs[half : 2 * half], refs[-2], refs[-1]
    per_part = kept[0].shape[1]
    for p in range(half):
        for b in range(per_part):
            all_ref[p * per_part + b] = (kept[p][0, b] + got[p][0, b].astype(F32)).astype(BF16)
    for s in range(out_ref.shape[0] * out_ref.shape[1]):
        out_ref[s // out_ref.shape[1], s % out_ref.shape[1]] = all_ref[jnp.maximum(slot_block_ref[s] - 3, 0)]


def pack(slot_block, kept, got, n_grp, slots):
    shape = kept[0].shape[2:]
    inside = pl.BlockSpec(memory_space=pltpu.VMEM)
    return pl.pallas_call(
        pack_body,
        in_specs=[pl.BlockSpec(memory_space=pltpu.SMEM)] + [inside] * (2 * len(kept)),
        out_specs=inside,
        out_shape=jax.ShapeDtypeStruct((n_grp, slots, *shape), BF16),
        scratch_shapes=[pltpu.VMEM((len(kept) * kept[0].shape[1], *shape), BF16)],
        compiler_params=pltpu.CompilerParams(vmem_limit_bytes=32 << 20),
        cost_estimate=SMALL,
        name="pack",
    )(slot_block, *kept, *got)


def rotate_in_body(mine_ref, keep_ref, got_ref, high_ref, low_ref, out_ref, grad_ref):
    slots, n_tok = got_ref.shape[1], out_ref.shape[0]
    rows, columns = got_ref.shape[2:]
    width = out_ref.shape[3]
    for s in range(slots):
        block = mine_ref[s]

        @pl.when(block < 3)
        def _(s=s, block=block):
            grad_ref[...] = keep_ref[jnp.minimum(block, 2)]

        @pl.when(block >= 3)
        def _(s=s):
            for g in range(got_ref.shape[0]):
                x, c = g // 2, g % 2
                grad_ref[x * rows : (x + 1) * rows, c * columns : (c + 1) * columns] = got_ref[g, s]

        grad = grad_ref[...]
        part = jnp.dot(grad, high_ref[s], preferred_element_type=F32)
        part = jnp.transpose(part + jnp.dot(grad, low_ref[s], preferred_element_type=F32))
        for r in range(n_tok):
            out_ref[r, s] = part[r * width : (r + 1) * width].astype(BF16)


def rotate_in(mine, keep, got, left, n_tok):
    slots, width = got.shape[1], keep.shape[1]
    inside = pl.BlockSpec(memory_space=pltpu.VMEM)
    return pl.pallas_call(
        rotate_in_body,
        in_specs=[pl.BlockSpec(memory_space=pltpu.SMEM)] + [inside] * 4,
        out_specs=inside,
        out_shape=jax.ShapeDtypeStruct((n_tok, slots, width, width), BF16),
        scratch_shapes=[pltpu.VMEM(keep.shape[1:], BF16)],
        compiler_params=pltpu.CompilerParams(vmem_limit_bytes=48 << 20),
        cost_estimate=SMALL,
        name="rotate_in",
    )(mine, keep, got, *left)


def moments_body(place, got_ref, high_ref, low_ref, one_ref, two_ref, new_one_ref, new_two_ref, out_ref):
    n_tok, slots, width = got_ref.shape[:3]
    for s in range(slots):
        rotated = jnp.zeros(one_ref.shape[1:], F32)
        for t in range(n_tok):
            at = slice(place[t] * width, (place[t] + 1) * width)
            part = got_ref[t, s]
            rotated = rotated + jnp.dot(part, high_ref[s, at], preferred_element_type=F32)
            rotated = rotated + jnp.dot(part, low_ref[s, at], preferred_element_type=F32)
        new_one = BETA_ONE * one_ref[s] + (1.0 - BETA_ONE) * rotated
        new_two = BETA_TWO * two_ref[s] + (1.0 - BETA_TWO) * rotated * rotated
        new_one_ref[s] = new_one
        new_two_ref[s] = new_two
        direction = (new_one / (jnp.sqrt(new_two) + ADAM_EPS)).astype(BF16)
        for t in range(n_tok):
            at = slice(place[t] * width, (place[t] + 1) * width)
            turned = outer_cols(direction, high_ref[s, at]) + outer_cols(direction, low_ref[s, at])
            out_ref[t, s] = turned.astype(BF16)


def moments(place, got, right, one, two):
    n_tok, slots, width = got.shape[:3]
    inside = pl.BlockSpec(memory_space=pltpu.VMEM)
    return pl.pallas_call(
        functools.partial(moments_body, tuple(place)),
        in_specs=[inside] * 5,
        out_specs=[inside] * 3,
        out_shape=[
            jax.ShapeDtypeStruct(one.shape, F32),
            jax.ShapeDtypeStruct(one.shape, F32),
            jax.ShapeDtypeStruct(got.shape, BF16),
        ],
        compiler_params=pltpu.CompilerParams(vmem_limit_bytes=48 << 20),
        cost_estimate=SMALL,
        name="moments",
    )(got, *right, one, two)


def rotate_out_body(got_ref, high_ref, low_ref, out_ref, rows_ref):
    n_tok, slots, width = got_ref.shape[:3]
    for s in range(slots):
        for r in range(n_tok):
            rows_ref[r * width : (r + 1) * width, :] = got_ref[r, s]
        rows = rows_ref[...]
        change = jnp.dot(high_ref[s], rows, preferred_element_type=F32)
        change = change + jnp.dot(low_ref[s], rows, preferred_element_type=F32)
        for r in range(n_tok):
            out_ref[r, s] = change[r * width : (r + 1) * width].astype(BF16)


def rotate_out(got, left):
    n_tok, slots, width = got.shape[:3]
    inside = pl.BlockSpec(memory_space=pltpu.VMEM)
    return pl.pallas_call(
        rotate_out_body,
        in_specs=[inside] * 3,
        out_specs=inside,
        out_shape=jax.ShapeDtypeStruct(got.shape, BF16),
        scratch_shapes=[pltpu.VMEM((n_tok * width, width), BF16)],
        compiler_params=pltpu.CompilerParams(vmem_limit_bytes=48 << 20),
        cost_estimate=SMALL,
        name="rotate_out",
    )(got, *left)


def apply_body(place, got_ref, master_ref, out_ref):
    n_tok, slots, width = got_ref.shape[:3]
    for s in range(slots):
        for t in range(n_tok):
            at = slice(place[t] * width, (place[t] + 1) * width)
            out_ref[s, :, at] = master_ref[s, :, at] - RATE_MATRIX * got_ref[t, s].astype(F32)


def apply_change(place, got, master):
    inside = pl.BlockSpec(memory_space=pltpu.VMEM)
    return pl.pallas_call(
        functools.partial(apply_body, tuple(place)),
        in_specs=[inside] * 2,
        out_specs=inside,
        out_shape=jax.ShapeDtypeStruct(master.shape, F32),
        compiler_params=pltpu.CompilerParams(vmem_limit_bytes=48 << 20),
        cost_estimate=SMALL,
        name="apply_change",
    )(got, master)


def swap(value, axis, bit):
    size = lax.axis_size(axis)
    return lax.ppermute(value, axis, [(i, i ^ bit) for i in range(size)])


def exchange_unit(parts):
    return [parts[0]] + [swap(parts[k], "tok", k) for k in range(1, UNIT)]


LINKS = {"x": ("grp", 2), "y": ("tok", 1), "zl": ("tok", 2), "zh": ("tok", 4)}


def starts_of(lengths):
    index = jnp.arange(lengths.shape[0])
    return jnp.sum(jnp.where(index[None, :] < index[:, None], lengths[None, :], 0), axis=1)


LINKS = {"x": ("grp", 2), "y": ("tok", 1), "zl": ("tok", 2), "zh": ("tok", 4)}


def starts_of(lengths):
    index = jnp.arange(lengths.shape[0])
    return jnp.sum(jnp.where(index[None, :] < index[:, None], lengths[None, :], 0), axis=1)


def total_of(value):
    for axis in ("grp", "tok"):
        bit = 1
        while bit < lax.axis_size(axis):
            value = value + swap(value, axis, bit)
            bit *= 2
    return value


def pick(values, index):
    return lax.dynamic_index_in_dim(values, index, 0, keepdims=False)


def split_heads(columns):
    query, keys, values = (c.reshape(HEADS_OWN, HEAD) for c in columns)
    zero = jnp.zeros((HEAD,), query.dtype)
    tiles = []
    for h in range(HEADS_OWN):
        tiles += [values[h], query[h], zero, keys[h]] if h % 2 == 0 else [query[h], values[h], keys[h], zero]
    return jnp.concatenate(tiles)


def join_heads(tiles):
    parts = tiles.reshape(HEADS_OWN, 4, HEAD, *tiles.shape[1:])
    at = [(1, 0), (3, 2), (0, 1)]
    return jnp.stack(
        [jnp.concatenate([parts[h, at[i][h % 2]] for h in range(HEADS_OWN)], axis=0) for i in range(3)]
    )


def doubled(value):
    high = value.astype(BF16)
    return high, (value - high.astype(F32)).astype(BF16)


def together(*groups):
    flat, tree = jax.tree.flatten(groups)
    return jax.tree.unflatten(tree, lax.optimization_barrier(flat))


def fast(
    tokens,
    cotangent,
    lengths,
    clusters,
    owners,
    master,
    bases,
    moment_one,
    moment_two,
    vectors,
    vector_one,
    vector_two,
):
    n_tok = lax.axis_size("tok")
    n_grp = lax.axis_size("grp")
    tok = lax.axis_index("tok")
    grp = lax.axis_index("grp")
    tok_count = tokens.shape[1]
    rows_dev = master.shape[0]
    slots = master.shape[1]
    blocks_all = slots * n_grp
    member = tok & (UNIT - 1)
    unit = tok >> 2
    place = [2 * (t % UNIT) + t // UNIT for t in range(n_tok)]
    own_width = HEADS_OWN * HEAD

    slot_block = jnp.argsort(owners, stable=True).astype(jnp.int32)
    block_slot = jnp.argsort(slot_block, stable=True).astype(jnp.int32)

    core, bit_x = grp & 1, grp >> 1
    inputs = tokens[0]

    near, far = swap(inputs, "tok", 1), swap(inputs, "tok", 2)
    local = jnp.transpose(master.astype(BF16), (1, 0, 2))
    beside, over = swap(local, "grp", 1), swap(local, "grp", 2)

    item_starts = starts_of(lengths[0])
    unit_start = unit * UNIT * tok_count
    middle = unit_start + UNIT // 2 * tok_count
    start_of_middle = jnp.max(jnp.where(item_starts <= middle, item_starts, 0))
    is_long = (start_of_middle <= unit_start).astype(jnp.int32).reshape(1)
    share = CLUSTER // UNIT * (2 - is_long)
    placed = places(jnp.concatenate([share, member.reshape(1)]), clusters[0])
    left, right = doubled(bases[0]), doubled(bases[1])
    (over, left, right, placed) = together(over, left, right, placed)
    across = swap(over, "grp", 1)

    orders = exchange_unit(placed)
    (near, far, beside, over, across) = together(near, far, beside, over, across)
    part_rows = rows_dev // 2

    scalars = jnp.concatenate([block_slot, jnp.stack([grp, core, member])]).astype(jnp.int32)
    *by_owner, rest_rows = arrange(scalars, [local, beside, over, across], blocks_all)
    theirs = exchange_unit(by_owner)
    half = tok_count // 2
    third = (swap(near[:half], "tok", 2), swap(far[half:], "tok", 1))
    (theirs, orders) = together(theirs, orders)
    theirs = jnp.stack(theirs)
    theirs_far = swap(theirs, "tok", UNIT)
    mine_all = jnp.concatenate([theirs, theirs_far], axis=0)
    others_all = swap(mine_all, "grp", 1)
    sources = tok ^ jnp.arange(2 * UNIT, dtype=jnp.int32)
    cores = core ^ jnp.arange(2, dtype=jnp.int32)
    firsts = (sources[None, :] * rows_dev + cores[:, None] * part_rows).reshape(-1)
    (third, others_all, rest_rows) = together(third, others_all, rest_rows)
    own_weights = assemble(firsts, [mine_all, others_all])

    def columns_of(value, m):
        return lax.dynamic_slice_in_dim(value, m * own_width, own_width, value.ndim - 1)

    own_bias = split_heads(
        [columns_of(vectors[4], member), jnp.zeros((own_width,), F32), columns_of(vectors[5], member)]
    ).reshape(1, -1)
    ring = [(i, (i + 2) % n_tok) for i in range(n_tok)]
    depth = n_tok // 2
    steps, flips, mine_rest, other_rest = [rest_rows], [], [], []

    def advance():
        if len(steps) < depth:
            steps.append(lax.ppermute(steps[-1], "tok", ring))
        flips.append(swap(steps[len(flips)], "tok", 1))

    def cross():
        k = len(mine_rest)
        mine_rest.append(jnp.stack([steps[k], flips[k]]))
        other_rest.append(swap(mine_rest[k], "grp", 1))

    advance()
    grouped = [sort_rows(orders[0], inputs, own_weights, own_bias)]
    grouped.append(sort_rows(orders[1], near, own_weights, own_bias))
    (grouped, far, third, steps[1], flips[0]) = together(grouped, far, third, steps[1], flips[0])
    advance()
    cross()
    grouped.append(sort_rows(orders[2], far, own_weights, own_bias))
    unit_inputs = [inputs, near, far, jnp.concatenate(third, axis=0)]
    grouped.append(sort_rows(orders[3], unit_inputs[3], own_weights, own_bias))
    (grouped, steps[2], flips[1], other_rest) = together(grouped, steps[2], flips[1], other_rest)
    advance()
    cross()
    sorted_out = attend(is_long, grouped)
    (sorted_out, steps[3], flips[2], other_rest) = together(sorted_out, steps[3], flips[2], other_rest)
    advance()
    cross()
    mixed = [None] * UNIT
    mixed[3] = mix(orders[3], sorted_out[3])
    mixed[2] = mix(orders[2], sorted_out[2])
    mixed[1] = mix(orders[1], sorted_out[1])
    (mixed[3], last) = together(mixed[3], sorted_out[0])
    mixed[0] = mix(orders[0], last)
    mixed_parts = exchange_unit(mixed)
    (mixed_parts, flips[-1], other_rest, held_weights) = together(
        mixed_parts, flips[-1], other_rest, own_weights
    )
    cross()
    shards = mine_rest + other_rest
    sources = (tok + n_tok - 2 * jnp.arange(depth, dtype=jnp.int32)) & (n_tok - 1)
    sources = (sources[:, None] ^ jnp.arange(2, dtype=jnp.int32)[None, :]).reshape(-1)
    firsts = (sources[None, :] * rows_dev + cores[:, None] * part_rows).reshape(-1)

    turned_weights = [swap(held_weights, "tok", k) for k in range(1, UNIT)]
    place_bits = jnp.stack([member, core, bit_x, tok & 1, (tok >> 1) & 1, tok >> 2]).astype(jnp.int32)
    table = jnp.concatenate([place_bits, firsts])
    result, grad_first, sums, kept, sent_pieces, *back = layer(
        table, shards, mixed_parts, inputs, cotangent[0], vectors
    )
    (turned_weights, kept, sent_pieces, back) = together(turned_weights, kept, sent_pieces, back)

    grad_parts = exchange_unit(back)
    other = swap(sent_pieces, "grp", 1)
    sums_of = [kept[p].astype(F32) + other[p].astype(F32) for p in range(3)]

    def halves(values):
        return [v[: v.shape[0] // 2] for v in values], [v[v.shape[0] // 2 :].astype(BF16) for v in values]

    def exchanged(sent_now, stage):
        return [swap(v, *LINKS[PART_ORDERS[p][stage]]) for p, v in enumerate(sent_now)]

    def joined(kept_now, got_now):
        return [k + g.astype(F32) for k, g in zip(kept_now, got_now)]

    kept_now, sent_now = halves(sums_of)
    sorted_grads = [sort_grads(orders[0], grad_parts[0])]
    (sent_now, grad_parts, sorted_grads) = together(sent_now, grad_parts, sorted_grads)
    got_now = exchanged(sent_now, 0)
    sorted_grads += [sort_grads(orders[k], grad_parts[k]) for k in range(1, UNIT)]
    sorted_back = attend_back(is_long, grouped, sorted_grads)
    kept_now, sent_now = halves(joined(kept_now, got_now))
    (sent_now, sorted_back) = together(sent_now, sorted_back)
    got_now = exchanged(sent_now, 1)
    own_grads = [None] * UNIT
    own_grads[3] = gather_grads(orders[3], sorted_back[3])
    own_grads[2] = gather_grads(orders[2], sorted_back[2])
    kept_now, sent_now = halves(joined(kept_now, got_now))
    own_grads[1] = gather_grads(orders[1], sorted_back[1])
    (sent_now, own_grads[1:], sorted_back) = together(sent_now, own_grads[1:], sorted_back)
    got_now = exchanged(sent_now, 2)
    home_grads = [None, None, None, swap(own_grads[3], "tok", 3)]
    own_grads[0] = gather_grads(orders[0], sorted_back[0])
    kept_qkv, sent_qkv, bias_qkv = qkv_back(jnp.stack([core, unit]).astype(jnp.int32), own_grads, unit_inputs)
    (got_now, kept_qkv, sent_qkv) = together(got_now, kept_qkv, sent_qkv)
    kept_now = joined(kept_now, got_now)
    sent_now = halves(kept_now)[1]
    got_now = exchanged(sent_now, 3)

    bias_query, _, bias_value = join_heads(bias_qkv[0])
    bias_rows = lax.dynamic_update_slice_in_dim(
        jnp.zeros((2, D), F32), jnp.stack([bias_query, bias_value]), member * own_width, 1
    )
    total = sums[: 8 + FFB] + jnp.pad(bias_rows, ((4, 2 + FFB), (0, 0)))

    more = swap(total, "grp", 1)
    keep = kept_qkv.astype(F32) + swap(sent_qkv, "grp", 1).astype(F32)
    (keep, more) = together(keep, more)
    total = total + more
    more = swap(total, "tok", 1)
    unit_got = swap(keep[1].astype(BF16), "tok", UNIT)
    keep = keep[0] + unit_got.astype(F32)
    (keep, more, got_now, home_grads[3]) = together(keep, more, got_now, home_grads[3])
    total = total + more
    more = swap(total, "tok", 2)
    home_grads[1] = swap(own_grads[1], "tok", 1)
    home_grads[2] = swap(own_grads[2], "tok", 2)
    sent = pack(slot_block, kept_now, got_now, n_grp, slots)
    got = lax.all_to_all(sent, "grp", split_axis=0, concat_axis=0, tiled=True)
    keep = (keep + swap(keep.astype(BF16), "grp", 2).astype(F32)).astype(BF16)
    kept_core = (keep, swap(keep, "grp", 1))
    keep = jnp.concatenate(
        [jnp.where(core == 0, kept_core[0], kept_core[1]), jnp.where(core == 0, kept_core[1], kept_core[0])],
        axis=-1,
    )
    mine = lax.dynamic_slice_in_dim(slot_block, grp * slots, slots, 0)

    def to_tok(value):
        return lax.all_to_all(value, "tok", split_axis=0, concat_axis=0, tiled=True)

    part = to_tok(rotate_in(mine, keep, got, left, n_tok))
    grad_inputs = grad_first + outer_cols(own_grads[0], own_weights)
    (part, home_grads, grad_inputs, more) = together(part, home_grads[1:], grad_inputs, more)
    total = total + more
    more = swap(total, "tok", 4)
    by_slot_of = lambda value: jnp.transpose(value, (1, 0, 2))
    new_one, new_two, turned = moments(
        place, part, right, by_slot_of(moment_one), by_slot_of(moment_two)
    )
    turned = to_tok(turned)
    grad_inputs = grad_inputs + outer_cols(home_grads[0], turned_weights[0])
    grad_inputs = grad_inputs + outer_cols(home_grads[1], turned_weights[1])
    (turned, more, grad_inputs, home_grads[2]) = together(turned, more, grad_inputs, home_grads[2])
    total = total + more
    change = to_tok(rotate_out(turned, left))
    vector_total = total + swap(total, "grp", 2)
    new_master = by_slot_of(apply_change(place, change, by_slot_of(master)))
    new_one, new_two = by_slot_of(new_one), by_slot_of(new_two)
    grad_inputs = grad_inputs + outer_cols(home_grads[2], turned_weights[2])
    new_vec_one = BETA_ONE * vector_one + (1.0 - BETA_ONE) * vector_total
    new_vec_two = BETA_TWO * vector_two + (1.0 - BETA_TWO) * vector_total * vector_total
    new_vectors = vectors - RATE_VECTOR * new_vec_one / (jnp.sqrt(new_vec_two) + ADAM_EPS)
    return (
        result[None],
        grad_inputs[None],
        new_one,
        new_two,
        new_master,
        new_vec_one,
        new_vec_two,
        new_vectors,
    )


def general(
    tokens,
    cotangent,
    lengths,
    clusters,
    owners,
    master,
    bases,
    moment_one,
    moment_two,
    vectors,
    vector_one,
    vector_two,
):
    n_tok = lax.axis_size("tok")
    tok_count = tokens.shape[1]
    rows_dev = master.shape[0]
    slot_block = jnp.argsort(owners, stable=True)
    block_slot = jnp.argsort(slot_block, stable=True)
    slot_part = lax.all_gather(master.astype(jnp.bfloat16), "grp", axis=1, tiled=True)
    weights = lax.all_gather(slot_part, "tok", axis=0, tiled=True)
    blocks = jnp.stack([pick(jnp.transpose(weights, (1, 0, 2)), block_slot[b]) for b in range(weights.shape[1])], axis=1)
    w_qkv = blocks[:, 0:3, :].reshape(D, 3 * D)
    w_out = blocks[:, 3, :]
    w_up = blocks[:, 4 : 4 + FF // D, :].reshape(D, FF)
    w_down = jnp.transpose(blocks[:, 4 + FF // D :, :], (1, 0, 2)).reshape(FF, D)
    inputs = tokens[0]
    gain_one = vectors[0]
    shift_one = vectors[1]
    gain_two = vectors[2]
    shift_two = vectors[3]
    bias_qkv = jnp.concatenate([vectors[4], jnp.zeros((D,), jnp.float32), vectors[5]])
    qkv = (jnp.dot(inputs, w_qkv, preferred_element_type=jnp.float32) + bias_qkv).astype(
        jnp.bfloat16
    )
    heads = jnp.transpose(qkv.reshape(tok_count, 3, H, HEAD), (2, 0, 1, 3)).reshape(
        H, tok_count, 3 * HEAD
    )
    pair_rows = jnp.broadcast_to(heads[None], (ROUNDS, H, tok_count, 3 * HEAD)).reshape(
        PAIRS * tok_count, 3 * HEAD
    )
    position = lax.axis_index("tok") * tok_count + jnp.arange(tok_count, dtype=jnp.int32)
    item_starts = starts_of(lengths[0])
    item_start = jnp.max(
        jnp.where(item_starts[None, :] <= position[:, None], item_starts[None, :], 0), axis=1
    )
    per_dev = tok_count // CLUSTER
    group_clusters = n_tok * per_dev
    pair_ids = jnp.arange(PAIRS, dtype=jnp.int32)[:, None]
    global_cluster = item_start[None, :] // CLUSTER + clusters[0]
    unit_ids = (pair_ids * group_clusters + global_cluster).reshape(-1)
    owner_ids = ((global_cluster + pair_ids * per_dev) % n_tok).reshape(-1)
    send_order = jnp.argsort(owner_ids * (PAIRS * group_clusters) + unit_ids, stable=True)
    restore = jnp.argsort(send_order, stable=True)
    slot_rows = PAIRS * tok_count // n_tok
    units_here = PAIRS * tok_count // CLUSTER
    sent_rows = pair_rows[send_order].reshape(n_tok, slot_rows // 2, 6 * HEAD)
    sent_units = unit_ids[send_order].reshape(n_tok, slot_rows)
    got_rows, got_units = (
        lax.all_to_all(sent_rows, "tok", split_axis=0, concat_axis=0, tiled=True),
        lax.all_to_all(sent_units, "tok", split_axis=0, concat_axis=0, tiled=True),
    )
    arrange = jnp.argsort(got_units.reshape(-1), stable=True)
    undo = jnp.argsort(arrange, stable=True)
    grouped = got_rows.reshape(PAIRS * tok_count, 3 * HEAD)[arrange].reshape(
        units_here, CLUSTER, 3 * HEAD
    )
    query_rows = grouped[..., :HEAD]
    key_rows = grouped[..., HEAD : 2 * HEAD]
    value_rows = grouped[..., 2 * HEAD :]
    score_scale = HEAD ** (-0.5)
    scores = (
        jnp.einsum("ucd,ued->uce", query_rows, key_rows, preferred_element_type=jnp.float32)
        * score_scale
    )
    row_max = jnp.max(scores, axis=-1, keepdims=True)
    row_total = jnp.sum(jnp.exp(scores - row_max), axis=-1, keepdims=True)
    log_total = row_max + jnp.log(row_total)
    probs = jnp.exp(scores - log_total)
    cluster_out = jnp.einsum(
        "uce,ued->ucd", probs.astype(jnp.bfloat16), value_rows, preferred_element_type=jnp.float32
    ).astype(jnp.bfloat16)
    back_rows = cluster_out.reshape(PAIRS * tok_count, HEAD)[undo].reshape(
        n_tok, slot_rows // 2, 2 * HEAD
    )
    home_rows = lax.all_to_all(back_rows, "tok", split_axis=0, concat_axis=0, tiled=True)
    home_rows = (
        home_rows.reshape(PAIRS * tok_count, HEAD)[restore]
        .reshape(ROUNDS, H, tok_count, HEAD)
        .astype(jnp.float32)
    )
    mixed_heads = 0.5 * (home_rows[0] + home_rows[1])
    mixed_low = jnp.transpose(mixed_heads, (1, 0, 2)).reshape(tok_count, D).astype(jnp.bfloat16)
    attention = jnp.dot(mixed_low, w_out, preferred_element_type=jnp.float32) + vectors[6]
    first_sum = inputs.astype(jnp.float32) + attention
    normed_one, rstd_one = normalize(first_sum)
    hidden = normed_one * gain_one + shift_one
    hidden_low = hidden.astype(jnp.bfloat16)
    up_proj = jnp.dot(hidden_low, w_up, preferred_element_type=jnp.float32) + vectors[8:].reshape(
        FF
    )
    act_low = jax.nn.gelu(up_proj, approximate=False).astype(jnp.bfloat16)
    down_proj = jnp.dot(act_low, w_down, preferred_element_type=jnp.float32) + vectors[7]
    second_sum = hidden + down_proj
    normed_two, rstd_two = normalize(second_sum)
    result = (normed_two * gain_two + shift_two).astype(jnp.bfloat16)
    grad_result = cotangent[0].astype(jnp.float32)
    grad_gain_two = jnp.sum(grad_result * normed_two, axis=0)
    grad_shift_two = jnp.sum(grad_result, axis=0)
    grad_second = norm_back(grad_result * gain_two, normed_two, rstd_two)
    grad_down_low = grad_second.astype(jnp.bfloat16)
    grad_w_down = inner_rows(act_low, grad_down_low)
    grad_bias_down = jnp.sum(grad_down_low.astype(jnp.float32), axis=0)
    grad_act = outer_cols(grad_down_low, w_down)
    grad_up_low = (grad_act * gelu_slope(up_proj)).astype(jnp.bfloat16)
    grad_w_up = inner_rows(hidden_low, grad_up_low)
    grad_bias_up = jnp.sum(grad_up_low.astype(jnp.float32), axis=0)
    grad_hidden = grad_second + outer_cols(grad_up_low, w_up)
    grad_gain_one = jnp.sum(grad_hidden * normed_one, axis=0)
    grad_shift_one = jnp.sum(grad_hidden, axis=0)
    grad_first = norm_back(grad_hidden * gain_one, normed_one, rstd_one)
    grad_attn_low = grad_first.astype(jnp.bfloat16)
    grad_w_out = inner_rows(mixed_low, grad_attn_low)
    grad_bias_out = jnp.sum(grad_attn_low.astype(jnp.float32), axis=0)
    grad_mixed = outer_cols(grad_attn_low, w_out)
    grad_heads = jnp.transpose((0.5 * grad_mixed).reshape(tok_count, H, HEAD), (1, 0, 2)).astype(
        jnp.bfloat16
    )
    grad_pairs = jnp.broadcast_to(grad_heads[None], (ROUNDS, H, tok_count, HEAD)).reshape(
        PAIRS * tok_count, HEAD
    )
    sent_grad = grad_pairs[send_order].reshape(n_tok, slot_rows // 2, 2 * HEAD)
    got_grad = lax.all_to_all(sent_grad, "tok", split_axis=0, concat_axis=0, tiled=True)
    grad_cluster = got_grad.reshape(PAIRS * tok_count, HEAD)[arrange].reshape(
        units_here, CLUSTER, HEAD
    )
    scores_again = (
        jnp.einsum("ucd,ued->uce", query_rows, key_rows, preferred_element_type=jnp.float32)
        * score_scale
    )
    probs_again = jnp.exp(scores_again - log_total)
    probs_low = probs_again.astype(jnp.bfloat16)
    grad_values = jnp.einsum(
        "uce,ucd->ued", probs_low, grad_cluster, preferred_element_type=jnp.float32
    )
    grad_probs = jnp.einsum(
        "ucd,ued->uce", grad_cluster, value_rows, preferred_element_type=jnp.float32
    )
    centre = jnp.sum(probs_again * grad_probs, axis=-1, keepdims=True)
    grad_scores = (probs_again * (grad_probs - centre)).astype(jnp.bfloat16)
    grad_query = (
        jnp.einsum("uce,ued->ucd", grad_scores, key_rows, preferred_element_type=jnp.float32)
        * score_scale
    )
    grad_keys = (
        jnp.einsum("uce,ucd->ued", grad_scores, query_rows, preferred_element_type=jnp.float32)
        * score_scale
    )
    grad_grouped = jnp.concatenate(
        [
            grad_query.astype(jnp.bfloat16),
            grad_keys.astype(jnp.bfloat16),
            grad_values.astype(jnp.bfloat16),
        ],
        axis=-1,
    )
    back_grad = grad_grouped.reshape(PAIRS * tok_count, 3 * HEAD)[undo].reshape(
        n_tok, slot_rows // 2, 6 * HEAD
    )
    home_grad = lax.all_to_all(back_grad, "tok", split_axis=0, concat_axis=0, tiled=True)
    home_grad = (
        home_grad.reshape(PAIRS * tok_count, 3 * HEAD)[restore]
        .reshape(ROUNDS, H, tok_count, 3, HEAD)
        .astype(jnp.float32)
    )
    grad_qkv = (home_grad[0] + home_grad[1]).astype(jnp.bfloat16)
    grad_qkv = jnp.transpose(grad_qkv, (1, 2, 0, 3)).reshape(tok_count, 3 * D)
    grad_w_qkv = inner_rows(inputs, grad_qkv)
    grad_bias_qkv = jnp.sum(grad_qkv.astype(jnp.float32), axis=0)
    grad_inputs = grad_first + outer_cols(grad_qkv, w_qkv)
    grad_blocks = jnp.concatenate(
        [
            grad_w_qkv.reshape(D, 3, D),
            grad_w_out[:, None, :],
            grad_w_up.reshape(D, FF // D, D),
            jnp.transpose(grad_w_down.reshape(FF // D, D, D), (1, 0, 2)),
        ],
        axis=1,
    )
    by_block = jnp.transpose(grad_blocks, (1, 0, 2))
    slot_grads = jnp.stack([pick(by_block, slot_block[s]) for s in range(by_block.shape[0])], axis=1)
    vector_grads = jnp.concatenate(
        [
            jnp.stack(
                [
                    grad_gain_one,
                    grad_shift_one,
                    grad_gain_two,
                    grad_shift_two,
                    grad_bias_qkv[:D],
                    grad_bias_qkv[2 * D :],
                    grad_bias_out,
                    grad_bias_down,
                ]
            ),
            grad_bias_up.reshape(FF // D, D),
        ],
        axis=0,
    )
    vector_total = lax.psum(vector_grads, ("tok", "grp"))
    row_total = lax.psum_scatter(slot_grads, "tok", scatter_dimension=0, tiled=True)
    reduced = lax.psum_scatter(
        row_total.astype(jnp.bfloat16), "grp", scatter_dimension=1, tiled=True
    ).astype(jnp.float32)
    left_basis = bases[0]
    right_basis = bases[1]
    first_row = lax.axis_index("tok") * rows_dev
    turned_in = jnp.einsum("rse,sef->rsf", reduced, right_basis, precision=lax.Precision.HIGHEST)
    left_rows = lax.dynamic_slice_in_dim(left_basis, first_row, rows_dev, 1)
    picked = left_rows
    rotated = lax.psum_scatter(
        jnp.einsum("sri,rsf->isf", picked, turned_in, precision=lax.Precision.HIGHEST),
        "tok",
        scatter_dimension=0,
        tiled=True,
    )
    new_one = BETA_ONE * moment_one + (1.0 - BETA_ONE) * rotated
    new_two = BETA_TWO * moment_two + (1.0 - BETA_TWO) * rotated * rotated
    direction = new_one / (jnp.sqrt(new_two) + ADAM_EPS)
    turned_out = jnp.einsum("rse,sfe->rsf", direction, right_basis, precision=lax.Precision.HIGHEST)
    left_cols = lax.dynamic_slice_in_dim(left_basis, first_row, rows_dev, 2)
    picked = left_cols
    change = lax.psum_scatter(
        jnp.einsum("sir,rsf->isf", picked, turned_out, precision=lax.Precision.HIGHEST),
        "tok",
        scatter_dimension=0,
        tiled=True,
    )
    new_master = master - RATE_MATRIX * change
    new_vec_one = BETA_ONE * vector_one + (1.0 - BETA_ONE) * vector_total
    new_vec_two = BETA_TWO * vector_two + (1.0 - BETA_TWO) * vector_total * vector_total
    new_vectors = vectors - RATE_VECTOR * new_vec_one / (jnp.sqrt(new_vec_two) + ADAM_EPS)
    return (
        result[None],
        grad_inputs[None],
        new_one,
        new_two,
        new_master,
        new_vec_one,
        new_vec_two,
        new_vectors,
    )

def solution(mesh):
    n_tok, n_grp = mesh.shape["tok"], mesh.shape["grp"]

    def on_device(*args):
        lengths, clusters = args[2], args[3]
        unit = n_tok // (lengths.shape[1] - 1)
        suits = unit == UNIT and n_tok == 2 * UNIT and n_grp == 4 and clusters.shape[2] == 1024
        return (fast if suits else general)(*args)

    return jax.shard_map(
        on_device,
        mesh=mesh,
        in_specs=(
            P("grp", "tok", None),
            P("grp", "tok", None),
            P("grp", None),
            P("grp", None, "tok"),
            P(),
            P("tok", "grp", None),
            P(None, "grp", None, None),
            P("tok", "grp", None),
            P("tok", "grp", None),
            P(),
            P(),
            P(),
        ),
        out_specs=(
            P("grp", "tok", None),
            P("grp", "tok", None),
            P("tok", "grp", None),
            P("tok", "grp", None),
            P("tok", "grp", None),
            P(),
            P(),
            P(),
        ),
        check_vma=False,
    )
```
